32 devices in a mesh: fsdp: 8 (over z, x), ctx: 4 (over y, core).
Axes of the slice: x: 2, y: 2, z: 4, core: 2. Of those that a mesh axis runs over, the one named last changes fastest.
Arguments:
- inputs: bfloat16 [8, 1024, 2048], P('fsdp', 'ctx'), may hold values from -6 to 6
- cotangent: bfloat16 [8, 1024, 2048], P('fsdp', 'ctx'), may hold values from -6 to 6
- lengths: int32 [8], P('fsdp'), may hold values from 1024 to 1024, as said below
- qkv_weight: bfloat16 [2048, 1536], P('fsdp'), may hold values from -0.125 to 0.125
- out_weight: bfloat16 [1024, 2048], P('fsdp'), may hold values from -3 to 3
- gate_up: bfloat16 [2048, 2, 4096], P('fsdp'), may hold values from -0.125 to 0.125
- down_weight: bfloat16 [4096, 2048], P('fsdp'), may hold values from -0.09375 to 0.09375
- attn_gain: bfloat16 [2048], P('fsdp'), may hold values from 0.5 to 1.5
- ffn_gain: bfloat16 [2048], P('fsdp'), may hold values from 0.5 to 1.5
- qk_gain: bfloat16 [2, 64], replicated, may hold values from 0.5 to 1.5
Outputs:
- layer_out: bfloat16 [8, 1024, 2048], P('fsdp', 'ctx')
- input_grad: bfloat16 [8, 1024, 2048], P('fsdp', 'ctx')
- qkv_grad: float32 [2048, 1536], P('fsdp')
- out_grad: float32 [1024, 2048], P('fsdp')
- gate_up_grad: float32 [2048, 2, 4096], P('fsdp')
- down_grad: float32 [4096, 2048], P('fsdp')
- attn_gain_grad: float32 [2048], P('fsdp')
- ffn_gain_grad: float32 [2048], P('fsdp')
- qk_gain_grad: float32 [2, 64], replicated
The draws below stay inside these ranges and needn't reach their ends.
Inputs may be any that keep to these rules, and one draw needn't show every extreme that they name: `lengths`: valid length of each slot; some slot is full, of length 1024.
All inputs are finite; a program needn't handle non-finite values.
Results may differ from the reference program's by a relative error of at most 0.02.
Values may be sent and summed in bfloat16 or wider, within the bound.
A program may use at most 384 MiB of HBM per device.

```python
import math
import jax
import jax.numpy as jnp
from jax import lax

D = 2048
HEADS = 16
KV_HEADS = 4
HEAD_DIM = 64
FF = 4096
MIN_LEN = 1024
SEQ = 1024
SLOTS = 8
QKV = 1536


def draw_lengths(key, part):
    first_key, second_key = jax.random.split(key)
    drawn = jax.random.randint(first_key, (SLOTS,), MIN_LEN, SEQ + 1)
    chosen = jax.random.randint(second_key, (), 0, SLOTS)
    return jnp.where(jnp.arange(SLOTS) == chosen, SEQ, drawn).astype(jnp.int32)


def block_levels(rng, extent, cuts, low, high):
    def one(axis_at, shards_of):
        heights = jax.random.uniform(jax.random.fold_in(jax.random.fold_in(rng, 6), axis_at), (shards_of,), jnp.float32, low / len(cuts), high / len(cuts))
        return jnp.repeat(jnp.exp(heights), extent[axis_at] // shards_of).reshape((-1,) + (1,) * (len(extent) - axis_at - 1))

    loudness = one(*cuts[0])
    for cut in cuts[1:]:
        loudness = loudness * one(*cut)
    return loudness


def gaussian(stream_key, dims, deviation, most, cuts=(), kind=jnp.bfloat16):
    entries = jax.random.normal(stream_key, dims, jnp.float32) * deviation
    if len(cuts) > 0:
        entries = block_levels(stream_key, dims, cuts, -0.22, 0.18) * entries
    return jnp.clip(entries, min=-most, max=most).astype(kind)


def setup_inputs(seed: int = 0) -> dict:
    streams_of = jax.random.split(jax.random.key(seed), 11)
    inputs = gaussian(streams_of[0], (SLOTS, SEQ, D), 1.0, 6.0, ((0, 8), (1, 4)))
    cotangent = gaussian(streams_of[1], (SLOTS, SEQ, D), 1.0, 6.0, ((0, 8), (1, 4)))
    lengths = draw_lengths(jax.random.fold_in(streams_of[10], 71), 0)
    qkv_weight = gaussian(streams_of[3], (D, QKV), D ** -0.5, 0.125, ((0, 8),))
    out_weight = gaussian(streams_of[4], (HEADS * HEAD_DIM, D), 4 ** -0.5, 3.0, ((0, 8),))
    gate_up = gaussian(streams_of[5], (D, 2, FF), D ** -0.5, 0.125, ((0, 8),))
    down_weight = gaussian(streams_of[6], (FF, D), FF ** -0.5, 0.09375, ((0, 8),))
    attn_gain = jnp.clip(1.0 + 0.1 * jax.random.normal(streams_of[7], (D,), jnp.float32), 0.5, 1.5).astype(jnp.bfloat16)
    ffn_gain = jnp.clip(1.0 + 0.1 * jax.random.normal(streams_of[8], (D,), jnp.float32), 0.5, 1.5).astype(jnp.bfloat16)
    qk_gain = jnp.clip(1.0 + 0.1 * jax.random.normal(streams_of[9], (2, HEAD_DIM), jnp.float32), 0.5, 1.5).astype(jnp.bfloat16)
    return {"inputs": inputs, "cotangent": cotangent, "lengths": lengths, "qkv_weight": qkv_weight, "out_weight": out_weight, "gate_up": gate_up, "down_weight": down_weight, "attn_gain": attn_gain, "ffn_gain": ffn_gain, "qk_gain": qk_gain}


EPSILON = 1e-06
HIGHEST = lax.Precision.HIGHEST

@jax.custom_vjp
def low(v):
    return lax.optimization_barrier(v.astype(jnp.bfloat16)).astype(jnp.float32)

@jax.custom_vjp
def low_back(v):
    return v

def low_keep(v):
    return (low(v), None)

def low_pass(kept, grad):
    return (grad,)

def back_keep(v):
    return (v, None)

def back_low(kept, grad):
    return (low(grad),)
low.defvjp(low_keep, low_pass)
low_back.defvjp(back_keep, back_low)

def root_norm(values, norm_gain):
    factor = lax.rsqrt(lax.optimization_barrier(jnp.mean(values * values, axis=-1, keepdims=True)) + EPSILON)
    return values * factor * norm_gain

def rotation_tables(positions):
    half_dim = HEAD_DIM // 2
    frequency = 10000.0 ** (-(2.0 * jnp.arange(half_dim, dtype=jnp.float32)) / HEAD_DIM)
    angles = positions.astype(jnp.float32)[:, None] * frequency[None, :]
    return (jnp.cos(angles), jnp.sin(angles))

def rotate(values, cos_table, sin_table):
    half_dim = values.shape[-1] // 2
    lower_half = values[..., :half_dim]
    upper_half = values[..., half_dim:]
    cos_part = cos_table[:, None, :]
    sin_part = sin_table[:, None, :]
    return jnp.concatenate([lower_half * cos_part - upper_half * sin_part, upper_half * cos_part + lower_half * sin_part], axis=-1)

def prepare_heads(qkv_out, head_gain, cos_table, sin_table):
    row_count = qkv_out.shape[0]
    query_cols = HEADS * HEAD_DIM
    key_cols = KV_HEADS * HEAD_DIM
    queries = qkv_out[:, :query_cols].reshape(row_count, HEADS, HEAD_DIM)
    key_part = qkv_out[:, query_cols:query_cols + key_cols].reshape(row_count, KV_HEADS, HEAD_DIM)
    value_part = qkv_out[:, query_cols + key_cols:]
    queries = rotate(root_norm(queries, head_gain[0]), cos_table, sin_table).reshape(row_count, query_cols)
    key_part = rotate(root_norm(key_part, head_gain[1]), cos_table, sin_table).reshape(row_count, key_cols)
    return (queries, key_part, value_part)

def activate(projected):
    gate_part = projected[:, 0]
    return gate_part * jax.nn.sigmoid(gate_part) * projected[:, 1]

def attend(query_use, key_use, value_use, length):
    group = HEADS // KV_HEADS
    block = 512 if SEQ % 512 == 0 else SEQ
    query_blocks = query_use.reshape(SEQ // block, block, KV_HEADS, group, HEAD_DIM)
    key_heads = key_use.reshape(SEQ, KV_HEADS, HEAD_DIM)
    value_heads = value_use.reshape(SEQ, KV_HEADS, HEAD_DIM)
    starts = jnp.arange(SEQ // block, dtype=jnp.int32) * block
    key_pos = jnp.arange(SEQ, dtype=jnp.int32)
    inv_root = 1.0 / math.sqrt(HEAD_DIM)

    def one_block(item):
        query_block, block_start = item
        scores = jnp.einsum('bhgd,thd->hgbt', query_block, key_heads, precision=HIGHEST) * inv_root
        query_pos = block_start + jnp.arange(block, dtype=jnp.int32)
        visible = (key_pos[None, :] <= query_pos[:, None]) & (key_pos[None, :] < length)
        scores = low_back(jnp.where(visible, scores, -1e+30))
        top_score = lax.optimization_barrier(jnp.max(scores, axis=-1, keepdims=True))
        expanded = jnp.exp(scores - top_score)
        probs = expanded / lax.optimization_barrier(jnp.sum(expanded, axis=-1, keepdims=True))
        return jnp.einsum('hgbt,thd->bhgd', low(probs), value_heads, precision=HIGHEST)
    attended = lax.map(jax.checkpoint(one_block), (query_blocks, starts))
    return attended.reshape(SEQ, HEADS * HEAD_DIM)

def slot_layer(weights, source, length):
    qkv_weight, out_weight, gate_up, down_weight, attn_gain, ffn_gain, qk_gain = weights
    positions = jnp.arange(SEQ, dtype=jnp.int32)
    row_keep = (positions < length).astype(source.dtype)[:, None]
    normed = low(root_norm(source, attn_gain))
    qkv_out = low_back(jnp.dot(normed, qkv_weight, precision=HIGHEST))
    cos_table, sin_table = rotation_tables(positions)
    queries, key_part, value_part = prepare_heads(qkv_out, qk_gain, cos_table, sin_table)
    query_use = low_back(low(queries))
    key_use = low_back(low(key_part))
    value_use = low_back(low(value_part))
    attended = attend(query_use, key_use, value_use, length)
    attended_use = low_back(low(attended))
    branch = low_back(jnp.dot(attended_use, out_weight, precision=HIGHEST))
    middle = source + branch
    normed_mid = low(root_norm(middle, ffn_gain))
    projected = low_back(jnp.einsum('td,dgf->tgf', normed_mid, gate_up, precision=HIGHEST))
    hidden = low(activate(projected))
    return row_keep * (middle + jnp.dot(hidden, down_weight, precision=HIGHEST))

def reference(inputs, cotangent, lengths, qkv_weight, out_weight, gate_up, down_weight, attn_gain, ffn_gain, qk_gain):
    weights = tuple((weight_arr.astype(jnp.float32) for weight_arr in (qkv_weight, out_weight, gate_up, down_weight, attn_gain, ffn_gain, qk_gain)))

    def forward(source_all, weight_set):

        def one_slot(carried, item):
            source, length = item
            return (carried, slot_layer(weight_set, source, length))
        carried, outputs = lax.scan(jax.checkpoint(one_slot), jnp.zeros((), jnp.float32), (source_all, lengths))
        return outputs
    layer_out, pull_back = jax.vjp(forward, inputs.astype(jnp.float32), weights)
    input_grad, weight_grads = pull_back(cotangent.astype(jnp.float32))
    return (layer_out.astype(jnp.bfloat16), input_grad.astype(jnp.bfloat16), weight_grads[0], weight_grads[1], weight_grads[2], weight_grads[3], weight_grads[4], weight_grads[5], weight_grads[6])
```

```python
import functools
import math

import jax
import jax.numpy as jnp
import numpy as np
from jax import lax
from jax.experimental import pallas as pl
from jax.experimental.pallas import tpu as pltpu
from jax.sharding import PartitionSpec as P

HEADS = 16
KV_HEADS = 4
HEAD_DIM = 64


EPSILON = 1e-06


def root_norm(values, norm_gain):
    factor = lax.rsqrt(jnp.mean(values * values, axis=-1, keepdims=True) + EPSILON)
    return values * factor * norm_gain


def rotation_tables(positions):
    half_dim = HEAD_DIM // 2
    frequency = 10000.0 ** (-(2.0 * jnp.arange(half_dim, dtype=jnp.float32)) / HEAD_DIM)
    angles = positions.astype(jnp.float32)[:, None] * frequency[None, :]
    return (jnp.cos(angles), jnp.sin(angles))


def rotate(values, cos_table, sin_table):
    half_dim = values.shape[-1] // 2
    lower_half = values[..., :half_dim]
    upper_half = values[..., half_dim:]
    cos_part = cos_table[:, None, :]
    sin_part = sin_table[:, None, :]
    return jnp.concatenate(
        [
            lower_half * cos_part - upper_half * sin_part,
            upper_half * cos_part + lower_half * sin_part,
        ],
        axis=-1,
    )


def prepare_heads(qkv_out, head_gain, cos_table, sin_table):
    row_count = qkv_out.shape[0]
    query_cols = HEADS * HEAD_DIM
    key_cols = KV_HEADS * HEAD_DIM
    queries = qkv_out[:, :query_cols].reshape(row_count, HEADS, HEAD_DIM)
    key_part = qkv_out[:, query_cols : query_cols + key_cols].reshape(row_count, KV_HEADS, HEAD_DIM)
    value_part = qkv_out[:, query_cols + key_cols :]
    queries = rotate(root_norm(queries, head_gain[0]), cos_table, sin_table).reshape(
        row_count, query_cols
    )
    key_part = rotate(root_norm(key_part, head_gain[1]), cos_table, sin_table).reshape(
        row_count, key_cols
    )
    return (queries, key_part, value_part)


def activate(projected):
    gate_part = projected[:, 0]
    return gate_part * jax.nn.sigmoid(gate_part) * projected[:, 1]


def contract_rows(left, right):
    return lax.dot_general(
        left, right, (((0,), (0,)), ((), ())), preferred_element_type=jnp.float32
    )


def contract_cols(left, right):
    return lax.dot_general(
        left, right, (((1,), (1,)), ((), ())), preferred_element_type=jnp.float32
    )


def on_device(
    inputs,
    cotangent,
    lengths,
    qkv_weight,
    out_weight,
    gate_up,
    down_weight,
    attn_gain,
    ffn_gain,
    qk_gain,
):
    token_count = inputs.shape[1]
    group = HEADS // KV_HEADS
    key_cols = KV_HEADS * HEAD_DIM
    seq_len = token_count * lax.axis_size("ctx")
    positions = lax.axis_index("ctx") * token_count + jnp.arange(token_count, dtype=jnp.int32)
    length = lengths[0]
    row_keep = (positions < length).astype(jnp.float32)[:, None]
    inv_root = 1.0 / math.sqrt(HEAD_DIM)
    source = inputs[0].astype(jnp.float32)
    qkv_full, out_full, attn_full, ffn_full = (
        lax.all_gather(qkv_weight, "fsdp", axis=0, tiled=True),
        lax.all_gather(out_weight, "fsdp", axis=0, tiled=True),
        lax.all_gather(attn_gain, "fsdp", axis=0, tiled=True),
        lax.all_gather(ffn_gain, "fsdp", axis=0, tiled=True),
    )
    attn_norm = attn_full.astype(jnp.float32)
    ffn_norm = ffn_full.astype(jnp.float32)
    normed = root_norm(source, attn_norm).astype(jnp.bfloat16)
    qkv_out = jnp.dot(normed, qkv_full, preferred_element_type=jnp.float32)
    cos_table, sin_table = rotation_tables(positions)
    head_gain = qk_gain.astype(jnp.float32)

    def head_pieces(qkv_values, gain_values):
        return prepare_heads(qkv_values, gain_values, cos_table, sin_table)

    head_values, head_pull = jax.vjp(head_pieces, qkv_out, head_gain)
    queries, key_part, value_part = head_values
    query_low = queries.astype(jnp.bfloat16).reshape(token_count, KV_HEADS, group, HEAD_DIM)
    kv_local = jnp.concatenate([key_part, value_part], axis=1).astype(jnp.bfloat16)
    kv_whole = lax.all_gather(kv_local, "ctx", axis=0, tiled=True)
    block = 512
    block_total = seq_len // block
    kv_blocks = kv_whole.reshape(block_total, block, 2, KV_HEADS, HEAD_DIM)
    starts = jnp.arange(block_total, dtype=jnp.int32) * block

    def block_scores(key_block, block_start):
        scores = (
            jnp.einsum("bhgd,thd->hgbt", query_low, key_block, preferred_element_type=jnp.float32)
            * inv_root
        )
        key_pos = block_start + jnp.arange(key_block.shape[0], dtype=jnp.int32)
        visible = (key_pos[None, :] <= positions[:, None]) & (key_pos[None, :] < length)
        return (scores, visible)

    def max_step(state, item):
        running_max, running_sum = state
        kv_block, block_start = item
        scores, visible = block_scores(kv_block[:, 0], block_start)
        new_max = jnp.maximum(running_max, jnp.max(jnp.where(visible, scores, -1e30), axis=-1))
        expanded = jnp.where(visible, jnp.exp(scores - new_max[..., None]), 0.0)
        running_sum = running_sum * jnp.exp(running_max - new_max) + jnp.sum(expanded, axis=-1)
        return ((new_max, running_sum), None)

    stat_shape = (KV_HEADS, group, token_count)
    start_state = (jnp.full(stat_shape, -1e30, jnp.float32), jnp.zeros(stat_shape, jnp.float32))
    final_state, unused_out = lax.scan(max_step, start_state, (kv_blocks, starts))
    log_total = final_state[0] + jnp.log(final_state[1])

    def block_probs(kv_block, block_start):
        scores, visible = block_scores(kv_block[:, 0], block_start)
        return jnp.where(visible, jnp.exp(scores - log_total[..., None]), 0.0)

    def value_step(totals, item):
        kv_block, block_start = item
        probs_low = block_probs(kv_block, block_start).astype(jnp.bfloat16)
        return (
            totals
            + jnp.einsum(
                "hgbt,thd->bhgd", probs_low, kv_block[:, 1], preferred_element_type=jnp.float32
            ),
            None,
        )

    attended, unused_out = lax.scan(
        value_step,
        jnp.zeros((token_count, KV_HEADS, group, HEAD_DIM), jnp.float32),
        (kv_blocks, starts),
    )
    attended_low = attended.reshape(token_count, HEADS * HEAD_DIM).astype(jnp.bfloat16)
    middle = source + jnp.dot(attended_low, out_full, preferred_element_type=jnp.float32)
    normed_mid = root_norm(middle, ffn_norm).astype(jnp.bfloat16)
    columns = normed_mid
    projected = jnp.einsum(
        "td,dgf->tgf",
        columns,
        lax.all_gather(gate_up, "fsdp", axis=0, tiled=True),
        preferred_element_type=jnp.float32,
    )
    act_value, act_pull = jax.vjp(activate, projected)
    hidden = act_value.astype(jnp.bfloat16)
    columns = hidden
    ffn_out = jnp.dot(
        columns,
        lax.all_gather(down_weight, "fsdp", axis=0, tiled=True),
        preferred_element_type=jnp.float32,
    )
    layer_out = (row_keep * (middle + ffn_out)).astype(jnp.bfloat16)[None]
    d_out = row_keep * cotangent[0].astype(jnp.float32)
    d_out_low = d_out.astype(jnp.bfloat16)
    down_shard = lax.psum_scatter(
        contract_rows(hidden, d_out_low).astype(jnp.bfloat16),
        "fsdp",
        scatter_dimension=0,
        tiled=True,
    )
    d_hidden = contract_cols(d_out_low, lax.all_gather(down_weight, "fsdp", axis=0, tiled=True))
    d_proj_low = act_pull(d_hidden)[0].astype(jnp.bfloat16)
    columns = normed_mid
    gate_up_shard = lax.psum_scatter(
        jnp.einsum("td,tgf->dgf", columns, d_proj_low, preferred_element_type=jnp.float32).astype(
            jnp.bfloat16
        ),
        "fsdp",
        scatter_dimension=0,
        tiled=True,
    )
    d_normed_mid = jnp.einsum(
        "tgf,dgf->td",
        d_proj_low,
        lax.all_gather(gate_up, "fsdp", axis=0, tiled=True),
        preferred_element_type=jnp.float32,
    )
    mid_value, mid_pull = jax.vjp(root_norm, middle, ffn_norm)
    d_mid_norm, ffn_gain_part = mid_pull(d_normed_mid)
    d_middle = d_out + d_mid_norm
    d_branch = d_middle.astype(jnp.bfloat16)
    out_term = contract_rows(attended_low, d_branch)
    d_attended = (
        contract_cols(d_branch, out_full)
        .astype(jnp.bfloat16)
        .reshape(token_count, KV_HEADS, group, HEAD_DIM)
    )
    delta = jnp.transpose(jnp.sum(d_attended.astype(jnp.float32) * attended, axis=-1), (1, 2, 0))

    def block_grads(kv_block, block_start):
        probs = block_probs(kv_block, block_start)
        d_probs = jnp.einsum(
            "bhgd,thd->hgbt", d_attended, kv_block[:, 1], preferred_element_type=jnp.float32
        )
        d_scores = (probs * (d_probs - delta[..., None])).astype(jnp.bfloat16)
        return (probs.astype(jnp.bfloat16), d_scores)

    def query_step(totals, item):
        kv_block, block_start = item
        probs_low, d_scores = block_grads(kv_block, block_start)
        return (
            totals
            + jnp.einsum(
                "hgbt,thd->bhgd", d_scores, kv_block[:, 0], preferred_element_type=jnp.float32
            ),
            None,
        )

    d_query_sum, unused_out = lax.scan(
        query_step,
        jnp.zeros((token_count, KV_HEADS, group, HEAD_DIM), jnp.float32),
        (kv_blocks, starts),
    )
    d_query = (d_query_sum * inv_root).reshape(token_count, HEADS * HEAD_DIM).astype(jnp.bfloat16)
    sub_block = 512
    sub_total = token_count * lax.axis_size("ctx") // sub_block
    pieces = kv_whole.reshape(sub_total, sub_block, 2, KV_HEADS, HEAD_DIM)
    sub_starts = jnp.arange(sub_total, dtype=jnp.int32) * sub_block

    def key_grads(item):
        kv_block, block_start = item
        probs_low, d_scores = block_grads(kv_block, block_start)
        d_keys = (
            jnp.einsum("hgbt,bhgd->thd", d_scores, query_low, preferred_element_type=jnp.float32)
            * inv_root
        )
        d_values = jnp.einsum(
            "hgbt,bhgd->thd", probs_low, d_attended, preferred_element_type=jnp.float32
        )
        return jnp.concatenate(
            [d_keys.reshape(sub_block, key_cols), d_values.reshape(sub_block, key_cols)], axis=1
        )

    kv_grad = lax.psum_scatter(
        lax.map(key_grads, (pieces, sub_starts))
        .reshape(token_count * lax.axis_size("ctx"), 2 * key_cols)
        .astype(jnp.bfloat16),
        "ctx",
        scatter_dimension=0,
        tiled=True,
    ).astype(jnp.float32)
    d_key_low = kv_grad[:, :key_cols].astype(jnp.bfloat16).astype(jnp.float32)
    d_value_low = kv_grad[:, key_cols:].astype(jnp.bfloat16).astype(jnp.float32)
    d_qkv_out, qk_part = head_pull((d_query.astype(jnp.float32), d_key_low, d_value_low))
    d_qkv = d_qkv_out.astype(jnp.bfloat16)
    qkv_term = contract_rows(normed, d_qkv)
    d_normed = contract_cols(d_qkv, qkv_full)
    first_value, first_pull = jax.vjp(root_norm, source, attn_norm)
    d_source_norm, attn_gain_part = first_pull(d_normed)
    input_grad = (d_middle + d_source_norm).astype(jnp.bfloat16)[None]
    qkv_shard, out_shard, attn_shard, ffn_shard = (
        lax.psum_scatter(
            qkv_term.astype(jnp.bfloat16), "fsdp", scatter_dimension=0, tiled=True
        ).astype(jnp.float32),
        lax.psum_scatter(
            out_term.astype(jnp.bfloat16), "fsdp", scatter_dimension=0, tiled=True
        ).astype(jnp.float32),
        lax.psum_scatter(
            attn_gain_part.astype(jnp.bfloat16), "fsdp", scatter_dimension=0, tiled=True
        ).astype(jnp.float32),
        lax.psum_scatter(
            ffn_gain_part.astype(jnp.bfloat16), "fsdp", scatter_dimension=0, tiled=True
        ).astype(jnp.float32),
    )
    summed = (
        lax.psum(qkv_shard.astype(jnp.bfloat16), "ctx").astype(jnp.float32),
        lax.psum(out_shard.astype(jnp.bfloat16), "ctx").astype(jnp.float32),
        lax.psum(gate_up_shard, "ctx").astype(jnp.float32),
        lax.psum(down_shard, "ctx").astype(jnp.float32),
        lax.psum(attn_shard.astype(jnp.bfloat16), "ctx").astype(jnp.float32),
        lax.psum(ffn_shard.astype(jnp.bfloat16), "ctx").astype(jnp.float32),
    )
    qk_total = lax.psum(qk_part, ("fsdp", "ctx"))
    return (
        layer_out,
        input_grad,
        summed[0],
        summed[1],
        summed[2],
        summed[3],
        summed[4],
        summed[5],
        qk_total,
    )


MESH = pl.DeviceIdType.MESH
F32 = jnp.float32
BF16 = jnp.bfloat16
VMEM_BYTES = 56 << 20
HBM = pl.BlockSpec(memory_space=pl.ANY)
VMEM = pl.BlockSpec(memory_space=pltpu.VMEM)


class Place:
    def __init__(self):
        self.f = lax.axis_index("fsdp")
        self.c = lax.axis_index("ctx")
        self.z, self.x = lax.div(self.f, 2), lax.rem(self.f, 2)
        self.y, self.core = lax.div(self.c, 2), lax.rem(self.c, 2)
        self.xo, self.yo, self.co = 1 - self.x, 1 - self.y, 1 - self.core
        upper = lax.div(self.z, 2)
        self.others = (self.z + 1 - 2 * lax.rem(self.z, 2), 2 - upper, 3 - 3 * upper)
        self.x_dev = (self.z * 2 + self.xo, self.c)
        self.c_core = self.y * 2 + self.co
        self.c_y = self.yo * 2 + self.core
        self.c_diag = self.yo * 2 + self.co
        self.core_dev = (self.f, self.c_core)
        self.y_dev = (self.f, self.c_y)
        self.diag_dev = (self.f, self.c_diag)

    def z_dev(self, z):
        return (z * 2 + self.x, self.c)

    def meet(self, partners):
        barrier = pltpu.get_barrier_semaphore()
        for partner in partners:
            pl.semaphore_signal(barrier, inc=1, device_id=partner, device_id_type=MESH)
        pl.semaphore_wait(barrier, len(partners))

    def neighbours(self):
        return [self.z_dev(o) for o in self.others] + [self.x_dev, self.core_dev, self.y_dev]


class Links:
    def __init__(self, place, send_sems, recv_sems, local_sems):
        self.place = place
        self.send_sems, self.recv_sems, self.local_sems = send_sems, recv_sems, local_sems
        self.sends = self.recvs = self.locals = 0
        self.open = []

    def slots(self, count):
        first = self.recvs
        self.recvs += count
        return first

    def copy(self, src, dst, slot, device):
        made = pltpu.make_async_remote_copy(
            src_ref=src,
            dst_ref=dst,
            send_sem=self.send_sems.at[self.sends],
            recv_sem=self.recv_sems.at[slot],
            device_id=device,
            device_id_type=MESH,
        )
        self.sends += 1
        return made

    def send(self, src, dst, slot, device):
        made = self.copy(src, dst, slot, device)
        made.start()
        self.open.append(made)

    def arrive(self, ref, slot):
        pltpu.make_async_remote_copy(
            src_ref=ref,
            dst_ref=ref,
            send_sem=self.send_sems.at[0],
            recv_sem=self.recv_sems.at[slot],
            device_id=self.place.x_dev,
            device_id_type=MESH,
        ).wait_recv()

    def local(self, src, dst):
        made = pltpu.make_async_copy(src, dst, self.local_sems.at[self.locals])
        self.locals += 1
        made.start()
        return made

    def finish(self):
        for made in self.open:
            made.wait_send()
        self.open = []


def spread_plane(links, place, chunks, ahead=2):
    z_slot, x_slot = links.slots(4 * len(chunks)), links.slots(4 * len(chunks))

    def begin(k):
        src, dst = chunks[k]
        for other in place.others:
            links.send(src, dst(place.f), z_slot + 4 * k + place.z, place.z_dev(other))
        links.send(src, dst(place.f), x_slot + 4 * k + place.z, place.x_dev)

    for k in range(min(ahead, len(chunks))):
        begin(k)
    yield
    for k in range(len(chunks)):
        dst = chunks[k][1]
        for other in place.others:
            block = dst(other * 2 + place.x)
            links.arrive(block, z_slot + 4 * k + other)
            links.send(block, block, x_slot + 4 * k + other, place.x_dev)
        if k + ahead < len(chunks):
            begin(k + ahead)
        yield
    for k in range(len(chunks)):
        for z in range(4):
            links.arrive(chunks[k][1](z * 2 + place.xo), x_slot + 4 * k + z)
    yield


def reduce_plane(links, place, chunks, own, from_x, to_z, from_z, total, done, ahead=2):
    count = len(chunks)
    x_slot, z_slot = links.slots(count), links.slots(4 * count)
    loads = {}

    def begin(k):
        links.send(chunks[k](place.xo), from_x.at[k], x_slot + k, place.x_dev)
        loads[k] = links.local(chunks[k](place.x), own.at[k])

    def middle(k):
        links.arrive(from_x.at[k], x_slot + k)
        loads[k].wait()
        for other in place.others:
            pair = own[k, other].astype(F32) + from_x[k, other].astype(F32)
            to_z[k, other] = pair.astype(BF16)
            links.send(
                to_z.at[k, other],
                from_z.at[k, place.z],
                z_slot + 4 * k + place.z,
                place.z_dev(other),
            )

    def end(k):
        sums = own[k, place.z].astype(F32) + from_x[k, place.z].astype(F32)
        for other in place.others:
            links.arrive(from_z.at[k, other], z_slot + 4 * k + other)
            sums += from_z[k, other].astype(F32)
        total[k] = sums.astype(BF16)
        done(k)

    for k in range(min(ahead, count)):
        begin(k)
    yield
    for k in range(count + 1):
        if k < count:
            middle(k)
            if k + ahead < count:
                begin(k + ahead)
            yield
        if k >= 1:
            end(k - 1)
            yield


class SpreadCtx:
    def __init__(self, links, place, out, parts):
        self.links, self.place, self.out, self.parts = links, place, out, parts
        self.slot = links.slots(3 * len(parts))

    def begin(self, k, src, y_too=True):
        place, rows = self.place, self.parts[k]
        self.links.send(src, self.out.at[place.c, rows], self.slot + 3 * k, place.core_dev)
        if y_too:
            self.begin_y(k, src)

    def begin_y(self, k, src):
        place, rows = self.place, self.parts[k]
        self.links.send(src, self.out.at[place.c, rows], self.slot + 3 * k + 1, place.y_dev)

    def forward(self, k):
        place = self.place
        block = self.out.at[place.c_y, self.parts[k]]
        self.links.arrive(block, self.slot + 3 * k + 1)
        self.links.send(block, block, self.slot + 3 * k + 2, place.core_dev)

    def end(self):
        place = self.place
        for k, rows in enumerate(self.parts):
            self.links.arrive(self.out.at[place.c_core, rows], self.slot + 3 * k)
            self.links.arrive(self.out.at[place.c_diag, rows], self.slot + 3 * k + 2)


class ReduceCtx:
    def __init__(self, links, place, part, parts, own, from_core, to_y, from_y):
        self.links, self.place, self.part, self.parts = links, place, part, parts
        self.own, self.from_core, self.to_y, self.from_y = own, from_core, to_y, from_y
        self.slot = links.slots(3 * len(parts))
        self.loads = {}

    def begin(self):
        place = self.place
        for side, y in ((0, place.yo), (1, place.y)):
            for k, rows in enumerate(self.parts):
                self.links.send(
                    self.part.at[y * 2 + place.co, rows],
                    self.from_core.at[side, rows],
                    self.slot + 3 * k + side,
                    place.core_dev,
                )
                self.loads[side, k] = self.links.local(
                    self.part.at[y * 2 + place.core, rows], self.own.at[side, rows]
                )

    def pair(self, side, k):
        rows = self.parts[k]
        self.links.arrive(self.from_core.at[side, rows], self.slot + 3 * k + side)
        self.loads[side, k].wait()
        return self.own[side, rows].astype(F32) + self.from_core[side, rows].astype(F32)

    def cross(self, k):
        rows = self.parts[k]
        self.to_y[rows] = self.pair(0, k).astype(BF16)
        self.links.send(
            self.to_y.at[rows], self.from_y.at[rows], self.slot + 3 * k + 2, self.place.y_dev
        )

    def total(self, k):
        rows = self.parts[k]
        sums = self.pair(1, k)
        self.links.arrive(self.from_y.at[rows], self.slot + 3 * k + 2)
        return sums + self.from_y[rows].astype(F32)


def halves(rows):
    return [pl.ds(0, rows // 2), pl.ds(rows // 2, rows // 2)]


def row_factor(values):
    return lax.rsqrt(jnp.mean(values * values, axis=-1, keepdims=True) + EPSILON)


def gather_kernel(
    qkv_s, out_s, gain_s, x_s, qkv_w, out_w, gains, x_all, send_sems, recv_sems, local_sems
):
    place = Place()
    links = Links(place, send_sems, recv_sems, local_sems)
    fellows = [lax.rem(place.f + d, 8) for d in range(1, 8)]
    place.meet([(f, place.c) for f in fellows] + [place.core_dev, place.y_dev])
    plane = spread_plane(links, place, [(qkv_s, lambda f: qkv_w.at[f])])
    next(plane)
    kept = [
        links.local(qkv_s, qkv_w.at[place.f]),
        links.local(gain_s, gains.at[place.f]),
        links.local(x_s, x_all.at[place.c]),
    ]
    parts = halves(x_s.shape[0])
    spread = SpreadCtx(links, place, x_all, parts)
    for k, rows in enumerate(parts):
        spread.begin(k, x_s.at[rows])
    gain_slot = links.slots(8)
    for f in fellows:
        links.send(gain_s, gains.at[place.f], gain_slot + place.f, (f, place.c))

    root_slot, side_slot = links.slots(1), links.slots(1)
    holds = place.z == place.c
    down = [
        links.copy(out_s, out_w.at[place.x], root_slot, place.z_dev(other))
        for other in place.others
    ]
    side = links.copy(out_s, out_w.at[place.x], side_slot, place.x_dev)
    onward = links.copy(out_w.at[place.x], out_w.at[place.x], side_slot, place.x_dev)
    own = pltpu.make_async_copy(out_s, out_w.at[place.x], local_sems.at[links.locals])
    links.locals += 1

    @pl.when(holds)
    def _():
        for made in down:
            made.start()
        side.start()
        own.start()

    next(plane)
    for k in range(len(parts)):
        spread.forward(k)

    @pl.when(jnp.logical_not(holds))
    def _():
        links.arrive(out_w.at[place.x], root_slot)
        onward.start()

    for f in fellows:
        links.arrive(gains.at[f], gain_slot + f)
    next(plane)
    spread.end()
    links.arrive(out_w.at[place.xo], side_slot)
    for made in kept:
        made.wait()
    links.finish()

    @pl.when(holds)
    def _():
        own.wait()
        for made in down:
            made.wait_send()
        side.wait_send()

    @pl.when(jnp.logical_not(holds))
    def _():
        onward.wait_send()


def feed_gather_kernel(
    gu_s, dn_s, dout_s, part, x_s, gain, gu_w, dn_w, dout_all, middle, mid_all,
    own, from_core, to_y, from_y, mid_low, send_sems, recv_sems, local_sems,
):
    place = Place()
    links = Links(place, send_sems, recv_sems, local_sems)
    place.meet(place.neighbours())
    step = 64
    chunks = []
    for src, dst in ((gu_s, gu_w), (dn_s, dn_w)):
        for first in range(0, src.shape[0], step):
            rows = pl.ds(first, step)
            chunks.append((src.at[rows], lambda f, dst=dst, rows=rows: dst.at[f, rows]))
    plane = spread_plane(links, place, chunks)
    next(plane)
    parts = halves(x_s.shape[0])
    reduce = ReduceCtx(links, place, part, parts, own, from_core, to_y, from_y)
    reduce.begin()
    kept = [
        links.local(gu_s, gu_w.at[place.f]),
        links.local(dn_s, dn_w.at[place.f]),
        links.local(dout_s, dout_all.at[place.c]),
    ]
    for k in range(2):
        reduce.cross(k)
    dout = SpreadCtx(links, place, dout_all, parts)
    for k, rows in enumerate(parts):
        dout.begin(k, dout_s.at[rows], y_too=False)
    next(plane)
    mid = SpreadCtx(links, place, mid_all, parts)
    for k, rows in enumerate(parts):
        value = x_s[rows].astype(F32) + reduce.total(k)
        middle[rows] = value
        mid_low[rows] = (value * row_factor(value) * gain[...]).astype(BF16)
        mid.begin(k, mid_low.at[rows])
        kept.append(links.local(mid_low.at[rows], mid_all.at[place.c, rows]))
    next(plane)
    for k in range(2):
        mid.forward(k)
    for k, rows in enumerate(parts):
        dout.begin_y(k, dout_s.at[rows])
    next(plane)
    next(plane)
    for k in range(2):
        dout.forward(k)
    for _ in plane:
        pass
    mid.end()
    dout.end()
    for made in kept:
        made.wait()
    links.finish()


def feed_reduce_kernel(
    gu_g, dn_g, ffn_part, dmid_part, middle, dout_s, keep, gain,
    gu_all, dn_all, layer_out, d_middle, gain_part, branch_all,
    own, from_x, to_z, from_z, total,
    own1, from_core1, to_y1, from_y1, own2, from_core2, to_y2, from_y2, branch,
    send_sems, recv_sems, local_sems,
):
    place = Place()
    links = Links(place, send_sems, recv_sems, local_sems)
    place.meet(place.neighbours())
    step = from_x.shape[2]
    chunks, where = [], []
    for grad, out in ((dn_g, dn_all), (gu_g, gu_all)):
        for first in range(0, grad.shape[2], step):
            rows = pl.ds(first, step)
            chunks.append(lambda x, grad=grad, rows=rows: grad.at[:, x, rows])
            where.append((out, rows))
    outs = [SpreadCtx(links, place, out, [rows]) for out, rows in where]
    kept = []

    def done(k):
        out, rows = where[k]
        outs[k].begin(0, total.at[k])
        kept.append(links.local(total.at[k], out.at[place.c, rows]))

    plane = reduce_plane(links, place, chunks, own, from_x, to_z, from_z, total, done)
    next(plane)
    parts = halves(middle.shape[0])
    dmid = ReduceCtx(links, place, dmid_part, parts, own1, from_core1, to_y1, from_y1)
    dmid.begin()
    for k in range(2):
        dmid.cross(k)
    next(plane)
    spread = SpreadCtx(links, place, branch_all, parts)
    gain_sum = None
    for k, rows in enumerate(parts):
        d_norm = dmid.total(k)
        value = middle[rows]
        factor = row_factor(value)
        term = jnp.sum(d_norm * value * factor, axis=0, keepdims=True)
        gain_sum = term if gain_sum is None else gain_sum + term
        scaled = d_norm * gain[...]
        inner = jnp.mean(scaled * value, axis=-1, keepdims=True)
        grad = dout_s[rows].astype(F32) + factor * scaled - value * (factor * factor * factor * inner)
        d_middle[rows] = grad
        branch[rows] = grad.astype(BF16)
        spread.begin(k, branch.at[rows])
        kept.append(links.local(branch.at[rows], branch_all.at[place.c, rows]))
    gain_part[...] = gain_sum
    next(plane)
    ffn = ReduceCtx(links, place, ffn_part, parts, own2, from_core2, to_y2, from_y2)
    ffn.begin()
    for k in range(2):
        spread.forward(k)
    for k in range(2):
        ffn.cross(k)
    next(plane)
    next(plane)
    for k, rows in enumerate(parts):
        layer_out[rows] = (keep[rows] * (middle[rows] + ffn.total(k))).astype(BF16)
    forwarded = 0
    for step_at, _ in enumerate(plane):
        if step_at % 2 == 1:
            outs[forwarded].forward(0)
            forwarded += 1
    for k in range(forwarded, len(outs)):
        outs[k].forward(0)
    spread.end()
    for out in outs:
        out.end()
    for made in kept:
        made.wait()
    links.finish()


def last_kernel(
    qkv_g, out_g, dnorm_part, x_s, d_middle, gain, ffn_part, qk_part,
    qkv_all, out_all, input_grad, stats,
    own, from_x, to_z, from_z, total,
    own1, from_core1, to_y1, from_y1,
    out_own, out_x, out_low, out_z,
    mine, plane_stats, ctx_stats, send_sems, recv_sems, local_sems,
):
    place = Place()
    links = Links(place, send_sems, recv_sems, local_sems)
    fellows = [lax.rem(place.f + d, 8) for d in range(1, 8)]
    place.meet(
        [(f, place.c) for f in fellows] + [place.core_dev, place.y_dev, place.diag_dev]
    )
    step = from_x.shape[2]
    chunks = []
    for first in range(0, qkv_g.shape[2], step):
        rows = pl.ds(first, step)
        chunks.append(lambda x, rows=rows: qkv_g.at[:, x, rows])
    outs = [
        SpreadCtx(links, place, qkv_all, [pl.ds(k * step, step)]) for k in range(len(chunks))
    ]
    kept = []

    def done(k):
        outs[k].begin(0, total.at[k])
        kept.append(links.local(total.at[k], qkv_all.at[place.c, pl.ds(k * step, step)]))

    out_slot = links.slots(1)
    links.send(out_g.at[place.xo], out_x, out_slot, place.x_dev)
    out_load = links.local(out_g.at[place.x], out_own)
    plane = reduce_plane(links, place, chunks, own, from_x, to_z, from_z, total, done)
    next(plane)
    parts = halves(x_s.shape[0])
    dnorm = ReduceCtx(links, place, dnorm_part, parts, own1, from_core1, to_y1, from_y1)
    dnorm.begin()
    for k in range(2):
        dnorm.cross(k)

    links.arrive(out_x, out_slot)
    out_load.wait()
    root_slot, final_slot = links.slots(4), links.slots(1)
    holds = place.z == place.c
    pair = out_own[...].astype(F32) + out_x[...].astype(F32)
    out_low[...] = pair.astype(BF16)
    to_root = links.copy(
        out_low, out_z.at[place.z], root_slot + place.z, (place.c * 2 + place.x, place.c)
    )

    @pl.when(jnp.logical_not(holds))
    def _():
        to_root.start()

    next(plane)
    gain_sum = None
    for k, rows in enumerate(parts):
        d_norm = dnorm.total(k)
        value = x_s[rows].astype(F32)
        factor = row_factor(value)
        term = jnp.sum(d_norm * value * factor, axis=0, keepdims=True)
        gain_sum = term if gain_sum is None else gain_sum + term
        scaled = d_norm * gain[...]
        inner = jnp.mean(scaled * value, axis=-1, keepdims=True)
        grad = d_middle[rows] + factor * scaled - value * (factor * factor * factor * inner)
        input_grad[rows] = grad.astype(BF16)
    mine[0:1] = gain_sum
    mine[1:2] = ffn_part[...]
    mine[2:3] = qk_part[...]
    mine[3:8] = jnp.zeros((5, mine.shape[1]), F32)
    plane_slot, ctx_slot = links.slots(8), links.slots(4)
    for f in fellows:
        links.send(mine, plane_stats.at[place.f], plane_slot + place.f, (f, place.c))
    plane_stats[place.f] = mine[...]

    final = [
        links.copy(out_all, out_all, final_slot, device)
        for device in (place.core_dev, place.y_dev)
    ]
    onward = links.copy(out_all, out_all, final_slot, place.core_dev)

    @pl.when(holds)
    def _():
        sums = out_own[...].astype(F32) + out_x[...].astype(F32)
        for other in place.others:
            links.arrive(out_z.at[other], root_slot + other)
            sums += out_z[other].astype(F32)
        out_all[...] = sums.astype(BF16)
        for made in final:
            made.start()

    for f in fellows:
        links.arrive(plane_stats.at[f], plane_slot + f)
    sums = plane_stats[0]
    for f in range(1, 8):
        sums += plane_stats[f]
    ctx_stats[place.c] = sums
    for device in (place.core_dev, place.y_dev, place.diag_dev):
        links.send(ctx_stats.at[place.c], ctx_stats.at[place.c], ctx_slot + place.c, device)
    for _ in plane:
        pass
    for out in outs:
        out.forward(0)
    relays = place.c_y == place.z

    @pl.when(jnp.logical_not(holds))
    def _():
        links.arrive(out_all, final_slot)

    @pl.when(relays)
    def _():
        onward.start()

    for c in (place.c_core, place.c_y, place.c_diag):
        links.arrive(ctx_stats.at[c], ctx_slot + c)
    stats[...] = ((ctx_stats[0] + ctx_stats[1]) + ctx_stats[2]) + ctx_stats[3]
    for out in outs:
        out.end()
    for made in kept:
        made.wait()
    links.finish()

    @pl.when(jnp.logical_not(holds))
    def _():
        to_root.wait_send()

    @pl.when(relays)
    def _():
        onward.wait_send()

    @pl.when(holds)
    def _():
        for made in final:
            made.wait_send()


def low_half(shape):
    return lax.rem(lax.broadcasted_iota(jnp.int32, shape, len(shape) - 1), 128) < 64


def partner(values):
    lane = lax.broadcasted_iota(jnp.int32, values.shape, len(values.shape) - 1)
    first = lax.rem(lane, 64) < 32
    return jnp.where(first, pltpu.roll(values, 96, 1), pltpu.roll(values, 32, 1))


def half_sums(values):
    low = low_half(values.shape)
    first = jnp.sum(jnp.where(low, values, 0.0), axis=-1, keepdims=True)
    second = jnp.sum(jnp.where(low, 0.0, values), axis=-1, keepdims=True)
    return jnp.where(low, first, second)


def row_loop(count, body):
    def step(index, carry):
        body(index)
        return carry

    lax.fori_loop(0, count, step, 0)


BLOCK = 256


def attention_scores(query, keys, key_bias, first, span):
    scores = lax.dot_general(
        query, keys, (((1,), (1,)), ((), ())), preferred_element_type=F32
    ) * (1.0 / math.sqrt(HEAD_DIM))
    rows = first + lax.broadcasted_iota(jnp.int32, scores.shape, 0)
    columns = lax.broadcasted_iota(jnp.int32, scores.shape, 1)
    return jnp.where(columns <= rows, scores, -1e30) + key_bias[:, :span]


def attention_kernel(
    x_all, qkv_w, out_w, gain, cos, sin, head_gain, key_bias,
    normed, qkv_raw, qkv_low, att_low, log_sums, part, keys, values,
):
    seq = x_all.shape[0]

    def project(index):
        rows = pl.ds(pl.multiple_of(index * BLOCK, BLOCK), BLOCK)
        source = x_all[rows].astype(F32)
        normed[rows] = (source * row_factor(source) * gain[...]).astype(BF16)
        raw = jnp.dot(normed[rows], qkv_w[...], preferred_element_type=F32)
        for b in range(3):
            block = raw[:, 128 * b : 128 * (b + 1)]
            qkv_raw[b, rows] = block
            factor = lax.rsqrt(half_sums(block * block) * (1.0 / HEAD_DIM) + EPSILON)
            scaled = block * factor * head_gain[b : b + 1]
            turned = scaled * cos[rows] + partner(scaled) * sin[rows]
            if b == 2:
                turned = jnp.where(low_half(turned.shape), turned, block)
            qkv_low[b, rows] = turned.astype(BF16)
            if b == 2:
                low = low_half(turned.shape)
                swapped = pltpu.roll(turned, 64, 1)
                keys[rows] = jnp.where(low, turned, swapped).astype(BF16)
                values[rows] = jnp.where(low, swapped, turned).astype(BF16)

    row_loop(seq // BLOCK, project)

    def heads(b):
        for i in range(seq // BLOCK):
            rows, span = pl.ds(i * BLOCK, BLOCK), (i + 1) * BLOCK
            query = qkv_low[b, rows]
            low = low_half(query.shape)
            outs, logs = [], []
            for half in range(2):
                chosen = jnp.where(low if half == 0 else jnp.logical_not(low), query, 0)
                scores = attention_scores(chosen, keys[:span], key_bias[0:1], i * BLOCK, span)
                top = jnp.max(scores, axis=-1, keepdims=True)
                expanded = jnp.exp(scores - top)
                sums = jnp.sum(expanded, axis=-1, keepdims=True)
                probs = (expanded * (1.0 / sums)).astype(BF16)
                outs.append(jnp.dot(probs, values[:span], preferred_element_type=F32))
                logs.append(top + jnp.log(sums))
            att_low[b, rows] = jnp.where(low, outs[0], outs[1]).astype(BF16)
            log_sums[b, rows] = jnp.where(low, logs[0], logs[1])

    row_loop(2, heads)

    def project_out(index):
        rows = pl.ds(pl.multiple_of(index * BLOCK, BLOCK), BLOCK)
        sums = jnp.dot(att_low[0, rows], out_w[0], preferred_element_type=F32)
        sums += jnp.dot(att_low[1, rows], out_w[1], preferred_element_type=F32)
        part[index] = sums.astype(BF16)

    row_loop(seq // BLOCK, project_out)


NT = (((1,), (1,)), ((), ()))
TN = (((0,), (0,)), ((), ()))


def attention_back_kernel(
    branch, qkv_w, out_w, cos, sin, head_gain, key_bias,
    normed, qkv_raw, qkv_low, att_low, log_sums,
    part, qkv_g, out_g, gain_g, keys, values, d_att, d_low, d_keys, d_values,
):
    seq = branch.shape[0]
    root = 1.0 / math.sqrt(HEAD_DIM)
    gain_g[...] = jnp.zeros_like(gain_g)
    d_keys[...] = jnp.zeros_like(d_keys)
    d_values[...] = jnp.zeros_like(d_values)

    def prepare(index):
        rows = pl.ds(pl.multiple_of(index * BLOCK, BLOCK), BLOCK)
        block = qkv_low[2, rows].astype(F32)
        low = low_half(block.shape)
        swapped = pltpu.roll(block, 64, 1)
        keys[rows] = jnp.where(low, block, swapped).astype(BF16)
        values[rows] = jnp.where(low, swapped, block).astype(BF16)
        for b in range(2):
            d_att[b, rows] = lax.dot_general(
                branch[rows], out_w[b], NT, preferred_element_type=F32
            ).astype(BF16)

    row_loop(seq // BLOCK, prepare)

    def unturn(row, rows, grads, block):
        back = grads * cos[rows] + partner(grads * sin[rows])
        factor = lax.rsqrt(half_sums(block * block) * (1.0 / HEAD_DIM) + EPSILON)
        gain_term = jnp.sum(back * block * factor, axis=0, keepdims=True)
        scaled = back * head_gain[row : row + 1]
        inner = half_sums(scaled * block) * (1.0 / HEAD_DIM)
        return factor * scaled - block * (factor * factor * factor * inner), gain_term

    def heads(b):
        out_g[b] = lax.dot_general(
            att_low[b], branch[...], TN, preferred_element_type=F32
        ).astype(BF16)
        for i in range(seq // BLOCK):
            rows, span = pl.ds(i * BLOCK, BLOCK), (i + 1) * BLOCK
            query, d_out = qkv_low[b, rows], d_att[b, rows]
            logs = log_sums[b, rows]
            low = low_half(query.shape)
            d_query = []
            for half in range(2):
                side = low if half == 0 else jnp.logical_not(low)
                chosen, d_chosen = jnp.where(side, query, 0), jnp.where(side, d_out, 0)
                scores = attention_scores(chosen, keys[:span], key_bias[0:1], i * BLOCK, span)
                probs = jnp.exp(scores - logs[:, 64 * half : 64 * half + 1])
                d_probs = lax.dot_general(
                    d_chosen, values[:span], NT, preferred_element_type=F32
                )
                delta = jnp.sum(probs * d_probs, axis=-1, keepdims=True)
                d_scores = (probs * (d_probs - delta)).astype(BF16)
                d_query.append(jnp.dot(d_scores, keys[:span], preferred_element_type=F32))
                d_keys[:span] += lax.dot_general(
                    d_scores, chosen, TN, preferred_element_type=F32
                )
                d_values[:span] += lax.dot_general(
                    probs.astype(BF16), d_chosen, TN, preferred_element_type=F32
                )
            grads = (jnp.where(low, d_query[0], d_query[1]) * root).astype(BF16).astype(F32)
            d_block, gain_term = unturn(0, rows, grads, qkv_raw[b, rows])
            d_low[b, rows] = d_block.astype(BF16)
            gain_g[0:1] += gain_term

    row_loop(2, heads)

    def finish(index):
        rows = pl.ds(pl.multiple_of(index * BLOCK, BLOCK), BLOCK)
        k_sum, v_sum = d_keys[rows], d_values[rows]
        low = low_half(k_sum.shape)
        k_sum = (k_sum + pltpu.roll(k_sum, 64, 1)) * root
        v_sum = v_sum + pltpu.roll(v_sum, 64, 1)
        grads = jnp.where(low, k_sum, v_sum).astype(BF16).astype(F32)
        d_block, gain_term = unturn(2, rows, grads, qkv_raw[2, rows])
        d_low[2, rows] = jnp.where(low, d_block, grads).astype(BF16)
        gain_g[1:2] += gain_term
        sums = jnp.zeros((BLOCK, part.shape[2]), F32)
        for b in range(3):
            sums += lax.dot_general(
                d_low[b, rows], qkv_w[:, 128 * b : 128 * (b + 1)], NT, preferred_element_type=F32
            )
        part[index] = sums.astype(BF16)

    row_loop(seq // BLOCK, finish)
    for b in range(3):
        grad = lax.dot_general(d_low[b], normed[...], TN, preferred_element_type=F32).astype(BF16)
        for f in range(8):
            qkv_g[f, 128 * b : 128 * (b + 1)] = grad[:, 256 * f : 256 * (f + 1)]


def shaped(shape, kind=BF16):
    return jax.ShapeDtypeStruct(shape, kind)


def call(kernel, ins, outs, scratch=(), sems=None, number=None, flops=0):
    scratch = list(scratch)
    extra = {}
    if sems is not None:
        scratch += [pltpu.SemaphoreType.DMA((n,)) for n in sems]
        extra = dict(collective_id=number, has_side_effects=True)
    return pl.pallas_call(
        kernel,
        out_shape=tuple(shape for shape, _ in outs),
        in_specs=[spec for _, spec in ins],
        out_specs=tuple(spec for _, spec in outs),
        scratch_shapes=scratch,
        compiler_params=pltpu.CompilerParams(vmem_limit_bytes=VMEM_BYTES, **extra),
    )(*[array for array, _ in ins])


def split_heads(
    inputs,
    cotangent,
    lengths,
    qkv_weight,
    out_weight,
    gate_up,
    down_weight,
    attn_gain,
    ffn_gain,
    qk_gain,
):
    tokens, width = inputs.shape[1:]
    seq = tokens * 4
    c = lax.axis_index("ctx")
    length = lengths[0]
    positions = c * tokens + jnp.arange(tokens, dtype=jnp.int32)
    keep = (positions < length).astype(F32)[:, None]
    all_positions = jnp.arange(seq, dtype=jnp.int32)
    key_bias = jnp.broadcast_to(jnp.where(all_positions < length, 0.0, -1e30)[None], (8, seq))
    source = inputs[0]
    d_out = (keep * cotangent[0].astype(F32)).astype(BF16)

    query_cols, key_cols = HEADS * HEAD_DIM, KV_HEADS * HEAD_DIM
    qkv_s = jnp.concatenate(
        [
            lax.dynamic_slice_in_dim(qkv_weight, c * 256, 256, 1),
            lax.dynamic_slice_in_dim(qkv_weight, query_cols + c * 64, 64, 1),
            lax.dynamic_slice_in_dim(qkv_weight, query_cols + key_cols + c * 64, 64, 1),
        ],
        axis=1,
    )
    rows, parts, units = gate_up.shape
    gu_s = lax.dynamic_index_in_dim(
        gate_up.reshape(rows, parts, 8, 4, units // 32), c, 3, keepdims=False
    ).reshape(rows, parts * units // 4)
    down_rows = down_weight.shape[0] // 4
    dn_s = lax.dynamic_slice_in_dim(down_weight, c * down_rows, down_rows, 0)
    gain_s = jnp.concatenate(
        [attn_gain[None], ffn_gain[None], jnp.zeros((6, rows), BF16)], axis=0
    ).astype(F32)

    half_dim = HEAD_DIM // 2
    angles = np.arange(seq)[:, None] * 10000.0 ** (-2.0 * np.arange(half_dim) / HEAD_DIM)[None]
    cos = jnp.tile(jnp.asarray(np.cos(angles), F32), (1, 4))
    sine = jnp.asarray(np.sin(angles), F32)
    sin = jnp.tile(jnp.concatenate([-sine, sine], axis=1), (1, 2))
    q_gain = jnp.tile(qk_gain[0].astype(F32), 2)
    k_gain = jnp.concatenate([qk_gain[1].astype(F32), jnp.ones((HEAD_DIM,), F32)])
    head_gain = jnp.concatenate(
        [q_gain[None], q_gain[None], k_gain[None], jnp.zeros((5, 128), F32)], axis=0
    )

    qkv_w, out_w, gains, x_all = call(
        gather_kernel,
        [(qkv_s, HBM), (out_weight, HBM), (gain_s, HBM), (source, HBM)],
        [
            (shaped((8, rows, 384)), HBM),
            (shaped((2, out_weight.shape[0], width)), HBM),
            (shaped((8, 8, rows), F32), HBM),
            (shaped((4, tokens, width)), HBM),
        ],
        sems=(40, 40, 8),
        number=0,
    )
    attn_norm = gains[:, 0].reshape(1, width)
    ffn_norm = gains[:, 1].reshape(1, width)
    qkv_w = qkv_w.reshape(width, 384)
    x_all = x_all.reshape(seq, width)
    tables = [(cos, VMEM), (sin, VMEM), (head_gain, VMEM), (key_bias, VMEM)]
    normed, qkv_raw, qkv_low, att_low, log_sums, part = call(
        attention_kernel,
        [(x_all, VMEM), (qkv_w, VMEM), (out_w, VMEM), (attn_norm, VMEM)] + tables,
        [
            (shaped((seq, width)), VMEM),
            (shaped((3, seq, 128), F32), VMEM),
            (shaped((3, seq, 128)), VMEM),
            (shaped((2, seq, 128)), VMEM),
            (shaped((2, seq, 128), F32), VMEM),
            (shaped((4, tokens, width)), VMEM),
        ],
        [pltpu.VMEM((seq, 128), BF16)] * 2,
    )
    ctx_scratch = [
        pltpu.VMEM((2, tokens, width), BF16),
        pltpu.VMEM((2, tokens, width), BF16),
        pltpu.VMEM((tokens, width), BF16),
        pltpu.VMEM((tokens, width), BF16),
    ]
    gu_w, dn_w, dout_all, middle, mid_all = call(
        feed_gather_kernel,
        [
            (gu_s, HBM),
            (dn_s, HBM),
            (d_out, HBM),
            (part, HBM),
            (source, VMEM),
            (ffn_norm, VMEM),
        ],
        [
            (shaped((8, rows, width)), HBM),
            (shaped((8, down_rows, width)), HBM),
            (shaped((4, tokens, width)), HBM),
            (shaped((tokens, width), F32), VMEM),
            (shaped((4, tokens, width)), HBM),
        ],
        ctx_scratch + [pltpu.VMEM((tokens, width), BF16)],
        sems=(80, 80, 16),
        number=1,
    )
    hidden_units = units // 4
    gu_full = gu_w.reshape(width, parts * hidden_units)
    dn_full = dn_w.reshape(hidden_units, width)
    mid_full = mid_all.reshape(seq, width)
    dout_full = dout_all.reshape(seq, width)
    projected = jnp.dot(mid_full, gu_full, preferred_element_type=F32)
    gate, up = projected[:, :hidden_units], projected[:, hidden_units:]
    sigmoid = jax.nn.sigmoid(gate)
    hidden = (gate * sigmoid * up).astype(BF16)
    ffn_part = jnp.dot(hidden, dn_full, preferred_element_type=F32).astype(BF16)
    d_hidden = contract_cols(dout_full, dn_full)
    d_projected = jnp.concatenate(
        [
            (d_hidden * up * (sigmoid * (1.0 + gate * (1.0 - sigmoid)))).astype(BF16),
            (d_hidden * gate * sigmoid).astype(BF16),
        ],
        axis=1,
    )
    dn_g = contract_rows(hidden, dout_full).astype(BF16)
    gu_g = contract_rows(mid_full, d_projected).astype(BF16)
    dmid_part = contract_cols(d_projected, gu_full).astype(BF16)

    step = 64
    count = (rows + down_rows) // step
    gu_all, dn_all, layer_out, d_middle, ffn_gain_part, branch_all = call(
        feed_reduce_kernel,
        [
            (gu_g.reshape(4, 2, rows, width), HBM),
            (dn_g.reshape(4, 2, down_rows, width), HBM),
            (ffn_part.reshape(4, tokens, width), HBM),
            (dmid_part.reshape(4, tokens, width), HBM),
            (middle, VMEM),
            (d_out, VMEM),
            (keep, VMEM),
            (ffn_norm, VMEM),
        ],
        [
            (shaped((4, rows, width)), HBM),
            (shaped((4, down_rows, width)), HBM),
            (shaped((tokens, width)), VMEM),
            (shaped((tokens, width), F32), VMEM),
            (shaped((1, width), F32), VMEM),
            (shaped((4, tokens, width)), HBM),
        ],
        [
            pltpu.VMEM((count, 4, step, width), BF16),
            pltpu.VMEM((count, 4, step, width), BF16),
            pltpu.VMEM((count, 4, step, width), BF16),
            pltpu.VMEM((count, 4, step, width), BF16),
            pltpu.VMEM((count, step, width), BF16),
        ]
        + ctx_scratch
        + ctx_scratch
        + [pltpu.VMEM((tokens, width), BF16)],
        sems=(80, 80, 40),
        number=2,
    )
    dnorm_part, qkv_g, out_g, head_gain_g = call(
        attention_back_kernel,
        [(branch_all.reshape(seq, width), VMEM), (qkv_w, VMEM), (out_w, VMEM)]
        + tables
        + [(a, VMEM) for a in (normed, qkv_raw, qkv_low, att_low, log_sums)],
        [
            (shaped((4, tokens, width)), VMEM),
            (shaped((8, 384, rows)), VMEM),
            (shaped((2, 128, width)), VMEM),
            (shaped((8, 128), F32), VMEM),
        ],
        [
            pltpu.VMEM((seq, 128), BF16),
            pltpu.VMEM((seq, 128), BF16),
            pltpu.VMEM((2, seq, 128), BF16),
            pltpu.VMEM((3, seq, 128), BF16),
            pltpu.VMEM((seq, 128), F32),
            pltpu.VMEM((seq, 128), F32),
        ],
    )
    qk_part = jnp.concatenate(
        [
            head_gain_g[0:1, :64] + head_gain_g[0:1, 64:],
            head_gain_g[1:2, :64],
            jnp.zeros((1, width - 128), F32),
        ],
        axis=1,
    )
    step = 192
    count = 384 // step
    qkv_all, out_all, input_grad, stats = call(
        last_kernel,
        [
            (qkv_g.reshape(4, 2, 384, rows), HBM),
            (out_g, HBM),
            (dnorm_part, HBM),
            (source, VMEM),
            (d_middle, VMEM),
            (attn_norm, VMEM),
            (ffn_gain_part, VMEM),
            (qk_part, VMEM),
        ],
        [
            (shaped((4, 384, rows)), HBM),
            (shaped((128, width)), VMEM),
            (shaped((tokens, width)), VMEM),
            (shaped((8, width), F32), VMEM),
        ],
        [
            pltpu.VMEM((count, 4, step, rows), BF16),
            pltpu.VMEM((count, 4, step, rows), BF16),
            pltpu.VMEM((count, 4, step, rows), BF16),
            pltpu.VMEM((count, 4, step, rows), BF16),
            pltpu.VMEM((count, step, rows), BF16),
        ]
        + ctx_scratch
        + [
            pltpu.VMEM((128, width), BF16),
            pltpu.VMEM((128, width), BF16),
            pltpu.VMEM((128, width), BF16),
            pltpu.VMEM((4, 128, width), BF16),
            pltpu.VMEM((8, width), F32),
            pltpu.VMEM((8, 8, width), F32),
            pltpu.VMEM((4, 8, width), F32),
        ],
        sems=(60, 60, 20),
        number=3,
    )
    f = lax.axis_index("fsdp")
    qkv_grad = jnp.concatenate(
        [
            jnp.transpose(qkv_all[:, :256], (2, 0, 1)).reshape(rows, query_cols),
            jnp.transpose(qkv_all[:, 256:320], (2, 0, 1)).reshape(rows, key_cols),
            jnp.transpose(qkv_all[:, 320:], (2, 0, 1)).reshape(rows, key_cols),
        ],
        axis=1,
    ).astype(F32)
    gate_up_grad = (
        jnp.transpose(gu_all.reshape(4, rows, parts, 8, units // 32), (1, 2, 3, 0, 4))
        .reshape(rows, parts, units)
        .astype(F32)
    )
    return (
        layer_out[None],
        input_grad[None],
        qkv_grad,
        out_all.astype(F32),
        gate_up_grad,
        dn_all.reshape(4 * down_rows, width).astype(F32),
        lax.dynamic_slice_in_dim(stats[0], f * rows, rows, 0),
        lax.dynamic_slice_in_dim(stats[1], f * rows, rows, 0),
        stats[2, :128].reshape(2, 64),
    )


def solution(mesh):
    sizes = (mesh.shape["fsdp"], mesh.shape["ctx"])
    return jax.shard_map(
        split_heads if sizes == (8, 4) else on_device,
        mesh=mesh,
        in_specs=(
            P("fsdp", "ctx", None),
            P("fsdp", "ctx", None),
            P("fsdp"),
            P("fsdp", None),
            P("fsdp", None),
            P("fsdp", None, None),
            P("fsdp", None),
            P("fsdp"),
            P("fsdp"),
            P(),
        ),
        out_specs=(
            P("fsdp", "ctx", None),
            P("fsdp", "ctx", None),
            P("fsdp", None),
            P("fsdp", None),
            P("fsdp", None, None),
            P("fsdp", None),
            P("fsdp"),
            P("fsdp"),
            P(),
        ),
        check_vma=False,
    )
```

```python
import functools
import math

import jax
import jax.numpy as jnp
import numpy as np
from jax import lax
from jax.experimental import pallas as pl
from jax.experimental.pallas import tpu as pltpu
from jax.sharding import PartitionSpec as P

HEADS = 16
KV_HEADS = 4
HEAD_DIM = 64


EPSILON = 1e-06


def root_norm(values, norm_gain):
    factor = lax.rsqrt(jnp.mean(values * values, axis=-1, keepdims=True) + EPSILON)
    return values * factor * norm_gain


def rotation_tables(positions):
    half_dim = HEAD_DIM // 2
    frequency = 10000.0 ** (-(2.0 * jnp.arange(half_dim, dtype=jnp.float32)) / HEAD_DIM)
    angles = positions.astype(jnp.float32)[:, None] * frequency[None, :]
    return (jnp.cos(angles), jnp.sin(angles))


def rotate(values, cos_table, sin_table):
    half_dim = values.shape[-1] // 2
    lower_half = values[..., :half_dim]
    upper_half = values[..., half_dim:]
    cos_part = cos_table[:, None, :]
    sin_part = sin_table[:, None, :]
    return jnp.concatenate(
        [
            lower_half * cos_part - upper_half * sin_part,
            upper_half * cos_part + lower_half * sin_part,
        ],
        axis=-1,
    )


def prepare_heads(qkv_out, head_gain, cos_table, sin_table):
    row_count = qkv_out.shape[0]
    query_cols = HEADS * HEAD_DIM
    key_cols = KV_HEADS * HEAD_DIM
    queries = qkv_out[:, :query_cols].reshape(row_count, HEADS, HEAD_DIM)
    key_part = qkv_out[:, query_cols : query_cols + key_cols].reshape(row_count, KV_HEADS, HEAD_DIM)
    value_part = qkv_out[:, query_cols + key_cols :]
    queries = rotate(root_norm(queries, head_gain[0]), cos_table, sin_table).reshape(
        row_count, query_cols
    )
    key_part = rotate(root_norm(key_part, head_gain[1]), cos_table, sin_table).reshape(
        row_count, key_cols
    )
    return (queries, key_part, value_part)


def activate(projected):
    gate_part = projected[:, 0]
    return gate_part * jax.nn.sigmoid(gate_part) * projected[:, 1]


def contract_rows(left, right):
    return lax.dot_general(
        left, right, (((0,), (0,)), ((), ())), preferred_element_type=jnp.float32
    )


def contract_cols(left, right):
    return lax.dot_general(
        left, right, (((1,), (1,)), ((), ())), preferred_element_type=jnp.float32
    )


def on_device(
    inputs,
    cotangent,
    lengths,
    qkv_weight,
    out_weight,
    gate_up,
    down_weight,
    attn_gain,
    ffn_gain,
    qk_gain,
):
    token_count = inputs.shape[1]
    group = HEADS // KV_HEADS
    key_cols = KV_HEADS * HEAD_DIM
    seq_len = token_count * lax.axis_size("ctx")
    positions = lax.axis_index("ctx") * token_count + jnp.arange(token_count, dtype=jnp.int32)
    length = lengths[0]
    row_keep = (positions < length).astype(jnp.float32)[:, None]
    inv_root = 1.0 / math.sqrt(HEAD_DIM)
    source = inputs[0].astype(jnp.float32)
    qkv_full, out_full, attn_full, ffn_full = (
        lax.all_gather(qkv_weight, "fsdp", axis=0, tiled=True),
        lax.all_gather(out_weight, "fsdp", axis=0, tiled=True),
        lax.all_gather(attn_gain, "fsdp", axis=0, tiled=True),
        lax.all_gather(ffn_gain, "fsdp", axis=0, tiled=True),
    )
    attn_norm = attn_full.astype(jnp.float32)
    ffn_norm = ffn_full.astype(jnp.float32)
    normed = root_norm(source, attn_norm).astype(jnp.bfloat16)
    qkv_out = jnp.dot(normed, qkv_full, preferred_element_type=jnp.float32)
    cos_table, sin_table = rotation_tables(positions)
    head_gain = qk_gain.astype(jnp.float32)

    def head_pieces(qkv_values, gain_values):
        return prepare_heads(qkv_values, gain_values, cos_table, sin_table)

    head_values, head_pull = jax.vjp(head_pieces, qkv_out, head_gain)
    queries, key_part, value_part = head_values
    query_low = queries.astype(jnp.bfloat16).reshape(token_count, KV_HEADS, group, HEAD_DIM)
    kv_local = jnp.concatenate([key_part, value_part], axis=1).astype(jnp.bfloat16)
    kv_whole = lax.all_gather(kv_local, "ctx", axis=0, tiled=True)
    block = 512
    block_total = seq_len // block
    kv_blocks = kv_whole.reshape(block_total, block, 2, KV_HEADS, HEAD_DIM)
    starts = jnp.arange(block_total, dtype=jnp.int32) * block

    def block_scores(key_block, block_start):
        scores = (
            jnp.einsum("bhgd,thd->hgbt", query_low, key_block, preferred_element_type=jnp.float32)
            * inv_root
        )
        key_pos = block_start + jnp.arange(key_block.shape[0], dtype=jnp.int32)
        visible = (key_pos[None, :] <= positions[:, None]) & (key_pos[None, :] < length)
        return (scores, visible)

    def max_step(state, item):
        running_max, running_sum = state
        kv_block, block_start = item
        scores, visible = block_scores(kv_block[:, 0], block_start)
        new_max = jnp.maximum(running_max, jnp.max(jnp.where(visible, scores, -1e30), axis=-1))
        expanded = jnp.where(visible, jnp.exp(scores - new_max[..., None]), 0.0)
        running_sum = running_sum * jnp.exp(running_max - new_max) + jnp.sum(expanded, axis=-1)
        return ((new_max, running_sum), None)

    stat_shape = (KV_HEADS, group, token_count)
    start_state = (jnp.full(stat_shape, -1e30, jnp.float32), jnp.zeros(stat_shape, jnp.float32))
    final_state, unused_out = lax.scan(max_step, start_state, (kv_blocks, starts))
    log_total = final_state[0] + jnp.log(final_state[1])

    def block_probs(kv_block, block_start):
        scores, visible = block_scores(kv_block[:, 0], block_start)
        return jnp.where(visible, jnp.exp(scores - log_total[..., None]), 0.0)

    def value_step(totals, item):
        kv_block, block_start = item
        probs_low = block_probs(kv_block, block_start).astype(jnp.bfloat16)
        return (
            totals
            + jnp.einsum(
                "hgbt,thd->bhgd", probs_low, kv_block[:, 1], preferred_element_type=jnp.float32
            ),
            None,
        )

    attended, unused_out = lax.scan(
        value_step,
        jnp.zeros((token_count, KV_HEADS, group, HEAD_DIM), jnp.float32),
        (kv_blocks, starts),
    )
    attended_low = attended.reshape(token_count, HEADS * HEAD_DIM).astype(jnp.bfloat16)
    middle = source + jnp.dot(attended_low, out_full, preferred_element_type=jnp.float32)
    normed_mid = root_norm(middle, ffn_norm).astype(jnp.bfloat16)
    columns = normed_mid
    projected = jnp.einsum(
        "td,dgf->tgf",
        columns,
        lax.all_gather(gate_up, "fsdp", axis=0, tiled=True),
        preferred_element_type=jnp.float32,
    )
    act_value, act_pull = jax.vjp(activate, projected)
    hidden = act_value.astype(jnp.bfloat16)
    columns = hidden
    ffn_out = jnp.dot(
        columns,
        lax.all_gather(down_weight, "fsdp", axis=0, tiled=True),
        preferred_element_type=jnp.float32,
    )
    layer_out = (row_keep * (middle + ffn_out)).astype(jnp.bfloat16)[None]
    d_out = row_keep * cotangent[0].astype(jnp.float32)
    d_out_low = d_out.astype(jnp.bfloat16)
    down_shard = lax.psum_scatter(
        contract_rows(hidden, d_out_low).astype(jnp.bfloat16),
        "fsdp",
        scatter_dimension=0,
        tiled=True,
    )
    d_hidden = contract_cols(d_out_low, lax.all_gather(down_weight, "fsdp", axis=0, tiled=True))
    d_proj_low = act_pull(d_hidden)[0].astype(jnp.bfloat16)
    columns = normed_mid
    gate_up_shard = lax.psum_scatter(
        jnp.einsum("td,tgf->dgf", columns, d_proj_low, preferred_element_type=jnp.float32).astype(
            jnp.bfloat16
        ),
        "fsdp",
        scatter_dimension=0,
        tiled=True,
    )
    d_normed_mid = jnp.einsum(
        "tgf,dgf->td",
        d_proj_low,
        lax.all_gather(gate_up, "fsdp", axis=0, tiled=True),
        preferred_element_type=jnp.float32,
    )
    mid_value, mid_pull = jax.vjp(root_norm, middle, ffn_norm)
    d_mid_norm, ffn_gain_part = mid_pull(d_normed_mid)
    d_middle = d_out + d_mid_norm
    d_branch = d_middle.astype(jnp.bfloat16)
    out_term = contract_rows(attended_low, d_branch)
    d_attended = (
        contract_cols(d_branch, out_full)
        .astype(jnp.bfloat16)
        .reshape(token_count, KV_HEADS, group, HEAD_DIM)
    )
    delta = jnp.transpose(jnp.sum(d_attended.astype(jnp.float32) * attended, axis=-1), (1, 2, 0))

    def block_grads(kv_block, block_start):
        probs = block_probs(kv_block, block_start)
        d_probs = jnp.einsum(
            "bhgd,thd->hgbt", d_attended, kv_block[:, 1], preferred_element_type=jnp.float32
        )
        d_scores = (probs * (d_probs - delta[..., None])).astype(jnp.bfloat16)
        return (probs.astype(jnp.bfloat16), d_scores)

    def query_step(totals, item):
        kv_block, block_start = item
        probs_low, d_scores = block_grads(kv_block, block_start)
        return (
            totals
            + jnp.einsum(
                "hgbt,thd->bhgd", d_scores, kv_block[:, 0], preferred_element_type=jnp.float32
            ),
            None,
        )

    d_query_sum, unused_out = lax.scan(
        query_step,
        jnp.zeros((token_count, KV_HEADS, group, HEAD_DIM), jnp.float32),
        (kv_blocks, starts),
    )
    d_query = (d_query_sum * inv_root).reshape(token_count, HEADS * HEAD_DIM).astype(jnp.bfloat16)
    sub_block = 512
    sub_total = token_count * lax.axis_size("ctx") // sub_block
    pieces = kv_whole.reshape(sub_total, sub_block, 2, KV_HEADS, HEAD_DIM)
    sub_starts = jnp.arange(sub_total, dtype=jnp.int32) * sub_block

    def key_grads(item):
        kv_block, block_start = item
        probs_low, d_scores = block_grads(kv_block, block_start)
        d_keys = (
            jnp.einsum("hgbt,bhgd->thd", d_scores, query_low, preferred_element_type=jnp.float32)
            * inv_root
        )
        d_values = jnp.einsum(
            "hgbt,bhgd->thd", probs_low, d_attended, preferred_element_type=jnp.float32
        )
        return jnp.concatenate(
            [d_keys.reshape(sub_block, key_cols), d_values.reshape(sub_block, key_cols)], axis=1
        )

    kv_grad = lax.psum_scatter(
        lax.map(key_grads, (pieces, sub_starts))
        .reshape(token_count * lax.axis_size("ctx"), 2 * key_cols)
        .astype(jnp.bfloat16),
        "ctx",
        scatter_dimension=0,
        tiled=True,
    ).astype(jnp.float32)
    d_key_low = kv_grad[:, :key_cols].astype(jnp.bfloat16).astype(jnp.float32)
    d_value_low = kv_grad[:, key_cols:].astype(jnp.bfloat16).astype(jnp.float32)
    d_qkv_out, qk_part = head_pull((d_query.astype(jnp.float32), d_key_low, d_value_low))
    d_qkv = d_qkv_out.astype(jnp.bfloat16)
    qkv_term = contract_rows(normed, d_qkv)
    d_normed = contract_cols(d_qkv, qkv_full)
    first_value, first_pull = jax.vjp(root_norm, source, attn_norm)
    d_source_norm, attn_gain_part = first_pull(d_normed)
    input_grad = (d_middle + d_source_norm).astype(jnp.bfloat16)[None]
    qkv_shard, out_shard, attn_shard, ffn_shard = (
        lax.psum_scatter(
            qkv_term.astype(jnp.bfloat16), "fsdp", scatter_dimension=0, tiled=True
        ).astype(jnp.float32),
        lax.psum_scatter(
            out_term.astype(jnp.bfloat16), "fsdp", scatter_dimension=0, tiled=True
        ).astype(jnp.float32),
        lax.psum_scatter(
            attn_gain_part.astype(jnp.bfloat16), "fsdp", scatter_dimension=0, tiled=True
        ).astype(jnp.float32),
        lax.psum_scatter(
            ffn_gain_part.astype(jnp.bfloat16), "fsdp", scatter_dimension=0, tiled=True
        ).astype(jnp.float32),
    )
    summed = (
        lax.psum(qkv_shard.astype(jnp.bfloat16), "ctx").astype(jnp.float32),
        lax.psum(out_shard.astype(jnp.bfloat16), "ctx").astype(jnp.float32),
        lax.psum(gate_up_shard, "ctx").astype(jnp.float32),
        lax.psum(down_shard, "ctx").astype(jnp.float32),
        lax.psum(attn_shard.astype(jnp.bfloat16), "ctx").astype(jnp.float32),
        lax.psum(ffn_shard.astype(jnp.bfloat16), "ctx").astype(jnp.float32),
    )
    qk_total = lax.psum(qk_part, ("fsdp", "ctx"))
    return (
        layer_out,
        input_grad,
        summed[0],
        summed[1],
        summed[2],
        summed[3],
        summed[4],
        summed[5],
        qk_total,
    )


MESH = pl.DeviceIdType.MESH
F32 = jnp.float32
BF16 = jnp.bfloat16
VMEM_BYTES = 56 << 20
HBM = pl.BlockSpec(memory_space=pl.ANY)
VMEM = pl.BlockSpec(memory_space=pltpu.VMEM)


class Place:
    def __init__(self):
        self.f = lax.axis_index("fsdp")
        self.c = lax.axis_index("ctx")
        self.z, self.x = lax.div(self.f, 2), lax.rem(self.f, 2)
        self.y, self.core = lax.div(self.c, 2), lax.rem(self.c, 2)
        self.xo, self.yo, self.co = 1 - self.x, 1 - self.y, 1 - self.core
        upper = lax.div(self.z, 2)
        self.others = (self.z + 1 - 2 * lax.rem(self.z, 2), 2 - upper, 3 - 3 * upper)
        self.x_dev = (self.z * 2 + self.xo, self.c)
        self.c_core = self.y * 2 + self.co
        self.c_y = self.yo * 2 + self.core
        self.c_diag = self.yo * 2 + self.co
        self.core_dev = (self.f, self.c_core)
        self.y_dev = (self.f, self.c_y)
        self.diag_dev = (self.f, self.c_diag)

    def z_dev(self, z):
        return (z * 2 + self.x, self.c)

    def meet(self, partners):
        barrier = pltpu.get_barrier_semaphore()
        for partner in partners:
            pl.semaphore_signal(barrier, inc=1, device_id=partner, device_id_type=MESH)
        pl.semaphore_wait(barrier, len(partners))

    def neighbours(self):
        return [self.z_dev(o) for o in self.others] + [self.x_dev, self.core_dev, self.y_dev]


class Links:
    def __init__(self, place, send_sems, recv_sems, local_sems):
        self.place = place
        self.send_sems, self.recv_sems, self.local_sems = send_sems, recv_sems, local_sems
        self.sends = self.recvs = self.locals = 0
        self.open = []

    def slots(self, count):
        first = self.recvs
        self.recvs += count
        return first

    def copy(self, src, dst, slot, device):
        made = pltpu.make_async_remote_copy(
            src_ref=src,
            dst_ref=dst,
            send_sem=self.send_sems.at[self.sends],
            recv_sem=self.recv_sems.at[slot],
            device_id=device,
            device_id_type=MESH,
        )
        self.sends += 1
        return made

    def send(self, src, dst, slot, device):
        made = self.copy(src, dst, slot, device)
        made.start()
        self.open.append(made)

    def arrive(self, ref, slot):
        pltpu.make_async_remote_copy(
            src_ref=ref,
            dst_ref=ref,
            send_sem=self.send_sems.at[0],
            recv_sem=self.recv_sems.at[slot],
            device_id=self.place.x_dev,
            device_id_type=MESH,
        ).wait_recv()

    def local(self, src, dst):
        made = pltpu.make_async_copy(src, dst, self.local_sems.at[self.locals])
        self.locals += 1
        made.start()
        return made

    def finish(self):
        for made in self.open:
            made.wait_send()
        self.open = []


class SpreadPlane:
    def __init__(self, links, place, chunks):
        self.links, self.place, self.chunks = links, place, chunks
        self.z_slot, self.x_slot = links.slots(4 * len(chunks)), links.slots(4 * len(chunks))

    def begin_z(self):
        place = self.place
        for k, (src, dst) in enumerate(self.chunks):
            slot = self.z_slot + 4 * k + place.z
            for other in place.others:
                self.links.send(src, dst(place.f), slot, place.z_dev(other))

    def begin_x(self, k):
        src, dst = self.chunks[k]
        slot = self.x_slot + 4 * k + self.place.z
        self.links.send(src, dst(self.place.f), slot, self.place.x_dev)

    def forward(self, k):
        place, dst = self.place, self.chunks[k][1]
        for other in place.others:
            block = dst(other * 2 + place.x)
            self.links.arrive(block, self.z_slot + 4 * k + other)
            self.links.send(block, block, self.x_slot + 4 * k + other, place.x_dev)

    def end(self):
        for k in range(len(self.chunks)):
            for z in range(4):
                block = self.chunks[k][1](z * 2 + self.place.xo)
                self.links.arrive(block, self.x_slot + 4 * k + z)


def reduce_plane(links, place, chunks, own, from_x, to_z, from_z, total, done, ahead=2):
    count = len(chunks)
    x_slot, z_slot = links.slots(count), links.slots(4 * count)
    loads = {}

    def begin(k):
        links.send(chunks[k](place.xo), from_x.at[k], x_slot + k, place.x_dev)
        loads[k] = links.local(chunks[k](place.x), own.at[k])

    def middle(k):
        links.arrive(from_x.at[k], x_slot + k)
        loads[k].wait()
        for other in place.others:
            pair = own[k, other].astype(F32) + from_x[k, other].astype(F32)
            to_z[k, other] = pair.astype(BF16)
            links.send(
                to_z.at[k, other],
                from_z.at[k, place.z],
                z_slot + 4 * k + place.z,
                place.z_dev(other),
            )

    def end(k):
        sums = own[k, place.z].astype(F32) + from_x[k, place.z].astype(F32)
        for other in place.others:
            links.arrive(from_z.at[k, other], z_slot + 4 * k + other)
            sums += from_z[k, other].astype(F32)
        total[k] = sums.astype(BF16)
        done(k)

    for k in range(min(ahead, count)):
        begin(k)
    yield
    for k in range(count + 1):
        if k < count:
            middle(k)
            if k + ahead < count:
                begin(k + ahead)
            yield
        if k >= 1:
            end(k - 1)
            yield


class SpreadCtx:
    def __init__(self, links, place, out, parts):
        self.links, self.place, self.out, self.parts = links, place, out, parts
        self.slot = links.slots(3 * len(parts))

    def begin(self, k, src, y_too=True):
        place, rows = self.place, self.parts[k]
        self.links.send(src, self.out.at[place.c, rows], self.slot + 3 * k, place.core_dev)
        if y_too:
            self.begin_y(k, src)

    def begin_y(self, k, src):
        place, rows = self.place, self.parts[k]
        self.links.send(src, self.out.at[place.c, rows], self.slot + 3 * k + 1, place.y_dev)

    def forward(self, k):
        place = self.place
        block = self.out.at[place.c_y, self.parts[k]]
        self.links.arrive(block, self.slot + 3 * k + 1)
        self.links.send(block, block, self.slot + 3 * k + 2, place.core_dev)

    def end(self):
        place = self.place
        for k, rows in enumerate(self.parts):
            self.links.arrive(self.out.at[place.c_core, rows], self.slot + 3 * k)
            self.links.arrive(self.out.at[place.c_diag, rows], self.slot + 3 * k + 2)


class ReduceCtx:
    def __init__(self, links, place, part, parts, own, from_core, to_y, from_y):
        self.links, self.place, self.part, self.parts = links, place, part, parts
        self.own, self.from_core, self.to_y, self.from_y = own, from_core, to_y, from_y
        self.slot = links.slots(3 * len(parts))
        self.loads = {}

    def begin(self):
        place = self.place
        for side, y in ((0, place.yo), (1, place.y)):
            for k, rows in enumerate(self.parts):
                self.links.send(
                    self.part.at[y * 2 + place.co, rows],
                    self.from_core.at[side, rows],
                    self.slot + 3 * k + side,
                    place.core_dev,
                )
                if self.own is not None:
                    self.loads[side, k] = self.links.local(
                        self.part.at[y * 2 + place.core, rows], self.own.at[side, rows]
                    )

    def pair(self, side, k):
        rows = self.parts[k]
        self.links.arrive(self.from_core.at[side, rows], self.slot + 3 * k + side)
        if self.own is None:
            y = self.place.y if side else self.place.yo
            own = self.part[y * 2 + self.place.core, rows]
        else:
            self.loads[side, k].wait()
            own = self.own[side, rows]
        return own.astype(F32) + self.from_core[side, rows].astype(F32)

    def cross(self, k):
        rows = self.parts[k]
        self.to_y[rows] = self.pair(0, k).astype(BF16)
        self.links.send(
            self.to_y.at[rows], self.from_y.at[rows], self.slot + 3 * k + 2, self.place.y_dev
        )

    def total(self, k):
        rows = self.parts[k]
        sums = self.pair(1, k)
        self.links.arrive(self.from_y.at[rows], self.slot + 3 * k + 2)
        return sums + self.from_y[rows].astype(F32)


def halves(rows):
    return [pl.ds(0, rows // 2), pl.ds(rows // 2, rows // 2)]


def row_factor(values):
    return lax.rsqrt(jnp.mean(values * values, axis=-1, keepdims=True) + EPSILON)


def feed_reduce_kernel(
    gu_g, dn_g, ffn_part, dmid_part, middle, dout_s, keep, gain,
    gu_all, dn_all, layer_out, d_middle, gain_part, branch_all,
    own, from_x, to_z, from_z, total,
    own1, from_core1, to_y1, from_y1, own2, from_core2, to_y2, from_y2, branch,
    send_sems, recv_sems, local_sems,
):
    place = Place()
    links = Links(place, send_sems, recv_sems, local_sems)
    place.meet(place.neighbours())
    step = from_x.shape[2]
    chunks, where = [], []
    for grad, out in ((dn_g, dn_all), (gu_g, gu_all)):
        for first in range(0, grad.shape[2], step):
            rows = pl.ds(first, step)
            chunks.append(lambda x, grad=grad, rows=rows: grad.at[:, x, rows])
            where.append((out, rows))
    outs = [SpreadCtx(links, place, out, [rows]) for out, rows in where]
    kept = []

    def done(k):
        out, rows = where[k]
        outs[k].begin(0, total.at[k])
        kept.append(links.local(total.at[k], out.at[place.c, rows]))

    plane = reduce_plane(links, place, chunks, own, from_x, to_z, from_z, total, done)
    next(plane)
    parts = halves(middle.shape[0])
    dmid = ReduceCtx(links, place, dmid_part, parts, own1, from_core1, to_y1, from_y1)
    dmid.begin()
    for k in range(2):
        dmid.cross(k)
    next(plane)
    spread = SpreadCtx(links, place, branch_all, parts)
    gain_sum = None
    for k, rows in enumerate(parts):
        d_norm = dmid.total(k)
        value = middle[rows]
        factor = row_factor(value)
        term = jnp.sum(d_norm * value * factor, axis=0, keepdims=True)
        gain_sum = term if gain_sum is None else gain_sum + term
        scaled = d_norm * gain[...]
        inner = jnp.mean(scaled * value, axis=-1, keepdims=True)
        grad = dout_s[rows].astype(F32) + factor * scaled - value * (factor * factor * factor * inner)
        d_middle[rows] = grad
        branch[rows] = grad.astype(BF16)
        spread.begin(k, branch.at[rows])
        kept.append(links.local(branch.at[rows], branch_all.at[place.c, rows]))
    gain_part[...] = gain_sum
    next(plane)
    ffn = ReduceCtx(links, place, ffn_part, parts, own2, from_core2, to_y2, from_y2)
    ffn.begin()
    for k in range(2):
        spread.forward(k)
    for k in range(2):
        ffn.cross(k)
    next(plane)
    next(plane)
    for k, rows in enumerate(parts):
        layer_out[rows] = (keep[rows] * (middle[rows] + ffn.total(k))).astype(BF16)
    forwarded = 0
    for step_at, _ in enumerate(plane):
        if step_at % 2 == 1:
            outs[forwarded].forward(0)
            forwarded += 1
    for k in range(forwarded, len(outs)):
        outs[k].forward(0)
    spread.end()
    for out in outs:
        out.end()
    for made in kept:
        made.wait()
    links.finish()


def last_kernel(
    qkv_g, out_g, dnorm_part, x_s, d_middle, gain, ffn_part, qk_part,
    qkv_all, out_all, input_grad, stats,
    own, from_x, to_z, from_z, total,
    own1, from_core1, to_y1, from_y1,
    out_own, out_x, out_low, out_z,
    mine, plane_stats, ctx_stats, send_sems, recv_sems, local_sems,
):
    place = Place()
    links = Links(place, send_sems, recv_sems, local_sems)
    fellows = [lax.rem(place.f + d, 8) for d in range(1, 8)]
    place.meet(
        [(f, place.c) for f in fellows] + [place.core_dev, place.y_dev, place.diag_dev]
    )
    step = from_x.shape[2]
    chunks = []
    for first in range(0, qkv_g.shape[2], step):
        rows = pl.ds(first, step)
        chunks.append(lambda x, rows=rows: qkv_g.at[:, x, rows])
    outs = [
        SpreadCtx(links, place, qkv_all, [pl.ds(k * step, step)]) for k in range(len(chunks))
    ]
    kept = []

    def done(k):
        outs[k].begin(0, total.at[k])
        kept.append(links.local(total.at[k], qkv_all.at[place.c, pl.ds(k * step, step)]))

    out_slot = links.slots(1)
    links.send(out_g.at[place.xo], out_x, out_slot, place.x_dev)
    out_load = links.local(out_g.at[place.x], out_own)
    plane = reduce_plane(links, place, chunks, own, from_x, to_z, from_z, total, done)
    next(plane)
    parts = halves(x_s.shape[0])
    dnorm = ReduceCtx(links, place, dnorm_part, parts, own1, from_core1, to_y1, from_y1)
    dnorm.begin()
    for k in range(2):
        dnorm.cross(k)

    links.arrive(out_x, out_slot)
    out_load.wait()
    root_slot, final_slot = links.slots(4), links.slots(1)
    holds = place.z == place.c
    pair = out_own[...].astype(F32) + out_x[...].astype(F32)
    out_low[...] = pair.astype(BF16)
    to_root = links.copy(
        out_low, out_z.at[place.z], root_slot + place.z, (place.c * 2 + place.x, place.c)
    )

    @pl.when(jnp.logical_not(holds))
    def _():
        to_root.start()

    next(plane)
    gain_sum = None
    for k, rows in enumerate(parts):
        d_norm = dnorm.total(k)
        value = x_s[rows].astype(F32)
        factor = row_factor(value)
        term = jnp.sum(d_norm * value * factor, axis=0, keepdims=True)
        gain_sum = term if gain_sum is None else gain_sum + term
        scaled = d_norm * gain[...]
        inner = jnp.mean(scaled * value, axis=-1, keepdims=True)
        grad = d_middle[rows] + factor * scaled - value * (factor * factor * factor * inner)
        input_grad[rows] = grad.astype(BF16)
    mine[0:1] = gain_sum
    mine[1:2] = ffn_part[...]
    mine[2:3] = qk_part[...]
    mine[3:8] = jnp.zeros((5, mine.shape[1]), F32)
    plane_slot, ctx_slot = links.slots(8), links.slots(4)
    for f in fellows:
        links.send(mine, plane_stats.at[place.f], plane_slot + place.f, (f, place.c))
    plane_stats[place.f] = mine[...]

    final = [
        links.copy(out_all, out_all, final_slot, device)
        for device in (place.core_dev, place.y_dev)
    ]
    onward = links.copy(out_all, out_all, final_slot, place.core_dev)

    @pl.when(holds)
    def _():
        sums = out_own[...].astype(F32) + out_x[...].astype(F32)
        for other in place.others:
            links.arrive(out_z.at[other], root_slot + other)
            sums += out_z[other].astype(F32)
        out_all[...] = sums.astype(BF16)
        for made in final:
            made.start()

    for f in fellows:
        links.arrive(plane_stats.at[f], plane_slot + f)
    sums = plane_stats[0]
    for f in range(1, 8):
        sums += plane_stats[f]
    ctx_stats[place.c] = sums
    for device in (place.core_dev, place.y_dev, place.diag_dev):
        links.send(ctx_stats.at[place.c], ctx_stats.at[place.c], ctx_slot + place.c, device)
    for _ in plane:
        pass
    for out in outs:
        out.forward(0)
    relays = place.c_y == place.z

    @pl.when(jnp.logical_not(holds))
    def _():
        links.arrive(out_all, final_slot)

    @pl.when(relays)
    def _():
        onward.start()

    for c in (place.c_core, place.c_y, place.c_diag):
        links.arrive(ctx_stats.at[c], ctx_slot + c)
    stats[...] = ((ctx_stats[0] + ctx_stats[1]) + ctx_stats[2]) + ctx_stats[3]
    for out in outs:
        out.end()
    for made in kept:
        made.wait()
    links.finish()

    @pl.when(jnp.logical_not(holds))
    def _():
        to_root.wait_send()

    @pl.when(relays)
    def _():
        onward.wait_send()

    @pl.when(holds)
    def _():
        for made in final:
            made.wait_send()


def low_half(shape):
    return lax.rem(lax.broadcasted_iota(jnp.int32, shape, len(shape) - 1), 128) < 64


def partner(values):
    lane = lax.broadcasted_iota(jnp.int32, values.shape, len(values.shape) - 1)
    first = lax.rem(lane, 64) < 32
    return jnp.where(first, pltpu.roll(values, 96, 1), pltpu.roll(values, 32, 1))


def half_sums(values):
    low = low_half(values.shape)
    first = jnp.sum(jnp.where(low, values, 0.0), axis=-1, keepdims=True)
    second = jnp.sum(jnp.where(low, 0.0, values), axis=-1, keepdims=True)
    return jnp.where(low, first, second)


def row_loop(count, body):
    def step(index, carry):
        body(index)
        return carry

    lax.fori_loop(0, count, step, 0)


BLOCK = 256


def attention_scores(query, keys, key_bias, first, span):
    scores = lax.dot_general(
        query, keys, (((1,), (1,)), ((), ())), preferred_element_type=F32
    ) * (1.0 / math.sqrt(HEAD_DIM))
    rows = first + lax.broadcasted_iota(jnp.int32, scores.shape, 0)
    columns = lax.broadcasted_iota(jnp.int32, scores.shape, 1)
    return jnp.where(columns <= rows, scores, -1e30) + key_bias[:, :span]


def forward_kernel(
    qkv_s, out_s, gain_s, x_s, gu_s, dn_s, dout_s, cos_h, sin_h, head_gain, key_bias,
    qkv_wh, out_wh, gains, normed_h, qkv_raw_h, qkv_low_h, att_low_h, log_sums_h,
    gu_w, dn_w, dout_all, middle, mid_all,
    cos, sin, gain_blocks, qkv_w, out_w, x_all, normed, qkv_raw, qkv_low, att_low, log_sums,
    part, keys, values, from_core, to_y, from_y, mid_low, send_sems, recv_sems, local_sems,
):
    place = Place()
    links = Links(place, send_sems, recv_sems, local_sems)
    fellows = [lax.rem(place.f + d, 8) for d in range(1, 8)]
    place.meet([(f, place.c) for f in fellows] + [place.core_dev, place.y_dev])

    qkv_plane = SpreadPlane(links, place, [(qkv_s, lambda f: qkv_w.at[f])])
    qkv_plane.begin_z()
    qkv_plane.begin_x(0)
    tokens = x_s.shape[0]
    parts = halves(tokens)
    x_spread = SpreadCtx(links, place, x_all, parts)
    for k, rows in enumerate(parts):
        x_spread.begin(k, x_s.at[rows])
    gain_slot = links.slots(8)
    for f in fellows:
        links.send(gain_s, gain_blocks.at[place.f], gain_slot + place.f, (f, place.c))
    kept = [
        links.local(qkv_s, qkv_w.at[place.f]),
        links.local(gain_s, gain_blocks.at[place.f]),
        links.local(x_s, x_all.at[place.c]),
        links.local(cos_h, cos),
        links.local(sin_h, sin),
    ]

    root_slot, side_slot = links.slots(1), links.slots(1)
    holds = place.z == place.c
    down = [
        links.copy(out_s, out_w.at[place.x], root_slot, place.z_dev(other))
        for other in place.others
    ]
    side = links.copy(out_s, out_w.at[place.x], side_slot, place.x_dev)
    onward = links.copy(out_w.at[place.x], out_w.at[place.x], side_slot, place.x_dev)
    own = pltpu.make_async_copy(out_s, out_w.at[place.x], local_sems.at[links.locals])
    links.locals += 1

    @pl.when(holds)
    def _():
        for made in down:
            made.start()
        side.start()
        own.start()

    step = 64
    chunks = []
    for src, dst in ((dn_s, dn_w), (gu_s, gu_w)):
        for first in range(0, src.shape[0], step):
            rows = pl.ds(first, step)
            chunks.append((src.at[rows], lambda f, dst=dst, rows=rows: dst.at[f, rows]))
    plane = SpreadPlane(links, place, chunks)
    plane.begin_z()
    plane.begin_x(0)
    plane.begin_x(1)
    qkv_plane.forward(0)
    for k in range(2, len(chunks)):
        plane.begin_x(k)
    last = [
        links.local(gu_s, gu_w.at[place.f]),
        links.local(dn_s, dn_w.at[place.f]),
        links.local(dout_s, dout_all.at[place.c]),
    ]
    for f in fellows:
        links.arrive(gain_blocks.at[f], gain_slot + f)
    for made in kept:
        made.wait()
    gains[...] = jnp.zeros_like(gains)
    for f in range(8):
        gains[0:2, 256 * f : 256 * (f + 1)] = gain_blocks[f, 0:2]
    dout = SpreadCtx(links, place, dout_all, parts)
    for k, rows in enumerate(parts):
        x_spread.forward(k)
        dout.begin(k, dout_s.at[rows])
    x_spread.end()
    qkv_plane.end()

    def project(index):
        rows = pl.ds(pl.multiple_of(index * BLOCK, BLOCK), BLOCK)
        source = x_all[index].astype(F32)
        normed[rows] = (source * row_factor(source) * gains[0:1]).astype(BF16)
        weight = qkv_w[...].reshape(normed.shape[1], qkv_w.shape[2])
        raw = jnp.dot(normed[rows], weight, preferred_element_type=F32)
        for b in range(3):
            block = raw[:, 128 * b : 128 * (b + 1)]
            qkv_raw[b, rows] = block
            factor = lax.rsqrt(half_sums(block * block) * (1.0 / HEAD_DIM) + EPSILON)
            scaled = block * factor * head_gain[b : b + 1]
            turned = scaled * cos[rows] + partner(scaled) * sin[rows]
            if b == 2:
                turned = jnp.where(low_half(turned.shape), turned, block)
            qkv_low[b, rows] = turned.astype(BF16)
            if b == 2:
                low = low_half(turned.shape)
                swapped = pltpu.roll(turned, 64, 1)
                keys[rows] = jnp.where(low, turned, swapped).astype(BF16)
                values[rows] = jnp.where(low, swapped, turned).astype(BF16)

    seq = normed.shape[0]
    row_loop(seq // BLOCK, project)
    last += [
        links.local(normed, normed_h),
        links.local(qkv_raw, qkv_raw_h),
        links.local(qkv_low, qkv_low_h),
        links.local(qkv_w, qkv_wh),
    ]

    def heads(b):
        for i in range(seq // BLOCK):
            rows, span = pl.ds(i * BLOCK, BLOCK), (i + 1) * BLOCK
            query = qkv_low[b, rows]
            low = low_half(query.shape)
            outs, logs = [], []
            for half in range(2):
                chosen = jnp.where(low if half == 0 else jnp.logical_not(low), query, 0)
                scores = attention_scores(chosen, keys[:span], key_bias[0:1], i * BLOCK, span)
                top = jnp.max(scores, axis=-1, keepdims=True)
                expanded = jnp.exp(scores - top)
                sums = jnp.sum(expanded, axis=-1, keepdims=True)
                probs = (expanded * (1.0 / sums)).astype(BF16)
                outs.append(jnp.dot(probs, values[:span], preferred_element_type=F32))
                logs.append(top + jnp.log(sums))
            att_low[b, rows] = jnp.where(low, outs[0], outs[1]).astype(BF16)
            log_sums[b, rows] = jnp.where(low, logs[0], logs[1])

    row_loop(2, heads)

    @pl.when(jnp.logical_not(holds))
    def _():
        links.arrive(out_w.at[place.x], root_slot)
        onward.start()

    @pl.when(holds)
    def _():
        own.wait()

    for k in range(len(parts)):
        dout.forward(k)
    links.arrive(out_w.at[place.xo], side_slot)

    def project_out(index):
        rows = pl.ds(pl.multiple_of(index * BLOCK, BLOCK), BLOCK)
        sums = jnp.dot(att_low[0, rows], out_w[0], preferred_element_type=F32)
        sums += jnp.dot(att_low[1, rows], out_w[1], preferred_element_type=F32)
        part[index] = sums.astype(BF16)

    row_loop(seq // BLOCK, project_out)
    reduce = ReduceCtx(links, place, part, parts, None, from_core, to_y, from_y)
    reduce.begin()
    last += [
        links.local(att_low, att_low_h),
        links.local(log_sums, log_sums_h),
        links.local(out_w, out_wh),
    ]
    for k in range(2):
        reduce.cross(k)
    plane.forward(0)
    plane.forward(1)
    mid = SpreadCtx(links, place, mid_all, parts)
    for k, rows in enumerate(parts):
        value = x_all[place.c, rows].astype(F32) + reduce.total(k)
        middle[rows] = value
        mid_low[rows] = (value * row_factor(value) * gains[1:2]).astype(BF16)
        mid.begin(k, mid_low.at[rows])
        last.append(links.local(mid_low.at[rows], mid_all.at[place.c, rows]))
    plane.forward(2)
    for k in range(2):
        mid.forward(k)
    for k in range(3, len(chunks)):
        plane.forward(k)
    plane.end()
    mid.end()
    dout.end()
    for made in last:
        made.wait()
    links.finish()

    @pl.when(holds)
    def _():
        for made in down:
            made.wait_send()
        side.wait_send()

    @pl.when(jnp.logical_not(holds))
    def _():
        onward.wait_send()


NT = (((1,), (1,)), ((), ()))
TN = (((0,), (0,)), ((), ()))


def attention_back_kernel(
    branch, qkv_w, out_w, cos, sin, head_gain, key_bias,
    normed, qkv_raw, qkv_low, att_low, log_sums,
    part, qkv_g, out_g, gain_g, keys, values, d_att, d_low, d_keys, d_values,
):
    seq = branch.shape[0]
    root = 1.0 / math.sqrt(HEAD_DIM)
    gain_g[...] = jnp.zeros_like(gain_g)
    d_keys[...] = jnp.zeros_like(d_keys)
    d_values[...] = jnp.zeros_like(d_values)

    def prepare(index):
        rows = pl.ds(pl.multiple_of(index * BLOCK, BLOCK), BLOCK)
        block = qkv_low[2, rows].astype(F32)
        low = low_half(block.shape)
        swapped = pltpu.roll(block, 64, 1)
        keys[rows] = jnp.where(low, block, swapped).astype(BF16)
        values[rows] = jnp.where(low, swapped, block).astype(BF16)
        for b in range(2):
            d_att[b, rows] = lax.dot_general(
                branch[rows], out_w[b], NT, preferred_element_type=F32
            ).astype(BF16)

    row_loop(seq // BLOCK, prepare)

    def unturn(row, rows, grads, block):
        back = grads * cos[rows] + partner(grads * sin[rows])
        factor = lax.rsqrt(half_sums(block * block) * (1.0 / HEAD_DIM) + EPSILON)
        gain_term = jnp.sum(back * block * factor, axis=0, keepdims=True)
        scaled = back * head_gain[row : row + 1]
        inner = half_sums(scaled * block) * (1.0 / HEAD_DIM)
        return factor * scaled - block * (factor * factor * factor * inner), gain_term

    def heads(b):
        out_g[b] = lax.dot_general(
            att_low[b], branch[...], TN, preferred_element_type=F32
        ).astype(BF16)
        for i in range(seq // BLOCK):
            rows, span = pl.ds(i * BLOCK, BLOCK), (i + 1) * BLOCK
            query, d_out = qkv_low[b, rows], d_att[b, rows]
            logs = log_sums[b, rows]
            low = low_half(query.shape)
            d_query = []
            for half in range(2):
                side = low if half == 0 else jnp.logical_not(low)
                chosen, d_chosen = jnp.where(side, query, 0), jnp.where(side, d_out, 0)
                scores = attention_scores(chosen, keys[:span], key_bias[0:1], i * BLOCK, span)
                probs = jnp.exp(scores - logs[:, 64 * half : 64 * half + 1])
                d_probs = lax.dot_general(
                    d_chosen, values[:span], NT, preferred_element_type=F32
                )
                delta = jnp.sum(probs * d_probs, axis=-1, keepdims=True)
                d_scores = (probs * (d_probs - delta)).astype(BF16)
                d_query.append(jnp.dot(d_scores, keys[:span], preferred_element_type=F32))
                d_keys[:span] += lax.dot_general(
                    d_scores, chosen, TN, preferred_element_type=F32
                )
                d_values[:span] += lax.dot_general(
                    probs.astype(BF16), d_chosen, TN, preferred_element_type=F32
                )
            grads = (jnp.where(low, d_query[0], d_query[1]) * root).astype(BF16).astype(F32)
            d_block, gain_term = unturn(0, rows, grads, qkv_raw[b, rows])
            d_low[b, rows] = d_block.astype(BF16)
            gain_g[0:1] += gain_term

    row_loop(2, heads)

    def finish(index):
        rows = pl.ds(pl.multiple_of(index * BLOCK, BLOCK), BLOCK)
        k_sum, v_sum = d_keys[rows], d_values[rows]
        low = low_half(k_sum.shape)
        k_sum = (k_sum + pltpu.roll(k_sum, 64, 1)) * root
        v_sum = v_sum + pltpu.roll(v_sum, 64, 1)
        grads = jnp.where(low, k_sum, v_sum).astype(BF16).astype(F32)
        d_block, gain_term = unturn(2, rows, grads, qkv_raw[2, rows])
        d_low[2, rows] = jnp.where(low, d_block, grads).astype(BF16)
        gain_g[1:2] += gain_term
        sums = jnp.zeros((BLOCK, part.shape[2]), F32)
        for b in range(3):
            sums += lax.dot_general(
                d_low[b, rows], qkv_w[:, 128 * b : 128 * (b + 1)], NT, preferred_element_type=F32
            )
        part[index] = sums.astype(BF16)

    row_loop(seq // BLOCK, finish)
    for b in range(3):
        grad = lax.dot_general(d_low[b], normed[...], TN, preferred_element_type=F32).astype(BF16)
        for f in range(8):
            qkv_g[f, 128 * b : 128 * (b + 1)] = grad[:, 256 * f : 256 * (f + 1)]


def shaped(shape, kind=BF16):
    return jax.ShapeDtypeStruct(shape, kind)


def call(kernel, ins, outs, scratch=(), sems=None, number=None, flops=0):
    scratch = list(scratch)
    extra = {}
    if sems is not None:
        scratch += [pltpu.SemaphoreType.DMA((n,)) for n in sems]
        extra = dict(collective_id=number, has_side_effects=True)
    return pl.pallas_call(
        kernel,
        out_shape=tuple(shape for shape, _ in outs),
        in_specs=[spec for _, spec in ins],
        out_specs=tuple(spec for _, spec in outs),
        scratch_shapes=scratch,
        compiler_params=pltpu.CompilerParams(vmem_limit_bytes=VMEM_BYTES, **extra),
    )(*[array for array, _ in ins])


def split_heads(
    inputs,
    cotangent,
    lengths,
    qkv_weight,
    out_weight,
    gate_up,
    down_weight,
    attn_gain,
    ffn_gain,
    qk_gain,
):
    tokens, width = inputs.shape[1:]
    seq = tokens * 4
    c = lax.axis_index("ctx")
    length = lengths[0]
    positions = c * tokens + jnp.arange(tokens, dtype=jnp.int32)
    keep = (positions < length).astype(F32)[:, None]
    all_positions = jnp.arange(seq, dtype=jnp.int32)
    key_bias = jnp.broadcast_to(jnp.where(all_positions < length, 0.0, -1e30)[None], (8, seq))
    source = inputs[0]
    d_out = (keep * cotangent[0].astype(F32)).astype(BF16)

    query_cols, key_cols = HEADS * HEAD_DIM, KV_HEADS * HEAD_DIM
    qkv_s = jnp.concatenate(
        [
            lax.dynamic_slice_in_dim(qkv_weight, c * 256, 256, 1),
            lax.dynamic_slice_in_dim(qkv_weight, query_cols + c * 64, 64, 1),
            lax.dynamic_slice_in_dim(qkv_weight, query_cols + key_cols + c * 64, 64, 1),
        ],
        axis=1,
    )
    rows, parts, units = gate_up.shape
    gu_s = lax.dynamic_index_in_dim(
        gate_up.reshape(rows, parts, 8, 4, units // 32), c, 3, keepdims=False
    ).reshape(rows, parts * units // 4)
    down_rows = down_weight.shape[0] // 4
    dn_s = lax.dynamic_slice_in_dim(down_weight, c * down_rows, down_rows, 0)
    gain_s = jnp.concatenate(
        [attn_gain[None], ffn_gain[None], jnp.zeros((6, rows), BF16)], axis=0
    ).astype(F32)

    half_dim = HEAD_DIM // 2
    angles = np.arange(seq)[:, None] * 10000.0 ** (-2.0 * np.arange(half_dim) / HEAD_DIM)[None]
    cos = jnp.tile(jnp.asarray(np.cos(angles), F32), (1, 4))
    sine = jnp.asarray(np.sin(angles), F32)
    sin = jnp.tile(jnp.concatenate([-sine, sine], axis=1), (1, 2))
    q_gain = jnp.tile(qk_gain[0].astype(F32), 2)
    k_gain = jnp.concatenate([qk_gain[1].astype(F32), jnp.ones((HEAD_DIM,), F32)])
    head_gain = jnp.concatenate(
        [q_gain[None], q_gain[None], k_gain[None], jnp.zeros((5, 128), F32)], axis=0
    )

    ctx_scratch = [
        pltpu.VMEM((2, tokens, width), BF16),
        pltpu.VMEM((2, tokens, width), BF16),
        pltpu.VMEM((tokens, width), BF16),
        pltpu.VMEM((tokens, width), BF16),
    ]
    table = pltpu.VMEM((seq, 128), F32)
    (
        qkv_w, out_w, gains, normed, qkv_raw, qkv_low, att_low, log_sums,
        gu_w, dn_w, dout_all, middle, mid_all,
    ) = call(
        forward_kernel,
        [(a, HBM) for a in (qkv_s, out_weight, gain_s, source, gu_s, dn_s, d_out, cos, sin)]
        + [(head_gain, VMEM), (key_bias, VMEM)],
        [
            (shaped((8, rows, 384)), HBM),
            (shaped((2, out_weight.shape[0], width)), HBM),
            (shaped((8, width), F32), VMEM),
            (shaped((seq, width)), HBM),
            (shaped((3, seq, 128), F32), HBM),
            (shaped((3, seq, 128)), HBM),
            (shaped((2, seq, 128)), HBM),
            (shaped((2, seq, 128), F32), HBM),
            (shaped((8, rows, width)), HBM),
            (shaped((8, down_rows, width)), HBM),
            (shaped((4, tokens, width)), HBM),
            (shaped((tokens, width), F32), VMEM),
            (shaped((4, tokens, width)), HBM),
        ],
        [
            table,
            table,
            pltpu.VMEM((8, 8, rows), F32),
            pltpu.VMEM((8, rows, 384), BF16),
            pltpu.VMEM((2, out_weight.shape[0], width), BF16),
            pltpu.VMEM((4, tokens, width), BF16),
            pltpu.VMEM((seq, width), BF16),
            pltpu.VMEM((3, seq, 128), F32),
            pltpu.VMEM((3, seq, 128), BF16),
            pltpu.VMEM((2, seq, 128), BF16),
            pltpu.VMEM((2, seq, 128), F32),
            pltpu.VMEM((4, tokens, width), BF16),
            pltpu.VMEM((seq, 128), BF16),
            pltpu.VMEM((seq, 128), BF16),
            pltpu.VMEM((2, tokens, width), BF16),
            pltpu.VMEM((tokens, width), BF16),
            pltpu.VMEM((tokens, width), BF16),
            pltpu.VMEM((tokens, width), BF16),
        ],
        sems=(90, 100, 24),
        number=0,
    )
    attn_norm, ffn_norm = gains[0:1], gains[1:2]
    qkv_w = qkv_w.reshape(width, 384)
    tables = [(cos, VMEM), (sin, VMEM), (head_gain, VMEM), (key_bias, VMEM)]
    hidden_units = units // 4
    gu_full = gu_w.reshape(width, parts * hidden_units)
    dn_full = dn_w.reshape(hidden_units, width)
    mid_full = mid_all.reshape(seq, width)
    dout_full = dout_all.reshape(seq, width)
    projected = jnp.dot(mid_full, gu_full, preferred_element_type=F32)
    gate, up = projected[:, :hidden_units], projected[:, hidden_units:]
    sigmoid = jax.nn.sigmoid(gate)
    hidden = (gate * sigmoid * up).astype(BF16)
    ffn_part = jnp.dot(hidden, dn_full, preferred_element_type=F32).astype(BF16)
    d_hidden = contract_cols(dout_full, dn_full)
    d_projected = jnp.concatenate(
        [
            (d_hidden * up * (sigmoid * (1.0 + gate * (1.0 - sigmoid)))).astype(BF16),
            (d_hidden * gate * sigmoid).astype(BF16),
        ],
        axis=1,
    )
    dn_g = contract_rows(hidden, dout_full).astype(BF16)
    gu_g = contract_rows(mid_full, d_projected).astype(BF16)
    dmid_part = contract_cols(d_projected, gu_full).astype(BF16)

    step = 64
    count = (rows + down_rows) // step
    gu_all, dn_all, layer_out, d_middle, ffn_gain_part, branch_all = call(
        feed_reduce_kernel,
        [
            (gu_g.reshape(4, 2, rows, width), HBM),
            (dn_g.reshape(4, 2, down_rows, width), HBM),
            (ffn_part.reshape(4, tokens, width), HBM),
            (dmid_part.reshape(4, tokens, width), HBM),
            (middle, VMEM),
            (d_out, VMEM),
            (keep, VMEM),
            (ffn_norm, VMEM),
        ],
        [
            (shaped((4, rows, width)), HBM),
            (shaped((4, down_rows, width)), HBM),
            (shaped((tokens, width)), VMEM),
            (shaped((tokens, width), F32), VMEM),
            (shaped((1, width), F32), VMEM),
            (shaped((4, tokens, width)), HBM),
        ],
        [
            pltpu.VMEM((count, 4, step, width), BF16),
            pltpu.VMEM((count, 4, step, width), BF16),
            pltpu.VMEM((count, 4, step, width), BF16),
            pltpu.VMEM((count, 4, step, width), BF16),
            pltpu.VMEM((count, step, width), BF16),
        ]
        + ctx_scratch
        + ctx_scratch
        + [pltpu.VMEM((tokens, width), BF16)],
        sems=(80, 80, 40),
        number=2,
    )
    dnorm_part, qkv_g, out_g, head_gain_g = call(
        attention_back_kernel,
        [(branch_all.reshape(seq, width), VMEM), (qkv_w, VMEM), (out_w, VMEM)]
        + tables
        + [(a, VMEM) for a in (normed, qkv_raw, qkv_low, att_low, log_sums)],
        [
            (shaped((4, tokens, width)), VMEM),
            (shaped((8, 384, rows)), VMEM),
            (shaped((2, 128, width)), VMEM),
            (shaped((8, 128), F32), VMEM),
        ],
        [
            pltpu.VMEM((seq, 128), BF16),
            pltpu.VMEM((seq, 128), BF16),
            pltpu.VMEM((2, seq, 128), BF16),
            pltpu.VMEM((3, seq, 128), BF16),
            pltpu.VMEM((seq, 128), F32),
            pltpu.VMEM((seq, 128), F32),
        ],
    )
    qk_part = jnp.concatenate(
        [
            head_gain_g[0:1, :64] + head_gain_g[0:1, 64:],
            head_gain_g[1:2, :64],
            jnp.zeros((1, width - 128), F32),
        ],
        axis=1,
    )
    step = 192
    count = 384 // step
    qkv_all, out_all, input_grad, stats = call(
        last_kernel,
        [
            (qkv_g.reshape(4, 2, 384, rows), HBM),
            (out_g, HBM),
            (dnorm_part, HBM),
            (source, VMEM),
            (d_middle, VMEM),
            (attn_norm, VMEM),
            (ffn_gain_part, VMEM),
            (qk_part, VMEM),
        ],
        [
            (shaped((4, 384, rows)), HBM),
            (shaped((128, width)), VMEM),
            (shaped((tokens, width)), VMEM),
            (shaped((8, width), F32), VMEM),
        ],
        [
            pltpu.VMEM((count, 4, step, rows), BF16),
            pltpu.VMEM((count, 4, step, rows), BF16),
            pltpu.VMEM((count, 4, step, rows), BF16),
            pltpu.VMEM((count, 4, step, rows), BF16),
            pltpu.VMEM((count, step, rows), BF16),
        ]
        + ctx_scratch
        + [
            pltpu.VMEM((128, width), BF16),
            pltpu.VMEM((128, width), BF16),
            pltpu.VMEM((128, width), BF16),
            pltpu.VMEM((4, 128, width), BF16),
            pltpu.VMEM((8, width), F32),
            pltpu.VMEM((8, 8, width), F32),
            pltpu.VMEM((4, 8, width), F32),
        ],
        sems=(60, 60, 20),
        number=3,
    )
    f = lax.axis_index("fsdp")
    qkv_grad = jnp.concatenate(
        [
            jnp.transpose(qkv_all[:, :256], (2, 0, 1)).reshape(rows, query_cols),
            jnp.transpose(qkv_all[:, 256:320], (2, 0, 1)).reshape(rows, key_cols),
            jnp.transpose(qkv_all[:, 320:], (2, 0, 1)).reshape(rows, key_cols),
        ],
        axis=1,
    ).astype(F32)
    gate_up_grad = (
        jnp.transpose(gu_all.reshape(4, rows, parts, 8, units // 32), (1, 2, 3, 0, 4))
        .reshape(rows, parts, units)
        .astype(F32)
    )
    return (
        layer_out[None],
        input_grad[None],
        qkv_grad,
        out_all.astype(F32),
        gate_up_grad,
        dn_all.reshape(4 * down_rows, width).astype(F32),
        lax.dynamic_slice_in_dim(stats[0], f * rows, rows, 0),
        lax.dynamic_slice_in_dim(stats[1], f * rows, rows, 0),
        stats[2, :128].reshape(2, 64),
    )


def solution(mesh):
    sizes = (mesh.shape["fsdp"], mesh.shape["ctx"])
    return jax.shard_map(
        split_heads if sizes == (8, 4) else on_device,
        mesh=mesh,
        in_specs=(
            P("fsdp", "ctx", None),
            P("fsdp", "ctx", None),
            P("fsdp"),
            P("fsdp", None),
            P("fsdp", None),
            P("fsdp", None, None),
            P("fsdp", None),
            P("fsdp"),
            P("fsdp"),
            P(),
        ),
        out_specs=(
            P("fsdp", "ctx", None),
            P("fsdp", "ctx", None),
            P("fsdp", None),
            P("fsdp", None),
            P("fsdp", None, None),
            P("fsdp", None),
            P("fsdp"),
            P("fsdp"),
            P(),
        ),
        check_vma=False,
    )
```

```python
import functools
import math

import jax
import jax.numpy as jnp
import numpy as np
from jax import lax
from jax.experimental import pallas as pl
from jax.experimental.pallas import tpu as pltpu
from jax.sharding import PartitionSpec as P

HEADS = 16
KV_HEADS = 4
HEAD_DIM = 64


EPSILON = 1e-06


def root_norm(values, norm_gain):
    factor = lax.rsqrt(jnp.mean(values * values, axis=-1, keepdims=True) + EPSILON)
    return values * factor * norm_gain


def rotation_tables(positions):
    half_dim = HEAD_DIM // 2
    frequency = 10000.0 ** (-(2.0 * jnp.arange(half_dim, dtype=jnp.float32)) / HEAD_DIM)
    angles = positions.astype(jnp.float32)[:, None] * frequency[None, :]
    return (jnp.cos(angles), jnp.sin(angles))


def rotate(values, cos_table, sin_table):
    half_dim = values.shape[-1] // 2
    lower_half = values[..., :half_dim]
    upper_half = values[..., half_dim:]
    cos_part = cos_table[:, None, :]
    sin_part = sin_table[:, None, :]
    return jnp.concatenate(
        [
            lower_half * cos_part - upper_half * sin_part,
            upper_half * cos_part + lower_half * sin_part,
        ],
        axis=-1,
    )


def prepare_heads(qkv_out, head_gain, cos_table, sin_table):
    row_count = qkv_out.shape[0]
    query_cols = HEADS * HEAD_DIM
    key_cols = KV_HEADS * HEAD_DIM
    queries = qkv_out[:, :query_cols].reshape(row_count, HEADS, HEAD_DIM)
    key_part = qkv_out[:, query_cols : query_cols + key_cols].reshape(row_count, KV_HEADS, HEAD_DIM)
    value_part = qkv_out[:, query_cols + key_cols :]
    queries = rotate(root_norm(queries, head_gain[0]), cos_table, sin_table).reshape(
        row_count, query_cols
    )
    key_part = rotate(root_norm(key_part, head_gain[1]), cos_table, sin_table).reshape(
        row_count, key_cols
    )
    return (queries, key_part, value_part)


def activate(projected):
    gate_part = projected[:, 0]
    return gate_part * jax.nn.sigmoid(gate_part) * projected[:, 1]


def contract_rows(left, right):
    return lax.dot_general(
        left, right, (((0,), (0,)), ((), ())), preferred_element_type=jnp.float32
    )


def contract_cols(left, right):
    return lax.dot_general(
        left, right, (((1,), (1,)), ((), ())), preferred_element_type=jnp.float32
    )


def on_device(
    inputs,
    cotangent,
    lengths,
    qkv_weight,
    out_weight,
    gate_up,
    down_weight,
    attn_gain,
    ffn_gain,
    qk_gain,
):
    token_count = inputs.shape[1]
    group = HEADS // KV_HEADS
    key_cols = KV_HEADS * HEAD_DIM
    seq_len = token_count * lax.axis_size("ctx")
    positions = lax.axis_index("ctx") * token_count + jnp.arange(token_count, dtype=jnp.int32)
    length = lengths[0]
    row_keep = (positions < length).astype(jnp.float32)[:, None]
    inv_root = 1.0 / math.sqrt(HEAD_DIM)
    source = inputs[0].astype(jnp.float32)
    qkv_full, out_full, attn_full, ffn_full = (
        lax.all_gather(qkv_weight, "fsdp", axis=0, tiled=True),
        lax.all_gather(out_weight, "fsdp", axis=0, tiled=True),
        lax.all_gather(attn_gain, "fsdp", axis=0, tiled=True),
        lax.all_gather(ffn_gain, "fsdp", axis=0, tiled=True),
    )
    attn_norm = attn_full.astype(jnp.float32)
    ffn_norm = ffn_full.astype(jnp.float32)
    normed = root_norm(source, attn_norm).astype(jnp.bfloat16)
    qkv_out = jnp.dot(normed, qkv_full, preferred_element_type=jnp.float32)
    cos_table, sin_table = rotation_tables(positions)
    head_gain = qk_gain.astype(jnp.float32)

    def head_pieces(qkv_values, gain_values):
        return prepare_heads(qkv_values, gain_values, cos_table, sin_table)

    head_values, head_pull = jax.vjp(head_pieces, qkv_out, head_gain)
    queries, key_part, value_part = head_values
    query_low = queries.astype(jnp.bfloat16).reshape(token_count, KV_HEADS, group, HEAD_DIM)
    kv_local = jnp.concatenate([key_part, value_part], axis=1).astype(jnp.bfloat16)
    kv_whole = lax.all_gather(kv_local, "ctx", axis=0, tiled=True)
    block = 512
    block_total = seq_len // block
    kv_blocks = kv_whole.reshape(block_total, block, 2, KV_HEADS, HEAD_DIM)
    starts = jnp.arange(block_total, dtype=jnp.int32) * block

    def block_scores(key_block, block_start):
        scores = (
            jnp.einsum("bhgd,thd->hgbt", query_low, key_block, preferred_element_type=jnp.float32)
            * inv_root
        )
        key_pos = block_start + jnp.arange(key_block.shape[0], dtype=jnp.int32)
        visible = (key_pos[None, :] <= positions[:, None]) & (key_pos[None, :] < length)
        return (scores, visible)

    def max_step(state, item):
        running_max, running_sum = state
        kv_block, block_start = item
        scores, visible = block_scores(kv_block[:, 0], block_start)
        new_max = jnp.maximum(running_max, jnp.max(jnp.where(visible, scores, -1e30), axis=-1))
        expanded = jnp.where(visible, jnp.exp(scores - new_max[..., None]), 0.0)
        running_sum = running_sum * jnp.exp(running_max - new_max) + jnp.sum(expanded, axis=-1)
        return ((new_max, running_sum), None)

    stat_shape = (KV_HEADS, group, token_count)
    start_state = (jnp.full(stat_shape, -1e30, jnp.float32), jnp.zeros(stat_shape, jnp.float32))
    final_state, unused_out = lax.scan(max_step, start_state, (kv_blocks, starts))
    log_total = final_state[0] + jnp.log(final_state[1])

    def block_probs(kv_block, block_start):
        scores, visible = block_scores(kv_block[:, 0], block_start)
        return jnp.where(visible, jnp.exp(scores - log_total[..., None]), 0.0)

    def value_step(totals, item):
        kv_block, block_start = item
        probs_low = block_probs(kv_block, block_start).astype(jnp.bfloat16)
        return (
            totals
            + jnp.einsum(
                "hgbt,thd->bhgd", probs_low, kv_block[:, 1], preferred_element_type=jnp.float32
            ),
            None,
        )

    attended, unused_out = lax.scan(
        value_step,
        jnp.zeros((token_count, KV_HEADS, group, HEAD_DIM), jnp.float32),
        (kv_blocks, starts),
    )
    attended_low = attended.reshape(token_count, HEADS * HEAD_DIM).astype(jnp.bfloat16)
    middle = source + jnp.dot(attended_low, out_full, preferred_element_type=jnp.float32)
    normed_mid = root_norm(middle, ffn_norm).astype(jnp.bfloat16)
    columns = normed_mid
    projected = jnp.einsum(
        "td,dgf->tgf",
        columns,
        lax.all_gather(gate_up, "fsdp", axis=0, tiled=True),
        preferred_element_type=jnp.float32,
    )
    act_value, act_pull = jax.vjp(activate, projected)
    hidden = act_value.astype(jnp.bfloat16)
    columns = hidden
    ffn_out = jnp.dot(
        columns,
        lax.all_gather(down_weight, "fsdp", axis=0, tiled=True),
        preferred_element_type=jnp.float32,
    )
    layer_out = (row_keep * (middle + ffn_out)).astype(jnp.bfloat16)[None]
    d_out = row_keep * cotangent[0].astype(jnp.float32)
    d_out_low = d_out.astype(jnp.bfloat16)
    down_shard = lax.psum_scatter(
        contract_rows(hidden, d_out_low).astype(jnp.bfloat16),
        "fsdp",
        scatter_dimension=0,
        tiled=True,
    )
    d_hidden = contract_cols(d_out_low, lax.all_gather(down_weight, "fsdp", axis=0, tiled=True))
    d_proj_low = act_pull(d_hidden)[0].astype(jnp.bfloat16)
    columns = normed_mid
    gate_up_shard = lax.psum_scatter(
        jnp.einsum("td,tgf->dgf", columns, d_proj_low, preferred_element_type=jnp.float32).astype(
            jnp.bfloat16
        ),
        "fsdp",
        scatter_dimension=0,
        tiled=True,
    )
    d_normed_mid = jnp.einsum(
        "tgf,dgf->td",
        d_proj_low,
        lax.all_gather(gate_up, "fsdp", axis=0, tiled=True),
        preferred_element_type=jnp.float32,
    )
    mid_value, mid_pull = jax.vjp(root_norm, middle, ffn_norm)
    d_mid_norm, ffn_gain_part = mid_pull(d_normed_mid)
    d_middle = d_out + d_mid_norm
    d_branch = d_middle.astype(jnp.bfloat16)
    out_term = contract_rows(attended_low, d_branch)
    d_attended = (
        contract_cols(d_branch, out_full)
        .astype(jnp.bfloat16)
        .reshape(token_count, KV_HEADS, group, HEAD_DIM)
    )
    delta = jnp.transpose(jnp.sum(d_attended.astype(jnp.float32) * attended, axis=-1), (1, 2, 0))

    def block_grads(kv_block, block_start):
        probs = block_probs(kv_block, block_start)
        d_probs = jnp.einsum(
            "bhgd,thd->hgbt", d_attended, kv_block[:, 1], preferred_element_type=jnp.float32
        )
        d_scores = (probs * (d_probs - delta[..., None])).astype(jnp.bfloat16)
        return (probs.astype(jnp.bfloat16), d_scores)

    def query_step(totals, item):
        kv_block, block_start = item
        probs_low, d_scores = block_grads(kv_block, block_start)
        return (
            totals
            + jnp.einsum(
                "hgbt,thd->bhgd", d_scores, kv_block[:, 0], preferred_element_type=jnp.float32
            ),
            None,
        )

    d_query_sum, unused_out = lax.scan(
        query_step,
        jnp.zeros((token_count, KV_HEADS, group, HEAD_DIM), jnp.float32),
        (kv_blocks, starts),
    )
    d_query = (d_query_sum * inv_root).reshape(token_count, HEADS * HEAD_DIM).astype(jnp.bfloat16)
    sub_block = 512
    sub_total = token_count * lax.axis_size("ctx") // sub_block
    pieces = kv_whole.reshape(sub_total, sub_block, 2, KV_HEADS, HEAD_DIM)
    sub_starts = jnp.arange(sub_total, dtype=jnp.int32) * sub_block

    def key_grads(item):
        kv_block, block_start = item
        probs_low, d_scores = block_grads(kv_block, block_start)
        d_keys = (
            jnp.einsum("hgbt,bhgd->thd", d_scores, query_low, preferred_element_type=jnp.float32)
            * inv_root
        )
        d_values = jnp.einsum(
            "hgbt,bhgd->thd", probs_low, d_attended, preferred_element_type=jnp.float32
        )
        return jnp.concatenate(
            [d_keys.reshape(sub_block, key_cols), d_values.reshape(sub_block, key_cols)], axis=1
        )

    kv_grad = lax.psum_scatter(
        lax.map(key_grads, (pieces, sub_starts))
        .reshape(token_count * lax.axis_size("ctx"), 2 * key_cols)
        .astype(jnp.bfloat16),
        "ctx",
        scatter_dimension=0,
        tiled=True,
    ).astype(jnp.float32)
    d_key_low = kv_grad[:, :key_cols].astype(jnp.bfloat16).astype(jnp.float32)
    d_value_low = kv_grad[:, key_cols:].astype(jnp.bfloat16).astype(jnp.float32)
    d_qkv_out, qk_part = head_pull((d_query.astype(jnp.float32), d_key_low, d_value_low))
    d_qkv = d_qkv_out.astype(jnp.bfloat16)
    qkv_term = contract_rows(normed, d_qkv)
    d_normed = contract_cols(d_qkv, qkv_full)
    first_value, first_pull = jax.vjp(root_norm, source, attn_norm)
    d_source_norm, attn_gain_part = first_pull(d_normed)
    input_grad = (d_middle + d_source_norm).astype(jnp.bfloat16)[None]
    qkv_shard, out_shard, attn_shard, ffn_shard = (
        lax.psum_scatter(
            qkv_term.astype(jnp.bfloat16), "fsdp", scatter_dimension=0, tiled=True
        ).astype(jnp.float32),
        lax.psum_scatter(
            out_term.astype(jnp.bfloat16), "fsdp", scatter_dimension=0, tiled=True
        ).astype(jnp.float32),
        lax.psum_scatter(
            attn_gain_part.astype(jnp.bfloat16), "fsdp", scatter_dimension=0, tiled=True
        ).astype(jnp.float32),
        lax.psum_scatter(
            ffn_gain_part.astype(jnp.bfloat16), "fsdp", scatter_dimension=0, tiled=True
        ).astype(jnp.float32),
    )
    summed = (
        lax.psum(qkv_shard.astype(jnp.bfloat16), "ctx").astype(jnp.float32),
        lax.psum(out_shard.astype(jnp.bfloat16), "ctx").astype(jnp.float32),
        lax.psum(gate_up_shard, "ctx").astype(jnp.float32),
        lax.psum(down_shard, "ctx").astype(jnp.float32),
        lax.psum(attn_shard.astype(jnp.bfloat16), "ctx").astype(jnp.float32),
        lax.psum(ffn_shard.astype(jnp.bfloat16), "ctx").astype(jnp.float32),
    )
    qk_total = lax.psum(qk_part, ("fsdp", "ctx"))
    return (
        layer_out,
        input_grad,
        summed[0],
        summed[1],
        summed[2],
        summed[3],
        summed[4],
        summed[5],
        qk_total,
    )


MESH = pl.DeviceIdType.MESH
F32 = jnp.float32
BF16 = jnp.bfloat16
VMEM_BYTES = 60 << 20
HBM = pl.BlockSpec(memory_space=pl.ANY)
VMEM = pl.BlockSpec(memory_space=pltpu.VMEM)


class Place:
    def __init__(self):
        self.f = lax.axis_index("fsdp")
        self.c = lax.axis_index("ctx")
        self.z, self.x = lax.div(self.f, 2), lax.rem(self.f, 2)
        self.y, self.core = lax.div(self.c, 2), lax.rem(self.c, 2)
        self.xo, self.yo, self.co = 1 - self.x, 1 - self.y, 1 - self.core
        upper = lax.div(self.z, 2)
        self.others = (self.z + 1 - 2 * lax.rem(self.z, 2), 2 - upper, 3 - 3 * upper)
        self.x_dev = (self.z * 2 + self.xo, self.c)
        self.c_core = self.y * 2 + self.co
        self.c_y = self.yo * 2 + self.core
        self.c_diag = self.yo * 2 + self.co
        self.core_dev = (self.f, self.c_core)
        self.y_dev = (self.f, self.c_y)
        self.diag_dev = (self.f, self.c_diag)

    def rank(self, source, target):
        return jnp.where(source > target, source - 1, source)

    def z_dev(self, z):
        return (z * 2 + self.x, self.c)

    def meet(self, partners):
        barrier = pltpu.get_barrier_semaphore()
        for partner in partners:
            pl.semaphore_signal(barrier, inc=1, device_id=partner, device_id_type=MESH)
        pl.semaphore_wait(barrier, len(partners))

    def neighbours(self):
        return [self.z_dev(o) for o in self.others] + [self.x_dev, self.core_dev, self.y_dev]


class Links:
    def __init__(self, place, send_sems, recv_sems, local_sems):
        self.place = place
        self.send_sems, self.recv_sems, self.local_sems = send_sems, recv_sems, local_sems
        self.sends = self.recvs = self.locals = 0
        self.open = []

    def slots(self, count):
        first = self.recvs
        self.recvs += count
        return first

    def copy(self, src, dst, slot, device):
        made = pltpu.make_async_remote_copy(
            src_ref=src,
            dst_ref=dst,
            send_sem=self.send_sems.at[self.sends],
            recv_sem=self.recv_sems.at[slot],
            device_id=device,
            device_id_type=MESH,
        )
        self.sends += 1
        return made

    def send(self, src, dst, slot, device):
        made = self.copy(src, dst, slot, device)
        made.start()
        self.open.append(made)
        return made

    def settle(self, sends):
        for made in sends:
            made.wait_send()
            self.open = [one for one in self.open if one is not made]

    def arrive(self, ref, slot):
        pltpu.make_async_remote_copy(
            src_ref=ref,
            dst_ref=ref,
            send_sem=self.send_sems.at[0],
            recv_sem=self.recv_sems.at[slot],
            device_id=self.place.x_dev,
            device_id_type=MESH,
        ).wait_recv()

    def local(self, src, dst):
        made = pltpu.make_async_copy(src, dst, self.local_sems.at[self.locals])
        self.locals += 1
        made.start()
        return made

    def finish(self):
        for made in self.open:
            made.wait_send()
        self.open = []


class SpreadPlane:
    def __init__(self, links, place, chunks):
        self.links, self.place, self.chunks = links, place, chunks
        self.z_slot, self.x_slot = links.slots(4 * len(chunks)), links.slots(4 * len(chunks))

    def begin_z(self):
        place = self.place
        for k, (src, dst) in enumerate(self.chunks):
            slot = self.z_slot + 4 * k + place.z
            for other in place.others:
                self.links.send(src, dst(place.f), slot, place.z_dev(other))

    def begin_x(self, k):
        src, dst = self.chunks[k]
        slot = self.x_slot + 4 * k + self.place.z
        self.links.send(src, dst(self.place.f), slot, self.place.x_dev)

    def forward(self, k):
        place, dst = self.place, self.chunks[k][1]
        for other in place.others:
            block = dst(other * 2 + place.x)
            self.links.arrive(block, self.z_slot + 4 * k + other)
            self.links.send(block, block, self.x_slot + 4 * k + other, place.x_dev)

    def end(self):
        for k in range(len(self.chunks)):
            for z in range(4):
                block = self.chunks[k][1](z * 2 + self.place.xo)
                self.links.arrive(block, self.x_slot + 4 * k + z)


class ReducePlane:
    def __init__(self, links, place, chunks, from_x, from_z, own=None):
        self.links, self.place, self.chunks = links, place, chunks
        self.from_x, self.from_z, self.own = from_x, from_z, own
        self.x_slot, self.z_slot = links.slots(len(chunks)), links.slots(3 * len(chunks))
        self.loads, self.z_sends = {}, {}

    def send_x(self, k):
        place = self.place
        self.links.send(self.chunks[k](place.xo), self.from_x.at[k], self.x_slot + k, place.x_dev)

    def load(self, k):
        slots = self.own.shape[0]
        for made in self.z_sends.pop(k - slots, []):
            made.wait_send()
        self.loads[k] = self.links.local(self.chunks[k](self.place.x), self.own.at[k % slots])

    def mine(self, k):
        if self.own is None:
            return self.chunks[k](self.place.x)
        return self.own.at[k % self.own.shape[0]]

    def middle(self, k):
        place = self.place
        self.links.arrive(self.from_x.at[k], self.x_slot + k)
        if k in self.loads:
            self.loads[k].wait()
        mine = self.mine(k)
        self.z_sends[k] = []
        for other in place.others:
            mine[other] = (mine[other].astype(F32) + self.from_x[k, other].astype(F32)).astype(BF16)
            rank = place.rank(place.z, other)
            made = self.links.copy(
                mine.at[other],
                self.from_z.at[k, rank],
                self.z_slot + 3 * k + rank,
                place.z_dev(other),
            )
            made.start()
            self.z_sends[k].append(made)

    def end(self, k):
        place = self.place
        mine = self.mine(k)
        sums = mine[place.z].astype(F32) + self.from_x[k, place.z].astype(F32)
        for rank in range(3):
            self.links.arrive(self.from_z.at[k, rank], self.z_slot + 3 * k + rank)
            sums += self.from_z[k, rank].astype(F32)
        total = self.from_x.at[k, place.z]
        total[...] = sums.astype(BF16)
        return total

    def finish(self):
        for sends in self.z_sends.values():
            for made in sends:
                made.wait_send()


class SpreadCtx:
    def __init__(self, links, place, out, parts):
        self.links, self.place, self.out, self.parts = links, place, out, parts
        self.slot = links.slots(3 * len(parts))
        self.sends = []

    def begin(self, k, src):
        place, rows = self.place, self.parts[k]
        out = self.out.at[place.c, rows]
        self.sends.append(self.links.send(src, out, self.slot + 3 * k + 1, place.y_dev))
        self.sends.append(self.links.send(src, out, self.slot + 3 * k, place.core_dev))

    def forward(self, k):
        place = self.place
        block = self.out.at[place.c_y, self.parts[k]]
        self.links.arrive(block, self.slot + 3 * k + 1)
        self.sends.append(self.links.send(block, block, self.slot + 3 * k + 2, place.core_dev))

    def end(self):
        place = self.place
        for k, rows in enumerate(self.parts):
            self.links.arrive(self.out.at[place.c_core, rows], self.slot + 3 * k)
            self.links.arrive(self.out.at[place.c_diag, rows], self.slot + 3 * k + 2)


class ReduceCtx:
    def __init__(self, links, place, part, parts, own, from_core, to_y, from_y):
        self.links, self.place, self.part, self.parts = links, place, part, parts
        self.own, self.from_core, self.to_y, self.from_y = own, from_core, to_y, from_y
        self.slot = links.slots(3 * len(parts))
        self.loads, self.sends = {}, []

    def begin(self):
        place = self.place
        for side, y in ((0, place.yo), (1, place.y)):
            for k, rows in enumerate(self.parts):
                self.links.send(
                    self.part.at[y * 2 + place.co, rows],
                    self.from_core.at[side, rows],
                    self.slot + 3 * k + side,
                    place.core_dev,
                )
                if self.own is not None:
                    self.loads[side, k] = self.links.local(
                        self.part.at[y * 2 + place.core, rows], self.own.at[side, rows]
                    )

    def pair(self, side, k):
        rows = self.parts[k]
        self.links.arrive(self.from_core.at[side, rows], self.slot + 3 * k + side)
        if self.own is None:
            y = self.place.y if side else self.place.yo
            own = self.part[y * 2 + self.place.core, rows]
        else:
            self.loads[side, k].wait()
            own = self.own[side, rows]
        return own.astype(F32) + self.from_core[side, rows].astype(F32)

    def cross(self, k):
        rows = self.parts[k]
        self.to_y[rows] = self.pair(0, k).astype(BF16)
        made = self.links.send(
            self.to_y.at[rows], self.from_y.at[rows], self.slot + 3 * k + 2, self.place.y_dev
        )
        self.sends.append(made)

    def total(self, k):
        rows = self.parts[k]
        sums = self.pair(1, k)
        self.links.arrive(self.from_y.at[rows], self.slot + 3 * k + 2)
        return sums + self.from_y[rows].astype(F32)


def halves(rows):
    return [pl.ds(0, rows // 2), pl.ds(rows // 2, rows // 2)]


def row_factor(values):
    return lax.rsqrt(jnp.mean(values * values, axis=-1, keepdims=True) + EPSILON)


def low_half(shape):
    return lax.rem(lax.broadcasted_iota(jnp.int32, shape, len(shape) - 1), 128) < 64


def partner(values):
    lane = lax.broadcasted_iota(jnp.int32, values.shape, len(values.shape) - 1)
    first = lax.rem(lane, 64) < 32
    return jnp.where(first, pltpu.roll(values, 96, 1), pltpu.roll(values, 32, 1))


def half_sums(values):
    low = low_half(values.shape)
    first = jnp.sum(jnp.where(low, values, 0.0), axis=-1, keepdims=True)
    second = jnp.sum(jnp.where(low, 0.0, values), axis=-1, keepdims=True)
    return jnp.where(low, first, second)


def row_loop(count, body):
    def step(index, carry):
        body(index)
        return carry

    lax.fori_loop(0, count, step, 0)


BLOCK = 256
SHORT = 128


def attention_scores(query, keys, key_bias, first, span):
    scores = lax.dot_general(
        query, keys, (((1,), (1,)), ((), ())), preferred_element_type=F32
    ) * (1.0 / math.sqrt(HEAD_DIM))
    rows = first + lax.broadcasted_iota(jnp.int32, scores.shape, 0)
    columns = lax.broadcasted_iota(jnp.int32, scores.shape, 1)
    return jnp.where(columns <= rows, scores, -1e30) + key_bias[:, :span]


def forward_kernel(
    qkv_s, out_s, gain_s, x_s, gate_up, dn_s, dout_s, cos_h, sin_h, head_gain, key_bias,
    qkv_wh, out_wh, gains, normed_h, qkv_raw_h, qkv_low_h, att_low_h, log_sums_h,
    gu_w, dn_w, dout_all, middle, mid_all,
    cos, sin, gain_blocks, qkv_w, out_w, x_all, normed, qkv_raw, qkv_low, att_low, log_sums,
    part, keys, values, from_core, to_y, from_y, mid_low, gu_pairs, gu_rows, gu_s, send_sems, recv_sems, local_sems,
):
    place = Place()
    links = Links(place, send_sems, recv_sems, local_sems)
    fellows = [lax.rem(place.f + d, 8) for d in range(1, 8)]
    place.meet([(f, place.c) for f in fellows] + [place.core_dev, place.y_dev])

    qkv_plane = SpreadPlane(links, place, [(qkv_s, lambda f: qkv_w.at[f])])
    qkv_plane.begin_z()
    qkv_plane.begin_x(0)
    picks = []
    for f in range(8):
        start = pl.multiple_of(512 * f + 128 * place.c, 128)
        picks.append(links.local(gate_up.at[:, :, pl.ds(start, 128)], gu_pairs.at[f]))
    tokens = x_s.shape[0]
    parts = halves(tokens)
    x_spread = SpreadCtx(links, place, x_all, parts)
    for k, rows in enumerate(parts):
        x_spread.begin(k, x_s.at[rows])
    gain_slot = links.slots(8)
    for f in fellows:
        links.send(gain_s, gain_blocks.at[place.f], gain_slot + place.f, (f, place.c))
    kept = [
        links.local(qkv_s, qkv_w.at[place.f]),
        links.local(gain_s, gain_blocks.at[place.f]),
        links.local(x_s, x_all.at[place.c]),
        links.local(cos_h, cos),
        links.local(sin_h, sin),
    ]

    root_slot, side_slot = links.slots(1), links.slots(1)
    holds = place.z == place.c
    down = [
        links.copy(out_s, out_w.at[place.x], root_slot, place.z_dev(other))
        for other in place.others
    ]
    sideways = links.copy(out_s, out_w.at[place.x], side_slot, place.x_dev)
    onward = links.copy(out_w.at[place.x], out_w.at[place.x], side_slot, place.x_dev)
    own = pltpu.make_async_copy(out_s, out_w.at[place.x], local_sems.at[links.locals])
    links.locals += 1

    @pl.when(holds)
    def _():
        for made in down:
            made.start()
        sideways.start()
        own.start()

    rows = gu_s.shape[0]
    for f in range(8):
        picks[f].wait()
        gu_rows[...] = gu_pairs.at[f].reshape(2 * rows, 128)[...].astype(F32)
        for side in range(2):
            first = 1024 * side + 128 * f
            picked = gu_rows[pl.ds(side, rows, stride=2), :]
            gu_s[:, first : first + 128] = picked.astype(BF16)
    step = 64
    chunks = []
    for src, dst in ((dn_s, dn_w), (gu_s, gu_w)):
        for first in range(0, src.shape[0], step):
            rows = pl.ds(first, step)
            chunks.append((src.at[rows], lambda f, dst=dst, rows=rows: dst.at[f, rows]))
    plane = SpreadPlane(links, place, chunks)
    plane.begin_z()
    plane.begin_x(0)
    plane.begin_x(1)
    qkv_plane.forward(0)
    for k in range(2, len(chunks)):
        plane.begin_x(k)
    last = [
        links.local(gu_s, gu_w.at[place.f]),
        links.local(dn_s, dn_w.at[place.f]),
        links.local(dout_s, dout_all.at[place.c]),
    ]
    for f in fellows:
        links.arrive(gain_blocks.at[f], gain_slot + f)
    for made in kept:
        made.wait()
    gains[...] = jnp.zeros_like(gains)
    for f in range(8):
        gains[0:2, 256 * f : 256 * (f + 1)] = gain_blocks[f, 0:2]
    dout = SpreadCtx(links, place, dout_all, parts)
    for k, rows in enumerate(parts):
        x_spread.forward(k)
        dout.begin(k, dout_s.at[rows])
    x_spread.end()
    qkv_plane.end()

    def project(index):
        rows = pl.ds(pl.multiple_of(index * BLOCK, BLOCK), BLOCK)
        source = x_all[index].astype(F32)
        normed[rows] = (source * row_factor(source) * gains[0:1]).astype(BF16)
        weight = qkv_w[...].reshape(normed.shape[1], qkv_w.shape[2])
        raw = jnp.dot(normed[rows], weight, preferred_element_type=F32)
        for b in range(3):
            block = raw[:, 128 * b : 128 * (b + 1)]
            qkv_raw[b, rows] = block
            factor = lax.rsqrt(half_sums(block * block) * (1.0 / HEAD_DIM) + EPSILON)
            scaled = block * factor * head_gain[b : b + 1]
            turned = scaled * cos[rows] + partner(scaled) * sin[rows]
            if b == 2:
                turned = jnp.where(low_half(turned.shape), turned, block)
            qkv_low[b, rows] = turned.astype(BF16)
            if b == 2:
                low = low_half(turned.shape)
                swapped = pltpu.roll(turned, 64, 1)
                keys[rows] = jnp.where(low, turned, swapped).astype(BF16)
                values[rows] = jnp.where(low, swapped, turned).astype(BF16)

    seq = normed.shape[0]
    row_loop(seq // BLOCK, project)
    last += [
        links.local(normed, normed_h),
        links.local(qkv_raw, qkv_raw_h),
        links.local(qkv_low, qkv_low_h),
        links.local(qkv_w, qkv_wh),
    ]

    def heads(b):
        for i in range(seq // BLOCK):
            rows, span = pl.ds(i * BLOCK, BLOCK), (i + 1) * BLOCK
            query = qkv_low[b, rows]
            low = low_half(query.shape)
            outs, logs = [], []
            for half in range(2):
                chosen = jnp.where(low if half == 0 else jnp.logical_not(low), query, 0)
                scores = attention_scores(chosen, keys[:span], key_bias[0:1], i * BLOCK, span)
                top = jnp.max(scores, axis=-1, keepdims=True)
                expanded = jnp.exp(scores - top)
                sums = jnp.sum(expanded, axis=-1, keepdims=True)
                probs = (expanded * (1.0 / sums)).astype(BF16)
                outs.append(jnp.dot(probs, values[:span], preferred_element_type=F32))
                logs.append(top + jnp.log(sums))
            att_low[b, rows] = jnp.where(low, outs[0], outs[1]).astype(BF16)
            log_sums[b, rows] = jnp.where(low, logs[0], logs[1])

    row_loop(2, heads)

    @pl.when(jnp.logical_not(holds))
    def _():
        links.arrive(out_w.at[place.x], root_slot)
        onward.start()

    @pl.when(holds)
    def _():
        own.wait()

    for k in range(len(parts)):
        dout.forward(k)
    links.arrive(out_w.at[place.xo], side_slot)

    def project_out(index):
        rows = pl.ds(pl.multiple_of(index * BLOCK, BLOCK), BLOCK)
        sums = jnp.dot(att_low[0, rows], out_w[0], preferred_element_type=F32)
        sums += jnp.dot(att_low[1, rows], out_w[1], preferred_element_type=F32)
        part[index] = sums.astype(BF16)

    row_loop(seq // BLOCK, project_out)
    reduce = ReduceCtx(links, place, part, parts, None, from_core, to_y, from_y)
    reduce.begin()
    last += [
        links.local(att_low, att_low_h),
        links.local(log_sums, log_sums_h),
        links.local(out_w, out_wh),
    ]
    for k in range(2):
        reduce.cross(k)
    plane.forward(0)
    plane.forward(1)
    mid = SpreadCtx(links, place, mid_all, parts)
    for k, rows in enumerate(parts):
        value = x_all[place.c, rows].astype(F32) + reduce.total(k)
        middle[rows] = value
        mid_low[rows] = (value * row_factor(value) * gains[1:2]).astype(BF16)
        mid.begin(k, mid_low.at[rows])
        last.append(links.local(mid_low.at[rows], mid_all.at[place.c, rows]))
    plane.forward(2)
    for k in range(2):
        mid.forward(k)
    for k in range(3, len(chunks)):
        plane.forward(k)
    plane.end()
    mid.end()
    dout.end()
    for made in last:
        made.wait()
    links.finish()

    @pl.when(holds)
    def _():
        for made in down:
            made.wait_send()
        sideways.wait_send()

    @pl.when(jnp.logical_not(holds))
    def _():
        onward.wait_send()


NT = (((1,), (1,)), ((), ()))
TN = (((0,), (0,)), ((), ()))


def norm_back(d_norm, value, gain):
    factor = row_factor(value)
    gain_sum = jnp.sum(d_norm * value * factor, axis=0, keepdims=True)
    scaled = d_norm * gain
    inner = jnp.mean(scaled * value, axis=-1, keepdims=True)
    return factor * scaled - value * (factor * factor * factor * inner), gain_sum


def backward_kernel(
    gu_g, dn_g, ffn_part, dmid_part, middle_h, dout_h, x_h, keep, gains,
    cos_h, sin_h, head_gain, key_bias,
    normed_h, qkv_raw_h, qkv_low_h, att_low_h, log_sums_h, qkv_wh, out_wh,
    gu_all, dn_all, layer_out, qkv_all, out_all, input_grad, stats,
    own, from_x, from_z,
    ctx_own, from_core1, to_y1, from_y1, from_core2, to_y2, from_y2,
    middle, dout_s, d_middle, branch_all, part,
    cos, sin, qkv_raw, qkv_low, att_low, log_sums, qkv_w, out_w,
    keys, values, d_att, d_low, d_keys, d_values, gain_g,
    qkv_g, qkv_x, qkv_z, out_g, out_x, out_z,
    mine, plane_stats, ctx_stats, free, send_sems, recv_sems, local_sems,
):
    place = Place()
    links = Links(place, send_sems, recv_sems, local_sems)
    fellows = [lax.rem(place.f + d, 8) for d in range(1, 8)]
    place.meet(
        [(f, place.c) for f in fellows] + [place.core_dev, place.y_dev, place.diag_dev]
    )
    step = from_x.shape[2]
    chunks, where = [], []
    for grad, out in ((dn_g, dn_all), (gu_g, gu_all)):
        for first in range(0, grad.shape[2], step):
            rows = pl.ds(first, step)
            chunks.append(lambda x, grad=grad, rows=rows: grad.at[:, x, rows])
            where.append((out, rows))
    count = len(chunks)
    plane = ReducePlane(links, place, chunks, from_x, from_z, own)
    outs = [SpreadCtx(links, place, out, [rows]) for out, rows in where]
    kept = []

    def end(k):
        total = plane.end(k)
        if k + own.shape[0] < count:
            plane.load(k + own.shape[0])
        out, rows = where[k]
        outs[k].begin(0, total)
        kept.append(links.local(total, out.at[place.c, rows]))

    tokens, width = middle.shape
    parts = halves(tokens)
    dmid = ReduceCtx(links, place, dmid_part, parts, ctx_own, from_core1, to_y1, from_y1)
    dmid.begin()
    for k in range(count):
        plane.send_x(k)
    early = [links.local(middle_h, middle), links.local(dout_h, dout_s)]
    for k in range(own.shape[0]):
        plane.load(k)
    late = [
        links.local(a, b)
        for a, b in (
            (out_wh, out_w), (qkv_low_h, qkv_low), (att_low_h, att_low), (log_sums_h, log_sums),
            (cos_h, cos), (sin_h, sin), (qkv_raw_h, qkv_raw), (qkv_wh, qkv_w),
        )
    ]
    for k in range(2):
        dmid.cross(k)
    for made in early:
        made.wait()
    gain_g[...] = jnp.zeros_like(gain_g)
    d_keys[...] = jnp.zeros_like(d_keys)
    d_values[...] = jnp.zeros_like(d_values)
    plane.middle(0)
    branch = SpreadCtx(links, place, branch_all, parts)
    ffn_gain = None
    for k, rows in enumerate(parts):
        grad, term = norm_back(dmid.total(k), middle[rows], gains[1:2])
        ffn_gain = term if ffn_gain is None else ffn_gain + term
        grad += dout_s[rows].astype(F32)
        d_middle[rows] = grad
        branch_all[place.c, rows] = grad.astype(BF16)
        branch.begin(k, branch_all.at[place.c, rows])
    ffn = ReduceCtx(links, place, ffn_part, parts, ctx_own, from_core2, to_y2, from_y2)
    ffn.begin()
    plane.middle(1)
    for k in range(2):
        branch.forward(k)
    for k in range(2):
        ffn.cross(k)
    end(0)
    branch.end()
    for made in late:
        made.wait()

    root = 1.0 / math.sqrt(HEAD_DIM)
    seq = 4 * tokens

    def prepare(index):
        rows = pl.ds(pl.multiple_of(index * BLOCK, BLOCK), BLOCK)
        block = qkv_low[2, rows].astype(F32)
        low = low_half(block.shape)
        swapped = pltpu.roll(block, 64, 1)
        keys[rows] = jnp.where(low, block, swapped).astype(BF16)
        values[rows] = jnp.where(low, swapped, block).astype(BF16)
        for b in range(2):
            d_att[b, rows] = lax.dot_general(
                branch_all[index], out_w[b], NT, preferred_element_type=F32
            ).astype(BF16)

    x_load = links.local(x_h, dout_s)
    row_loop(seq // BLOCK, prepare)
    for b in range(2):
        left = att_low[b].T
        for j in range(8):
            columns = slice(256 * j, 256 * (j + 1))
            right = branch_all[:, :, columns].reshape(seq, 256)
            out_g[b, :, columns] = jnp.dot(left, right, preferred_element_type=F32).astype(BF16)
    out_slot = links.slots(1)
    links.send(out_g.at[place.xo], out_x, out_slot, place.x_dev)
    links.settle(branch.sends)
    normed_load = links.local(normed_h, branch_all)
    plane.middle(2)

    def unturn(row, rows, grads, block):
        back = grads * cos[rows] + partner(grads * sin[rows])
        factor = lax.rsqrt(half_sums(block * block) * (1.0 / HEAD_DIM) + EPSILON)
        gain_term = jnp.sum(back * block * factor, axis=0, keepdims=True)
        scaled = back * head_gain[row : row + 1]
        inner = half_sums(scaled * block) * (1.0 / HEAD_DIM)
        return factor * scaled - block * (factor * factor * factor * inner), gain_term

    def heads(b):
        for i in range(seq // SHORT):
            rows, span = pl.ds(i * SHORT, SHORT), (i + 1) * SHORT
            query, d_out = qkv_low[b, rows], d_att[b, rows]
            logs = log_sums[b, rows]
            low = low_half(query.shape)
            d_query = []
            for half in range(2):
                side = low if half == 0 else jnp.logical_not(low)
                chosen, d_chosen = jnp.where(side, query, 0), jnp.where(side, d_out, 0)
                scores = attention_scores(chosen, keys[:span], key_bias[0:1], i * SHORT, span)
                probs = jnp.exp(scores - logs[:, 64 * half : 64 * half + 1])
                d_probs = lax.dot_general(
                    d_chosen, values[:span], NT, preferred_element_type=F32
                )
                delta = jnp.sum(probs * d_probs, axis=-1, keepdims=True)
                d_scores = (probs * (d_probs - delta)).astype(BF16)
                d_query.append(jnp.dot(d_scores, keys[:span], preferred_element_type=F32))
                d_keys[:span] += lax.dot_general(
                    d_scores, chosen, TN, preferred_element_type=F32
                )
                d_values[:span] += lax.dot_general(
                    probs.astype(BF16), d_chosen, TN, preferred_element_type=F32
                )
            grads = (jnp.where(low, d_query[0], d_query[1]) * root).astype(BF16).astype(F32)
            d_block, gain_term = unturn(0, rows, grads, qkv_raw[b, rows])
            d_low[b, rows] = d_block.astype(BF16)
            gain_g[0:1] += gain_term

    row_loop(2, heads)
    end(1)
    plane.middle(3)

    def finish(index):
        rows = pl.ds(pl.multiple_of(index * BLOCK, BLOCK), BLOCK)
        k_sum, v_sum = d_keys[rows], d_values[rows]
        low = low_half(k_sum.shape)
        k_sum = (k_sum + pltpu.roll(k_sum, 64, 1)) * root
        v_sum = v_sum + pltpu.roll(v_sum, 64, 1)
        grads = jnp.where(low, k_sum, v_sum).astype(BF16).astype(F32)
        d_block, gain_term = unturn(2, rows, grads, qkv_raw[2, rows])
        d_low[2, rows] = jnp.where(low, d_block, grads).astype(BF16)
        gain_g[1:2] += gain_term
        for j in range(4):
            columns = slice(512 * j, 512 * (j + 1))
            sums = jnp.zeros((BLOCK, 512), F32)
            for b in range(3):
                weight = qkv_w[columns, 128 * b : 128 * (b + 1)]
                sums += lax.dot_general(d_low[b, rows], weight, NT, preferred_element_type=F32)
            part[index, :, columns] = sums.astype(BF16)

    row_loop(seq // BLOCK, finish)

    for k, rows in enumerate(parts):
        layer_out[rows] = (keep[rows] * (middle[rows] + ffn.total(k))).astype(BF16)
    links.settle(ffn.sends)
    for device in (place.core_dev, place.y_dev):
        pl.semaphore_signal(free, inc=1, device_id=device, device_id_type=MESH)
    pl.semaphore_wait(free, 2)
    dnorm = ReduceCtx(links, place, part, parts, None, from_core2, to_y2, from_y2)
    dnorm.begin()
    normed_load.wait()
    for b in range(3):
        left = d_low[b].T
        for f in range(8):
            right = branch_all[:, :, 256 * f : 256 * (f + 1)].reshape(seq, 256)
            qkv_g[f // 2, f % 2, 128 * b : 128 * (b + 1)] = jnp.dot(
                left, right, preferred_element_type=F32
            ).astype(BF16)
    qkv_step = qkv_x.shape[2]
    qkv_rows = [pl.ds(k * qkv_step, qkv_step) for k in range(qkv_x.shape[0])]
    qkv_chunks = [lambda x, rows=rows: qkv_g.at[:, x, rows] for rows in qkv_rows]
    qkv_plane = ReducePlane(links, place, qkv_chunks, qkv_x, qkv_z)
    qkv_outs = [SpreadCtx(links, place, qkv_all, [rows]) for rows in qkv_rows]
    for k in range(len(qkv_chunks)):
        qkv_plane.send_x(k)
    for k in range(2):
        dnorm.cross(k)
    end(2)
    plane.middle(4)
    outs[0].forward(0)
    end(3)
    plane.middle(5)
    outs[1].forward(0)

    attn_gain = None
    x_load.wait()
    for k, rows in enumerate(parts):
        grad, term = norm_back(dnorm.total(k), dout_s[rows].astype(F32), gains[0:1])
        attn_gain = term if attn_gain is None else attn_gain + term
        input_grad[rows] = (d_middle[rows] + grad).astype(BF16)
    mine[0:1] = attn_gain
    mine[1:2] = ffn_gain
    mine[2:8] = jnp.zeros((6, width), F32)
    mine[2:3, 0:128] = gain_g[0:1]
    mine[2:3, 128:256] = gain_g[1:2]
    plane_slot, ctx_slot = links.slots(8), links.slots(4)
    for f in fellows:
        links.send(mine, plane_stats.at[place.f], plane_slot + place.f, (f, place.c))
    plane_stats[place.f] = mine[...]

    links.arrive(out_x, out_slot)
    root_slot, final_slot = links.slots(3), links.slots(1)
    holds = place.z == place.c
    out_mine = out_g.at[place.x]
    out_mine[...] = (out_mine[...].astype(F32) + out_x[...].astype(F32)).astype(BF16)
    rank = place.rank(place.z, place.c)
    to_root = links.copy(
        out_mine,
        out_z.at[lax.rem(rank, 3)],
        root_slot + lax.rem(rank, 3),
        (place.c * 2 + place.x, place.c),
    )

    @pl.when(jnp.logical_not(holds))
    def _():
        to_root.start()

    for k in range(len(qkv_chunks)):
        qkv_plane.middle(k)
    for k in range(4, count):
        end(k)
    for k in range(2, 4):
        outs[k].forward(0)
    for f in fellows:
        links.arrive(plane_stats.at[f], plane_slot + f)
    sums = plane_stats[0]
    for f in range(1, 8):
        sums += plane_stats[f]
    ctx_stats[place.c] = sums
    for device in (place.core_dev, place.y_dev, place.diag_dev):
        links.send(ctx_stats.at[place.c], ctx_stats.at[place.c], ctx_slot + place.c, device)

    final = [
        links.copy(out_all, out_all, final_slot, device)
        for device in (place.core_dev, place.y_dev)
    ]
    onward = links.copy(out_all, out_all, final_slot, place.core_dev)

    @pl.when(holds)
    def _():
        sums = out_mine[...].astype(F32)
        for other in range(3):
            links.arrive(out_z.at[other], root_slot + other)
            sums += out_z[other].astype(F32)
        out_all[...] = sums.astype(BF16)
        for made in final:
            made.start()

    for k in range(len(qkv_chunks)):
        total = qkv_plane.end(k)
        qkv_outs[k].begin(0, total)
        kept.append(links.local(total, qkv_all.at[place.c, qkv_rows[k]]))
    for k in range(4, count):
        outs[k].forward(0)
    relays = place.c_y == place.z

    @pl.when(jnp.logical_not(holds))
    def _():
        links.arrive(out_all, final_slot)

    @pl.when(relays)
    def _():
        onward.start()

    for c in (place.c_core, place.c_y, place.c_diag):
        links.arrive(ctx_stats.at[c], ctx_slot + c)
    stats[...] = ((ctx_stats[0] + ctx_stats[1]) + ctx_stats[2]) + ctx_stats[3]
    for out in qkv_outs:
        out.forward(0)
    for out in outs + qkv_outs:
        out.end()
    for made in kept:
        made.wait()
    links.finish()
    plane.finish()
    qkv_plane.finish()

    @pl.when(jnp.logical_not(holds))
    def _():
        to_root.wait_send()

    @pl.when(relays)
    def _():
        onward.wait_send()

    @pl.when(holds)
    def _():
        for made in final:
            made.wait_send()


def interleave_kernel(parts, out, pairs, sems):
    rows = parts.shape[1]
    first = pl.multiple_of(pl.program_id(0) * rows, rows)
    sent = []
    for c in range(4):
        for f in range(8):
            b = 4 * f + c
            for side in range(2):
                column = 1024 * side + 128 * f
                block = parts[c, :, column : column + 128]
                pairs[b, pl.ds(side, rows, stride=2), :] = block.astype(F32)
            made = pltpu.make_async_copy(
                pairs.at[b].reshape(rows, 2, 128),
                out.at[pl.ds(first, rows), :, pl.ds(128 * b, 128)],
                sems.at[b],
            )
            made.start()
            sent.append(made)
    for made in sent:
        made.wait()


def shaped(shape, kind=BF16):
    return jax.ShapeDtypeStruct(shape, kind)


def call(kernel, ins, outs, scratch=(), sems=None, number=None, flops=0):
    scratch = list(scratch)
    extra = {}
    if sems is not None:
        scratch += [pltpu.SemaphoreType.DMA((n,)) for n in sems]
        extra = dict(collective_id=number, has_side_effects=True)
    return pl.pallas_call(
        kernel,
        out_shape=tuple(shape for shape, _ in outs),
        in_specs=[spec for _, spec in ins],
        out_specs=tuple(spec for _, spec in outs),
        scratch_shapes=scratch,
        compiler_params=pltpu.CompilerParams(vmem_limit_bytes=VMEM_BYTES, **extra),
    )(*[array for array, _ in ins])


def split_heads(
    inputs,
    cotangent,
    lengths,
    qkv_weight,
    out_weight,
    gate_up,
    down_weight,
    attn_gain,
    ffn_gain,
    qk_gain,
):
    tokens, width = inputs.shape[1:]
    seq = tokens * 4
    c = lax.axis_index("ctx")
    length = lengths[0]
    positions = c * tokens + jnp.arange(tokens, dtype=jnp.int32)
    keep = (positions < length).astype(F32)[:, None]
    all_positions = jnp.arange(seq, dtype=jnp.int32)
    key_bias = jnp.broadcast_to(jnp.where(all_positions < length, 0.0, -1e30)[None], (8, seq))
    source = inputs[0]
    d_out = (keep * cotangent[0].astype(F32)).astype(BF16)

    query_cols, key_cols = HEADS * HEAD_DIM, KV_HEADS * HEAD_DIM
    qkv_s = jnp.concatenate(
        [
            lax.dynamic_slice_in_dim(qkv_weight, c * 256, 256, 1),
            lax.dynamic_slice_in_dim(qkv_weight, query_cols + c * 64, 64, 1),
            lax.dynamic_slice_in_dim(qkv_weight, query_cols + key_cols + c * 64, 64, 1),
        ],
        axis=1,
    )
    rows, parts, units = gate_up.shape
    down_rows = down_weight.shape[0] // 4
    dn_s = lax.dynamic_slice_in_dim(down_weight, c * down_rows, down_rows, 0)
    gain_s = jnp.concatenate(
        [attn_gain[None], ffn_gain[None], jnp.zeros((6, rows), BF16)], axis=0
    ).astype(F32)

    half_dim = HEAD_DIM // 2
    angles = np.arange(seq)[:, None] * 10000.0 ** (-2.0 * np.arange(half_dim) / HEAD_DIM)[None]
    cos = jnp.tile(jnp.asarray(np.cos(angles), F32), (1, 4))
    sine = jnp.asarray(np.sin(angles), F32)
    sin = jnp.tile(jnp.concatenate([-sine, sine], axis=1), (1, 2))
    q_gain = jnp.tile(qk_gain[0].astype(F32), 2)
    k_gain = jnp.concatenate([qk_gain[1].astype(F32), jnp.ones((HEAD_DIM,), F32)])
    head_gain = jnp.concatenate(
        [q_gain[None], q_gain[None], k_gain[None], jnp.zeros((5, 128), F32)], axis=0
    )

    table = pltpu.VMEM((seq, 128), F32)
    (
        qkv_w, out_w, gains, normed, qkv_raw, qkv_low, att_low, log_sums,
        gu_w, dn_w, dout_all, middle, mid_all,
    ) = call(
        forward_kernel,
        [(a, HBM) for a in (qkv_s, out_weight, gain_s, source, gate_up, dn_s, d_out, cos, sin)]
        + [(head_gain, VMEM), (key_bias, VMEM)],
        [
            (shaped((8, rows, 384)), HBM),
            (shaped((2, out_weight.shape[0], width)), HBM),
            (shaped((8, width), F32), VMEM),
            (shaped((seq, width)), HBM),
            (shaped((3, seq, 128), F32), HBM),
            (shaped((3, seq, 128)), HBM),
            (shaped((2, seq, 128)), HBM),
            (shaped((2, seq, 128), F32), HBM),
            (shaped((8, rows, width)), HBM),
            (shaped((8, down_rows, width)), HBM),
            (shaped((4, tokens, width)), HBM),
            (shaped((tokens, width), F32), VMEM),
            (shaped((4, tokens, width)), HBM),
        ],
        [
            table,
            table,
            pltpu.VMEM((8, 8, rows), F32),
            pltpu.VMEM((8, rows, 384), BF16),
            pltpu.VMEM((2, out_weight.shape[0], width), BF16),
            pltpu.VMEM((4, tokens, width), BF16),
            pltpu.VMEM((seq, width), BF16),
            pltpu.VMEM((3, seq, 128), F32),
            pltpu.VMEM((3, seq, 128), BF16),
            pltpu.VMEM((2, seq, 128), BF16),
            pltpu.VMEM((2, seq, 128), F32),
            pltpu.VMEM((4, tokens, width), BF16),
            pltpu.VMEM((seq, 128), BF16),
            pltpu.VMEM((seq, 128), BF16),
            pltpu.VMEM((2, tokens, width), BF16),
            pltpu.VMEM((tokens, width), BF16),
            pltpu.VMEM((tokens, width), BF16),
            pltpu.VMEM((tokens, width), BF16),
            pltpu.VMEM((8, rows, 2, 128), BF16),
            pltpu.VMEM((2 * rows, 128), F32),
            pltpu.VMEM((rows, width), BF16),
        ],
        sems=(90, 100, 32),
        number=0,
    )
    qkv_w = qkv_w.reshape(width, 384)
    hidden_units = units // 4
    gu_full = gu_w.reshape(width, parts * hidden_units)
    dn_full = dn_w.reshape(hidden_units, width)
    mid_full = mid_all.reshape(seq, width)
    dout_full = dout_all.reshape(seq, width)
    projected = jnp.dot(mid_full, gu_full, preferred_element_type=F32)
    gate, up = projected[:, :hidden_units], projected[:, hidden_units:]
    sigmoid = jax.nn.sigmoid(gate)
    hidden = (gate * sigmoid * up).astype(BF16)
    ffn_part = jnp.dot(hidden, dn_full, preferred_element_type=F32).astype(BF16)
    d_hidden = contract_cols(dout_full, dn_full)
    d_projected = jnp.concatenate(
        [
            (d_hidden * up * (sigmoid * (1.0 + gate * (1.0 - sigmoid)))).astype(BF16),
            (d_hidden * gate * sigmoid).astype(BF16),
        ],
        axis=1,
    )
    dn_g = contract_rows(hidden, dout_full).astype(BF16)
    gu_g = contract_rows(mid_full, d_projected).astype(BF16)
    dmid_part = contract_cols(d_projected, gu_full).astype(BF16)

    step = 64
    count = (rows + down_rows) // step
    block = pltpu.VMEM((tokens, width), BF16)
    pair = pltpu.VMEM((2, tokens, width), BF16)
    heads = pltpu.VMEM((seq, 128), BF16)
    gu_all, dn_all, layer_out, qkv_all, out_all, input_grad, stats = call(
        backward_kernel,
        [
            (gu_g.reshape(4, 2, rows, width), HBM),
            (dn_g.reshape(4, 2, down_rows, width), HBM),
            (ffn_part.reshape(4, tokens, width), HBM),
            (dmid_part.reshape(4, tokens, width), HBM),
            (middle, HBM),
            (d_out, HBM),
            (source, HBM),
            (keep, VMEM),
            (gains, VMEM),
            (cos, HBM),
            (sin, HBM),
            (head_gain, VMEM),
            (key_bias, VMEM),
            (normed.reshape(4, tokens, width), HBM),
        ]
        + [(a, HBM) for a in (qkv_raw, qkv_low, att_low, log_sums, qkv_w, out_w)],
        [
            (shaped((4, rows, width)), HBM),
            (shaped((4, down_rows, width)), HBM),
            (shaped((tokens, width)), VMEM),
            (shaped((4, 384, rows)), HBM),
            (shaped((128, width)), VMEM),
            (shaped((tokens, width)), VMEM),
            (shaped((8, width), F32), VMEM),
        ],
        [
            pltpu.VMEM((2, 4, step, width), BF16),
            pltpu.VMEM((count, 4, step, width), BF16),
            pltpu.VMEM((count, 3, step, width), BF16),
            pair, pair, block, block, pair, block, block,
            pltpu.VMEM((tokens, width), F32),
            block,
            pltpu.VMEM((tokens, width), F32),
            pltpu.VMEM((4, tokens, width), BF16),
            pltpu.VMEM((4, tokens, width), BF16),
            table,
            table,
            pltpu.VMEM((3, seq, 128), F32),
            pltpu.VMEM((3, seq, 128), BF16),
            pltpu.VMEM((2, seq, 128), BF16),
            pltpu.VMEM((2, seq, 128), F32),
            pltpu.VMEM((width, 384), BF16),
            pltpu.VMEM((2, 128, width), BF16),
            heads,
            heads,
            pltpu.VMEM((2, seq, 128), BF16),
            pltpu.VMEM((3, seq, 128), BF16),
            table,
            table,
            pltpu.VMEM((8, 128), F32),
            pltpu.VMEM((4, 2, 384, rows), BF16),
            pltpu.VMEM((2, 4, 192, rows), BF16),
            pltpu.VMEM((2, 3, 192, rows), BF16),
            pltpu.VMEM((2, 128, width), BF16),
            pltpu.VMEM((128, width), BF16),
            pltpu.VMEM((3, 128, width), BF16),
            pltpu.VMEM((8, width), F32),
            pltpu.VMEM((8, 8, width), F32),
            pltpu.VMEM((4, 8, width), F32),
            pltpu.SemaphoreType.REGULAR,
        ],
        sems=(120, 120, 50),
        number=1,
    )
    f = lax.axis_index("fsdp")
    qkv_grad = jnp.concatenate(
        [
            jnp.transpose(qkv_all[:, :256], (2, 0, 1)).reshape(rows, query_cols),
            jnp.transpose(qkv_all[:, 256:320], (2, 0, 1)).reshape(rows, key_cols),
            jnp.transpose(qkv_all[:, 320:], (2, 0, 1)).reshape(rows, key_cols),
        ],
        axis=1,
    ).astype(F32)
    some = 64
    gate_up_grad = pl.pallas_call(
        interleave_kernel,
        grid=(rows // some,),
        in_specs=[pl.BlockSpec((4, some, width), lambda i: (0, i, 0))],
        out_specs=HBM,
        out_shape=shaped((rows, parts, units), F32),
        scratch_shapes=[
            pltpu.VMEM((32, 2 * some, 128), F32),
            pltpu.SemaphoreType.DMA((32,)),
        ],
        compiler_params=pltpu.CompilerParams(vmem_limit_bytes=VMEM_BYTES),
    )(gu_all)
    return (
        layer_out[None],
        input_grad[None],
        qkv_grad,
        out_all.astype(F32),
        gate_up_grad,
        dn_all.reshape(4 * down_rows, width).astype(F32),
        lax.dynamic_slice_in_dim(stats[0], f * rows, rows, 0),
        lax.dynamic_slice_in_dim(stats[1], f * rows, rows, 0),
        jnp.stack([stats[2, :64] + stats[2, 64:128], stats[2, 128:192]]),
    )


def solution(mesh):
    sizes = (mesh.shape["fsdp"], mesh.shape["ctx"])
    return jax.shard_map(
        split_heads if sizes == (8, 4) else on_device,
        mesh=mesh,
        in_specs=(
            P("fsdp", "ctx", None),
            P("fsdp", "ctx", None),
            P("fsdp"),
            P("fsdp", None),
            P("fsdp", None),
            P("fsdp", None, None),
            P("fsdp", None),
            P("fsdp"),
            P("fsdp"),
            P(),
        ),
        out_specs=(
            P("fsdp", "ctx", None),
            P("fsdp", "ctx", None),
            P("fsdp", None),
            P("fsdp", None),
            P("fsdp", None, None),
            P("fsdp", None),
            P("fsdp"),
            P("fsdp"),
            P(),
        ),
        check_vma=False,
    )
```

```python
import functools
import math

import jax
import jax.numpy as jnp
import numpy as np
from jax import lax
from jax.experimental import pallas as pl
from jax.experimental.pallas import tpu as pltpu
from jax.sharding import PartitionSpec as P

HEADS = 16
KV_HEADS = 4
HEAD_DIM = 64


EPSILON = 1e-06


def root_norm(values, norm_gain):
    factor = lax.rsqrt(jnp.mean(values * values, axis=-1, keepdims=True) + EPSILON)
    return values * factor * norm_gain


def rotation_tables(positions):
    half_dim = HEAD_DIM // 2
    frequency = 10000.0 ** (-(2.0 * jnp.arange(half_dim, dtype=jnp.float32)) / HEAD_DIM)
    angles = positions.astype(jnp.float32)[:, None] * frequency[None, :]
    return (jnp.cos(angles), jnp.sin(angles))


def rotate(values, cos_table, sin_table):
    half_dim = values.shape[-1] // 2
    lower_half = values[..., :half_dim]
    upper_half = values[..., half_dim:]
    cos_part = cos_table[:, None, :]
    sin_part = sin_table[:, None, :]
    return jnp.concatenate(
        [
            lower_half * cos_part - upper_half * sin_part,
            upper_half * cos_part + lower_half * sin_part,
        ],
        axis=-1,
    )


def prepare_heads(qkv_out, head_gain, cos_table, sin_table):
    row_count = qkv_out.shape[0]
    query_cols = HEADS * HEAD_DIM
    key_cols = KV_HEADS * HEAD_DIM
    queries = qkv_out[:, :query_cols].reshape(row_count, HEADS, HEAD_DIM)
    key_part = qkv_out[:, query_cols : query_cols + key_cols].reshape(row_count, KV_HEADS, HEAD_DIM)
    value_part = qkv_out[:, query_cols + key_cols :]
    queries = rotate(root_norm(queries, head_gain[0]), cos_table, sin_table).reshape(
        row_count, query_cols
    )
    key_part = rotate(root_norm(key_part, head_gain[1]), cos_table, sin_table).reshape(
        row_count, key_cols
    )
    return (queries, key_part, value_part)


def activate(projected):
    gate_part = projected[:, 0]
    return gate_part * jax.nn.sigmoid(gate_part) * projected[:, 1]


def contract_rows(left, right):
    return lax.dot_general(
        left, right, (((0,), (0,)), ((), ())), preferred_element_type=jnp.float32
    )


def contract_cols(left, right):
    return lax.dot_general(
        left, right, (((1,), (1,)), ((), ())), preferred_element_type=jnp.float32
    )


def on_device(
    inputs,
    cotangent,
    lengths,
    qkv_weight,
    out_weight,
    gate_up,
    down_weight,
    attn_gain,
    ffn_gain,
    qk_gain,
):
    token_count = inputs.shape[1]
    group = HEADS // KV_HEADS
    key_cols = KV_HEADS * HEAD_DIM
    seq_len = token_count * lax.axis_size("ctx")
    positions = lax.axis_index("ctx") * token_count + jnp.arange(token_count, dtype=jnp.int32)
    length = lengths[0]
    row_keep = (positions < length).astype(jnp.float32)[:, None]
    inv_root = 1.0 / math.sqrt(HEAD_DIM)
    source = inputs[0].astype(jnp.float32)
    qkv_full, out_full, attn_full, ffn_full = (
        lax.all_gather(qkv_weight, "fsdp", axis=0, tiled=True),
        lax.all_gather(out_weight, "fsdp", axis=0, tiled=True),
        lax.all_gather(attn_gain, "fsdp", axis=0, tiled=True),
        lax.all_gather(ffn_gain, "fsdp", axis=0, tiled=True),
    )
    attn_norm = attn_full.astype(jnp.float32)
    ffn_norm = ffn_full.astype(jnp.float32)
    normed = root_norm(source, attn_norm).astype(jnp.bfloat16)
    qkv_out = jnp.dot(normed, qkv_full, preferred_element_type=jnp.float32)
    cos_table, sin_table = rotation_tables(positions)
    head_gain = qk_gain.astype(jnp.float32)

    def head_pieces(qkv_values, gain_values):
        return prepare_heads(qkv_values, gain_values, cos_table, sin_table)

    head_values, head_pull = jax.vjp(head_pieces, qkv_out, head_gain)
    queries, key_part, value_part = head_values
    query_low = queries.astype(jnp.bfloat16).reshape(token_count, KV_HEADS, group, HEAD_DIM)
    kv_local = jnp.concatenate([key_part, value_part], axis=1).astype(jnp.bfloat16)
    kv_whole = lax.all_gather(kv_local, "ctx", axis=0, tiled=True)
    block = 512
    block_total = seq_len // block
    kv_blocks = kv_whole.reshape(block_total, block, 2, KV_HEADS, HEAD_DIM)
    starts = jnp.arange(block_total, dtype=jnp.int32) * block

    def block_scores(key_block, block_start):
        scores = (
            jnp.einsum("bhgd,thd->hgbt", query_low, key_block, preferred_element_type=jnp.float32)
            * inv_root
        )
        key_pos = block_start + jnp.arange(key_block.shape[0], dtype=jnp.int32)
        visible = (key_pos[None, :] <= positions[:, None]) & (key_pos[None, :] < length)
        return (scores, visible)

    def max_step(state, item):
        running_max, running_sum = state
        kv_block, block_start = item
        scores, visible = block_scores(kv_block[:, 0], block_start)
        new_max = jnp.maximum(running_max, jnp.max(jnp.where(visible, scores, -1e30), axis=-1))
        expanded = jnp.where(visible, jnp.exp(scores - new_max[..., None]), 0.0)
        running_sum = running_sum * jnp.exp(running_max - new_max) + jnp.sum(expanded, axis=-1)
        return ((new_max, running_sum), None)

    stat_shape = (KV_HEADS, group, token_count)
    start_state = (jnp.full(stat_shape, -1e30, jnp.float32), jnp.zeros(stat_shape, jnp.float32))
    final_state, unused_out = lax.scan(max_step, start_state, (kv_blocks, starts))
    log_total = final_state[0] + jnp.log(final_state[1])

    def block_probs(kv_block, block_start):
        scores, visible = block_scores(kv_block[:, 0], block_start)
        return jnp.where(visible, jnp.exp(scores - log_total[..., None]), 0.0)

    def value_step(totals, item):
        kv_block, block_start = item
        probs_low = block_probs(kv_block, block_start).astype(jnp.bfloat16)
        return (
            totals
            + jnp.einsum(
                "hgbt,thd->bhgd", probs_low, kv_block[:, 1], preferred_element_type=jnp.float32
            ),
            None,
        )

    attended, unused_out = lax.scan(
        value_step,
        jnp.zeros((token_count, KV_HEADS, group, HEAD_DIM), jnp.float32),
        (kv_blocks, starts),
    )
    attended_low = attended.reshape(token_count, HEADS * HEAD_DIM).astype(jnp.bfloat16)
    middle = source + jnp.dot(attended_low, out_full, preferred_element_type=jnp.float32)
    normed_mid = root_norm(middle, ffn_norm).astype(jnp.bfloat16)
    columns = normed_mid
    projected = jnp.einsum(
        "td,dgf->tgf",
        columns,
        lax.all_gather(gate_up, "fsdp", axis=0, tiled=True),
        preferred_element_type=jnp.float32,
    )
    act_value, act_pull = jax.vjp(activate, projected)
    hidden = act_value.astype(jnp.bfloat16)
    columns = hidden
    ffn_out = jnp.dot(
        columns,
        lax.all_gather(down_weight, "fsdp", axis=0, tiled=True),
        preferred_element_type=jnp.float32,
    )
    layer_out = (row_keep * (middle + ffn_out)).astype(jnp.bfloat16)[None]
    d_out = row_keep * cotangent[0].astype(jnp.float32)
    d_out_low = d_out.astype(jnp.bfloat16)
    down_shard = lax.psum_scatter(
        contract_rows(hidden, d_out_low).astype(jnp.bfloat16),
        "fsdp",
        scatter_dimension=0,
        tiled=True,
    )
    d_hidden = contract_cols(d_out_low, lax.all_gather(down_weight, "fsdp", axis=0, tiled=True))
    d_proj_low = act_pull(d_hidden)[0].astype(jnp.bfloat16)
    columns = normed_mid
    gate_up_shard = lax.psum_scatter(
        jnp.einsum("td,tgf->dgf", columns, d_proj_low, preferred_element_type=jnp.float32).astype(
            jnp.bfloat16
        ),
        "fsdp",
        scatter_dimension=0,
        tiled=True,
    )
    d_normed_mid = jnp.einsum(
        "tgf,dgf->td",
        d_proj_low,
        lax.all_gather(gate_up, "fsdp", axis=0, tiled=True),
        preferred_element_type=jnp.float32,
    )
    mid_value, mid_pull = jax.vjp(root_norm, middle, ffn_norm)
    d_mid_norm, ffn_gain_part = mid_pull(d_normed_mid)
    d_middle = d_out + d_mid_norm
    d_branch = d_middle.astype(jnp.bfloat16)
    out_term = contract_rows(attended_low, d_branch)
    d_attended = (
        contract_cols(d_branch, out_full)
        .astype(jnp.bfloat16)
        .reshape(token_count, KV_HEADS, group, HEAD_DIM)
    )
    delta = jnp.transpose(jnp.sum(d_attended.astype(jnp.float32) * attended, axis=-1), (1, 2, 0))

    def block_grads(kv_block, block_start):
        probs = block_probs(kv_block, block_start)
        d_probs = jnp.einsum(
            "bhgd,thd->hgbt", d_attended, kv_block[:, 1], preferred_element_type=jnp.float32
        )
        d_scores = (probs * (d_probs - delta[..., None])).astype(jnp.bfloat16)
        return (probs.astype(jnp.bfloat16), d_scores)

    def query_step(totals, item):
        kv_block, block_start = item
        probs_low, d_scores = block_grads(kv_block, block_start)
        return (
            totals
            + jnp.einsum(
                "hgbt,thd->bhgd", d_scores, kv_block[:, 0], preferred_element_type=jnp.float32
            ),
            None,
        )

    d_query_sum, unused_out = lax.scan(
        query_step,
        jnp.zeros((token_count, KV_HEADS, group, HEAD_DIM), jnp.float32),
        (kv_blocks, starts),
    )
    d_query = (d_query_sum * inv_root).reshape(token_count, HEADS * HEAD_DIM).astype(jnp.bfloat16)
    sub_block = 512
    sub_total = token_count * lax.axis_size("ctx") // sub_block
    pieces = kv_whole.reshape(sub_total, sub_block, 2, KV_HEADS, HEAD_DIM)
    sub_starts = jnp.arange(sub_total, dtype=jnp.int32) * sub_block

    def key_grads(item):
        kv_block, block_start = item
        probs_low, d_scores = block_grads(kv_block, block_start)
        d_keys = (
            jnp.einsum("hgbt,bhgd->thd", d_scores, query_low, preferred_element_type=jnp.float32)
            * inv_root
        )
        d_values = jnp.einsum(
            "hgbt,bhgd->thd", probs_low, d_attended, preferred_element_type=jnp.float32
        )
        return jnp.concatenate(
            [d_keys.reshape(sub_block, key_cols), d_values.reshape(sub_block, key_cols)], axis=1
        )

    kv_grad = lax.psum_scatter(
        lax.map(key_grads, (pieces, sub_starts))
        .reshape(token_count * lax.axis_size("ctx"), 2 * key_cols)
        .astype(jnp.bfloat16),
        "ctx",
        scatter_dimension=0,
        tiled=True,
    ).astype(jnp.float32)
    d_key_low = kv_grad[:, :key_cols].astype(jnp.bfloat16).astype(jnp.float32)
    d_value_low = kv_grad[:, key_cols:].astype(jnp.bfloat16).astype(jnp.float32)
    d_qkv_out, qk_part = head_pull((d_query.astype(jnp.float32), d_key_low, d_value_low))
    d_qkv = d_qkv_out.astype(jnp.bfloat16)
    qkv_term = contract_rows(normed, d_qkv)
    d_normed = contract_cols(d_qkv, qkv_full)
    first_value, first_pull = jax.vjp(root_norm, source, attn_norm)
    d_source_norm, attn_gain_part = first_pull(d_normed)
    input_grad = (d_middle + d_source_norm).astype(jnp.bfloat16)[None]
    qkv_shard, out_shard, attn_shard, ffn_shard = (
        lax.psum_scatter(
            qkv_term.astype(jnp.bfloat16), "fsdp", scatter_dimension=0, tiled=True
        ).astype(jnp.float32),
        lax.psum_scatter(
            out_term.astype(jnp.bfloat16), "fsdp", scatter_dimension=0, tiled=True
        ).astype(jnp.float32),
        lax.psum_scatter(
            attn_gain_part.astype(jnp.bfloat16), "fsdp", scatter_dimension=0, tiled=True
        ).astype(jnp.float32),
        lax.psum_scatter(
            ffn_gain_part.astype(jnp.bfloat16), "fsdp", scatter_dimension=0, tiled=True
        ).astype(jnp.float32),
    )
    summed = (
        lax.psum(qkv_shard.astype(jnp.bfloat16), "ctx").astype(jnp.float32),
        lax.psum(out_shard.astype(jnp.bfloat16), "ctx").astype(jnp.float32),
        lax.psum(gate_up_shard, "ctx").astype(jnp.float32),
        lax.psum(down_shard, "ctx").astype(jnp.float32),
        lax.psum(attn_shard.astype(jnp.bfloat16), "ctx").astype(jnp.float32),
        lax.psum(ffn_shard.astype(jnp.bfloat16), "ctx").astype(jnp.float32),
    )
    qk_total = lax.psum(qk_part, ("fsdp", "ctx"))
    return (
        layer_out,
        input_grad,
        summed[0],
        summed[1],
        summed[2],
        summed[3],
        summed[4],
        summed[5],
        qk_total,
    )


MESH = pl.DeviceIdType.MESH
F32 = jnp.float32
BF16 = jnp.bfloat16
VMEM_BYTES = 60 << 20
HBM = pl.BlockSpec(memory_space=pl.ANY)
VMEM = pl.BlockSpec(memory_space=pltpu.VMEM)


class Place:
    def __init__(self):
        self.f = lax.axis_index("fsdp")
        self.c = lax.axis_index("ctx")
        self.z, self.x = lax.div(self.f, 2), lax.rem(self.f, 2)
        self.y, self.core = lax.div(self.c, 2), lax.rem(self.c, 2)
        self.xo, self.yo, self.co = 1 - self.x, 1 - self.y, 1 - self.core
        upper = lax.div(self.z, 2)
        self.others = (self.z + 1 - 2 * lax.rem(self.z, 2), 2 - upper, 3 - 3 * upper)
        self.inner = lax.rem(self.z, 2) + upper == 1
        self.far = 2 - 2 * upper
        self.x_dev = (self.z * 2 + self.xo, self.c)
        self.c_core = self.y * 2 + self.co
        self.c_y = self.yo * 2 + self.core
        self.c_diag = self.yo * 2 + self.co
        self.core_dev = (self.f, self.c_core)
        self.y_dev = (self.f, self.c_y)
        self.diag_dev = (self.f, self.c_diag)

    def rank(self, source, target):
        return jnp.where(source > target, source - 1, source)

    def z_dev(self, z):
        return (z * 2 + self.x, self.c)

    def meet(self, partners):
        barrier = pltpu.get_barrier_semaphore()
        for partner in partners:
            pl.semaphore_signal(barrier, inc=1, device_id=partner, device_id_type=MESH)
        pl.semaphore_wait(barrier, len(partners))

    def neighbours(self):
        return [self.z_dev(o) for o in self.others] + [self.x_dev, self.core_dev, self.y_dev]


class Links:
    def __init__(self, place, send_sems, recv_sems, local_sems):
        self.place = place
        self.send_sems, self.recv_sems, self.local_sems = send_sems, recv_sems, local_sems
        self.sends = self.recvs = self.locals = 0
        self.open = []

    def slots(self, count):
        first = self.recvs
        self.recvs += count
        return first

    def copy(self, src, dst, slot, device):
        made = pltpu.make_async_remote_copy(
            src_ref=src,
            dst_ref=dst,
            send_sem=self.send_sems.at[self.sends],
            recv_sem=self.recv_sems.at[slot],
            device_id=device,
            device_id_type=MESH,
        )
        self.sends += 1
        return made

    def send(self, src, dst, slot, device):
        made = self.copy(src, dst, slot, device)
        made.start()
        self.open.append(made)
        return made

    def settle(self, sends):
        for made in sends:
            made.wait_send()
            self.open = [one for one in self.open if one is not made]

    def arrive(self, ref, slot):
        pltpu.make_async_remote_copy(
            src_ref=ref,
            dst_ref=ref,
            send_sem=self.send_sems.at[0],
            recv_sem=self.recv_sems.at[slot],
            device_id=self.place.x_dev,
            device_id_type=MESH,
        ).wait_recv()

    def local(self, src, dst):
        made = pltpu.make_async_copy(src, dst, self.local_sems.at[self.locals])
        self.locals += 1
        made.start()
        return made

    def finish(self):
        for made in self.open:
            made.wait_send()
        self.open = []


class SpreadPlane:
    def __init__(self, links, place, chunks):
        self.links, self.place, self.chunks = links, place, chunks
        self.z_slot, self.x_slot = links.slots(4 * len(chunks)), links.slots(4 * len(chunks))

    def begin_z(self):
        place = self.place
        for k, (src, dst) in enumerate(self.chunks):
            slot = self.z_slot + 4 * k + place.z
            for other in place.others:
                self.links.send(src, dst(place.f), slot, place.z_dev(other))

    def begin_x(self, k):
        src, dst = self.chunks[k]
        slot = self.x_slot + 4 * k + self.place.z
        self.links.send(src, dst(self.place.f), slot, self.place.x_dev)

    def forward(self, k):
        place, dst = self.place, self.chunks[k][1]
        for other in place.others:
            block = dst(other * 2 + place.x)
            self.links.arrive(block, self.z_slot + 4 * k + other)
            self.links.send(block, block, self.x_slot + 4 * k + other, place.x_dev)

    def end(self):
        for k in range(len(self.chunks)):
            for z in range(4):
                block = self.chunks[k][1](z * 2 + self.place.xo)
                self.links.arrive(block, self.x_slot + 4 * k + z)


class SpreadTree(SpreadPlane):
    def begin_z(self):
        place = self.place
        self.passed = []
        for k, (src, dst) in enumerate(self.chunks):
            slot = self.z_slot + 4 * k + place.z
            for other in place.others[:2]:
                self.links.send(src, dst(place.f), slot, place.z_dev(other))

    def onward(self, k):
        place, dst = self.place, self.chunks[k][1]
        blocks = [(dst(o * 2 + place.x), self.z_slot + 4 * k + o) for o in place.others[1:]]
        made = [
            self.links.copy(block, block, slot, place.z_dev(place.others[0]))
            for block, slot in blocks
        ]
        self.passed += made

        @pl.when(place.inner)
        def _():
            for (block, slot), one in zip(blocks, made):
                self.links.arrive(block, slot)
                one.start()

    def forward(self, k):
        place, dst = self.place, self.chunks[k][1]
        blocks = [(dst(o * 2 + place.x), self.z_slot + 4 * k + o) for o in place.others]
        self.links.arrive(*blocks[0])
        near = self.x_slot + 4 * k + place.others[0]
        self.links.send(blocks[0][0], blocks[0][0], near, place.x_dev)

        @pl.when(jnp.logical_not(place.inner))
        def _():
            for block, slot in blocks[1:]:
                self.links.arrive(block, slot)

        for other, (block, _) in zip(place.others[1:], blocks[1:]):
            self.links.send(block, block, self.x_slot + 4 * k + other, place.x_dev)

    def finish(self):
        @pl.when(self.place.inner)
        def _():
            for made in self.passed:
                made.wait_send()


class ReducePlane:
    def __init__(self, links, place, chunks, from_x, from_z, own=None):
        self.links, self.place, self.chunks = links, place, chunks
        self.from_x, self.from_z, self.own = from_x, from_z, own
        self.summed = 0
        self.x_slot, self.z_slot = links.slots(len(chunks)), links.slots(3 * len(chunks))
        self.loads, self.z_sends = {}, {}

    def send_x(self, k):
        place = self.place
        from_x = self.from_x.at[k - self.summed]
        self.links.send(self.chunks[k](place.xo), from_x, self.x_slot + k, place.x_dev)

    def load(self, k):
        slots = self.own.shape[0]
        for made in self.z_sends.pop(k - slots, []):
            made.wait_send()
        self.loads[k] = self.links.local(self.chunks[k](self.place.x), self.own.at[k % slots])

    def mine(self, k):
        if self.own is None:
            return self.chunks[k](self.place.x)
        return self.own.at[k % self.own.shape[0]]

    def middle(self, k):
        place = self.place
        self.links.arrive(self.from_x.at[k], self.x_slot + k)
        if k in self.loads:
            self.loads[k].wait()
        mine = self.mine(k)
        self.z_sends[k] = []
        for other in place.others:
            mine[other] = (mine[other].astype(F32) + self.from_x[k, other].astype(F32)).astype(BF16)
            rank = place.rank(place.z, other)
            made = self.links.copy(
                mine.at[other],
                self.from_z.at[k, rank],
                self.z_slot + 3 * k + rank,
                place.z_dev(other),
            )
            made.start()
            self.z_sends[k].append(made)

    def end(self, k):
        place = self.place
        mine = self.mine(k)
        sums = mine[place.z].astype(F32) + self.from_x[k, place.z].astype(F32)
        for rank in range(3):
            self.links.arrive(self.from_z.at[k, rank], self.z_slot + 3 * k + rank)
            sums += self.from_z[k, rank].astype(F32)
        total = self.from_x.at[k, place.z]
        total[...] = sums.astype(BF16)
        return total

    def finish(self):
        for sends in self.z_sends.values():
            for made in sends:
                made.wait_send()


class ReduceTree(ReducePlane):
    def __init__(self, links, place, chunks, from_x, from_z, via, own, summed):
        super().__init__(links, place, chunks, from_x, from_z, own)
        self.summed = summed
        self.via, self.via_slot = via, links.slots(len(chunks))
        self.outer = jnp.logical_not(place.inner)

    def load(self, k):
        slots = self.own.shape[0]
        self.settle(self.z_sends.pop(k - slots, []))
        self.loads[k] = self.links.local(self.chunks[k](self.place.x), self.own.at[k % slots])

    def settle(self, sends):
        for made, when in sends:
            if when is None:
                made.wait_send()
            else:
                pl.when(when)(made.wait_send)

    def middle(self, k):
        place = self.place
        self.loads[k].wait()
        mine = self.mine(k)
        if k >= self.summed:
            from_x = self.from_x.at[k - self.summed]
            self.links.arrive(from_x, self.x_slot + k)
            for other in place.others:
                pair = mine[other].astype(F32) + from_x[other].astype(F32)
                mine[other] = pair.astype(BF16)
        near = place.others[0]
        device = place.z_dev(near)
        direct = self.links.copy(mine.at[near], self.from_z.at[k, 0], self.z_slot + 3 * k, device)
        direct.start()
        far = self.links.copy(
            mine.at[pl.ds(place.far, 2)], self.via.at[k], self.via_slot + k, device
        )
        pl.when(self.outer)(far.start)
        self.z_sends[k] = [(direct, None), (far, self.outer)]

    def combine(self, k):
        place = self.place
        mine = self.mine(k)

        sent = [
            self.links.copy(
                mine.at[place.far + j],
                self.from_z.at[k, 1],
                self.z_slot + 3 * k + 1,
                place.z_dev(place.far + j),
            )
            for j in range(2)
        ]

        @pl.when(place.inner)
        def _():
            self.links.arrive(self.via.at[k], self.via_slot + k)
            for j in range(2):
                here = mine[place.far + j].astype(F32) + self.via[k, j].astype(F32)
                mine[place.far + j] = here.astype(BF16)
                sent[j].start()

        self.z_sends[k] += [(made, place.inner) for made in sent]

    def end(self, k):
        place = self.place
        sums = self.mine(k)[place.z].astype(F32)
        if k >= self.summed:
            sums += self.from_x[k - self.summed, place.z].astype(F32)
        for side in range(2):
            self.links.arrive(self.from_z.at[k, side], self.z_slot + 3 * k + side)
            sums += self.from_z[k, side].astype(F32)
        total = self.from_z.at[k, 0]
        total[...] = sums.astype(BF16)
        return total

    def finish(self):
        for sends in self.z_sends.values():
            self.settle(sends)


class SpreadCtx:
    def __init__(self, links, place, out, parts):
        self.links, self.place, self.out, self.parts = links, place, out, parts
        self.slot = links.slots(3 * len(parts))
        self.sends = []

    def begin(self, k, src):
        place, rows = self.place, self.parts[k]
        out = self.out.at[place.c, rows]
        self.sends.append(self.links.send(src, out, self.slot + 3 * k + 1, place.y_dev))
        self.sends.append(self.links.send(src, out, self.slot + 3 * k, place.core_dev))

    def forward(self, k):
        place = self.place
        block = self.out.at[place.c_y, self.parts[k]]
        self.links.arrive(block, self.slot + 3 * k + 1)
        self.sends.append(self.links.send(block, block, self.slot + 3 * k + 2, place.core_dev))

    def end(self):
        place = self.place
        for k, rows in enumerate(self.parts):
            self.links.arrive(self.out.at[place.c_core, rows], self.slot + 3 * k)
            self.links.arrive(self.out.at[place.c_diag, rows], self.slot + 3 * k + 2)


class ReduceCtx:
    def __init__(self, links, place, part, parts, own, from_core, to_y, from_y):
        self.links, self.place, self.part, self.parts = links, place, part, parts
        self.own, self.from_core, self.to_y, self.from_y = own, from_core, to_y, from_y
        self.slot = links.slots(3 * len(parts))
        self.loads, self.sends = {}, []

    def begin(self):
        place = self.place
        for side, y in ((0, place.yo), (1, place.y)):
            for k, rows in enumerate(self.parts):
                self.links.send(
                    self.part.at[y * 2 + place.co, rows],
                    self.from_core.at[side, rows],
                    self.slot + 3 * k + side,
                    place.core_dev,
                )
                if self.own is not None and side == 0:
                    self.load(0, k)

    def load(self, side, k):
        rows = self.parts[k]
        y = self.place.y if side else self.place.yo
        self.loads[side, k] = self.links.local(
            self.part.at[y * 2 + self.place.core, rows], self.own.at[rows]
        )

    def pair(self, side, k):
        rows = self.parts[k]
        self.links.arrive(self.from_core.at[side, rows], self.slot + 3 * k + side)
        if self.own is None:
            y = self.place.y if side else self.place.yo
            own = self.part[y * 2 + self.place.core, rows]
        else:
            self.loads[side, k].wait()
            own = self.own[rows]
        return own.astype(F32) + self.from_core[side, rows].astype(F32)

    def cross(self, k):
        rows = self.parts[k]
        self.to_y[rows] = self.pair(0, k).astype(BF16)
        if self.own is not None:
            self.load(1, k)
        made = self.links.send(
            self.to_y.at[rows], self.from_y.at[rows], self.slot + 3 * k + 2, self.place.y_dev
        )
        self.sends.append(made)

    def total(self, k):
        rows = self.parts[k]
        sums = self.pair(1, k)
        self.links.arrive(self.from_y.at[rows], self.slot + 3 * k + 2)
        return sums + self.from_y[rows].astype(F32)


def halves(rows):
    return [pl.ds(0, rows // 2), pl.ds(rows // 2, rows // 2)]


def row_factor(values):
    return lax.rsqrt(jnp.mean(values * values, axis=-1, keepdims=True) + EPSILON)


def low_half(shape):
    return lax.rem(lax.broadcasted_iota(jnp.int32, shape, len(shape) - 1), 128) < 64


def partner(values):
    lane = lax.broadcasted_iota(jnp.int32, values.shape, len(values.shape) - 1)
    first = lax.rem(lane, 64) < 32
    return jnp.where(first, pltpu.roll(values, 96, 1), pltpu.roll(values, 32, 1))


def half_sums(values):
    low = low_half(values.shape)
    first = jnp.sum(jnp.where(low, values, 0.0), axis=-1, keepdims=True)
    second = jnp.sum(jnp.where(low, 0.0, values), axis=-1, keepdims=True)
    return jnp.where(low, first, second)


def row_loop(count, body, first=0):
    def step(index, carry):
        body(index)
        return carry

    lax.fori_loop(first, first + count, step, 0)


BLOCK = 256
SHORT = 128


def attention_scores(query, keys, key_bias, first, span):
    scores = lax.dot_general(
        query, keys, (((1,), (1,)), ((), ())), preferred_element_type=F32
    ) * (1.0 / math.sqrt(HEAD_DIM))
    rows = first + lax.broadcasted_iota(jnp.int32, scores.shape, 0)
    columns = lax.broadcasted_iota(jnp.int32, scores.shape, 1)
    return jnp.where(columns <= rows, scores, -1e30) + key_bias[:, :span]


def forward_kernel(
    qkv_s, out_s, gain_s, x_s, gate_up, dn_s, dout_s, cos_h, sin_h, head_gain, key_bias,
    qkv_wh, out_wh, gains, normed_h, qkv_raw_h, qkv_low_h, att_low_h, log_sums_h,
    gu_w, dn_w, dout_all, middle, mid_all,
    cos, sin, gain_blocks, qkv_w, out_w, x_all, normed, qkv_raw, qkv_low, att_low, log_sums,
    part, keys, values, from_core, to_y, from_y, mid_low, gu_pairs, gu_rows, gu_s, send_sems, recv_sems, local_sems,
):
    place = Place()
    links = Links(place, send_sems, recv_sems, local_sems)
    fellows = [lax.rem(place.f + d, 8) for d in range(1, 8)]
    place.meet([(f, place.c) for f in fellows] + [place.core_dev, place.y_dev])

    qkv_plane = SpreadPlane(links, place, [(qkv_s, lambda f: qkv_w.at[f])])
    qkv_plane.begin_z()
    qkv_plane.begin_x(0)
    picks = []
    for f in range(8):
        start = pl.multiple_of(512 * f + 128 * place.c, 128)
        picks.append(links.local(gate_up.at[:, :, pl.ds(start, 128)], gu_pairs.at[f]))
    tokens = x_s.shape[0]
    parts = halves(tokens)
    x_spread = SpreadCtx(links, place, x_all, parts)
    for k, rows in enumerate(parts):
        x_spread.begin(k, x_s.at[rows])
    gain_slot = links.slots(8)
    for f in fellows:
        links.send(gain_s, gain_blocks.at[place.f], gain_slot + place.f, (f, place.c))
    kept = [
        links.local(qkv_s, qkv_w.at[place.f]),
        links.local(gain_s, gain_blocks.at[place.f]),
        links.local(x_s, x_all.at[place.c]),
        links.local(cos_h, cos),
        links.local(sin_h, sin),
    ]

    root_slot, side_slot = links.slots(1), links.slots(1)
    holds = place.z == place.c
    down = [
        links.copy(out_s, out_w.at[place.x], root_slot, place.z_dev(other))
        for other in place.others[:2]
    ]
    relay = links.copy(out_w.at[place.x], out_w.at[place.x], root_slot, place.z_dev(place.others[0]))
    across = lax.div(place.c, 2) != lax.div(place.z, 2)
    relays = jnp.logical_and(place.inner, across)
    sideways = links.copy(out_s, out_w.at[place.x], side_slot, place.x_dev)
    onward = links.copy(out_w.at[place.x], out_w.at[place.x], side_slot, place.x_dev)
    own = pltpu.make_async_copy(out_s, out_w.at[place.x], local_sems.at[links.locals])
    links.locals += 1

    @pl.when(holds)
    def _():
        for made in down:
            made.start()
        sideways.start()
        own.start()

    rows = gu_s.shape[0]
    for f in range(8):
        picks[f].wait()
        gu_rows[...] = gu_pairs.at[f].reshape(2 * rows, 128)[...].astype(F32)
        for side in range(2):
            first = 1024 * side + 128 * f
            picked = gu_rows[pl.ds(side, rows, stride=2), :]
            gu_s[:, first : first + 128] = picked.astype(BF16)
    step = 32
    chunks = []
    for src, dst in ((dn_s, dn_w), (gu_s, gu_w)):
        for first in range(0, src.shape[0], step):
            rows = pl.ds(first, step)
            chunks.append((src.at[rows], lambda f, dst=dst, rows=rows: dst.at[f, rows]))
    plane = SpreadTree(links, place, chunks)
    plane.begin_z()
    for k in range(4):
        plane.begin_x(k)
    qkv_plane.forward(0)
    for k in range(4, len(chunks)):
        plane.begin_x(k)
    last = [
        links.local(gu_s, gu_w.at[place.f]),
        links.local(dn_s, dn_w.at[place.f]),
        links.local(dout_s, dout_all.at[place.c]),
    ]
    for f in fellows:
        links.arrive(gain_blocks.at[f], gain_slot + f)
    for made in kept:
        made.wait()
    gains[...] = jnp.zeros_like(gains)
    for f in range(8):
        gains[0:2, 256 * f : 256 * (f + 1)] = gain_blocks[f, 0:2]
    dout = SpreadCtx(links, place, dout_all, parts)
    for k, rows in enumerate(parts):
        x_spread.forward(k)
        dout.begin(k, dout_s.at[rows])
    x_spread.end()
    qkv_plane.end()

    def project(index):
        rows = pl.ds(pl.multiple_of(index * BLOCK, BLOCK), BLOCK)
        source = x_all[index].astype(F32)
        normed[rows] = (source * row_factor(source) * gains[0:1]).astype(BF16)
        weight = qkv_w[...].reshape(normed.shape[1], qkv_w.shape[2])
        raw = jnp.dot(normed[rows], weight, preferred_element_type=F32)
        for b in range(3):
            block = raw[:, 128 * b : 128 * (b + 1)]
            qkv_raw[b, rows] = block
            factor = lax.rsqrt(half_sums(block * block) * (1.0 / HEAD_DIM) + EPSILON)
            scaled = block * factor * head_gain[b : b + 1]
            turned = scaled * cos[rows] + partner(scaled) * sin[rows]
            if b == 2:
                turned = jnp.where(low_half(turned.shape), turned, block)
            qkv_low[b, rows] = turned.astype(BF16)
            if b == 2:
                low = low_half(turned.shape)
                swapped = pltpu.roll(turned, 64, 1)
                keys[rows] = jnp.where(low, turned, swapped).astype(BF16)
                values[rows] = jnp.where(low, swapped, turned).astype(BF16)

    seq = normed.shape[0]
    att_low[...] = jnp.zeros_like(att_low)
    log_sums[...] = jnp.zeros_like(log_sums)
    row_loop(seq // BLOCK, project)
    last += [
        links.local(normed, normed_h),
        links.local(qkv_raw, qkv_raw_h),
        links.local(qkv_low, qkv_low_h),
        links.local(qkv_w, qkv_wh),
    ]

    def heads(index):
        b, half = lax.div(index, 2), lax.rem(index, 2)
        for i in range(seq // BLOCK):
            rows, span = pl.ds(i * BLOCK, BLOCK), (i + 1) * BLOCK
            query = qkv_low[b, rows]
            side = lax.div(lax.broadcasted_iota(jnp.int32, query.shape, 1), 64) == half
            chosen = jnp.where(side, query, 0)
            scores = attention_scores(chosen, keys[:span], key_bias[0:1], i * BLOCK, span)
            top = jnp.max(scores, axis=-1, keepdims=True)
            expanded = jnp.exp(scores - top)
            sums = jnp.sum(expanded, axis=-1, keepdims=True)
            probs = (expanded * (1.0 / sums)).astype(BF16)
            out = jnp.dot(probs, values[:span], preferred_element_type=F32)
            att_low[b, rows] = jnp.where(side, out.astype(BF16), att_low[b, rows])
            log_sums[b, rows] = jnp.where(side, top + jnp.log(sums), log_sums[b, rows])

    @pl.when(relays)
    def _():
        links.arrive(out_w.at[place.x], root_slot)
        relay.start()
        onward.start()

    plane.onward(0)
    row_loop(2, heads)
    plane.onward(1)
    plane.onward(2)
    row_loop(2, heads, 2)
    plane.onward(3)
    for k in range(3):
        plane.forward(k)

    @pl.when(jnp.logical_not(jnp.logical_or(holds, relays)))
    def _():
        links.arrive(out_w.at[place.x], root_slot)
        onward.start()

    @pl.when(holds)
    def _():
        own.wait()

    for k in range(len(parts)):
        dout.forward(k)
    links.arrive(out_w.at[place.xo], side_slot)

    def project_out(index):
        rows = pl.ds(pl.multiple_of(index * BLOCK, BLOCK), BLOCK)
        sums = jnp.dot(att_low[0, rows], out_w[0], preferred_element_type=F32)
        sums += jnp.dot(att_low[1, rows], out_w[1], preferred_element_type=F32)
        part[index] = sums.astype(BF16)

    row_loop(seq // BLOCK, project_out)
    reduce = ReduceCtx(links, place, part, parts, None, from_core, to_y, from_y)
    reduce.begin()
    last += [
        links.local(att_low, att_low_h),
        links.local(log_sums, log_sums_h),
        links.local(out_w, out_wh),
    ]
    plane.onward(4)
    for k in range(2):
        reduce.cross(k)
    plane.forward(3)
    plane.onward(5)
    plane.onward(6)
    plane.forward(4)
    plane.onward(7)
    plane.forward(5)
    plane.onward(8)
    plane.forward(6)
    mid = SpreadCtx(links, place, mid_all, parts)
    for k, rows in enumerate(parts):
        value = x_all[place.c, rows].astype(F32) + reduce.total(k)
        middle[rows] = value
        mid_low[rows] = (value * row_factor(value) * gains[1:2]).astype(BF16)
        mid.begin(k, mid_low.at[rows])
        last.append(links.local(mid_low.at[rows], mid_all.at[place.c, rows]))
    for k in range(9, len(chunks)):
        plane.onward(k)
    plane.forward(7)
    plane.forward(8)
    for k in range(2):
        mid.forward(k)
    for k in range(9, len(chunks)):
        plane.forward(k)
    plane.end()
    mid.end()
    dout.end()
    for made in last:
        made.wait()
    links.finish()
    plane.finish()

    @pl.when(holds)
    def _():
        for made in down:
            made.wait_send()
        sideways.wait_send()

    @pl.when(relays)
    def _():
        relay.wait_send()

    @pl.when(jnp.logical_not(holds))
    def _():
        onward.wait_send()


NT = (((1,), (1,)), ((), ()))
TN = (((0,), (0,)), ((), ()))


def norm_back(d_norm, value, gain):
    factor = row_factor(value)
    gain_sum = jnp.sum(d_norm * value * factor, axis=0, keepdims=True)
    scaled = d_norm * gain
    inner = jnp.mean(scaled * value, axis=-1, keepdims=True)
    return factor * scaled - value * (factor * factor * factor * inner), gain_sum


def feed_kernel(
    gu_h, dn_h, dout_h, mid_h, middle_h, gains,
    gu_g, dn_pair, ffn_h, d_middle_h, branch_s, ffn_gain,
    gu_w, dn_w, dout, mid, hidden, d_proj, dn_g, from_x, stage,
    part, from_core, to_y, from_y, middle, branch, send_sems, recv_sems, local_sems,
):
    place = Place()
    links = Links(place, send_sems, recv_sems, local_sems)
    shards, rows, width = gu_w.shape
    units, seq = hidden.shape[1], hidden.shape[0]
    tokens = mid.shape[1]
    first = [links.local(mid_h, mid)]
    later, loads = [], []
    for n in range(units // 256):
        gate, up = pl.ds(256 * n, 256), pl.ds(units + 256 * n, 256)
        loads.append([
            links.local(gu_h.at[:, :, gate], gu_w.at[:, :, gate]),
            links.local(gu_h.at[:, :, up], gu_w.at[:, :, up]),
        ])
        if n == 0:
            first += [links.local(dout_h, dout), links.local(dn_h, dn_w)]
    later.append(links.local(middle_h, middle))
    place.meet([place.x_dev, place.core_dev, place.y_dev])
    for made in first:
        made.wait()

    x_slot = links.slots(4)
    for n in range(units // 256):
        for made in loads[n]:
            made.wait()
        gate_columns, up_columns = slice(256 * n, 256 * (n + 1)), slice(units + 256 * n, units + 256 * (n + 1))

        def activation(index, gate_columns=gate_columns, up_columns=up_columns, n=n):
            low = mid[index]
            gate = jnp.dot(
                low, gu_w[:, :, gate_columns].reshape(width, 256), preferred_element_type=F32
            )
            up = jnp.dot(
                low, gu_w[:, :, up_columns].reshape(width, 256), preferred_element_type=F32
            )
            d_hidden = lax.dot_general(
                dout[index], dn_w[2 * n : 2 * n + 2].reshape(256, width), NT,
                preferred_element_type=F32,
            )
            at = pl.ds(pl.multiple_of(index * tokens, tokens), tokens)
            sigmoid = 1.0 / (1.0 + jnp.exp(-gate))
            silu = gate * sigmoid
            hidden[at, gate_columns] = (silu * up).astype(BF16)
            d_gate = d_hidden * up * (sigmoid * (1.0 + gate * (1.0 - sigmoid)))
            d_proj[at, gate_columns] = d_gate.astype(BF16)
            d_proj[at, up_columns] = (d_hidden * silu).astype(BF16)

        row_loop(4, activation)
        left = hidden[:, gate_columns].T

        def down_grad(j, left=left, n=n):
            wide = pl.ds(pl.multiple_of(512 * j, 512), 512)
            right = dout[:, :, wide].reshape(seq, 512)
            grad = jnp.dot(left, right, preferred_element_type=F32).astype(BF16)
            dn_g[n, 0, :, wide] = grad[:128]
            dn_g[n, 1, :, wide] = grad[128:]

        row_loop(4, down_grad)
        links.send(dn_g.at[n, place.xo], from_x.at[n], x_slot + n, place.x_dev)

    def mid_grad(f):
        grad = lax.dot_general(d_proj[...], gu_w[f], NT, preferred_element_type=F32)
        columns = pl.ds(pl.multiple_of(rows * f, rows), rows)
        part[:, :, columns] = grad.astype(BF16).reshape(4, tokens, rows)

    row_loop(shards, mid_grad)
    parts = halves(tokens)
    dmid = ReduceCtx(links, place, part, parts, None, from_core, to_y, from_y)
    dmid.begin()

    def gate_up_grad(z):
        for x in range(2):
            columns = pl.ds(pl.multiple_of(2 * rows * z + rows * x, rows), rows)
            left = mid[:, :, columns].reshape(seq, rows).T
            for j in range(4):
                wide = slice(512 * j, 512 * (j + 1))
                grad = jnp.dot(left, d_proj[:, wide], preferred_element_type=F32)
                stage[x, :, wide] = grad.astype(BF16)
        made = pltpu.make_async_copy(stage, gu_g.at[z], local_sems.at[links.locals])
        made.start()
        made.wait()

    row_loop(1, gate_up_grad)
    for k in range(2):
        dmid.cross(k)
    lax.fori_loop(1, 4, lambda z, carry: (gate_up_grad(z), carry)[1], 0)
    links.locals += 1

    def feed_out(index):
        at = pl.ds(pl.multiple_of(index * tokens, tokens), tokens)
        for j in range(4):
            wide = slice(512 * j, 512 * (j + 1))
            right = dn_w[:, :, wide].reshape(units, 512)
            sums = jnp.dot(hidden[at], right, preferred_element_type=F32)
            mid[index, :, wide] = sums.astype(BF16)

    row_loop(4, feed_out)
    later.append(links.local(mid, ffn_h))
    later[0].wait()
    gain_sum = None
    for k, at in enumerate(parts):
        grad, term = norm_back(dmid.total(k), middle[at], gains[1:2])
        gain_sum = term if gain_sum is None else gain_sum + term
        middle[at] = grad + dout[place.c, at].astype(F32)
        branch[at] = middle[at].astype(BF16)
        later.append(links.local(middle.at[at], d_middle_h.at[at]))
        later.append(links.local(branch.at[at], branch_s.at[at]))
    ffn_gain[...] = gain_sum
    for n in range(4):
        links.arrive(from_x.at[n], x_slot + n)
        pair = dn_g[n, place.x].astype(F32) + from_x[n].astype(F32)
        from_x[n] = pair.astype(BF16)
        later.append(links.local(from_x.at[n], dn_pair.at[n]))
    for made in later[1:]:
        made.wait()
    links.finish()


def backward_kernel(
    gu_g, dn_pair, ffn_part, middle_h, d_middle_h, branch_s, x_h, keep, gains, ffn_gain,
    cos_h, sin_h, head_gain, key_bias,
    normed_h, qkv_raw_h, qkv_low_h, att_low_h, log_sums_h, qkv_wh, out_wh,
    gu_all, dn_all, layer_out, qkv_all, out_all, input_grad, stats,
    own, from_x, from_z, via,
    ctx_own, from_core1, to_y1, from_y1, from_core2, to_y2, from_y2,
    middle, x_s, d_middle, branch_all, part,
    cos, sin, qkv_raw, qkv_low, att_low, log_sums, qkv_w, out_w,
    keys, values, d_att, d_low, d_keys, d_values, gain_g,
    qkv_g, qkv_x, qkv_z, out_g, out_x, out_z,
    mine, plane_stats, ctx_stats, send_sems, recv_sems, local_sems,
):
    place = Place()
    links = Links(place, send_sems, recv_sems, local_sems)
    fellows = [lax.rem(place.f + d, 8) for d in range(1, 8)]
    place.meet(
        [(f, place.c) for f in fellows] + [place.core_dev, place.y_dev, place.diag_dev]
    )
    step = from_x.shape[2]
    chunks, where = [], []
    for first in range(0, dn_pair.shape[1], step):
        rows = pl.ds(first, step)
        chunks.append(lambda x, rows=rows: dn_pair.at[:, rows])
        where.append((dn_all, rows))
    summed = len(chunks)
    for first in range(0, gu_g.shape[2], step):
        rows = pl.ds(first, step)
        chunks.append(lambda x, rows=rows: gu_g.at[:, x, rows])
        where.append((gu_all, rows))
    count = len(chunks)
    plane = ReduceTree(links, place, chunks, from_x, from_z, via, own, summed)
    outs = [SpreadCtx(links, place, out, [rows]) for out, rows in where]
    kept = []

    def end(k):
        total = plane.end(k)
        if k + own.shape[0] < count:
            plane.load(k + own.shape[0])
        out, rows = where[k]
        outs[k].begin(0, total)
        kept.append(links.local(total, out.at[place.c, rows]))

    tokens, width = middle.shape
    parts = halves(tokens)
    branch = SpreadCtx(links, place, branch_all, parts)
    for k, rows in enumerate(parts):
        branch.begin(k, branch_s.at[rows])
    for k in (2, 3):
        plane.send_x(k)
    ffn = ReduceCtx(links, place, ffn_part, parts, ctx_own, from_core1, to_y1, from_y1)
    ffn.begin()
    for k in range(own.shape[0]):
        plane.load(k)
    late = [
        links.local(a, b)
        for a, b in (
            (branch_s, branch_all.at[place.c]),
            (out_wh, out_w), (qkv_low_h, qkv_low), (att_low_h, att_low), (log_sums_h, log_sums),
            (cos_h, cos), (sin_h, sin), (qkv_raw_h, qkv_raw), (qkv_wh, qkv_w),
            (middle_h, middle), (d_middle_h, d_middle), (x_h, x_s),
        )
    ]
    gain_g[...] = jnp.zeros_like(gain_g)
    d_keys[...] = jnp.zeros_like(d_keys)
    d_low[...] = jnp.zeros_like(d_low)
    d_values[...] = jnp.zeros_like(d_values)
    plane.middle(0)
    plane.middle(1)
    for k in range(2):
        ffn.cross(k)
    branch.forward(0)
    plane.combine(0)
    branch.forward(1)
    plane.middle(2)
    plane.combine(1)
    branch.end()
    for made in late:
        made.wait()

    root = 1.0 / math.sqrt(HEAD_DIM)
    seq = 4 * tokens

    def prepare(index):
        rows = pl.ds(pl.multiple_of(index * BLOCK, BLOCK), BLOCK)
        block = qkv_low[2, rows].astype(F32)
        low = low_half(block.shape)
        swapped = pltpu.roll(block, 64, 1)
        keys[rows] = jnp.where(low, block, swapped).astype(BF16)
        values[rows] = jnp.where(low, swapped, block).astype(BF16)
        for b in range(2):
            d_att[b, rows] = lax.dot_general(
                branch_all[index], out_w[b], NT, preferred_element_type=F32
            ).astype(BF16)

    row_loop(seq // BLOCK, prepare)
    for b in range(2):
        left = att_low[b].T
        for j in range(8):
            columns = slice(256 * j, 256 * (j + 1))
            right = branch_all[:, :, columns].reshape(seq, 256)
            out_g[b, :, columns] = jnp.dot(left, right, preferred_element_type=F32).astype(BF16)
    out_slot = links.slots(1)
    links.send(out_g.at[place.xo], out_x, out_slot, place.x_dev)
    for k in range(4, count):
        plane.send_x(k)
    links.settle(branch.sends)
    normed_load = links.local(normed_h, branch_all)
    plane.middle(3)

    def unturn(row, rows, grads, block):
        back = grads * cos[rows] + partner(grads * sin[rows])
        factor = lax.rsqrt(half_sums(block * block) * (1.0 / HEAD_DIM) + EPSILON)
        gain_term = jnp.sum(back * block * factor, axis=0, keepdims=True)
        scaled = back * head_gain[row : row + 1]
        inner = half_sums(scaled * block) * (1.0 / HEAD_DIM)
        return factor * scaled - block * (factor * factor * factor * inner), gain_term

    def heads(index):
        b, half = lax.div(index, 2), lax.rem(index, 2)
        for i in range(seq // SHORT):
            rows, span = pl.ds(i * SHORT, SHORT), (i + 1) * SHORT
            query = qkv_low[b, rows]
            lane = lax.broadcasted_iota(jnp.int32, query.shape, 1)
            side = lax.div(lane, 64) == half
            chosen = jnp.where(side, query, 0)
            d_chosen = jnp.where(side, d_att[b, rows], 0)
            logs = jnp.max(jnp.where(side, log_sums[b, rows], -1e30), axis=-1, keepdims=True)
            scores = attention_scores(chosen, keys[:span], key_bias[0:1], i * SHORT, span)
            probs = jnp.exp(scores - logs)
            d_probs = lax.dot_general(d_chosen, values[:span], NT, preferred_element_type=F32)
            delta = jnp.sum(probs * d_probs, axis=-1, keepdims=True)
            d_scores = (probs * (d_probs - delta)).astype(BF16)
            d_query = jnp.dot(d_scores, keys[:span], preferred_element_type=F32) * root
            d_keys[:span] += lax.dot_general(d_scores, chosen, TN, preferred_element_type=F32)
            d_values[:span] += lax.dot_general(
                probs.astype(BF16), d_chosen, TN, preferred_element_type=F32
            )
            d_low[b, rows] = jnp.where(side, d_query.astype(BF16), d_low[b, rows])

    def unturn_queries(index):
        rows = pl.ds(pl.multiple_of(index * BLOCK, BLOCK), BLOCK)
        for b in range(2):
            grads = d_low[b, rows].astype(F32)
            d_block, gain_term = unturn(0, rows, grads, qkv_raw[b, rows])
            d_low[b, rows] = d_block.astype(BF16)
            gain_g[0:1] += gain_term

    row_loop(2, heads)
    plane.combine(2)
    end(0)
    row_loop(2, heads, 2)
    plane.combine(3)
    end(1)
    row_loop(seq // BLOCK, unturn_queries)

    def finish(index):
        rows = pl.ds(pl.multiple_of(index * BLOCK, BLOCK), BLOCK)
        k_sum, v_sum = d_keys[rows], d_values[rows]
        low = low_half(k_sum.shape)
        k_sum = (k_sum + pltpu.roll(k_sum, 64, 1)) * root
        v_sum = v_sum + pltpu.roll(v_sum, 64, 1)
        grads = jnp.where(low, k_sum, v_sum).astype(BF16).astype(F32)
        d_block, gain_term = unturn(2, rows, grads, qkv_raw[2, rows])
        d_low[2, rows] = jnp.where(low, d_block, grads).astype(BF16)
        gain_g[1:2] += gain_term
        for j in range(4):
            columns = slice(512 * j, 512 * (j + 1))
            sums = jnp.zeros((BLOCK, 512), F32)
            for b in range(3):
                weight = qkv_w[columns, 128 * b : 128 * (b + 1)]
                sums += lax.dot_general(d_low[b, rows], weight, NT, preferred_element_type=F32)
            part[index, :, columns] = sums.astype(BF16)

    row_loop(seq // BLOCK, finish)

    dnorm = ReduceCtx(links, place, part, parts, None, from_core2, to_y2, from_y2)
    dnorm.begin()
    normed_load.wait()
    for b in range(3):
        left = d_low[b].T
        for f in range(8):
            right = branch_all[:, :, 256 * f : 256 * (f + 1)].reshape(seq, 256)
            qkv_g[f // 2, f % 2, 128 * b : 128 * (b + 1)] = jnp.dot(
                left, right, preferred_element_type=F32
            ).astype(BF16)
    qkv_step = qkv_x.shape[2]
    qkv_rows = [pl.ds(k * qkv_step, qkv_step) for k in range(qkv_x.shape[0])]
    qkv_chunks = [lambda x, rows=rows: qkv_g.at[:, x, rows] for rows in qkv_rows]
    qkv_plane = ReducePlane(links, place, qkv_chunks, qkv_x, qkv_z)
    qkv_outs = [SpreadCtx(links, place, qkv_all, [rows]) for rows in qkv_rows]
    for k in range(len(qkv_chunks)):
        qkv_plane.send_x(k)
    plane.middle(4)
    for k in range(2):
        dnorm.cross(k)
    end(2)
    outs[0].forward(0)
    outs[1].forward(0)
    end(3)
    for k, rows in enumerate(parts):
        layer_out[rows] = (keep[rows] * (middle[rows] + ffn.total(k))).astype(BF16)
    plane.middle(5)
    plane.combine(4)
    outs[2].forward(0)
    links.arrive(out_x, out_slot)
    root_slot, final_slot = links.slots(3), links.slots(1)
    holds = place.z == place.c
    out_mine = out_g.at[place.x]
    out_mine[...] = (out_mine[...].astype(F32) + out_x[...].astype(F32)).astype(BF16)
    rank = place.rank(place.z, place.c)
    to_root = links.copy(
        out_mine,
        out_z.at[lax.rem(rank, 3)],
        root_slot + lax.rem(rank, 3),
        (place.c * 2 + place.x, place.c),
    )

    @pl.when(jnp.logical_not(holds))
    def _():
        to_root.start()

    attn_gain = None
    for k, rows in enumerate(parts):
        grad, term = norm_back(dnorm.total(k), x_s[rows].astype(F32), gains[0:1])
        attn_gain = term if attn_gain is None else attn_gain + term
        input_grad[rows] = (d_middle[rows] + grad).astype(BF16)
    mine[...] = jnp.zeros_like(mine)
    for f in range(8):
        mine[f, 0:1] = attn_gain[:, 256 * f : 256 * (f + 1)]
        mine[f, 1:2] = ffn_gain[:, 256 * f : 256 * (f + 1)]
        mine[f, 2:3, 0:128] = gain_g[0:1]
        mine[f, 2:3, 128:256] = gain_g[1:2]
    plane_slot, ctx_slot = links.slots(8), links.slots(4)
    for f in fellows:
        links.send(mine.at[f], plane_stats.at[place.f], plane_slot + place.f, (f, place.c))
    plane_stats[place.f] = mine[place.f]

    end(4)
    outs[3].forward(0)
    for k in range(len(qkv_chunks)):
        qkv_plane.middle(k)
    plane.combine(5)
    end(5)
    for f in fellows:
        links.arrive(plane_stats.at[f], plane_slot + f)
    sums = plane_stats[0]
    for f in range(1, 8):
        sums += plane_stats[f]
    ctx_stats[place.c] = sums
    for device in (place.core_dev, place.y_dev, place.diag_dev):
        links.send(ctx_stats.at[place.c], ctx_stats.at[place.c], ctx_slot + place.c, device)

    final = [
        links.copy(out_all, out_all, final_slot, device)
        for device in (place.core_dev, place.y_dev)
    ]
    onward = links.copy(out_all, out_all, final_slot, place.core_dev)

    @pl.when(holds)
    def _():
        sums = out_mine[...].astype(F32)
        for other in range(3):
            links.arrive(out_z.at[other], root_slot + other)
            sums += out_z[other].astype(F32)
        out_all[...] = sums.astype(BF16)
        for made in final:
            made.start()

    for k in range(len(qkv_chunks)):
        total = qkv_plane.end(k)
        qkv_outs[k].begin(0, total)
        kept.append(links.local(total, qkv_all.at[place.c, qkv_rows[k]]))
    for k in range(4, count):
        outs[k].forward(0)
    relays = place.c_y == place.z

    @pl.when(jnp.logical_not(holds))
    def _():
        links.arrive(out_all, final_slot)

    @pl.when(relays)
    def _():
        onward.start()

    for c in (place.c_core, place.c_y, place.c_diag):
        links.arrive(ctx_stats.at[c], ctx_slot + c)
    stats[...] = ((ctx_stats[0] + ctx_stats[1]) + ctx_stats[2]) + ctx_stats[3]
    for out in qkv_outs:
        out.forward(0)
    for out in outs + qkv_outs:
        out.end()
    for made in kept:
        made.wait()
    links.finish()
    plane.finish()
    qkv_plane.finish()

    @pl.when(jnp.logical_not(holds))
    def _():
        to_root.wait_send()

    @pl.when(relays)
    def _():
        onward.wait_send()

    @pl.when(holds)
    def _():
        for made in final:
            made.wait_send()


def interleave_kernel(parts, out, pairs, sems):
    rows = parts.shape[1]
    first = pl.multiple_of(pl.program_id(0) * rows, rows)
    sent = []
    for c in range(4):
        for f in range(8):
            b = 4 * f + c
            for side in range(2):
                column = 1024 * side + 128 * f
                block = parts[c, :, column : column + 128]
                pairs[b, pl.ds(side, rows, stride=2), :] = block.astype(F32)
            made = pltpu.make_async_copy(
                pairs.at[b].reshape(rows, 2, 128),
                out.at[pl.ds(first, rows), :, pl.ds(128 * b, 128)],
                sems.at[b],
            )
            made.start()
            sent.append(made)
    for made in sent:
        made.wait()


def shaped(shape, kind=BF16):
    return jax.ShapeDtypeStruct(shape, kind)


def call(kernel, ins, outs, scratch=(), sems=None, number=None, flops=0):
    scratch = list(scratch)
    extra = {}
    if sems is not None:
        scratch += [pltpu.SemaphoreType.DMA((n,)) for n in sems]
        extra = dict(collective_id=number, has_side_effects=True)
    return pl.pallas_call(
        kernel,
        out_shape=tuple(shape for shape, _ in outs),
        in_specs=[spec for _, spec in ins],
        out_specs=tuple(spec for _, spec in outs),
        scratch_shapes=scratch,
        compiler_params=pltpu.CompilerParams(vmem_limit_bytes=VMEM_BYTES, **extra),
    )(*[array for array, _ in ins])


def split_heads(
    inputs,
    cotangent,
    lengths,
    qkv_weight,
    out_weight,
    gate_up,
    down_weight,
    attn_gain,
    ffn_gain,
    qk_gain,
):
    tokens, width = inputs.shape[1:]
    seq = tokens * 4
    c = lax.axis_index("ctx")
    length = lengths[0]
    positions = c * tokens + jnp.arange(tokens, dtype=jnp.int32)
    keep = (positions < length).astype(F32)[:, None]
    all_positions = jnp.arange(seq, dtype=jnp.int32)
    key_bias = jnp.broadcast_to(jnp.where(all_positions < length, 0.0, -1e30)[None], (8, seq))
    source = inputs[0]
    d_out = (keep * cotangent[0].astype(F32)).astype(BF16)

    query_cols, key_cols = HEADS * HEAD_DIM, KV_HEADS * HEAD_DIM
    qkv_s = jnp.concatenate(
        [
            lax.dynamic_slice_in_dim(qkv_weight, c * 256, 256, 1),
            lax.dynamic_slice_in_dim(qkv_weight, query_cols + c * 64, 64, 1),
            lax.dynamic_slice_in_dim(qkv_weight, query_cols + key_cols + c * 64, 64, 1),
        ],
        axis=1,
    )
    rows, parts, units = gate_up.shape
    down_rows = down_weight.shape[0] // 4
    dn_s = lax.dynamic_slice_in_dim(down_weight, c * down_rows, down_rows, 0)
    gain_s = jnp.concatenate(
        [attn_gain[None], ffn_gain[None], jnp.zeros((6, rows), BF16)], axis=0
    ).astype(F32)

    half_dim = HEAD_DIM // 2
    angles = np.arange(seq)[:, None] * 10000.0 ** (-2.0 * np.arange(half_dim) / HEAD_DIM)[None]
    cos = jnp.tile(jnp.asarray(np.cos(angles), F32), (1, 4))
    sine = jnp.asarray(np.sin(angles), F32)
    sin = jnp.tile(jnp.concatenate([-sine, sine], axis=1), (1, 2))
    q_gain = jnp.tile(qk_gain[0].astype(F32), 2)
    k_gain = jnp.concatenate([qk_gain[1].astype(F32), jnp.ones((HEAD_DIM,), F32)])
    head_gain = jnp.concatenate(
        [q_gain[None], q_gain[None], k_gain[None], jnp.zeros((5, 128), F32)], axis=0
    )

    table = pltpu.VMEM((seq, 128), F32)
    (
        qkv_w, out_w, gains, normed, qkv_raw, qkv_low, att_low, log_sums,
        gu_w, dn_w, dout_all, middle, mid_all,
    ) = call(
        forward_kernel,
        [(a, HBM) for a in (qkv_s, out_weight, gain_s, source, gate_up, dn_s, d_out, cos, sin)]
        + [(head_gain, VMEM), (key_bias, VMEM)],
        [
            (shaped((8, rows, 384)), HBM),
            (shaped((2, out_weight.shape[0], width)), HBM),
            (shaped((8, width), F32), VMEM),
            (shaped((seq, width)), HBM),
            (shaped((3, seq, 128), F32), HBM),
            (shaped((3, seq, 128)), HBM),
            (shaped((2, seq, 128)), HBM),
            (shaped((2, seq, 128), F32), HBM),
            (shaped((8, rows, width)), HBM),
            (shaped((8, down_rows, width)), HBM),
            (shaped((4, tokens, width)), HBM),
            (shaped((tokens, width), F32), VMEM),
            (shaped((4, tokens, width)), HBM),
        ],
        [
            table,
            table,
            pltpu.VMEM((8, 8, rows), F32),
            pltpu.VMEM((8, rows, 384), BF16),
            pltpu.VMEM((2, out_weight.shape[0], width), BF16),
            pltpu.VMEM((4, tokens, width), BF16),
            pltpu.VMEM((seq, width), BF16),
            pltpu.VMEM((3, seq, 128), F32),
            pltpu.VMEM((3, seq, 128), BF16),
            pltpu.VMEM((2, seq, 128), BF16),
            pltpu.VMEM((2, seq, 128), F32),
            pltpu.VMEM((4, tokens, width), BF16),
            pltpu.VMEM((seq, 128), BF16),
            pltpu.VMEM((seq, 128), BF16),
            pltpu.VMEM((2, tokens, width), BF16),
            pltpu.VMEM((tokens, width), BF16),
            pltpu.VMEM((tokens, width), BF16),
            pltpu.VMEM((tokens, width), BF16),
            pltpu.VMEM((8, rows, 2, 128), BF16),
            pltpu.VMEM((2 * rows, 128), F32),
            pltpu.VMEM((rows, width), BF16),
        ],
        sems=(170, 170, 32),
        number=0,
    )
    qkv_w = qkv_w.reshape(width, 384)
    block = pltpu.VMEM((tokens, width), BF16)
    pair = pltpu.VMEM((2, tokens, width), BF16)
    whole = pltpu.VMEM((4, tokens, width), BF16)
    hidden_units = units // 4
    gu_g, dn_pair, ffn_part, d_middle, branch_s, ffn_gain_part = call(
        feed_kernel,
        [(a, HBM) for a in (gu_w, dn_w, dout_all, mid_all, middle)] + [(gains, VMEM)],
        [
            (shaped((4, 2, rows, width)), HBM),
            (shaped((4, down_rows, width)), HBM),
            (shaped((4, tokens, width)), HBM),
            (shaped((tokens, width), F32), HBM),
            (shaped((tokens, width)), HBM),
            (shaped((1, width), F32), VMEM),
        ],
        [
            pltpu.VMEM((8, rows, width), BF16),
            pltpu.VMEM((8, down_rows, width), BF16),
            whole,
            whole,
            pltpu.VMEM((seq, hidden_units), BF16),
            pltpu.VMEM((seq, parts * hidden_units), BF16),
            pltpu.VMEM((4, 2, down_rows, width), BF16),
            pltpu.VMEM((4, down_rows, width), BF16),
            pltpu.VMEM((2, rows, width), BF16),
            whole,
            pair,
            block,
            block,
            pltpu.VMEM((tokens, width), F32),
            block,
        ],
        sems=(16, 16, 24),
        number=2,
    )
    step = 64
    count = (rows + down_rows) // step
    heads = pltpu.VMEM((seq, 128), BF16)
    gu_all, dn_all, layer_out, qkv_all, out_all, input_grad, stats = call(
        backward_kernel,
        [
            (gu_g, HBM),
            (dn_pair, HBM),
            (ffn_part, HBM),
            (middle, HBM),
            (d_middle, HBM),
            (branch_s, HBM),
            (source, HBM),
            (keep, VMEM),
            (gains, VMEM),
            (ffn_gain_part, VMEM),
            (cos, HBM),
            (sin, HBM),
            (head_gain, VMEM),
            (key_bias, VMEM),
            (normed.reshape(4, tokens, width), HBM),
        ]
        + [(a, HBM) for a in (qkv_raw, qkv_low, att_low, log_sums, qkv_w, out_w)],
        [
            (shaped((4, rows, width)), HBM),
            (shaped((4, down_rows, width)), HBM),
            (shaped((tokens, width)), VMEM),
            (shaped((4, 384, rows)), HBM),
            (shaped((128, width)), VMEM),
            (shaped((tokens, width)), VMEM),
            (shaped((8, rows), F32), VMEM),
        ],
        [
            pltpu.VMEM((4, 4, step, width), BF16),
            pltpu.VMEM((rows // step, 4, step, width), BF16),
            pltpu.VMEM((count, 2, step, width), BF16),
            pltpu.VMEM((count, 2, step, width), BF16),
            block, pair, block, block, pair, block, block,
            pltpu.VMEM((tokens, width), F32),
            block,
            pltpu.VMEM((tokens, width), F32),
            pltpu.VMEM((4, tokens, width), BF16),
            pltpu.VMEM((4, tokens, width), BF16),
            table,
            table,
            pltpu.VMEM((3, seq, 128), F32),
            pltpu.VMEM((3, seq, 128), BF16),
            pltpu.VMEM((2, seq, 128), BF16),
            pltpu.VMEM((2, seq, 128), F32),
            pltpu.VMEM((width, 384), BF16),
            pltpu.VMEM((2, 128, width), BF16),
            heads,
            heads,
            pltpu.VMEM((2, seq, 128), BF16),
            pltpu.VMEM((3, seq, 128), BF16),
            table,
            table,
            pltpu.VMEM((8, 128), F32),
            pltpu.VMEM((4, 2, 384, rows), BF16),
            pltpu.VMEM((2, 4, 192, rows), BF16),
            pltpu.VMEM((2, 3, 192, rows), BF16),
            pltpu.VMEM((2, 128, width), BF16),
            pltpu.VMEM((128, width), BF16),
            pltpu.VMEM((3, 128, width), BF16),
            pltpu.VMEM((8, 8, rows), F32),
            pltpu.VMEM((8, 8, rows), F32),
            pltpu.VMEM((4, 8, rows), F32),
        ],
        sems=(120, 120, 50),
        number=1,
    )
    qkv_grad = jnp.concatenate(
        [
            jnp.transpose(qkv_all[:, :256], (2, 0, 1)).reshape(rows, query_cols),
            jnp.transpose(qkv_all[:, 256:320], (2, 0, 1)).reshape(rows, key_cols),
            jnp.transpose(qkv_all[:, 320:], (2, 0, 1)).reshape(rows, key_cols),
        ],
        axis=1,
    ).astype(F32)
    some = 64
    gate_up_grad = pl.pallas_call(
        interleave_kernel,
        grid=(rows // some,),
        in_specs=[pl.BlockSpec((4, some, width), lambda i: (0, i, 0))],
        out_specs=HBM,
        out_shape=shaped((rows, parts, units), F32),
        scratch_shapes=[
            pltpu.VMEM((32, 2 * some, 128), F32),
            pltpu.SemaphoreType.DMA((32,)),
        ],
        compiler_params=pltpu.CompilerParams(vmem_limit_bytes=VMEM_BYTES),
    )(gu_all)
    return (
        layer_out[None],
        input_grad[None],
        qkv_grad,
        out_all.astype(F32),
        gate_up_grad,
        dn_all.reshape(4 * down_rows, width).astype(F32),
        stats[0],
        stats[1],
        jnp.stack([stats[2, :64] + stats[2, 64:128], stats[2, 128:192]]),
    )


def solution(mesh):
    sizes = (mesh.shape["fsdp"], mesh.shape["ctx"])
    return jax.shard_map(
        split_heads if sizes == (8, 4) else on_device,
        mesh=mesh,
        in_specs=(
            P("fsdp", "ctx", None),
            P("fsdp", "ctx", None),
            P("fsdp"),
            P("fsdp", None),
            P("fsdp", None),
            P("fsdp", None, None),
            P("fsdp", None),
            P("fsdp"),
            P("fsdp"),
            P(),
        ),
        out_specs=(
            P("fsdp", "ctx", None),
            P("fsdp", "ctx", None),
            P("fsdp", None),
            P("fsdp", None),
            P("fsdp", None, None),
            P("fsdp", None),
            P("fsdp"),
            P("fsdp"),
            P(),
        ),
        check_vma=False,
    )
```

```python
import functools
import math

import jax
import jax.numpy as jnp
import numpy as np
from jax import lax
from jax.experimental import pallas as pl
from jax.experimental.pallas import tpu as pltpu
from jax.sharding import PartitionSpec as P

HEADS = 16
KV_HEADS = 4
HEAD_DIM = 64


EPSILON = 1e-06


def root_norm(values, norm_gain):
    factor = lax.rsqrt(jnp.mean(values * values, axis=-1, keepdims=True) + EPSILON)
    return values * factor * norm_gain


def rotation_tables(positions):
    half_dim = HEAD_DIM // 2
    frequency = 10000.0 ** (-(2.0 * jnp.arange(half_dim, dtype=jnp.float32)) / HEAD_DIM)
    angles = positions.astype(jnp.float32)[:, None] * frequency[None, :]
    return (jnp.cos(angles), jnp.sin(angles))


def rotate(values, cos_table, sin_table):
    half_dim = values.shape[-1] // 2
    lower_half = values[..., :half_dim]
    upper_half = values[..., half_dim:]
    cos_part = cos_table[:, None, :]
    sin_part = sin_table[:, None, :]
    return jnp.concatenate(
        [
            lower_half * cos_part - upper_half * sin_part,
            upper_half * cos_part + lower_half * sin_part,
        ],
        axis=-1,
    )


def prepare_heads(qkv_out, head_gain, cos_table, sin_table):
    row_count = qkv_out.shape[0]
    query_cols = HEADS * HEAD_DIM
    key_cols = KV_HEADS * HEAD_DIM
    queries = qkv_out[:, :query_cols].reshape(row_count, HEADS, HEAD_DIM)
    key_part = qkv_out[:, query_cols : query_cols + key_cols].reshape(row_count, KV_HEADS, HEAD_DIM)
    value_part = qkv_out[:, query_cols + key_cols :]
    queries = rotate(root_norm(queries, head_gain[0]), cos_table, sin_table).reshape(
        row_count, query_cols
    )
    key_part = rotate(root_norm(key_part, head_gain[1]), cos_table, sin_table).reshape(
        row_count, key_cols
    )
    return (queries, key_part, value_part)


def activate(projected):
    gate_part = projected[:, 0]
    return gate_part * jax.nn.sigmoid(gate_part) * projected[:, 1]


def contract_rows(left, right):
    return lax.dot_general(
        left, right, (((0,), (0,)), ((), ())), preferred_element_type=jnp.float32
    )


def contract_cols(left, right):
    return lax.dot_general(
        left, right, (((1,), (1,)), ((), ())), preferred_element_type=jnp.float32
    )


def on_device(
    inputs,
    cotangent,
    lengths,
    qkv_weight,
    out_weight,
    gate_up,
    down_weight,
    attn_gain,
    ffn_gain,
    qk_gain,
):
    token_count = inputs.shape[1]
    group = HEADS // KV_HEADS
    key_cols = KV_HEADS * HEAD_DIM
    seq_len = token_count * lax.axis_size("ctx")
    positions = lax.axis_index("ctx") * token_count + jnp.arange(token_count, dtype=jnp.int32)
    length = lengths[0]
    row_keep = (positions < length).astype(jnp.float32)[:, None]
    inv_root = 1.0 / math.sqrt(HEAD_DIM)
    source = inputs[0].astype(jnp.float32)
    qkv_full, out_full, attn_full, ffn_full = (
        lax.all_gather(qkv_weight, "fsdp", axis=0, tiled=True),
        lax.all_gather(out_weight, "fsdp", axis=0, tiled=True),
        lax.all_gather(attn_gain, "fsdp", axis=0, tiled=True),
        lax.all_gather(ffn_gain, "fsdp", axis=0, tiled=True),
    )
    attn_norm = attn_full.astype(jnp.float32)
    ffn_norm = ffn_full.astype(jnp.float32)
    normed = root_norm(source, attn_norm).astype(jnp.bfloat16)
    qkv_out = jnp.dot(normed, qkv_full, preferred_element_type=jnp.float32)
    cos_table, sin_table = rotation_tables(positions)
    head_gain = qk_gain.astype(jnp.float32)

    def head_pieces(qkv_values, gain_values):
        return prepare_heads(qkv_values, gain_values, cos_table, sin_table)

    head_values, head_pull = jax.vjp(head_pieces, qkv_out, head_gain)
    queries, key_part, value_part = head_values
    query_low = queries.astype(jnp.bfloat16).reshape(token_count, KV_HEADS, group, HEAD_DIM)
    kv_local = jnp.concatenate([key_part, value_part], axis=1).astype(jnp.bfloat16)
    kv_whole = lax.all_gather(kv_local, "ctx", axis=0, tiled=True)
    block = 512
    block_total = seq_len // block
    kv_blocks = kv_whole.reshape(block_total, block, 2, KV_HEADS, HEAD_DIM)
    starts = jnp.arange(block_total, dtype=jnp.int32) * block

    def block_scores(key_block, block_start):
        scores = (
            jnp.einsum("bhgd,thd->hgbt", query_low, key_block, preferred_element_type=jnp.float32)
            * inv_root
        )
        key_pos = block_start + jnp.arange(key_block.shape[0], dtype=jnp.int32)
        visible = (key_pos[None, :] <= positions[:, None]) & (key_pos[None, :] < length)
        return (scores, visible)

    def max_step(state, item):
        running_max, running_sum = state
        kv_block, block_start = item
        scores, visible = block_scores(kv_block[:, 0], block_start)
        new_max = jnp.maximum(running_max, jnp.max(jnp.where(visible, scores, -1e30), axis=-1))
        expanded = jnp.where(visible, jnp.exp(scores - new_max[..., None]), 0.0)
        running_sum = running_sum * jnp.exp(running_max - new_max) + jnp.sum(expanded, axis=-1)
        return ((new_max, running_sum), None)

    stat_shape = (KV_HEADS, group, token_count)
    start_state = (jnp.full(stat_shape, -1e30, jnp.float32), jnp.zeros(stat_shape, jnp.float32))
    final_state, unused_out = lax.scan(max_step, start_state, (kv_blocks, starts))
    log_total = final_state[0] + jnp.log(final_state[1])

    def block_probs(kv_block, block_start):
        scores, visible = block_scores(kv_block[:, 0], block_start)
        return jnp.where(visible, jnp.exp(scores - log_total[..., None]), 0.0)

    def value_step(totals, item):
        kv_block, block_start = item
        probs_low = block_probs(kv_block, block_start).astype(jnp.bfloat16)
        return (
            totals
            + jnp.einsum(
                "hgbt,thd->bhgd", probs_low, kv_block[:, 1], preferred_element_type=jnp.float32
            ),
            None,
        )

    attended, unused_out = lax.scan(
        value_step,
        jnp.zeros((token_count, KV_HEADS, group, HEAD_DIM), jnp.float32),
        (kv_blocks, starts),
    )
    attended_low = attended.reshape(token_count, HEADS * HEAD_DIM).astype(jnp.bfloat16)
    middle = source + jnp.dot(attended_low, out_full, preferred_element_type=jnp.float32)
    normed_mid = root_norm(middle, ffn_norm).astype(jnp.bfloat16)
    columns = normed_mid
    projected = jnp.einsum(
        "td,dgf->tgf",
        columns,
        lax.all_gather(gate_up, "fsdp", axis=0, tiled=True),
        preferred_element_type=jnp.float32,
    )
    act_value, act_pull = jax.vjp(activate, projected)
    hidden = act_value.astype(jnp.bfloat16)
    columns = hidden
    ffn_out = jnp.dot(
        columns,
        lax.all_gather(down_weight, "fsdp", axis=0, tiled=True),
        preferred_element_type=jnp.float32,
    )
    layer_out = (row_keep * (middle + ffn_out)).astype(jnp.bfloat16)[None]
    d_out = row_keep * cotangent[0].astype(jnp.float32)
    d_out_low = d_out.astype(jnp.bfloat16)
    down_shard = lax.psum_scatter(
        contract_rows(hidden, d_out_low).astype(jnp.bfloat16),
        "fsdp",
        scatter_dimension=0,
        tiled=True,
    )
    d_hidden = contract_cols(d_out_low, lax.all_gather(down_weight, "fsdp", axis=0, tiled=True))
    d_proj_low = act_pull(d_hidden)[0].astype(jnp.bfloat16)
    columns = normed_mid
    gate_up_shard = lax.psum_scatter(
        jnp.einsum("td,tgf->dgf", columns, d_proj_low, preferred_element_type=jnp.float32).astype(
            jnp.bfloat16
        ),
        "fsdp",
        scatter_dimension=0,
        tiled=True,
    )
    d_normed_mid = jnp.einsum(
        "tgf,dgf->td",
        d_proj_low,
        lax.all_gather(gate_up, "fsdp", axis=0, tiled=True),
        preferred_element_type=jnp.float32,
    )
    mid_value, mid_pull = jax.vjp(root_norm, middle, ffn_norm)
    d_mid_norm, ffn_gain_part = mid_pull(d_normed_mid)
    d_middle = d_out + d_mid_norm
    d_branch = d_middle.astype(jnp.bfloat16)
    out_term = contract_rows(attended_low, d_branch)
    d_attended = (
        contract_cols(d_branch, out_full)
        .astype(jnp.bfloat16)
        .reshape(token_count, KV_HEADS, group, HEAD_DIM)
    )
    delta = jnp.transpose(jnp.sum(d_attended.astype(jnp.float32) * attended, axis=-1), (1, 2, 0))

    def block_grads(kv_block, block_start):
        probs = block_probs(kv_block, block_start)
        d_probs = jnp.einsum(
            "bhgd,thd->hgbt", d_attended, kv_block[:, 1], preferred_element_type=jnp.float32
        )
        d_scores = (probs * (d_probs - delta[..., None])).astype(jnp.bfloat16)
        return (probs.astype(jnp.bfloat16), d_scores)

    def query_step(totals, item):
        kv_block, block_start = item
        probs_low, d_scores = block_grads(kv_block, block_start)
        return (
            totals
            + jnp.einsum(
                "hgbt,thd->bhgd", d_scores, kv_block[:, 0], preferred_element_type=jnp.float32
            ),
            None,
        )

    d_query_sum, unused_out = lax.scan(
        query_step,
        jnp.zeros((token_count, KV_HEADS, group, HEAD_DIM), jnp.float32),
        (kv_blocks, starts),
    )
    d_query = (d_query_sum * inv_root).reshape(token_count, HEADS * HEAD_DIM).astype(jnp.bfloat16)
    sub_block = 512
    sub_total = token_count * lax.axis_size("ctx") // sub_block
    pieces = kv_whole.reshape(sub_total, sub_block, 2, KV_HEADS, HEAD_DIM)
    sub_starts = jnp.arange(sub_total, dtype=jnp.int32) * sub_block

    def key_grads(item):
        kv_block, block_start = item
        probs_low, d_scores = block_grads(kv_block, block_start)
        d_keys = (
            jnp.einsum("hgbt,bhgd->thd", d_scores, query_low, preferred_element_type=jnp.float32)
            * inv_root
        )
        d_values = jnp.einsum(
            "hgbt,bhgd->thd", probs_low, d_attended, preferred_element_type=jnp.float32
        )
        return jnp.concatenate(
            [d_keys.reshape(sub_block, key_cols), d_values.reshape(sub_block, key_cols)], axis=1
        )

    kv_grad = lax.psum_scatter(
        lax.map(key_grads, (pieces, sub_starts))
        .reshape(token_count * lax.axis_size("ctx"), 2 * key_cols)
        .astype(jnp.bfloat16),
        "ctx",
        scatter_dimension=0,
        tiled=True,
    ).astype(jnp.float32)
    d_key_low = kv_grad[:, :key_cols].astype(jnp.bfloat16).astype(jnp.float32)
    d_value_low = kv_grad[:, key_cols:].astype(jnp.bfloat16).astype(jnp.float32)
    d_qkv_out, qk_part = head_pull((d_query.astype(jnp.float32), d_key_low, d_value_low))
    d_qkv = d_qkv_out.astype(jnp.bfloat16)
    qkv_term = contract_rows(normed, d_qkv)
    d_normed = contract_cols(d_qkv, qkv_full)
    first_value, first_pull = jax.vjp(root_norm, source, attn_norm)
    d_source_norm, attn_gain_part = first_pull(d_normed)
    input_grad = (d_middle + d_source_norm).astype(jnp.bfloat16)[None]
    qkv_shard, out_shard, attn_shard, ffn_shard = (
        lax.psum_scatter(
            qkv_term.astype(jnp.bfloat16), "fsdp", scatter_dimension=0, tiled=True
        ).astype(jnp.float32),
        lax.psum_scatter(
            out_term.astype(jnp.bfloat16), "fsdp", scatter_dimension=0, tiled=True
        ).astype(jnp.float32),
        lax.psum_scatter(
            attn_gain_part.astype(jnp.bfloat16), "fsdp", scatter_dimension=0, tiled=True
        ).astype(jnp.float32),
        lax.psum_scatter(
            ffn_gain_part.astype(jnp.bfloat16), "fsdp", scatter_dimension=0, tiled=True
        ).astype(jnp.float32),
    )
    summed = (
        lax.psum(qkv_shard.astype(jnp.bfloat16), "ctx").astype(jnp.float32),
        lax.psum(out_shard.astype(jnp.bfloat16), "ctx").astype(jnp.float32),
        lax.psum(gate_up_shard, "ctx").astype(jnp.float32),
        lax.psum(down_shard, "ctx").astype(jnp.float32),
        lax.psum(attn_shard.astype(jnp.bfloat16), "ctx").astype(jnp.float32),
        lax.psum(ffn_shard.astype(jnp.bfloat16), "ctx").astype(jnp.float32),
    )
    qk_total = lax.psum(qk_part, ("fsdp", "ctx"))
    return (
        layer_out,
        input_grad,
        summed[0],
        summed[1],
        summed[2],
        summed[3],
        summed[4],
        summed[5],
        qk_total,
    )


MESH = pl.DeviceIdType.MESH
F32 = jnp.float32
BF16 = jnp.bfloat16
VMEM_BYTES = 60 << 20
HBM = pl.BlockSpec(memory_space=pl.ANY)
VMEM = pl.BlockSpec(memory_space=pltpu.VMEM)


class Place:
    def __init__(self):
        self.f = lax.axis_index("fsdp")
        self.c = lax.axis_index("ctx")
        self.z, self.x = lax.div(self.f, 2), lax.rem(self.f, 2)
        self.y, self.core = lax.div(self.c, 2), lax.rem(self.c, 2)
        self.xo, self.yo, self.co = 1 - self.x, 1 - self.y, 1 - self.core
        upper = lax.div(self.z, 2)
        self.others = (self.z + 1 - 2 * lax.rem(self.z, 2), 2 - upper, 3 - 3 * upper)
        self.inner = lax.rem(self.z, 2) + upper == 1
        self.far = 2 - 2 * upper
        self.x_dev = (self.z * 2 + self.xo, self.c)
        self.c_core = self.y * 2 + self.co
        self.c_y = self.yo * 2 + self.core
        self.c_diag = self.yo * 2 + self.co
        self.core_dev = (self.f, self.c_core)
        self.y_dev = (self.f, self.c_y)
        self.diag_dev = (self.f, self.c_diag)

    def rank(self, source, target):
        return jnp.where(source > target, source - 1, source)

    def z_dev(self, z):
        return (z * 2 + self.x, self.c)

    def meet(self, partners):
        barrier = pltpu.get_barrier_semaphore()
        for partner in partners:
            pl.semaphore_signal(barrier, inc=1, device_id=partner, device_id_type=MESH)
        pl.semaphore_wait(barrier, len(partners))

    def neighbours(self):
        return [self.z_dev(o) for o in self.others] + [self.x_dev, self.core_dev, self.y_dev]


class Links:
    def __init__(self, place, send_sems, recv_sems, local_sems):
        self.place = place
        self.send_sems, self.recv_sems, self.local_sems = send_sems, recv_sems, local_sems
        self.sends = self.recvs = self.locals = 0
        self.open = []

    def slots(self, count):
        first = self.recvs
        self.recvs += count
        return first

    def copy(self, src, dst, slot, device):
        made = pltpu.make_async_remote_copy(
            src_ref=src,
            dst_ref=dst,
            send_sem=self.send_sems.at[self.sends],
            recv_sem=self.recv_sems.at[slot],
            device_id=device,
            device_id_type=MESH,
        )
        self.sends += 1
        return made

    def send(self, src, dst, slot, device):
        made = self.copy(src, dst, slot, device)
        made.start()
        self.open.append(made)
        return made

    def settle(self, sends):
        for made in sends:
            made.wait_send()
            self.open = [one for one in self.open if one is not made]

    def arrive(self, ref, slot):
        pltpu.make_async_remote_copy(
            src_ref=ref,
            dst_ref=ref,
            send_sem=self.send_sems.at[0],
            recv_sem=self.recv_sems.at[slot],
            device_id=self.place.x_dev,
            device_id_type=MESH,
        ).wait_recv()

    def local(self, src, dst):
        made = pltpu.make_async_copy(src, dst, self.local_sems.at[self.locals])
        self.locals += 1
        made.start()
        return made

    def finish(self):
        for made in self.open:
            made.wait_send()
        self.open = []


class SpreadPlane:
    def __init__(self, links, place, chunks):
        self.links, self.place, self.chunks = links, place, chunks
        self.z_slot, self.x_slot = links.slots(4 * len(chunks)), links.slots(4 * len(chunks))

    def begin_z(self):
        place = self.place
        for k, (src, dst) in enumerate(self.chunks):
            slot = self.z_slot + 4 * k + place.z
            for other in place.others:
                self.links.send(src, dst(place.f), slot, place.z_dev(other))

    def begin_x(self, k):
        src, dst = self.chunks[k]
        slot = self.x_slot + 4 * k + self.place.z
        self.links.send(src, dst(self.place.f), slot, self.place.x_dev)

    def forward(self, k):
        place, dst = self.place, self.chunks[k][1]
        for other in place.others:
            block = dst(other * 2 + place.x)
            self.links.arrive(block, self.z_slot + 4 * k + other)
            self.links.send(block, block, self.x_slot + 4 * k + other, place.x_dev)

    def end(self):
        for k in range(len(self.chunks)):
            for z in range(4):
                block = self.chunks[k][1](z * 2 + self.place.xo)
                self.links.arrive(block, self.x_slot + 4 * k + z)


class SpreadTree(SpreadPlane):
    def begin_z(self):
        place = self.place
        self.passed = []
        for k, (src, dst) in enumerate(self.chunks):
            slot = self.z_slot + 4 * k + place.z
            for other in place.others[:2]:
                self.links.send(src, dst(place.f), slot, place.z_dev(other))

    def onward(self, k):
        place, dst = self.place, self.chunks[k][1]
        blocks = [(dst(o * 2 + place.x), self.z_slot + 4 * k + o) for o in place.others[1:]]
        made = [
            self.links.copy(block, block, slot, place.z_dev(place.others[0]))
            for block, slot in blocks
        ]
        self.passed += made

        @pl.when(place.inner)
        def _():
            for (block, slot), one in zip(blocks, made):
                self.links.arrive(block, slot)
                one.start()

    def forward(self, k):
        place, dst = self.place, self.chunks[k][1]
        blocks = [(dst(o * 2 + place.x), self.z_slot + 4 * k + o) for o in place.others]
        self.links.arrive(*blocks[0])
        near = self.x_slot + 4 * k + place.others[0]
        self.links.send(blocks[0][0], blocks[0][0], near, place.x_dev)

        @pl.when(jnp.logical_not(place.inner))
        def _():
            for block, slot in blocks[1:]:
                self.links.arrive(block, slot)

        for other, (block, _) in zip(place.others[1:], blocks[1:]):
            self.links.send(block, block, self.x_slot + 4 * k + other, place.x_dev)

    def finish(self):
        @pl.when(self.place.inner)
        def _():
            for made in self.passed:
                made.wait_send()


class ReducePlane:
    def __init__(self, links, place, chunks, from_x, from_z, own=None):
        self.links, self.place, self.chunks = links, place, chunks
        self.from_x, self.from_z, self.own = from_x, from_z, own
        self.summed = 0
        self.x_slot, self.z_slot = links.slots(len(chunks)), links.slots(3 * len(chunks))
        self.loads, self.z_sends = {}, {}

    def send_x(self, k):
        place = self.place
        from_x = self.from_x.at[k - self.summed]
        self.links.send(self.chunks[k](place.xo), from_x, self.x_slot + k, place.x_dev)

    def load(self, k):
        slots = self.own.shape[0]
        for made in self.z_sends.pop(k - slots, []):
            made.wait_send()
        self.loads[k] = self.links.local(self.chunks[k](self.place.x), self.own.at[k % slots])

    def mine(self, k):
        if self.own is None:
            return self.chunks[k](self.place.x)
        return self.own.at[k % self.own.shape[0]]

    def middle(self, k):
        place = self.place
        self.links.arrive(self.from_x.at[k], self.x_slot + k)
        if k in self.loads:
            self.loads[k].wait()
        mine = self.mine(k)
        self.z_sends[k] = []
        for other in place.others:
            mine[other] = (mine[other].astype(F32) + self.from_x[k, other].astype(F32)).astype(BF16)
            rank = place.rank(place.z, other)
            made = self.links.copy(
                mine.at[other],
                self.from_z.at[k, rank],
                self.z_slot + 3 * k + rank,
                place.z_dev(other),
            )
            made.start()
            self.z_sends[k].append(made)

    def end(self, k):
        place = self.place
        mine = self.mine(k)
        sums = mine[place.z].astype(F32) + self.from_x[k, place.z].astype(F32)
        for rank in range(3):
            self.links.arrive(self.from_z.at[k, rank], self.z_slot + 3 * k + rank)
            sums += self.from_z[k, rank].astype(F32)
        total = self.from_x.at[k, place.z]
        total[...] = sums.astype(BF16)
        return total

    def finish(self):
        for sends in self.z_sends.values():
            for made in sends:
                made.wait_send()


class ReduceTree(ReducePlane):
    def __init__(self, links, place, chunks, from_x, from_z, via, own, summed):
        super().__init__(links, place, chunks, from_x, from_z, own)
        self.summed = summed
        self.via, self.via_slot = via, links.slots(len(chunks))
        self.outer = jnp.logical_not(place.inner)

    def load(self, k):
        slots = self.own.shape[0]
        self.settle(self.z_sends.pop(k - slots, []))
        self.loads[k] = self.links.local(self.chunks[k](self.place.x), self.own.at[k % slots])

    def settle(self, sends):
        for made, when in sends:
            if when is None:
                made.wait_send()
            else:
                pl.when(when)(made.wait_send)

    def middle(self, k):
        place = self.place
        self.loads[k].wait()
        mine = self.mine(k)
        if k >= self.summed:
            from_x = self.from_x.at[k - self.summed]
            self.links.arrive(from_x, self.x_slot + k)
            for other in place.others:
                pair = mine[other].astype(F32) + from_x[other].astype(F32)
                mine[other] = pair.astype(BF16)
        near = place.others[0]
        device = place.z_dev(near)
        direct = self.links.copy(mine.at[near], self.from_z.at[k, 0], self.z_slot + 3 * k, device)
        direct.start()
        far = self.links.copy(
            mine.at[pl.ds(place.far, 2)], self.via.at[k], self.via_slot + k, device
        )
        pl.when(self.outer)(far.start)
        self.z_sends[k] = [(direct, None), (far, self.outer)]

    def combine(self, k):
        place = self.place
        mine = self.mine(k)

        sent = [
            self.links.copy(
                mine.at[place.far + j],
                self.from_z.at[k, 1],
                self.z_slot + 3 * k + 1,
                place.z_dev(place.far + j),
            )
            for j in range(2)
        ]

        @pl.when(place.inner)
        def _():
            self.links.arrive(self.via.at[k], self.via_slot + k)
            for j in range(2):
                here = mine[place.far + j].astype(F32) + self.via[k, j].astype(F32)
                mine[place.far + j] = here.astype(BF16)
                sent[j].start()

        self.z_sends[k] += [(made, place.inner) for made in sent]

    def end(self, k):
        place = self.place
        sums = self.mine(k)[place.z].astype(F32)
        if k >= self.summed:
            sums += self.from_x[k - self.summed, place.z].astype(F32)
        for side in range(2):
            self.links.arrive(self.from_z.at[k, side], self.z_slot + 3 * k + side)
            sums += self.from_z[k, side].astype(F32)
        total = self.from_z.at[k, 0]
        total[...] = sums.astype(BF16)
        return total

    def finish(self):
        for sends in self.z_sends.values():
            self.settle(sends)


class SpreadCtx:
    def __init__(self, links, place, out, parts):
        self.links, self.place, self.out, self.parts = links, place, out, parts
        self.slot = links.slots(3 * len(parts))
        self.sends = []

    def begin(self, k, src):
        place, rows = self.place, self.parts[k]
        out = self.out.at[place.c, rows]
        self.sends.append(self.links.send(src, out, self.slot + 3 * k + 1, place.y_dev))
        self.sends.append(self.links.send(src, out, self.slot + 3 * k, place.core_dev))

    def forward(self, k):
        place = self.place
        block = self.out.at[place.c_y, self.parts[k]]
        self.links.arrive(block, self.slot + 3 * k + 1)
        self.sends.append(self.links.send(block, block, self.slot + 3 * k + 2, place.core_dev))

    def end(self):
        place = self.place
        for k, rows in enumerate(self.parts):
            self.links.arrive(self.out.at[place.c_core, rows], self.slot + 3 * k)
            self.links.arrive(self.out.at[place.c_diag, rows], self.slot + 3 * k + 2)


class ReduceCtx:
    def __init__(self, links, place, part, parts, own, from_core, to_y, from_y):
        self.links, self.place, self.part = links, place, part
        self.parts = [rows if isinstance(rows, tuple) else (rows,) for rows in parts]
        self.own, self.from_core, self.to_y, self.from_y = own, from_core, to_y, from_y
        self.slot = links.slots(3 * len(parts))
        self.loads, self.sends = {}, []

    def begin(self, only=None):
        place = self.place
        for side, y in ((0, place.yo), (1, place.y)):
            for k, rows in enumerate(self.parts):
                if only not in (None, k):
                    continue
                self.links.send(
                    self.part.at[y * 2 + place.co, *rows],
                    self.from_core.at[side, *rows],
                    self.slot + 3 * k + side,
                    place.core_dev,
                )
                if self.own is not None and side == 0:
                    self.load(0, k)

    def load(self, side, k):
        rows = self.parts[k]
        y = self.place.y if side else self.place.yo
        self.loads[side, k] = self.links.local(
            self.part.at[y * 2 + self.place.core, *rows], self.own.at[rows]
        )

    def pair(self, side, k):
        rows = self.parts[k]
        self.links.arrive(self.from_core.at[side, *rows], self.slot + 3 * k + side)
        if self.own is None:
            y = self.place.y if side else self.place.yo
            own = self.part[y * 2 + self.place.core, *rows]
        else:
            self.loads[side, k].wait()
            own = self.own[rows]
        return own.astype(F32) + self.from_core[side, *rows].astype(F32)

    def cross(self, k):
        rows = self.parts[k]
        self.to_y[rows] = self.pair(0, k).astype(BF16)
        if self.own is not None:
            self.load(1, k)
        made = self.links.send(
            self.to_y.at[rows], self.from_y.at[rows], self.slot + 3 * k + 2, self.place.y_dev
        )
        self.sends.append(made)

    def total(self, k):
        rows = self.parts[k]
        sums = self.pair(1, k)
        self.links.arrive(self.from_y.at[rows], self.slot + 3 * k + 2)
        return sums + self.from_y[rows].astype(F32)


def halves(rows):
    return [pl.ds(0, rows // 2), pl.ds(rows // 2, rows // 2)]


def row_factor(values):
    return lax.rsqrt(jnp.mean(values * values, axis=-1, keepdims=True) + EPSILON)


def low_half(shape):
    return lax.rem(lax.broadcasted_iota(jnp.int32, shape, len(shape) - 1), 128) < 64


def partner(values):
    lane = lax.broadcasted_iota(jnp.int32, values.shape, len(values.shape) - 1)
    first = lax.rem(lane, 64) < 32
    return jnp.where(first, pltpu.roll(values, 96, 1), pltpu.roll(values, 32, 1))


def half_sums(values):
    low = low_half(values.shape)
    first = jnp.sum(jnp.where(low, values, 0.0), axis=-1, keepdims=True)
    second = jnp.sum(jnp.where(low, 0.0, values), axis=-1, keepdims=True)
    return jnp.where(low, first, second)


def row_loop(count, body, first=0):
    def step(index, carry):
        body(index)
        return carry

    lax.fori_loop(first, first + count, step, 0)


BLOCK = 256
SHORT = 128


def attention_scores(query, keys, key_bias, first, span):
    scores = lax.dot_general(
        query, keys, (((1,), (1,)), ((), ())), preferred_element_type=F32
    ) * (1.0 / math.sqrt(HEAD_DIM))
    rows = first + lax.broadcasted_iota(jnp.int32, scores.shape, 0)
    columns = lax.broadcasted_iota(jnp.int32, scores.shape, 1)
    return jnp.where(columns <= rows, scores, -1e30) + key_bias[:, :span]


def turn_tables(angles, cos, sin):
    for i in range(16):
        rows = slice(64 * i, 64 * (i + 1))
        cos_high, sin_high = angles[i : i + 1], angles[16 + i : 17 + i]
        cos_low, sin_low = angles[32:96], angles[96:160]
        cos[rows] = cos_high * cos_low - sin_high * sin_low
        sin[rows] = sin_high * cos_low + cos_high * sin_low


def forward_kernel(
    lengths, qkv_weight, out_s, gain_s, x_s, gate_up, down_weight, cotangent, angles, qk_gain,
    qkv_wh, out_wh, gains, normed_h, qkv_raw_h, qkv_low_h, att_low_h, log_sums_h,
    gu_w, dn_w, dout_all, middle, mid_all, head_gain, key_bias,
    kv_pairs, kv_s, dout_s, cos, sin, gain_blocks, qkv_w, out_w, x_all, normed, qkv_raw, qkv_low, att_low, log_sums,
    part, keys, values, from_core, to_y, from_y, mid_low, gu_pairs, gu_rows, gu_s, send_sems, recv_sems, local_sems,
):
    place = Place()
    links = Links(place, send_sems, recv_sems, local_sems)
    fellows = [lax.rem(place.f + d, 8) for d in range(1, 8)]
    place.meet([(f, place.c) for f in fellows] + [place.core_dev, place.y_dev])

    q_columns = pl.ds(pl.multiple_of(256 * place.c, 256), 256)
    for j in range(2):
        pair = pl.ds(pl.multiple_of(1024 + 256 * j + 128 * place.y, 128), 128)
        links.local(qkv_weight.at[:, pair], kv_pairs.at[j]).wait()
    cot_load = links.local(cotangent, dout_s)
    low = low_half(kv_pairs.shape[1:])
    first, second = [], []
    for j in range(2):
        value = kv_pairs[j].astype(F32)
        swapped = pltpu.roll(value, 64, 1)
        first.append(jnp.where(place.core == 0, value, swapped))
        second.append(jnp.where(place.core == 0, swapped, value))
    kv_s[...] = jnp.where(low, first[0], second[1]).astype(BF16)
    qkv_plane = SpreadPlane(
        links,
        place,
        [
            (qkv_weight.at[:, q_columns], lambda f: qkv_w.at[f, :, 0:256]),
            (kv_s, lambda f: qkv_w.at[f, :, 256:384]),
        ],
    )
    qkv_plane.begin_z()
    qkv_plane.begin_x(0)
    qkv_plane.begin_x(1)
    picks = []
    for f in range(8):
        start = pl.multiple_of(512 * f + 128 * place.c, 128)
        picks.append(links.local(gate_up.at[:, :, pl.ds(start, 128)], gu_pairs.at[f]))
    tokens = x_s.shape[0]
    parts = halves(tokens)
    x_spread = SpreadCtx(links, place, x_all, parts)
    for k, rows in enumerate(parts):
        x_spread.begin(k, x_s.at[rows])
    gain_slot = links.slots(8)
    for f in fellows:
        links.send(gain_s, gain_blocks.at[place.f], gain_slot + place.f, (f, place.c))
    kept = [
        links.local(qkv_weight.at[:, q_columns], qkv_w.at[place.f, :, 0:256]),
        links.local(kv_s, qkv_w.at[place.f, :, 256:384]),
        links.local(gain_s, gain_blocks.at[place.f]),
        links.local(x_s, x_all.at[place.c]),
    ]

    root_slot, side_slot = links.slots(1), links.slots(1)
    holds = place.z == place.c
    down = [
        links.copy(out_s, out_w.at[place.x], root_slot, place.z_dev(other))
        for other in place.others[:2]
    ]
    relay = links.copy(out_w.at[place.x], out_w.at[place.x], root_slot, place.z_dev(place.others[0]))
    across = lax.div(place.c, 2) != lax.div(place.z, 2)
    relays = jnp.logical_and(place.inner, across)
    sideways = links.copy(out_s, out_w.at[place.x], side_slot, place.x_dev)
    onward = links.copy(out_w.at[place.x], out_w.at[place.x], side_slot, place.x_dev)
    own = pltpu.make_async_copy(out_s, out_w.at[place.x], local_sems.at[links.locals])
    links.locals += 1

    @pl.when(holds)
    def _():
        for made in down:
            made.start()
        sideways.start()
        own.start()

    rows = gu_s.shape[0]
    for f in range(8):
        picks[f].wait()
        gu_rows[...] = gu_pairs.at[f].reshape(2 * rows, 128)[...].astype(F32)
        for side in range(2):
            first = 1024 * side + 128 * f
            picked = gu_rows[pl.ds(side, rows, stride=2), :]
            gu_s[:, first : first + 128] = picked.astype(BF16)
    step = 32
    chunks = []
    dn_s = down_weight.at[pl.ds(pl.multiple_of(128 * place.c, 128), dn_w.shape[1])]
    for src, dst in ((dn_s, dn_w), (gu_s, gu_w)):
        for first in range(0, src.shape[0], step):
            rows = pl.ds(first, step)
            chunks.append((src.at[rows], lambda f, dst=dst, rows=rows: dst.at[f, rows]))
    plane = SpreadTree(links, place, chunks)
    plane.begin_z()
    cot_load.wait()
    length = lengths[0]
    positions = tokens * place.c + lax.broadcasted_iota(jnp.int32, (tokens, 1), 0)
    dout_s[...] = jnp.where(positions < length, dout_s[...].astype(F32), 0.0).astype(BF16)
    for k in range(4):
        plane.begin_x(k)
    qkv_plane.forward(0)
    qkv_plane.forward(1)
    for k in range(4, len(chunks)):
        plane.begin_x(k)
    last = [
        links.local(gu_s, gu_w.at[place.f]),
        links.local(dn_s, dn_w.at[place.f]),
        links.local(dout_s, dout_all.at[place.c]),
    ]
    turn_tables(angles, cos, sin)
    columns = lax.broadcasted_iota(jnp.int32, key_bias.shape, 1)
    key_bias[...] = jnp.where(columns < length, 0.0, -1e30)
    ones = jnp.ones((1, HEAD_DIM), F32)
    q_gain, k_gain = qk_gain[0:1].astype(F32), qk_gain[1:2].astype(F32)
    head_gain[...] = jnp.zeros_like(head_gain)
    for b in range(2):
        head_gain[b : b + 1] = jnp.concatenate([q_gain, q_gain], axis=1)
    head_gain[2:3] = jnp.concatenate([k_gain, ones], axis=1)
    for f in fellows:
        links.arrive(gain_blocks.at[f], gain_slot + f)
    for made in kept:
        made.wait()
    gains[...] = jnp.zeros_like(gains)
    for f in range(8):
        gains[0:2, 256 * f : 256 * (f + 1)] = gain_blocks[f, 0:2]
    dout = SpreadCtx(links, place, dout_all, parts)
    for k, rows in enumerate(parts):
        x_spread.forward(k)
        dout.begin(k, dout_s.at[rows])
    x_spread.end()
    qkv_plane.end()

    def project(index):
        rows = pl.ds(pl.multiple_of(index * BLOCK, BLOCK), BLOCK)
        source = x_all[index].astype(F32)
        normed[rows] = (source * row_factor(source) * gains[0:1]).astype(BF16)
        weight = qkv_w[...].reshape(normed.shape[1], qkv_w.shape[2])
        raw = jnp.dot(normed[rows], weight, preferred_element_type=F32)
        for b in range(3):
            block = raw[:, 128 * b : 128 * (b + 1)]
            qkv_raw[b, rows] = block
            factor = lax.rsqrt(half_sums(block * block) * (1.0 / HEAD_DIM) + EPSILON)
            scaled = block * factor * head_gain[b : b + 1]
            turned = scaled * cos[rows] + partner(scaled) * sin[rows]
            if b == 2:
                turned = jnp.where(low_half(turned.shape), turned, block)
            qkv_low[b, rows] = turned.astype(BF16)
            if b == 2:
                low = low_half(turned.shape)
                swapped = pltpu.roll(turned, 64, 1)
                keys[rows] = jnp.where(low, turned, swapped).astype(BF16)
                values[rows] = jnp.where(low, swapped, turned).astype(BF16)

    seq = normed.shape[0]
    att_low[...] = jnp.zeros_like(att_low)
    log_sums[...] = jnp.zeros_like(log_sums)
    row_loop(seq // BLOCK, project)
    last += [
        links.local(normed, normed_h),
        links.local(qkv_raw, qkv_raw_h),
        links.local(qkv_low, qkv_low_h),
        links.local(qkv_w, qkv_wh),
    ]

    def heads(index):
        b, half = lax.div(index, 2), lax.rem(index, 2)
        for i in range(seq // BLOCK):
            rows, span = pl.ds(i * BLOCK, BLOCK), (i + 1) * BLOCK
            query = qkv_low[b, rows]
            side = lax.div(lax.broadcasted_iota(jnp.int32, query.shape, 1), 64) == half
            chosen = jnp.where(side, query, 0)
            scores = attention_scores(chosen, keys[:span], key_bias[0:1], i * BLOCK, span)
            top = jnp.max(scores, axis=-1, keepdims=True)
            expanded = jnp.exp(scores - top)
            sums = jnp.sum(expanded, axis=-1, keepdims=True)
            probs = (expanded * (1.0 / sums)).astype(BF16)
            out = jnp.dot(probs, values[:span], preferred_element_type=F32)
            att_low[b, rows] = jnp.where(side, out.astype(BF16), att_low[b, rows])
            log_sums[b, rows] = jnp.where(side, top + jnp.log(sums), log_sums[b, rows])

    @pl.when(relays)
    def _():
        links.arrive(out_w.at[place.x], root_slot)
        relay.start()
        onward.start()

    plane.onward(0)
    row_loop(2, heads)
    plane.onward(1)
    plane.onward(2)
    plane.forward(0)
    row_loop(2, heads, 2)
    plane.onward(3)
    for k in range(1, 3):
        plane.forward(k)

    @pl.when(jnp.logical_not(jnp.logical_or(holds, relays)))
    def _():
        links.arrive(out_w.at[place.x], root_slot)
        onward.start()

    @pl.when(holds)
    def _():
        own.wait()

    for k in range(len(parts)):
        dout.forward(k)
    links.arrive(out_w.at[place.xo], side_slot)

    def project_out(index):
        rows = pl.ds(pl.multiple_of(index * BLOCK, BLOCK), BLOCK)
        sums = jnp.dot(att_low[0, rows], out_w[0], preferred_element_type=F32)
        sums += jnp.dot(att_low[1, rows], out_w[1], preferred_element_type=F32)
        part[index] = sums.astype(BF16)

    row_loop(seq // BLOCK, project_out)
    reduce = ReduceCtx(links, place, part, parts, None, from_core, to_y, from_y)
    reduce.begin()
    last += [
        links.local(att_low, att_low_h),
        links.local(log_sums, log_sums_h),
        links.local(out_w, out_wh),
    ]
    plane.onward(4)
    for k in range(2):
        reduce.cross(k)
    plane.forward(3)
    plane.onward(5)
    plane.onward(6)
    plane.forward(4)
    plane.onward(7)
    plane.forward(5)
    plane.onward(8)
    plane.forward(6)
    mid = SpreadCtx(links, place, mid_all, parts)
    for k, rows in enumerate(parts):
        value = x_all[place.c, rows].astype(F32) + reduce.total(k)
        middle[rows] = value
        mid_low[rows] = (value * row_factor(value) * gains[1:2]).astype(BF16)
        mid.begin(k, mid_low.at[rows])
        last.append(links.local(mid_low.at[rows], mid_all.at[place.c, rows]))
    for k in range(9, len(chunks)):
        plane.onward(k)
    plane.forward(7)
    plane.forward(8)
    for k in range(2):
        mid.forward(k)
    for k in range(9, len(chunks)):
        plane.forward(k)
    plane.end()
    mid.end()
    dout.end()
    for made in last:
        made.wait()
    links.finish()
    plane.finish()

    @pl.when(holds)
    def _():
        for made in down:
            made.wait_send()
        sideways.wait_send()

    @pl.when(relays)
    def _():
        relay.wait_send()

    @pl.when(jnp.logical_not(holds))
    def _():
        onward.wait_send()


NT = (((1,), (1,)), ((), ()))
TN = (((0,), (0,)), ((), ()))


def norm_back(d_norm, value, gain):
    factor = row_factor(value)
    gain_sum = jnp.sum(d_norm * value * factor, axis=0, keepdims=True)
    scaled = d_norm * gain
    inner = jnp.mean(scaled * value, axis=-1, keepdims=True)
    return factor * scaled - value * (factor * factor * factor * inner), gain_sum


def feed_kernel(
    gu_h, dn_h, dout_h, mid_h, middle_h, gains,
    gu_g, dn_pair, ffn_h, d_middle_h, branch_s, ffn_gain,
    gu_w, dn_w, dout, mid, hidden, d_proj, dn_g, from_x, stage,
    part, from_core, to_y, from_y, middle, d_norm, branch, send_sems, recv_sems, local_sems,
):
    place = Place()
    links = Links(place, send_sems, recv_sems, local_sems)
    shards, rows, width = gu_w.shape
    units, seq = hidden.shape[1], hidden.shape[0]
    tokens = mid.shape[1]
    first = [links.local(mid_h, mid)]
    later, loads = [], []
    for n in range(units // 256):
        gate, up = pl.ds(256 * n, 256), pl.ds(units + 256 * n, 256)
        loads.append([
            links.local(gu_h.at[:, :, gate], gu_w.at[:, :, gate]),
            links.local(gu_h.at[:, :, up], gu_w.at[:, :, up]),
        ])
        if n == 0:
            first += [links.local(dout_h, dout), links.local(dn_h, dn_w)]
    later.append(links.local(middle_h, middle))
    place.meet([place.x_dev, place.core_dev, place.y_dev])
    for made in first:
        made.wait()

    x_slot = links.slots(4)
    for n in range(units // 256):
        for made in loads[n]:
            made.wait()
        gate_columns, up_columns = slice(256 * n, 256 * (n + 1)), slice(units + 256 * n, units + 256 * (n + 1))

        def activation(index, gate_columns=gate_columns, up_columns=up_columns, n=n):
            low = mid[index]
            gate = jnp.dot(
                low, gu_w[:, :, gate_columns].reshape(width, 256), preferred_element_type=F32
            )
            up = jnp.dot(
                low, gu_w[:, :, up_columns].reshape(width, 256), preferred_element_type=F32
            )
            d_hidden = lax.dot_general(
                dout[index], dn_w[2 * n : 2 * n + 2].reshape(256, width), NT,
                preferred_element_type=F32,
            )
            at = pl.ds(pl.multiple_of(index * tokens, tokens), tokens)
            sigmoid = 1.0 / (1.0 + jnp.exp(-gate))
            silu = gate * sigmoid
            hidden[at, gate_columns] = (silu * up).astype(BF16)
            d_gate = d_hidden * up * (sigmoid * (1.0 + gate * (1.0 - sigmoid)))
            d_proj[at, gate_columns] = d_gate.astype(BF16)
            d_proj[at, up_columns] = (d_hidden * silu).astype(BF16)

        row_loop(4, activation)
        left = hidden[:, gate_columns].T

        def down_grad(j, left=left, n=n):
            wide = pl.ds(pl.multiple_of(512 * j, 512), 512)
            right = dout[:, :, wide].reshape(seq, 512)
            grad = jnp.dot(left, right, preferred_element_type=F32).astype(BF16)
            dn_g[n, 0, :, wide] = grad[:128]
            dn_g[n, 1, :, wide] = grad[128:]

        row_loop(4, down_grad)
        links.send(dn_g.at[n, place.xo], from_x.at[n], x_slot + n, place.x_dev)

    def mid_grad(f):
        grad = lax.dot_general(d_proj[...], gu_w[f], NT, preferred_element_type=F32)
        columns = pl.ds(pl.multiple_of(rows * f, rows), rows)
        part[:, :, columns] = grad.astype(BF16).reshape(4, tokens, rows)

    parts = halves(tokens)
    sides = [(slice(None), side) for side in halves(width)]
    dmid = ReduceCtx(links, place, part, sides, None, from_core, to_y, from_y)
    row_loop(shards // 2, mid_grad)
    dmid.begin(0)
    row_loop(shards // 2, mid_grad, shards // 2)
    dmid.begin(1)
    dmid.cross(0)

    def gate_up_grad(z):
        for x in range(2):
            columns = pl.ds(pl.multiple_of(2 * rows * z + rows * x, rows), rows)
            left = mid[:, :, columns].reshape(seq, rows).T
            for j in range(4):
                wide = slice(512 * j, 512 * (j + 1))
                grad = jnp.dot(left, d_proj[:, wide], preferred_element_type=F32)
                stage[x, :, wide] = grad.astype(BF16)
        made = pltpu.make_async_copy(stage, gu_g.at[z], local_sems.at[links.locals])
        made.start()
        made.wait()

    row_loop(1, gate_up_grad)
    dmid.cross(1)
    row_loop(3, gate_up_grad, 1)
    links.locals += 1

    def feed_out(index):
        at = pl.ds(pl.multiple_of(index * tokens, tokens), tokens)
        for j in range(4):
            wide = slice(512 * j, 512 * (j + 1))
            right = dn_w[:, :, wide].reshape(units, 512)
            sums = jnp.dot(hidden[at], right, preferred_element_type=F32)
            mid[index, :, wide] = sums.astype(BF16)

    row_loop(4, feed_out)
    later.append(links.local(mid, ffn_h))
    later[0].wait()
    for k in range(2):
        d_norm[sides[k]] = dmid.total(k)
    gain_sum = None
    for k, at in enumerate(parts):
        grad, term = norm_back(d_norm[at], middle[at], gains[1:2])
        gain_sum = term if gain_sum is None else gain_sum + term
        middle[at] = grad + dout[place.c, at].astype(F32)
        branch[at] = middle[at].astype(BF16)
        later.append(links.local(middle.at[at], d_middle_h.at[at]))
        later.append(links.local(branch.at[at], branch_s.at[at]))
    ffn_gain[...] = gain_sum
    for n in range(4):
        links.arrive(from_x.at[n], x_slot + n)
        pair = dn_g[n, place.x].astype(F32) + from_x[n].astype(F32)
        from_x[n] = pair.astype(BF16)
        later.append(links.local(from_x.at[n], dn_pair.at[n]))
    for made in later[1:]:
        made.wait()
    links.finish()


def backward_kernel(
    gu_g, dn_pair, ffn_part, middle_h, d_middle_h, branch_s, x_h, lengths, gains, ffn_gain,
    angles, head_gain, key_bias,
    normed_h, qkv_raw_h, qkv_low_h, att_low_h, log_sums_h, qkv_wh, out_wh,
    gu_all, dn_all, layer_out, qkv_all, out_all, input_grad, stats,
    own, from_x, from_z, via,
    ctx_own, from_core1, to_y1, from_y1, from_core2, to_y2, from_y2,
    middle, x_s, d_middle, branch_all, part,
    cos, sin, qkv_raw, qkv_low, att_low, log_sums, qkv_w, out_w,
    keys, values, d_att, d_low, d_keys, d_values, gain_g,
    qkv_g, qkv_x, qkv_z, out_g, out_x, out_z,
    mine, plane_stats, ctx_stats, send_sems, recv_sems, local_sems,
):
    place = Place()
    links = Links(place, send_sems, recv_sems, local_sems)
    fellows = [lax.rem(place.f + d, 8) for d in range(1, 8)]
    place.meet(
        [(f, place.c) for f in fellows] + [place.core_dev, place.y_dev, place.diag_dev]
    )
    step = from_x.shape[2]
    chunks, where = [], []
    for first in range(0, dn_pair.shape[1], step):
        rows = pl.ds(first, step)
        chunks.append(lambda x, rows=rows: dn_pair.at[:, rows])
        where.append((dn_all, rows))
    summed = len(chunks)
    for first in range(0, gu_g.shape[2], step):
        rows = pl.ds(first, step)
        chunks.append(lambda x, rows=rows: gu_g.at[:, x, rows])
        where.append((gu_all, rows))
    count = len(chunks)
    plane = ReduceTree(links, place, chunks, from_x, from_z, via, own, summed)
    outs = [SpreadCtx(links, place, out, [rows]) for out, rows in where]
    kept = []

    def end(k):
        total = plane.end(k)
        if k + own.shape[0] < count:
            plane.load(k + own.shape[0])
        out, rows = where[k]
        outs[k].begin(0, total)
        kept.append(links.local(total, out.at[place.c, rows]))

    tokens, width = middle.shape
    parts = halves(tokens)
    branch = SpreadCtx(links, place, branch_all, parts)
    for k, rows in enumerate(parts):
        branch.begin(k, branch_s.at[rows])
    for k in range(summed, count - 1):
        plane.send_x(k)
    ffn = ReduceCtx(links, place, ffn_part, parts, ctx_own, from_core1, to_y1, from_y1)
    ffn.begin()
    for k in range(own.shape[0]):
        plane.load(k)
    late = [
        links.local(a, b)
        for a, b in (
            (branch_s, branch_all.at[place.c]),
            (out_wh, out_w), (qkv_low_h, qkv_low), (att_low_h, att_low), (log_sums_h, log_sums),
            (qkv_raw_h, qkv_raw), (qkv_wh, qkv_w),
            (middle_h, middle), (d_middle_h, d_middle), (x_h, x_s),
        )
    ]
    turn_tables(angles, cos, sin)
    gain_g[...] = jnp.zeros_like(gain_g)
    d_keys[...] = jnp.zeros_like(d_keys)
    d_low[...] = jnp.zeros_like(d_low)
    d_values[...] = jnp.zeros_like(d_values)
    plane.middle(0)
    plane.middle(1)
    for k in range(2):
        ffn.cross(k)
    branch.forward(0)
    plane.combine(0)
    branch.forward(1)
    plane.middle(2)
    plane.combine(1)
    branch.end()
    for made in late:
        made.wait()

    root = 1.0 / math.sqrt(HEAD_DIM)
    seq = 4 * tokens

    def prepare(index):
        rows = pl.ds(pl.multiple_of(index * BLOCK, BLOCK), BLOCK)
        block = qkv_low[2, rows].astype(F32)
        low = low_half(block.shape)
        swapped = pltpu.roll(block, 64, 1)
        keys[rows] = jnp.where(low, block, swapped).astype(BF16)
        values[rows] = jnp.where(low, swapped, block).astype(BF16)
        for b in range(2):
            d_att[b, rows] = lax.dot_general(
                branch_all[index], out_w[b], NT, preferred_element_type=F32
            ).astype(BF16)

    row_loop(seq // BLOCK, prepare)
    for b in range(2):
        left = att_low[b].T
        for j in range(8):
            columns = slice(256 * j, 256 * (j + 1))
            right = branch_all[:, :, columns].reshape(seq, 256)
            out_g[b, :, columns] = jnp.dot(left, right, preferred_element_type=F32).astype(BF16)
    out_slot = links.slots(1)
    links.send(out_g.at[place.xo], out_x, out_slot, place.x_dev)
    plane.send_x(count - 1)
    links.settle(branch.sends)
    normed_load = links.local(normed_h, branch_all)
    plane.middle(3)

    def unturn(row, rows, grads, block):
        back = grads * cos[rows] + partner(grads * sin[rows])
        factor = lax.rsqrt(half_sums(block * block) * (1.0 / HEAD_DIM) + EPSILON)
        gain_term = jnp.sum(back * block * factor, axis=0, keepdims=True)
        scaled = back * head_gain[row : row + 1]
        inner = half_sums(scaled * block) * (1.0 / HEAD_DIM)
        return factor * scaled - block * (factor * factor * factor * inner), gain_term

    def heads(index):
        b, half = lax.div(index, 2), lax.rem(index, 2)
        for i in range(seq // SHORT):
            rows, span = pl.ds(i * SHORT, SHORT), (i + 1) * SHORT
            query = qkv_low[b, rows]
            lane = lax.broadcasted_iota(jnp.int32, query.shape, 1)
            side = lax.div(lane, 64) == half
            chosen = jnp.where(side, query, 0)
            d_chosen = jnp.where(side, d_att[b, rows], 0)
            logs = jnp.max(jnp.where(side, log_sums[b, rows], -1e30), axis=-1, keepdims=True)
            scores = attention_scores(chosen, keys[:span], key_bias[0:1], i * SHORT, span)
            probs = jnp.exp(scores - logs)
            d_probs = lax.dot_general(d_chosen, values[:span], NT, preferred_element_type=F32)
            delta = jnp.sum(probs * d_probs, axis=-1, keepdims=True)
            d_scores = (probs * (d_probs - delta)).astype(BF16)
            d_query = jnp.dot(d_scores, keys[:span], preferred_element_type=F32) * root
            d_keys[:span] += lax.dot_general(d_scores, chosen, TN, preferred_element_type=F32)
            d_values[:span] += lax.dot_general(
                probs.astype(BF16), d_chosen, TN, preferred_element_type=F32
            )
            d_low[b, rows] = jnp.where(side, d_query.astype(BF16), d_low[b, rows])

    def unturn_queries(index):
        rows = pl.ds(pl.multiple_of(index * BLOCK, BLOCK), BLOCK)
        for b in range(2):
            grads = d_low[b, rows].astype(F32)
            d_block, gain_term = unturn(0, rows, grads, qkv_raw[b, rows])
            d_low[b, rows] = d_block.astype(BF16)
            gain_g[0:1] += gain_term

    row_loop(2, heads)
    plane.combine(2)
    end(0)
    row_loop(2, heads, 2)
    plane.middle(4)
    plane.combine(3)
    end(1)
    row_loop(seq // BLOCK, unturn_queries)

    def finish(index):
        rows = pl.ds(pl.multiple_of(index * BLOCK, BLOCK), BLOCK)
        k_sum, v_sum = d_keys[rows], d_values[rows]
        low = low_half(k_sum.shape)
        k_sum = (k_sum + pltpu.roll(k_sum, 64, 1)) * root
        v_sum = v_sum + pltpu.roll(v_sum, 64, 1)
        grads = jnp.where(low, k_sum, v_sum).astype(BF16).astype(F32)
        d_block, gain_term = unturn(2, rows, grads, qkv_raw[2, rows])
        d_low[2, rows] = jnp.where(low, d_block, grads).astype(BF16)
        gain_g[1:2] += gain_term
        for j in range(4):
            columns = slice(512 * j, 512 * (j + 1))
            sums = jnp.zeros((BLOCK, 512), F32)
            for b in range(3):
                weight = qkv_w[columns, 128 * b : 128 * (b + 1)]
                sums += lax.dot_general(d_low[b, rows], weight, NT, preferred_element_type=F32)
            part[index, :, columns] = sums.astype(BF16)

    row_loop(seq // BLOCK, finish)

    dnorm = ReduceCtx(links, place, part, parts, None, from_core2, to_y2, from_y2)
    dnorm.begin()
    normed_load.wait()
    for b in range(3):
        left = d_low[b].T
        for f in range(8):
            right = branch_all[:, :, 256 * f : 256 * (f + 1)].reshape(seq, 256)
            qkv_g[f // 2, f % 2, 128 * b : 128 * (b + 1)] = jnp.dot(
                left, right, preferred_element_type=F32
            ).astype(BF16)
    qkv_step = qkv_x.shape[2]
    qkv_rows = [pl.ds(k * qkv_step, qkv_step) for k in range(qkv_x.shape[0])]
    qkv_chunks = [lambda x, rows=rows: qkv_g.at[:, x, rows] for rows in qkv_rows]
    qkv_plane = ReducePlane(links, place, qkv_chunks, qkv_x, qkv_z)
    qkv_outs = [SpreadCtx(links, place, qkv_all, [rows]) for rows in qkv_rows]
    for k in range(len(qkv_chunks)):
        qkv_plane.send_x(k)
    links.arrive(out_x, out_slot)
    root_slot, final_slot = links.slots(3), links.slots(1)
    holds = place.z == place.c
    out_mine = out_g.at[place.x]
    out_mine[...] = (out_mine[...].astype(F32) + out_x[...].astype(F32)).astype(BF16)
    rank = place.rank(place.z, place.c)
    to_root = links.copy(
        out_mine,
        out_z.at[lax.rem(rank, 3)],
        root_slot + lax.rem(rank, 3),
        (place.c * 2 + place.x, place.c),
    )

    @pl.when(jnp.logical_not(holds))
    def _():
        to_root.start()

    for k in range(2):
        dnorm.cross(k)
    plane.combine(4)
    end(2)
    outs[0].forward(0)
    outs[1].forward(0)
    end(3)
    for k, rows in enumerate(parts):
        value = middle[rows] + ffn.total(k)
        positions = lax.broadcasted_iota(jnp.int32, (value.shape[0], 1), 0)
        positions += tokens * place.c + k * value.shape[0]
        layer_out[rows] = jnp.where(positions < lengths[0], value, 0.0).astype(BF16)
    plane.middle(5)
    outs[2].forward(0)
    attn_gain = None
    for k, rows in enumerate(parts):
        grad, term = norm_back(dnorm.total(k), x_s[rows].astype(F32), gains[0:1])
        attn_gain = term if attn_gain is None else attn_gain + term
        input_grad[rows] = (d_middle[rows] + grad).astype(BF16)
    mine[...] = jnp.zeros_like(mine)
    for f in range(8):
        mine[f, 0:1] = attn_gain[:, 256 * f : 256 * (f + 1)]
        mine[f, 1:2] = ffn_gain[:, 256 * f : 256 * (f + 1)]
        mine[f, 2:3, 0:128] = gain_g[0:1]
        mine[f, 2:3, 128:256] = gain_g[1:2]
    plane_slot, ctx_slot = links.slots(8), links.slots(4)
    for f in fellows:
        links.send(mine.at[f], plane_stats.at[place.f], plane_slot + place.f, (f, place.c))
    plane_stats[place.f] = mine[place.f]

    end(4)
    outs[3].forward(0)
    for k in range(len(qkv_chunks)):
        qkv_plane.middle(k)
    plane.combine(5)
    end(5)
    for f in fellows:
        links.arrive(plane_stats.at[f], plane_slot + f)
    sums = plane_stats[0]
    for f in range(1, 8):
        sums += plane_stats[f]
    ctx_stats[place.c] = sums
    for device in (place.core_dev, place.y_dev, place.diag_dev):
        links.send(ctx_stats.at[place.c], ctx_stats.at[place.c], ctx_slot + place.c, device)

    final = [
        links.copy(out_all, out_all, final_slot, device)
        for device in (place.core_dev, place.y_dev)
    ]
    onward = links.copy(out_all, out_all, final_slot, place.core_dev)

    @pl.when(holds)
    def _():
        sums = out_mine[...].astype(F32)
        for other in range(3):
            links.arrive(out_z.at[other], root_slot + other)
            sums += out_z[other].astype(F32)
        out_all[...] = sums.astype(BF16)
        for made in final:
            made.start()

    for k in range(len(qkv_chunks)):
        total = qkv_plane.end(k)
        qkv_outs[k].begin(0, total)
        kept.append(links.local(total, qkv_all.at[place.c, qkv_rows[k]]))
    for k in range(4, count):
        outs[k].forward(0)
    relays = place.c_y == place.z

    @pl.when(jnp.logical_not(holds))
    def _():
        links.arrive(out_all, final_slot)

    @pl.when(relays)
    def _():
        onward.start()

    for c in (place.c_core, place.c_y, place.c_diag):
        links.arrive(ctx_stats.at[c], ctx_slot + c)
    stats[...] = ((ctx_stats[0] + ctx_stats[1]) + ctx_stats[2]) + ctx_stats[3]
    for out in qkv_outs:
        out.forward(0)
    for out in outs + qkv_outs:
        out.end()
    for made in kept:
        made.wait()
    links.finish()
    plane.finish()
    qkv_plane.finish()

    @pl.when(jnp.logical_not(holds))
    def _():
        to_root.wait_send()

    @pl.when(relays)
    def _():
        onward.wait_send()

    @pl.when(holds)
    def _():
        for made in final:
            made.wait_send()


def finish_kernel(
    gu_parts, dn_parts, out_s, qkv_parts, layer_s, input_s, stats,
    out, dn_out, out_out, qkv_out, layer_out, input_out, attn_out, ffn_out, pairs, sems,
):
    rows = gu_parts.shape[1]
    first = pl.multiple_of(pl.program_id(0) * rows, rows)
    sent = []
    for c in range(4):
        for f in range(8):
            b = 4 * f + c
            for side in range(2):
                column = 1024 * side + 128 * f
                block = gu_parts[c, :, column : column + 128]
                pairs[b, pl.ds(side, rows, stride=2), :] = block.astype(F32)
            made = pltpu.make_async_copy(
                pairs.at[b].reshape(rows, 2, 128),
                out.at[pl.ds(first, rows), :, pl.ds(128 * b, 128)],
                sems.at[b],
            )
            made.start()
            sent.append(made)
    dn_out[...] = dn_parts[...].astype(F32)
    out_out[...] = out_s[...].astype(F32)
    layer_out[...] = layer_s[...]
    input_out[...] = input_s[...]

    @pl.when(pl.program_id(0) == 0)
    def _():
        attn_out[...] = stats[0:1]
        ffn_out[...] = stats[1:2]
        for c in range(4):
            qkv_out[:, 256 * c : 256 * (c + 1)] = qkv_parts[c, 0:256].astype(F32).T
        for y in range(2):
            for j in range(2):
                from_row = 256 + 64 * j
                both = [qkv_parts[2 * y + core, from_row : from_row + 64] for core in range(2)]
                column = 1024 + 256 * j + 128 * y
                qkv_out[:, column : column + 128] = jnp.concatenate(both, axis=0).astype(F32).T

    for made in sent:
        made.wait()


def shaped(shape, kind=BF16):
    return jax.ShapeDtypeStruct(shape, kind)


def call(kernel, ins, outs, scratch=(), sems=None, number=None, flops=0):
    scratch = list(scratch)
    extra = {}
    if sems is not None:
        scratch += [pltpu.SemaphoreType.DMA((n,)) for n in sems]
        extra = dict(collective_id=number, has_side_effects=True)
    return pl.pallas_call(
        kernel,
        out_shape=tuple(shape for shape, _ in outs),
        in_specs=[spec for _, spec in ins],
        out_specs=tuple(spec for _, spec in outs),
        scratch_shapes=scratch,
        compiler_params=pltpu.CompilerParams(vmem_limit_bytes=VMEM_BYTES, **extra),
    )(*[array for array, _ in ins])


def split_heads(
    inputs,
    cotangent,
    lengths,
    qkv_weight,
    out_weight,
    gate_up,
    down_weight,
    attn_gain,
    ffn_gain,
    qk_gain,
):
    tokens, width = inputs.shape[1:]
    seq = tokens * 4
    source = inputs[0]
    rows, parts, units = gate_up.shape
    down_rows = down_weight.shape[0] // 4
    gain_s = jnp.concatenate(
        [attn_gain[None], ffn_gain[None], jnp.zeros((6, rows), BF16)], axis=0
    ).astype(F32)

    half_dim = HEAD_DIM // 2
    frequency = 10000.0 ** (-2.0 * np.arange(half_dim) / HEAD_DIM)
    turns = [np.arange(0, seq, 64)[:, None] * frequency, np.arange(64)[:, None] * frequency]
    signs = np.repeat([-1.0, 1.0, -1.0, 1.0], half_dim)
    angles = jnp.asarray(
        np.concatenate(
            [part for t in turns for part in (np.tile(np.cos(t), 4), np.tile(np.sin(t), 4) * signs)]
        ),
        F32,
    )
    table = pltpu.VMEM((seq, 128), F32)
    (
        qkv_w, out_w, gains, normed, qkv_raw, qkv_low, att_low, log_sums,
        gu_w, dn_w, dout_all, middle, mid_all, head_gain, key_bias,
    ) = call(
        forward_kernel,
        [(lengths, pl.BlockSpec(memory_space=pltpu.SMEM))]
        + [
            (a, HBM)
            for a in (qkv_weight, out_weight, gain_s, source, gate_up, down_weight, cotangent[0])
        ]
        + [(angles, VMEM), (qk_gain, VMEM)],
        [
            (shaped((8, rows, 384)), HBM),
            (shaped((2, out_weight.shape[0], width)), HBM),
            (shaped((8, width), F32), VMEM),
            (shaped((seq, width)), HBM),
            (shaped((3, seq, 128), F32), HBM),
            (shaped((3, seq, 128)), HBM),
            (shaped((2, seq, 128)), HBM),
            (shaped((2, seq, 128), F32), HBM),
            (shaped((8, rows, width)), HBM),
            (shaped((8, down_rows, width)), HBM),
            (shaped((4, tokens, width)), HBM),
            (shaped((tokens, width), F32), VMEM),
            (shaped((4, tokens, width)), HBM),
            (shaped((8, 128), F32), VMEM),
            (shaped((8, seq), F32), VMEM),
        ],
        [
            pltpu.VMEM((2, rows, 128), BF16),
            pltpu.VMEM((rows, 128), BF16),
            pltpu.VMEM((tokens, width), BF16),
            table,
            table,
            pltpu.VMEM((8, 8, rows), F32),
            pltpu.VMEM((8, rows, 384), BF16),
            pltpu.VMEM((2, out_weight.shape[0], width), BF16),
            pltpu.VMEM((4, tokens, width), BF16),
            pltpu.VMEM((seq, width), BF16),
            pltpu.VMEM((3, seq, 128), F32),
            pltpu.VMEM((3, seq, 128), BF16),
            pltpu.VMEM((2, seq, 128), BF16),
            pltpu.VMEM((2, seq, 128), F32),
            pltpu.VMEM((4, tokens, width), BF16),
            pltpu.VMEM((seq, 128), BF16),
            pltpu.VMEM((seq, 128), BF16),
            pltpu.VMEM((2, tokens, width), BF16),
            pltpu.VMEM((tokens, width), BF16),
            pltpu.VMEM((tokens, width), BF16),
            pltpu.VMEM((tokens, width), BF16),
            pltpu.VMEM((8, rows, 2, 128), BF16),
            pltpu.VMEM((2 * rows, 128), F32),
            pltpu.VMEM((rows, width), BF16),
        ],
        sems=(170, 170, 32),
        number=0,
    )
    qkv_w = qkv_w.reshape(width, 384)
    block = pltpu.VMEM((tokens, width), BF16)
    pair = pltpu.VMEM((2, tokens, width), BF16)
    whole = pltpu.VMEM((4, tokens, width), BF16)
    hidden_units = units // 4
    gu_g, dn_pair, ffn_part, d_middle, branch_s, ffn_gain_part = call(
        feed_kernel,
        [(a, HBM) for a in (gu_w, dn_w, dout_all, mid_all, middle)] + [(gains, VMEM)],
        [
            (shaped((4, 2, rows, width)), HBM),
            (shaped((4, down_rows, width)), HBM),
            (shaped((4, tokens, width)), HBM),
            (shaped((tokens, width), F32), HBM),
            (shaped((tokens, width)), HBM),
            (shaped((1, width), F32), VMEM),
        ],
        [
            pltpu.VMEM((8, rows, width), BF16),
            pltpu.VMEM((8, down_rows, width), BF16),
            whole,
            whole,
            pltpu.VMEM((seq, hidden_units), BF16),
            pltpu.VMEM((seq, parts * hidden_units), BF16),
            pltpu.VMEM((4, 2, down_rows, width), BF16),
            pltpu.VMEM((4, down_rows, width), BF16),
            pltpu.VMEM((2, rows, width), BF16),
            whole,
            pair,
            block,
            block,
            pltpu.VMEM((tokens, width), F32),
            pltpu.VMEM((tokens, width), F32),
            block,
        ],
        sems=(16, 16, 24),
        number=2,
    )
    step = 64
    count = (rows + down_rows) // step
    heads = pltpu.VMEM((seq, 128), BF16)
    gu_all, dn_all, layer_out, qkv_all, out_all, input_grad, stats = call(
        backward_kernel,
        [
            (gu_g, HBM),
            (dn_pair, HBM),
            (ffn_part, HBM),
            (middle, HBM),
            (d_middle, HBM),
            (branch_s, HBM),
            (source, HBM),
            (lengths, pl.BlockSpec(memory_space=pltpu.SMEM)),
            (gains, VMEM),
            (ffn_gain_part, VMEM),
            (angles, VMEM),
            (head_gain, VMEM),
            (key_bias, VMEM),
            (normed.reshape(4, tokens, width), HBM),
        ]
        + [(a, HBM) for a in (qkv_raw, qkv_low, att_low, log_sums, qkv_w, out_w)],
        [
            (shaped((4, rows, width)), HBM),
            (shaped((4, down_rows, width)), HBM),
            (shaped((tokens, width)), VMEM),
            (shaped((4, 384, rows)), HBM),
            (shaped((128, width)), VMEM),
            (shaped((tokens, width)), VMEM),
            (shaped((8, rows), F32), VMEM),
        ],
        [
            pltpu.VMEM((4, 4, step, width), BF16),
            pltpu.VMEM((rows // step, 4, step, width), BF16),
            pltpu.VMEM((count, 2, step, width), BF16),
            pltpu.VMEM((count, 2, step, width), BF16),
            block, pair, block, block, pair, block, block,
            pltpu.VMEM((tokens, width), F32),
            block,
            pltpu.VMEM((tokens, width), F32),
            pltpu.VMEM((4, tokens, width), BF16),
            pltpu.VMEM((4, tokens, width), BF16),
            table,
            table,
            pltpu.VMEM((3, seq, 128), F32),
            pltpu.VMEM((3, seq, 128), BF16),
            pltpu.VMEM((2, seq, 128), BF16),
            pltpu.VMEM((2, seq, 128), F32),
            pltpu.VMEM((width, 384), BF16),
            pltpu.VMEM((2, 128, width), BF16),
            heads,
            heads,
            pltpu.VMEM((2, seq, 128), BF16),
            pltpu.VMEM((3, seq, 128), BF16),
            table,
            table,
            pltpu.VMEM((8, 128), F32),
            pltpu.VMEM((4, 2, 384, rows), BF16),
            pltpu.VMEM((2, 4, 192, rows), BF16),
            pltpu.VMEM((2, 3, 192, rows), BF16),
            pltpu.VMEM((2, 128, width), BF16),
            pltpu.VMEM((128, width), BF16),
            pltpu.VMEM((3, 128, width), BF16),
            pltpu.VMEM((8, 8, rows), F32),
            pltpu.VMEM((8, 8, rows), F32),
            pltpu.VMEM((4, 8, rows), F32),
        ],
        sems=(120, 120, 50),
        number=1,
    )
    some = 64
    steps = rows // some
    few = down_rows // steps
    out_rows = out_weight.shape[0]
    block_of = lambda n: pl.BlockSpec((n, width), lambda i: (i, 0))
    fixed = lambda *shape: pl.BlockSpec(shape, lambda i: (0,) * len(shape))
    gate_up_grad, down_grad, out_grad, qkv_grad, layer_out, input_grad, attn_g, ffn_g = pl.pallas_call(
        finish_kernel,
        grid=(steps,),
        in_specs=[
            pl.BlockSpec((4, some, width), lambda i: (0, i, 0)),
            pl.BlockSpec((4, few, width), lambda i: (0, i, 0)),
            block_of(out_rows // steps),
            fixed(4, 384, rows),
            block_of(tokens // steps),
            block_of(tokens // steps),
            fixed(8, rows),
        ],
        out_specs=[
            HBM,
            pl.BlockSpec((4, few, width), lambda i: (0, i, 0)),
            block_of(out_rows // steps),
            fixed(rows, qkv_weight.shape[1]),
            block_of(tokens // steps),
            block_of(tokens // steps),
            fixed(1, rows),
            fixed(1, rows),
        ],
        out_shape=[
            shaped((rows, parts, units), F32),
            shaped((4, down_rows, width), F32),
            shaped((out_rows, width), F32),
            shaped((rows, qkv_weight.shape[1]), F32),
            shaped((tokens, width)),
            shaped((tokens, width)),
            shaped((1, rows), F32),
            shaped((1, rows), F32),
        ],
        scratch_shapes=[
            pltpu.VMEM((32, 2 * some, 128), F32),
            pltpu.SemaphoreType.DMA((32,)),
        ],
        compiler_params=pltpu.CompilerParams(vmem_limit_bytes=VMEM_BYTES),
    )(gu_all, dn_all, out_all, qkv_all, layer_out, input_grad, stats)
    return (
        layer_out[None],
        input_grad[None],
        qkv_grad,
        out_grad,
        gate_up_grad,
        down_grad.reshape(4 * down_rows, width),
        attn_g[0],
        ffn_g[0],
        jnp.stack([stats[2, :64] + stats[2, 64:128], stats[2, 128:192]]),
    )


def solution(mesh):
    sizes = (mesh.shape["fsdp"], mesh.shape["ctx"])
    return jax.shard_map(
        split_heads if sizes == (8, 4) else on_device,
        mesh=mesh,
        in_specs=(
            P("fsdp", "ctx", None),
            P("fsdp", "ctx", None),
            P("fsdp"),
            P("fsdp", None),
            P("fsdp", None),
            P("fsdp", None, None),
            P("fsdp", None),
            P("fsdp"),
            P("fsdp"),
            P(),
        ),
        out_specs=(
            P("fsdp", "ctx", None),
            P("fsdp", "ctx", None),
            P("fsdp", None),
            P("fsdp", None),
            P("fsdp", None, None),
            P("fsdp", None),
            P("fsdp"),
            P("fsdp"),
            P(),
        ),
        check_vma=False,
    )
```

```python
import functools
import math

import jax
import jax.numpy as jnp
import numpy as np
from jax import lax
from jax.experimental import pallas as pl
from jax.experimental.pallas import tpu as pltpu
from jax.sharding import PartitionSpec as P

HEADS = 16
KV_HEADS = 4
HEAD_DIM = 64


EPSILON = 1e-06


def root_norm(values, norm_gain):
    factor = lax.rsqrt(jnp.mean(values * values, axis=-1, keepdims=True) + EPSILON)
    return values * factor * norm_gain


def rotation_tables(positions):
    half_dim = HEAD_DIM // 2
    frequency = 10000.0 ** (-(2.0 * jnp.arange(half_dim, dtype=jnp.float32)) / HEAD_DIM)
    angles = positions.astype(jnp.float32)[:, None] * frequency[None, :]
    return (jnp.cos(angles), jnp.sin(angles))


def rotate(values, cos_table, sin_table):
    half_dim = values.shape[-1] // 2
    lower_half = values[..., :half_dim]
    upper_half = values[..., half_dim:]
    cos_part = cos_table[:, None, :]
    sin_part = sin_table[:, None, :]
    return jnp.concatenate(
        [
            lower_half * cos_part - upper_half * sin_part,
            upper_half * cos_part + lower_half * sin_part,
        ],
        axis=-1,
    )


def prepare_heads(qkv_out, head_gain, cos_table, sin_table):
    row_count = qkv_out.shape[0]
    query_cols = HEADS * HEAD_DIM
    key_cols = KV_HEADS * HEAD_DIM
    queries = qkv_out[:, :query_cols].reshape(row_count, HEADS, HEAD_DIM)
    key_part = qkv_out[:, query_cols : query_cols + key_cols].reshape(row_count, KV_HEADS, HEAD_DIM)
    value_part = qkv_out[:, query_cols + key_cols :]
    queries = rotate(root_norm(queries, head_gain[0]), cos_table, sin_table).reshape(
        row_count, query_cols
    )
    key_part = rotate(root_norm(key_part, head_gain[1]), cos_table, sin_table).reshape(
        row_count, key_cols
    )
    return (queries, key_part, value_part)


def activate(projected):
    gate_part = projected[:, 0]
    return gate_part * jax.nn.sigmoid(gate_part) * projected[:, 1]


def contract_rows(left, right):
    return lax.dot_general(
        left, right, (((0,), (0,)), ((), ())), preferred_element_type=jnp.float32
    )


def contract_cols(left, right):
    return lax.dot_general(
        left, right, (((1,), (1,)), ((), ())), preferred_element_type=jnp.float32
    )


def on_device(
    inputs,
    cotangent,
    lengths,
    qkv_weight,
    out_weight,
    gate_up,
    down_weight,
    attn_gain,
    ffn_gain,
    qk_gain,
):
    token_count = inputs.shape[1]
    group = HEADS // KV_HEADS
    key_cols = KV_HEADS * HEAD_DIM
    seq_len = token_count * lax.axis_size("ctx")
    positions = lax.axis_index("ctx") * token_count + jnp.arange(token_count, dtype=jnp.int32)
    length = lengths[0]
    row_keep = (positions < length).astype(jnp.float32)[:, None]
    inv_root = 1.0 / math.sqrt(HEAD_DIM)
    source = inputs[0].astype(jnp.float32)
    qkv_full, out_full, attn_full, ffn_full = (
        lax.all_gather(qkv_weight, "fsdp", axis=0, tiled=True),
        lax.all_gather(out_weight, "fsdp", axis=0, tiled=True),
        lax.all_gather(attn_gain, "fsdp", axis=0, tiled=True),
        lax.all_gather(ffn_gain, "fsdp", axis=0, tiled=True),
    )
    attn_norm = attn_full.astype(jnp.float32)
    ffn_norm = ffn_full.astype(jnp.float32)
    normed = root_norm(source, attn_norm).astype(jnp.bfloat16)
    qkv_out = jnp.dot(normed, qkv_full, preferred_element_type=jnp.float32)
    cos_table, sin_table = rotation_tables(positions)
    head_gain = qk_gain.astype(jnp.float32)

    def head_pieces(qkv_values, gain_values):
        return prepare_heads(qkv_values, gain_values, cos_table, sin_table)

    head_values, head_pull = jax.vjp(head_pieces, qkv_out, head_gain)
    queries, key_part, value_part = head_values
    query_low = queries.astype(jnp.bfloat16).reshape(token_count, KV_HEADS, group, HEAD_DIM)
    kv_local = jnp.concatenate([key_part, value_part], axis=1).astype(jnp.bfloat16)
    kv_whole = lax.all_gather(kv_local, "ctx", axis=0, tiled=True)
    block = 512
    block_total = seq_len // block
    kv_blocks = kv_whole.reshape(block_total, block, 2, KV_HEADS, HEAD_DIM)
    starts = jnp.arange(block_total, dtype=jnp.int32) * block

    def block_scores(key_block, block_start):
        scores = (
            jnp.einsum("bhgd,thd->hgbt", query_low, key_block, preferred_element_type=jnp.float32)
            * inv_root
        )
        key_pos = block_start + jnp.arange(key_block.shape[0], dtype=jnp.int32)
        visible = (key_pos[None, :] <= positions[:, None]) & (key_pos[None, :] < length)
        return (scores, visible)

    def max_step(state, item):
        running_max, running_sum = state
        kv_block, block_start = item
        scores, visible = block_scores(kv_block[:, 0], block_start)
        new_max = jnp.maximum(running_max, jnp.max(jnp.where(visible, scores, -1e30), axis=-1))
        expanded = jnp.where(visible, jnp.exp(scores - new_max[..., None]), 0.0)
        running_sum = running_sum * jnp.exp(running_max - new_max) + jnp.sum(expanded, axis=-1)
        return ((new_max, running_sum), None)

    stat_shape = (KV_HEADS, group, token_count)
    start_state = (jnp.full(stat_shape, -1e30, jnp.float32), jnp.zeros(stat_shape, jnp.float32))
    final_state, unused_out = lax.scan(max_step, start_state, (kv_blocks, starts))
    log_total = final_state[0] + jnp.log(final_state[1])

    def block_probs(kv_block, block_start):
        scores, visible = block_scores(kv_block[:, 0], block_start)
        return jnp.where(visible, jnp.exp(scores - log_total[..., None]), 0.0)

    def value_step(totals, item):
        kv_block, block_start = item
        probs_low = block_probs(kv_block, block_start).astype(jnp.bfloat16)
        return (
            totals
            + jnp.einsum(
                "hgbt,thd->bhgd", probs_low, kv_block[:, 1], preferred_element_type=jnp.float32
            ),
            None,
        )

    attended, unused_out = lax.scan(
        value_step,
        jnp.zeros((token_count, KV_HEADS, group, HEAD_DIM), jnp.float32),
        (kv_blocks, starts),
    )
    attended_low = attended.reshape(token_count, HEADS * HEAD_DIM).astype(jnp.bfloat16)
    middle = source + jnp.dot(attended_low, out_full, preferred_element_type=jnp.float32)
    normed_mid = root_norm(middle, ffn_norm).astype(jnp.bfloat16)
    columns = normed_mid
    projected = jnp.einsum(
        "td,dgf->tgf",
        columns,
        lax.all_gather(gate_up, "fsdp", axis=0, tiled=True),
        preferred_element_type=jnp.float32,
    )
    act_value, act_pull = jax.vjp(activate, projected)
    hidden = act_value.astype(jnp.bfloat16)
    columns = hidden
    ffn_out = jnp.dot(
        columns,
        lax.all_gather(down_weight, "fsdp", axis=0, tiled=True),
        preferred_element_type=jnp.float32,
    )
    layer_out = (row_keep * (middle + ffn_out)).astype(jnp.bfloat16)[None]
    d_out = row_keep * cotangent[0].astype(jnp.float32)
    d_out_low = d_out.astype(jnp.bfloat16)
    down_shard = lax.psum_scatter(
        contract_rows(hidden, d_out_low).astype(jnp.bfloat16),
        "fsdp",
        scatter_dimension=0,
        tiled=True,
    )
    d_hidden = contract_cols(d_out_low, lax.all_gather(down_weight, "fsdp", axis=0, tiled=True))
    d_proj_low = act_pull(d_hidden)[0].astype(jnp.bfloat16)
    columns = normed_mid
    gate_up_shard = lax.psum_scatter(
        jnp.einsum("td,tgf->dgf", columns, d_proj_low, preferred_element_type=jnp.float32).astype(
            jnp.bfloat16
        ),
        "fsdp",
        scatter_dimension=0,
        tiled=True,
    )
    d_normed_mid = jnp.einsum(
        "tgf,dgf->td",
        d_proj_low,
        lax.all_gather(gate_up, "fsdp", axis=0, tiled=True),
        preferred_element_type=jnp.float32,
    )
    mid_value, mid_pull = jax.vjp(root_norm, middle, ffn_norm)
    d_mid_norm, ffn_gain_part = mid_pull(d_normed_mid)
    d_middle = d_out + d_mid_norm
    d_branch = d_middle.astype(jnp.bfloat16)
    out_term = contract_rows(attended_low, d_branch)
    d_attended = (
        contract_cols(d_branch, out_full)
        .astype(jnp.bfloat16)
        .reshape(token_count, KV_HEADS, group, HEAD_DIM)
    )
    delta = jnp.transpose(jnp.sum(d_attended.astype(jnp.float32) * attended, axis=-1), (1, 2, 0))

    def block_grads(kv_block, block_start):
        probs = block_probs(kv_block, block_start)
        d_probs = jnp.einsum(
            "bhgd,thd->hgbt", d_attended, kv_block[:, 1], preferred_element_type=jnp.float32
        )
        d_scores = (probs * (d_probs - delta[..., None])).astype(jnp.bfloat16)
        return (probs.astype(jnp.bfloat16), d_scores)

    def query_step(totals, item):
        kv_block, block_start = item
        probs_low, d_scores = block_grads(kv_block, block_start)
        return (
            totals
            + jnp.einsum(
                "hgbt,thd->bhgd", d_scores, kv_block[:, 0], preferred_element_type=jnp.float32
            ),
            None,
        )

    d_query_sum, unused_out = lax.scan(
        query_step,
        jnp.zeros((token_count, KV_HEADS, group, HEAD_DIM), jnp.float32),
        (kv_blocks, starts),
    )
    d_query = (d_query_sum * inv_root).reshape(token_count, HEADS * HEAD_DIM).astype(jnp.bfloat16)
    sub_block = 512
    sub_total = token_count * lax.axis_size("ctx") // sub_block
    pieces = kv_whole.reshape(sub_total, sub_block, 2, KV_HEADS, HEAD_DIM)
    sub_starts = jnp.arange(sub_total, dtype=jnp.int32) * sub_block

    def key_grads(item):
        kv_block, block_start = item
        probs_low, d_scores = block_grads(kv_block, block_start)
        d_keys = (
            jnp.einsum("hgbt,bhgd->thd", d_scores, query_low, preferred_element_type=jnp.float32)
            * inv_root
        )
        d_values = jnp.einsum(
            "hgbt,bhgd->thd", probs_low, d_attended, preferred_element_type=jnp.float32
        )
        return jnp.concatenate(
            [d_keys.reshape(sub_block, key_cols), d_values.reshape(sub_block, key_cols)], axis=1
        )

    kv_grad = lax.psum_scatter(
        lax.map(key_grads, (pieces, sub_starts))
        .reshape(token_count * lax.axis_size("ctx"), 2 * key_cols)
        .astype(jnp.bfloat16),
        "ctx",
        scatter_dimension=0,
        tiled=True,
    ).astype(jnp.float32)
    d_key_low = kv_grad[:, :key_cols].astype(jnp.bfloat16).astype(jnp.float32)
    d_value_low = kv_grad[:, key_cols:].astype(jnp.bfloat16).astype(jnp.float32)
    d_qkv_out, qk_part = head_pull((d_query.astype(jnp.float32), d_key_low, d_value_low))
    d_qkv = d_qkv_out.astype(jnp.bfloat16)
    qkv_term = contract_rows(normed, d_qkv)
    d_normed = contract_cols(d_qkv, qkv_full)
    first_value, first_pull = jax.vjp(root_norm, source, attn_norm)
    d_source_norm, attn_gain_part = first_pull(d_normed)
    input_grad = (d_middle + d_source_norm).astype(jnp.bfloat16)[None]
    qkv_shard, out_shard, attn_shard, ffn_shard = (
        lax.psum_scatter(
            qkv_term.astype(jnp.bfloat16), "fsdp", scatter_dimension=0, tiled=True
        ).astype(jnp.float32),
        lax.psum_scatter(
            out_term.astype(jnp.bfloat16), "fsdp", scatter_dimension=0, tiled=True
        ).astype(jnp.float32),
        lax.psum_scatter(
            attn_gain_part.astype(jnp.bfloat16), "fsdp", scatter_dimension=0, tiled=True
        ).astype(jnp.float32),
        lax.psum_scatter(
            ffn_gain_part.astype(jnp.bfloat16), "fsdp", scatter_dimension=0, tiled=True
        ).astype(jnp.float32),
    )
    summed = (
        lax.psum(qkv_shard.astype(jnp.bfloat16), "ctx").astype(jnp.float32),
        lax.psum(out_shard.astype(jnp.bfloat16), "ctx").astype(jnp.float32),
        lax.psum(gate_up_shard, "ctx").astype(jnp.float32),
        lax.psum(down_shard, "ctx").astype(jnp.float32),
        lax.psum(attn_shard.astype(jnp.bfloat16), "ctx").astype(jnp.float32),
        lax.psum(ffn_shard.astype(jnp.bfloat16), "ctx").astype(jnp.float32),
    )
    qk_total = lax.psum(qk_part, ("fsdp", "ctx"))
    return (
        layer_out,
        input_grad,
        summed[0],
        summed[1],
        summed[2],
        summed[3],
        summed[4],
        summed[5],
        qk_total,
    )


MESH = pl.DeviceIdType.MESH
F32 = jnp.float32
BF16 = jnp.bfloat16
VMEM_BYTES = 60 << 20
HBM = pl.BlockSpec(memory_space=pl.ANY)
VMEM = pl.BlockSpec(memory_space=pltpu.VMEM)


class Place:
    def __init__(self):
        self.f = lax.axis_index("fsdp")
        self.c = lax.axis_index("ctx")
        self.z, self.x = lax.div(self.f, 2), lax.rem(self.f, 2)
        self.y, self.core = lax.div(self.c, 2), lax.rem(self.c, 2)
        self.xo, self.yo, self.co = 1 - self.x, 1 - self.y, 1 - self.core
        upper = lax.div(self.z, 2)
        self.others = (self.z + 1 - 2 * lax.rem(self.z, 2), 2 - upper, 3 - 3 * upper)
        self.inner = lax.rem(self.z, 2) + upper == 1
        self.far = 2 - 2 * upper
        self.x_dev = (self.z * 2 + self.xo, self.c)
        self.c_core = self.y * 2 + self.co
        self.c_y = self.yo * 2 + self.core
        self.c_diag = self.yo * 2 + self.co
        self.core_dev = (self.f, self.c_core)
        self.y_dev = (self.f, self.c_y)
        self.diag_dev = (self.f, self.c_diag)

    def rank(self, source, target):
        return jnp.where(source > target, source - 1, source)

    def z_dev(self, z):
        return (z * 2 + self.x, self.c)

    def meet(self, partners):
        barrier = pltpu.get_barrier_semaphore()
        for partner in partners:
            pl.semaphore_signal(barrier, inc=1, device_id=partner, device_id_type=MESH)
        pl.semaphore_wait(barrier, len(partners))

    def neighbours(self):
        return [self.z_dev(o) for o in self.others] + [self.x_dev, self.core_dev, self.y_dev]


class Links:
    def __init__(self, place, send_sems, recv_sems, local_sems):
        self.place = place
        self.send_sems, self.recv_sems, self.local_sems = send_sems, recv_sems, local_sems
        self.sends = self.recvs = self.locals = 0
        self.open = []

    def slots(self, count):
        first = self.recvs
        self.recvs += count
        return first

    def copy(self, src, dst, slot, device):
        made = pltpu.make_async_remote_copy(
            src_ref=src,
            dst_ref=dst,
            send_sem=self.send_sems.at[self.sends],
            recv_sem=self.recv_sems.at[slot],
            device_id=device,
            device_id_type=MESH,
        )
        self.sends += 1
        return made

    def send(self, src, dst, slot, device):
        made = self.copy(src, dst, slot, device)
        made.start()
        self.open.append(made)
        return made

    def settle(self, sends):
        for made in sends:
            made.wait_send()
            self.open = [one for one in self.open if one is not made]

    def arrive(self, ref, slot):
        pltpu.make_async_remote_copy(
            src_ref=ref,
            dst_ref=ref,
            send_sem=self.send_sems.at[0],
            recv_sem=self.recv_sems.at[slot],
            device_id=self.place.x_dev,
            device_id_type=MESH,
        ).wait_recv()

    def local(self, src, dst):
        made = pltpu.make_async_copy(src, dst, self.local_sems.at[self.locals])
        self.locals += 1
        made.start()
        return made

    def finish(self):
        for made in self.open:
            made.wait_send()
        self.open = []


class SpreadPlane:
    def __init__(self, links, place, chunks):
        self.links, self.place, self.chunks = links, place, chunks
        self.z_slot, self.x_slot = links.slots(4 * len(chunks)), links.slots(4 * len(chunks))

    def begin_z(self):
        place = self.place
        for k, (src, dst) in enumerate(self.chunks):
            slot = self.z_slot + 4 * k + place.z
            for other in place.others:
                self.links.send(src, dst(place.f), slot, place.z_dev(other))

    def begin_x(self, k):
        src, dst = self.chunks[k]
        slot = self.x_slot + 4 * k + self.place.z
        self.links.send(src, dst(self.place.f), slot, self.place.x_dev)

    def forward(self, k):
        place, dst = self.place, self.chunks[k][1]
        for other in place.others:
            block = dst(other * 2 + place.x)
            self.links.arrive(block, self.z_slot + 4 * k + other)
            self.links.send(block, block, self.x_slot + 4 * k + other, place.x_dev)

    def end(self):
        for k in range(len(self.chunks)):
            for z in range(4):
                block = self.chunks[k][1](z * 2 + self.place.xo)
                self.links.arrive(block, self.x_slot + 4 * k + z)


class SpreadTree(SpreadPlane):
    def __init__(self, links, place, chunks, crossed):
        super().__init__(links, place, chunks)
        self.plain = len(chunks) - crossed
        self.passed = []

    def begin_z(self, ahead=4):
        place = self.place
        self.near = {}
        for k, (src, dst) in enumerate(self.chunks):
            slot = self.z_slot + 4 * k + place.z
            near = self.links.copy(src, dst(place.f), slot, place.z_dev(place.others[0]))
            self.links.open.append(near)
            if k < ahead:
                near.start()
            else:
                pl.when(jnp.logical_not(place.inner))(near.start)
                self.near[k - ahead] = near
            self.links.send(src, dst(place.f), slot, place.z_dev(place.others[1]))

    def cross_z(self, k):
        place = self.place
        block = self.chunks[k][1](place.z * 2 + place.xo)
        slot = self.x_slot + 4 * k + place.z
        self.links.arrive(block, slot)
        for other in place.others[:2]:
            self.links.send(block, block, slot, place.z_dev(other))

    def blocks(self, k, other):
        place, dst = self.place, self.chunks[k][1]
        found = [(dst(other * 2 + place.x), self.z_slot + 4 * k + other)]
        if k >= self.plain:
            found.append((dst(other * 2 + place.xo), self.x_slot + 4 * k + other))
        return found

    def onward(self, k):
        place = self.place
        blocks = [pair for other in place.others[1:] for pair in self.blocks(k, other)]
        made = [
            self.links.copy(block, block, slot, place.z_dev(place.others[0]))
            for block, slot in blocks
        ]
        self.passed += made

        @pl.when(place.inner)
        def _():
            for (block, slot), one in zip(blocks, made):
                self.links.arrive(block, slot)
                one.start()
            if k in self.near:
                self.near[k].start()

    def forward(self, k):
        place = self.place
        near, *far = [self.blocks(k, other) for other in place.others]
        far = far[0] + far[1]
        for pair in near:
            self.links.arrive(*pair)
        if k < self.plain:
            slot = self.x_slot + 4 * k + place.others[0]
            self.links.send(near[0][0], near[0][0], slot, place.x_dev)

        @pl.when(jnp.logical_not(place.inner))
        def _():
            for pair in far:
                self.links.arrive(*pair)

        if k < self.plain:
            for other, (block, _) in zip(place.others[1:], far):
                self.links.send(block, block, self.x_slot + 4 * k + other, place.x_dev)

    def end(self):
        for k in range(self.plain):
            for z in range(4):
                block = self.chunks[k][1](z * 2 + self.place.xo)
                self.links.arrive(block, self.x_slot + 4 * k + z)

    def finish(self):
        @pl.when(self.place.inner)
        def _():
            for made in self.passed:
                made.wait_send()


class ReducePlane:
    def __init__(self, links, place, chunks, from_x, from_z, own=None):
        self.links, self.place, self.chunks = links, place, chunks
        self.from_x, self.from_z, self.own = from_x, from_z, own
        self.summed = 0
        self.x_slot, self.z_slot = links.slots(len(chunks)), links.slots(3 * len(chunks))
        self.loads, self.z_sends = {}, {}

    def send_x(self, k):
        place = self.place
        from_x = self.from_x.at[k - self.summed]
        self.links.send(self.chunks[k](place.xo), from_x, self.x_slot + k, place.x_dev)

    def load(self, k):
        slots = self.own.shape[0]
        for made in self.z_sends.pop(k - slots, []):
            made.wait_send()
        self.loads[k] = self.links.local(self.chunks[k](self.place.x), self.own.at[k % slots])

    def mine(self, k):
        if self.own is None:
            return self.chunks[k](self.place.x)
        return self.own.at[k % self.own.shape[0]]

    def middle(self, k):
        place = self.place
        self.links.arrive(self.from_x.at[k], self.x_slot + k)
        if k in self.loads:
            self.loads[k].wait()
        mine = self.mine(k)
        self.z_sends[k] = []
        for other in place.others:
            mine[other] = (mine[other].astype(F32) + self.from_x[k, other].astype(F32)).astype(BF16)
            rank = place.rank(place.z, other)
            made = self.links.copy(
                mine.at[other],
                self.from_z.at[k, rank],
                self.z_slot + 3 * k + rank,
                place.z_dev(other),
            )
            made.start()
            self.z_sends[k].append(made)

    def end(self, k):
        place = self.place
        mine = self.mine(k)
        sums = mine[place.z].astype(F32) + self.from_x[k, place.z].astype(F32)
        for rank in range(3):
            self.links.arrive(self.from_z.at[k, rank], self.z_slot + 3 * k + rank)
            sums += self.from_z[k, rank].astype(F32)
        total = self.from_x.at[k, place.z]
        total[...] = sums.astype(BF16)
        return total

    def finish(self):
        for sends in self.z_sends.values():
            for made in sends:
                made.wait_send()


class ReduceTree(ReducePlane):
    def __init__(self, links, place, chunks, from_x, from_z, via, own, summed):
        super().__init__(links, place, chunks, from_x, from_z, own)
        self.summed = summed
        self.via, self.via_slot = via, links.slots(len(chunks))
        self.outer = jnp.logical_not(place.inner)

    def load(self, k):
        slots = self.own.shape[0]
        self.settle(self.z_sends.pop(k - slots, []))
        self.loads[k] = self.links.local(self.chunks[k](self.place.x), self.own.at[k % slots])

    def settle(self, sends):
        for made, when in sends:
            if when is None:
                made.wait_send()
            else:
                pl.when(when)(made.wait_send)

    def middle(self, k):
        place = self.place
        self.loads[k].wait()
        mine = self.mine(k)
        if k >= self.summed:
            from_x = self.from_x.at[k - self.summed]
            self.links.arrive(from_x, self.x_slot + k)
            for other in place.others:
                pair = mine[other].astype(F32) + from_x[other].astype(F32)
                mine[other] = pair.astype(BF16)
        near = place.others[0]
        device = place.z_dev(near)
        direct = self.links.copy(mine.at[near], self.from_z.at[k, 0], self.z_slot + 3 * k, device)
        direct.start()
        far = self.links.copy(
            mine.at[pl.ds(place.far, 2)], self.via.at[k], self.via_slot + k, device
        )
        pl.when(self.outer)(far.start)
        self.z_sends[k] = [(direct, None), (far, self.outer)]

    def combine(self, k):
        place = self.place
        mine = self.mine(k)

        sent = [
            self.links.copy(
                mine.at[place.far + j],
                self.from_z.at[k, 1],
                self.z_slot + 3 * k + 1,
                place.z_dev(place.far + j),
            )
            for j in range(2)
        ]

        @pl.when(place.inner)
        def _():
            self.links.arrive(self.via.at[k], self.via_slot + k)
            for j in range(2):
                here = mine[place.far + j].astype(F32) + self.via[k, j].astype(F32)
                mine[place.far + j] = here.astype(BF16)
                sent[j].start()

        self.z_sends[k] += [(made, place.inner) for made in sent]

    def end(self, k):
        place = self.place
        sums = self.mine(k)[place.z].astype(F32)
        if k >= self.summed:
            sums += self.from_x[k - self.summed, place.z].astype(F32)
        for side in range(2):
            self.links.arrive(self.from_z.at[k, side], self.z_slot + 3 * k + side)
            sums += self.from_z[k, side].astype(F32)
        total = self.from_z.at[k, 0]
        total[...] = sums.astype(BF16)
        return total

    def finish(self):
        for sends in self.z_sends.values():
            self.settle(sends)


class SpreadCtx:
    def __init__(self, links, place, out, parts):
        self.links, self.place, self.out, self.parts = links, place, out, parts
        self.slot = links.slots(3 * len(parts))
        self.sends = []

    def begin(self, k, src):
        place, rows = self.place, self.parts[k]
        out = self.out.at[place.c, rows]
        self.sends.append(self.links.send(src, out, self.slot + 3 * k + 1, place.y_dev))
        self.sends.append(self.links.send(src, out, self.slot + 3 * k, place.core_dev))

    def forward(self, k):
        place = self.place
        block = self.out.at[place.c_y, self.parts[k]]
        self.links.arrive(block, self.slot + 3 * k + 1)
        self.sends.append(self.links.send(block, block, self.slot + 3 * k + 2, place.core_dev))

    def end(self):
        place = self.place
        for k, rows in enumerate(self.parts):
            self.links.arrive(self.out.at[place.c_core, rows], self.slot + 3 * k)
            self.links.arrive(self.out.at[place.c_diag, rows], self.slot + 3 * k + 2)


class ReduceCtx:
    def __init__(self, links, place, part, parts, own, from_core, to_y, from_y):
        self.links, self.place, self.part = links, place, part
        self.parts = [rows if isinstance(rows, tuple) else (rows,) for rows in parts]
        self.own, self.from_core, self.to_y, self.from_y = own, from_core, to_y, from_y
        self.slot = links.slots(3 * len(parts))
        self.loads, self.sends = {}, []

    def begin(self, only=None):
        place = self.place
        for side, y in ((0, place.yo), (1, place.y)):
            for k, rows in enumerate(self.parts):
                if only not in (None, k):
                    continue
                self.links.send(
                    self.part.at[y * 2 + place.co, *rows],
                    self.from_core.at[side, *rows],
                    self.slot + 3 * k + side,
                    place.core_dev,
                )
                if self.own is not None and side == 0:
                    self.load(0, k)

    def load(self, side, k):
        rows = self.parts[k]
        y = self.place.y if side else self.place.yo
        self.loads[side, k] = self.links.local(
            self.part.at[y * 2 + self.place.core, *rows], self.own.at[rows]
        )

    def pair(self, side, k):
        rows = self.parts[k]
        self.links.arrive(self.from_core.at[side, *rows], self.slot + 3 * k + side)
        if self.own is None:
            y = self.place.y if side else self.place.yo
            own = self.part[y * 2 + self.place.core, *rows]
        else:
            self.loads[side, k].wait()
            own = self.own[rows]
        return own.astype(F32) + self.from_core[side, *rows].astype(F32)

    def cross(self, k):
        rows = self.parts[k]
        self.to_y[rows] = self.pair(0, k).astype(BF16)
        if self.own is not None:
            self.load(1, k)
        made = self.links.send(
            self.to_y.at[rows], self.from_y.at[rows], self.slot + 3 * k + 2, self.place.y_dev
        )
        self.sends.append(made)

    def total(self, k):
        rows = self.parts[k]
        sums = self.pair(1, k)
        self.links.arrive(self.from_y.at[rows], self.slot + 3 * k + 2)
        return sums + self.from_y[rows].astype(F32)


def halves(rows):
    return [pl.ds(0, rows // 2), pl.ds(rows // 2, rows // 2)]


def row_factor(values):
    return lax.rsqrt(jnp.mean(values * values, axis=-1, keepdims=True) + EPSILON)


def low_half(shape):
    return lax.rem(lax.broadcasted_iota(jnp.int32, shape, len(shape) - 1), 128) < 64


def partner(values):
    lane = lax.broadcasted_iota(jnp.int32, values.shape, len(values.shape) - 1)
    first = lax.rem(lane, 64) < 32
    return jnp.where(first, pltpu.roll(values, 96, 1), pltpu.roll(values, 32, 1))


def half_sums(values):
    low = low_half(values.shape)
    first = jnp.sum(jnp.where(low, values, 0.0), axis=-1, keepdims=True)
    second = jnp.sum(jnp.where(low, 0.0, values), axis=-1, keepdims=True)
    return jnp.where(low, first, second)


def row_loop(count, body, first=0):
    def step(index, carry):
        body(index)
        return carry

    lax.fori_loop(first, first + count, step, 0)


BLOCK = 256
SHORT = 128


def attention_scores(query, keys, key_bias, first, span):
    scores = lax.dot_general(
        query, keys, (((1,), (1,)), ((), ())), preferred_element_type=F32
    ) * (1.0 / math.sqrt(HEAD_DIM))
    rows = first + lax.broadcasted_iota(jnp.int32, scores.shape, 0)
    columns = lax.broadcasted_iota(jnp.int32, scores.shape, 1)
    return jnp.where(columns <= rows, scores, -1e30) + key_bias[:, :span]


def turn_tables(angles, cos, sin):
    for i in range(16):
        rows = slice(64 * i, 64 * (i + 1))
        cos_high, sin_high = angles[i : i + 1], angles[16 + i : 17 + i]
        cos_low, sin_low = angles[32:96], angles[96:160]
        cos[rows] = cos_high * cos_low - sin_high * sin_low
        sin[rows] = sin_high * cos_low + cos_high * sin_low


def forward_kernel(
    lengths, qkv_weight, out_s, gain_s, x_s, gate_up, down_weight, cotangent, angles, qk_gain,
    qkv_wh, out_wh, gains, normed_h, qkv_raw_h, qkv_low_h, att_low_h, log_sums_h,
    gu_w, dn_w, dout_all, middle, mid_all, head_gain, key_bias,
    kv_pairs, kv_s, dout_s, cos, sin, gain_blocks, qkv_w, out_w, x_all, normed, qkv_raw, qkv_low, att_low, log_sums,
    part, keys, values, from_core, to_y, from_y, mid_low, gu_pairs, gu_rows, gu_s, send_sems, recv_sems, local_sems,
):
    place = Place()
    links = Links(place, send_sems, recv_sems, local_sems)
    fellows = [lax.rem(place.f + d, 8) for d in range(1, 8)]
    place.meet([(f, place.c) for f in fellows] + [place.core_dev, place.y_dev])

    q_columns = pl.ds(pl.multiple_of(256 * place.c, 256), 256)
    for j in range(2):
        pair = pl.ds(pl.multiple_of(1024 + 256 * j + 128 * place.y, 128), 128)
        links.local(qkv_weight.at[:, pair], kv_pairs.at[j]).wait()
    cot_load = links.local(cotangent, dout_s)
    low = low_half(kv_pairs.shape[1:])
    first, second = [], []
    for j in range(2):
        value = kv_pairs[j].astype(F32)
        swapped = pltpu.roll(value, 64, 1)
        first.append(jnp.where(place.core == 0, value, swapped))
        second.append(jnp.where(place.core == 0, swapped, value))
    kv_s[...] = jnp.where(low, first[0], second[1]).astype(BF16)
    qkv_plane = SpreadPlane(
        links,
        place,
        [
            (qkv_weight.at[:, q_columns], lambda f: qkv_w.at[f, :, 0:256]),
            (kv_s, lambda f: qkv_w.at[f, :, 256:384]),
        ],
    )
    qkv_plane.begin_z()
    qkv_plane.begin_x(0)
    qkv_plane.begin_x(1)
    picks = []
    for f in range(8):
        start = pl.multiple_of(512 * f + 128 * place.c, 128)
        picks.append(links.local(gate_up.at[:, :, pl.ds(start, 128)], gu_pairs.at[f]))
    tokens = x_s.shape[0]
    parts = halves(tokens)
    x_spread = SpreadCtx(links, place, x_all, parts)
    for k, rows in enumerate(parts):
        x_spread.begin(k, x_s.at[rows])
    gain_slot = links.slots(8)
    for f in fellows:
        links.send(gain_s, gain_blocks.at[place.f], gain_slot + place.f, (f, place.c))
    kept = [
        links.local(qkv_weight.at[:, q_columns], qkv_w.at[place.f, :, 0:256]),
        links.local(kv_s, qkv_w.at[place.f, :, 256:384]),
        links.local(gain_s, gain_blocks.at[place.f]),
        links.local(x_s, x_all.at[place.c]),
    ]

    root_slot, side_slot = links.slots(1), links.slots(1)
    holds = place.z == place.c
    down = [
        links.copy(out_s, out_w.at[place.x], root_slot, place.z_dev(other))
        for other in place.others[:2]
    ]
    relay = links.copy(out_w.at[place.x], out_w.at[place.x], root_slot, place.z_dev(place.others[0]))
    across = lax.div(place.c, 2) != lax.div(place.z, 2)
    relays = jnp.logical_and(place.inner, across)
    sideways = links.copy(out_s, out_w.at[place.x], side_slot, place.x_dev)
    onward = links.copy(out_w.at[place.x], out_w.at[place.x], side_slot, place.x_dev)
    own = pltpu.make_async_copy(out_s, out_w.at[place.x], local_sems.at[links.locals])
    links.locals += 1

    @pl.when(holds)
    def _():
        for made in down:
            made.start()
        sideways.start()
        own.start()

    rows = gu_s.shape[0]
    for f in range(8):
        picks[f].wait()
        gu_rows[...] = gu_pairs.at[f].reshape(2 * rows, 128)[...].astype(F32)
        for side in range(2):
            first = 1024 * side + 128 * f
            picked = gu_rows[pl.ds(side, rows, stride=2), :]
            gu_s[:, first : first + 128] = picked.astype(BF16)
    step = 32
    chunks = []
    dn_s = down_weight.at[pl.ds(pl.multiple_of(128 * place.c, 128), dn_w.shape[1])]
    for src, dst in ((dn_s, dn_w), (gu_s, gu_w)):
        for first in range(0, src.shape[0], step):
            rows = pl.ds(first, step)
            chunks.append((src.at[rows], lambda f, dst=dst, rows=rows: dst.at[f, rows]))
    plane = SpreadTree(links, place, chunks, 2)
    plane.begin_z()
    cot_load.wait()
    length = lengths[0]
    positions = tokens * place.c + lax.broadcasted_iota(jnp.int32, (tokens, 1), 0)
    dout_s[...] = jnp.where(positions < length, dout_s[...].astype(F32), 0.0).astype(BF16)
    for k in range(plane.plain, len(chunks)):
        plane.begin_x(k)
    for k in range(3):
        plane.begin_x(k)
    qkv_plane.forward(0)
    qkv_plane.forward(1)
    for k in range(3, plane.plain):
        plane.begin_x(k)
    for k in range(plane.plain, len(chunks)):
        plane.cross_z(k)
    last = [
        links.local(gu_s, gu_w.at[place.f]),
        links.local(dn_s, dn_w.at[place.f]),
        links.local(dout_s, dout_all.at[place.c]),
    ]
    turn_tables(angles, cos, sin)
    columns = lax.broadcasted_iota(jnp.int32, key_bias.shape, 1)
    key_bias[...] = jnp.where(columns < length, 0.0, -1e30)
    ones = jnp.ones((1, HEAD_DIM), F32)
    q_gain, k_gain = qk_gain[0:1].astype(F32), qk_gain[1:2].astype(F32)
    head_gain[...] = jnp.zeros_like(head_gain)
    for b in range(2):
        head_gain[b : b + 1] = jnp.concatenate([q_gain, q_gain], axis=1)
    head_gain[2:3] = jnp.concatenate([k_gain, ones], axis=1)
    for f in fellows:
        links.arrive(gain_blocks.at[f], gain_slot + f)
    for made in kept:
        made.wait()
    gains[...] = jnp.zeros_like(gains)
    for f in range(8):
        gains[0:2, 256 * f : 256 * (f + 1)] = gain_blocks[f, 0:2]
    dout = SpreadCtx(links, place, dout_all, parts)
    for k, rows in enumerate(parts):
        x_spread.forward(k)
        dout.begin(k, dout_s.at[rows])
    x_spread.end()
    qkv_plane.end()

    def project(index):
        rows = pl.ds(pl.multiple_of(index * BLOCK, BLOCK), BLOCK)
        source = x_all[index].astype(F32)
        normed[rows] = (source * row_factor(source) * gains[0:1]).astype(BF16)
        weight = qkv_w[...].reshape(normed.shape[1], qkv_w.shape[2])
        raw = jnp.dot(normed[rows], weight, preferred_element_type=F32)
        for b in range(3):
            block = raw[:, 128 * b : 128 * (b + 1)]
            qkv_raw[b, rows] = block
            factor = lax.rsqrt(half_sums(block * block) * (1.0 / HEAD_DIM) + EPSILON)
            scaled = block * factor * head_gain[b : b + 1]
            turned = scaled * cos[rows] + partner(scaled) * sin[rows]
            if b == 2:
                turned = jnp.where(low_half(turned.shape), turned, block)
            qkv_low[b, rows] = turned.astype(BF16)
            if b == 2:
                low = low_half(turned.shape)
                swapped = pltpu.roll(turned, 64, 1)
                keys[rows] = jnp.where(low, turned, swapped).astype(BF16)
                values[rows] = jnp.where(low, swapped, turned).astype(BF16)

    seq = normed.shape[0]
    att_low[...] = jnp.zeros_like(att_low)
    log_sums[...] = jnp.zeros_like(log_sums)
    row_loop(seq // BLOCK, project)
    last += [
        links.local(normed, normed_h),
        links.local(qkv_raw, qkv_raw_h),
        links.local(qkv_low, qkv_low_h),
        links.local(qkv_w, qkv_wh),
    ]

    def heads(index):
        b, half = lax.div(index, 2), lax.rem(index, 2)
        for i in range(seq // BLOCK):
            rows, span = pl.ds(i * BLOCK, BLOCK), (i + 1) * BLOCK
            query = qkv_low[b, rows]
            side = lax.div(lax.broadcasted_iota(jnp.int32, query.shape, 1), 64) == half
            chosen = jnp.where(side, query, 0)
            scores = attention_scores(chosen, keys[:span], key_bias[0:1], i * BLOCK, span)
            top = jnp.max(scores, axis=-1, keepdims=True)
            expanded = jnp.exp(scores - top)
            sums = jnp.sum(expanded, axis=-1, keepdims=True)
            probs = (expanded * (1.0 / sums)).astype(BF16)
            out = jnp.dot(probs, values[:span], preferred_element_type=F32)
            att_low[b, rows] = jnp.where(side, out.astype(BF16), att_low[b, rows])
            log_sums[b, rows] = jnp.where(side, top + jnp.log(sums), log_sums[b, rows])

    @pl.when(relays)
    def _():
        links.arrive(out_w.at[place.x], root_slot)
        relay.start()
        onward.start()

    plane.onward(0)
    row_loop(2, heads)
    plane.onward(1)
    plane.onward(2)
    plane.forward(0)
    row_loop(2, heads, 2)
    plane.onward(3)
    for k in range(1, 3):
        plane.forward(k)

    @pl.when(jnp.logical_not(jnp.logical_or(holds, relays)))
    def _():
        links.arrive(out_w.at[place.x], root_slot)
        onward.start()

    @pl.when(holds)
    def _():
        own.wait()

    for k in range(len(parts)):
        dout.forward(k)
    links.arrive(out_w.at[place.xo], side_slot)

    def project_out(index):
        rows = pl.ds(pl.multiple_of(index * BLOCK, BLOCK), BLOCK)
        sums = jnp.dot(att_low[0, rows], out_w[0], preferred_element_type=F32)
        sums += jnp.dot(att_low[1, rows], out_w[1], preferred_element_type=F32)
        part[index] = sums.astype(BF16)

    row_loop(seq // BLOCK, project_out)
    reduce = ReduceCtx(links, place, part, parts, None, from_core, to_y, from_y)
    reduce.begin()
    last += [
        links.local(att_low, att_low_h),
        links.local(log_sums, log_sums_h),
        links.local(out_w, out_wh),
    ]
    plane.onward(4)
    for k in range(2):
        reduce.cross(k)
    plane.forward(3)
    plane.onward(5)
    plane.onward(6)
    plane.forward(4)
    plane.onward(7)
    plane.forward(5)
    plane.onward(8)
    plane.forward(6)
    mid = SpreadCtx(links, place, mid_all, parts)
    for k, rows in enumerate(parts):
        value = x_all[place.c, rows].astype(F32) + reduce.total(k)
        middle[rows] = value
        mid_low[rows] = (value * row_factor(value) * gains[1:2]).astype(BF16)
        mid.begin(k, mid_low.at[rows])
        last.append(links.local(mid_low.at[rows], mid_all.at[place.c, rows]))
    plane.onward(9)
    plane.forward(7)
    plane.forward(8)
    for k in range(2):
        mid.forward(k)
    plane.forward(9)
    for k in range(plane.plain, len(chunks)):
        plane.onward(k)
    for k in range(plane.plain, len(chunks)):
        plane.forward(k)
    plane.end()
    mid.end()
    dout.end()
    for made in last:
        made.wait()
    links.finish()
    plane.finish()

    @pl.when(holds)
    def _():
        for made in down:
            made.wait_send()
        sideways.wait_send()

    @pl.when(relays)
    def _():
        relay.wait_send()

    @pl.when(jnp.logical_not(holds))
    def _():
        onward.wait_send()


NT = (((1,), (1,)), ((), ()))
TN = (((0,), (0,)), ((), ()))


def norm_back(d_norm, value, gain):
    factor = row_factor(value)
    gain_sum = jnp.sum(d_norm * value * factor, axis=0, keepdims=True)
    scaled = d_norm * gain
    inner = jnp.mean(scaled * value, axis=-1, keepdims=True)
    return factor * scaled - value * (factor * factor * factor * inner), gain_sum


def feed_kernel(
    gu_h, dn_h, dout_h, mid_h, middle_h, gains,
    gu_g, dn_pair, ffn_h, d_middle_h, branch_s, ffn_gain,
    gu_w, dn_w, dout, mid, hidden, d_proj, dn_g, from_x, stage,
    part, from_core, to_y, from_y, middle, d_norm, branch, send_sems, recv_sems, local_sems,
):
    place = Place()
    links = Links(place, send_sems, recv_sems, local_sems)
    shards, rows, width = gu_w.shape
    units, seq = hidden.shape[1], hidden.shape[0]
    tokens = mid.shape[1]
    first = [links.local(mid_h, mid)]
    later, loads = [], []
    for n in range(units // 256):
        gate, up = pl.ds(256 * n, 256), pl.ds(units + 256 * n, 256)
        loads.append([
            links.local(gu_h.at[:, :, gate], gu_w.at[:, :, gate]),
            links.local(gu_h.at[:, :, up], gu_w.at[:, :, up]),
        ])
        if n == 0:
            first += [links.local(dout_h, dout), links.local(dn_h, dn_w)]
    later.append(links.local(middle_h, middle))
    place.meet([place.x_dev, place.core_dev, place.y_dev])
    for made in first:
        made.wait()

    x_slot = links.slots(4)
    for n in range(units // 256):
        for made in loads[n]:
            made.wait()
        gate_columns, up_columns = slice(256 * n, 256 * (n + 1)), slice(units + 256 * n, units + 256 * (n + 1))

        def activation(index, gate_columns=gate_columns, up_columns=up_columns, n=n):
            low = mid[index]
            gate = jnp.dot(
                low, gu_w[:, :, gate_columns].reshape(width, 256), preferred_element_type=F32
            )
            up = jnp.dot(
                low, gu_w[:, :, up_columns].reshape(width, 256), preferred_element_type=F32
            )
            d_hidden = lax.dot_general(
                dout[index], dn_w[2 * n : 2 * n + 2].reshape(256, width), NT,
                preferred_element_type=F32,
            )
            at = pl.ds(pl.multiple_of(index * tokens, tokens), tokens)
            sigmoid = 1.0 / (1.0 + jnp.exp(-gate))
            silu = gate * sigmoid
            hidden[at, gate_columns] = (silu * up).astype(BF16)
            d_gate = d_hidden * up * (sigmoid * (1.0 + gate * (1.0 - sigmoid)))
            d_proj[at, gate_columns] = d_gate.astype(BF16)
            d_proj[at, up_columns] = (d_hidden * silu).astype(BF16)

        row_loop(4, activation)
        left = hidden[:, gate_columns].T

        def down_grad(j, left=left, n=n):
            wide = pl.ds(pl.multiple_of(512 * j, 512), 512)
            right = dout[:, :, wide].reshape(seq, 512)
            grad = jnp.dot(left, right, preferred_element_type=F32).astype(BF16)
            dn_g[n, 0, :, wide] = grad[:128]
            dn_g[n, 1, :, wide] = grad[128:]

        row_loop(4, down_grad)
        links.send(dn_g.at[n, place.xo], from_x.at[n], x_slot + n, place.x_dev)

    def mid_grad(f):
        grad = lax.dot_general(d_proj[...], gu_w[f], NT, preferred_element_type=F32)
        columns = pl.ds(pl.multiple_of(rows * f, rows), rows)
        part[:, :, columns] = grad.astype(BF16).reshape(4, tokens, rows)

    parts = halves(tokens)
    sides = [(slice(None), side) for side in halves(width)]
    dmid = ReduceCtx(links, place, part, sides, None, from_core, to_y, from_y)
    row_loop(shards // 2, mid_grad)
    dmid.begin(0)
    row_loop(shards // 2, mid_grad, shards // 2)
    dmid.begin(1)
    dmid.cross(0)

    def gate_up_grad(z):
        for x in range(2):
            columns = pl.ds(pl.multiple_of(2 * rows * z + rows * x, rows), rows)
            left = mid[:, :, columns].reshape(seq, rows).T
            for j in range(4):
                wide = slice(512 * j, 512 * (j + 1))
                grad = jnp.dot(left, d_proj[:, wide], preferred_element_type=F32)
                stage[x, :, wide] = grad.astype(BF16)
        made = pltpu.make_async_copy(stage, gu_g.at[z], local_sems.at[links.locals])
        made.start()
        made.wait()

    row_loop(1, gate_up_grad)
    dmid.cross(1)
    row_loop(3, gate_up_grad, 1)
    links.locals += 1

    def feed_out(index):
        at = pl.ds(pl.multiple_of(index * tokens, tokens), tokens)
        for j in range(4):
            wide = slice(512 * j, 512 * (j + 1))
            right = dn_w[:, :, wide].reshape(units, 512)
            sums = jnp.dot(hidden[at], right, preferred_element_type=F32)
            mid[index, :, wide] = sums.astype(BF16)

    row_loop(4, feed_out)
    later.append(links.local(mid, ffn_h))
    later[0].wait()
    for k in range(2):
        d_norm[sides[k]] = dmid.total(k)
    gain_sum = None
    for k, at in enumerate(parts):
        grad, term = norm_back(d_norm[at], middle[at], gains[1:2])
        gain_sum = term if gain_sum is None else gain_sum + term
        middle[at] = grad + dout[place.c, at].astype(F32)
        branch[at] = middle[at].astype(BF16)
        later.append(links.local(middle.at[at], d_middle_h.at[at]))
        later.append(links.local(branch.at[at], branch_s.at[at]))
    ffn_gain[...] = gain_sum
    for n in range(4):
        links.arrive(from_x.at[n], x_slot + n)
        pair = dn_g[n, place.x].astype(F32) + from_x[n].astype(F32)
        from_x[n] = pair.astype(BF16)
        later.append(links.local(from_x.at[n], dn_pair.at[n]))
    for made in later[1:]:
        made.wait()
    links.finish()


def backward_kernel(
    gu_g, dn_pair, ffn_part, middle_h, d_middle_h, branch_s, x_h, lengths, gains, ffn_gain,
    angles, head_gain, key_bias,
    normed_h, qkv_raw_h, qkv_low_h, att_low_h, log_sums_h, qkv_wh, out_wh,
    gu_all, dn_all, layer_out, qkv_all, out_all, input_grad, stats,
    own, from_x, from_z, via,
    ctx_own, from_core1, to_y1, from_y1, from_core2, to_y2, from_y2,
    middle, x_s, d_middle, branch_all, part,
    cos, sin, qkv_raw, qkv_low, att_low, log_sums, qkv_w, out_w,
    keys, values, d_att, d_low, d_keys, d_values, gain_g,
    qkv_g, qkv_x, qkv_z, out_g, out_x, out_z,
    mine, plane_stats, ctx_stats, send_sems, recv_sems, local_sems,
):
    place = Place()
    links = Links(place, send_sems, recv_sems, local_sems)
    fellows = [lax.rem(place.f + d, 8) for d in range(1, 8)]
    place.meet(
        [(f, place.c) for f in fellows] + [place.core_dev, place.y_dev, place.diag_dev]
    )
    step = from_x.shape[2]
    chunks, where = [], []
    for first in range(0, dn_pair.shape[1], step):
        rows = pl.ds(first, step)
        chunks.append(lambda x, rows=rows: dn_pair.at[:, rows])
        where.append((dn_all, rows))
    summed = len(chunks)
    for first in range(0, gu_g.shape[2], step):
        rows = pl.ds(first, step)
        chunks.append(lambda x, rows=rows: gu_g.at[:, x, rows])
        where.append((gu_all, rows))
    count = len(chunks)
    plane = ReduceTree(links, place, chunks, from_x, from_z, via, own, summed)
    outs = [SpreadCtx(links, place, out, [rows]) for out, rows in where]
    kept = []

    def end(k):
        total = plane.end(k)
        if k + own.shape[0] < count:
            plane.load(k + own.shape[0])
        out, rows = where[k]
        outs[k].begin(0, total)
        kept.append(links.local(total, out.at[place.c, rows]))

    tokens, width = middle.shape
    parts = halves(tokens)
    branch = SpreadCtx(links, place, branch_all, parts)
    for k, rows in enumerate(parts):
        branch.begin(k, branch_s.at[rows])
    for k in range(summed, count - 1):
        plane.send_x(k)
    ffn = ReduceCtx(links, place, ffn_part, parts, ctx_own, from_core1, to_y1, from_y1)
    ffn.begin()
    for k in range(own.shape[0]):
        plane.load(k)
    late = [
        links.local(a, b)
        for a, b in (
            (branch_s, branch_all.at[place.c]),
            (out_wh, out_w), (qkv_low_h, qkv_low), (att_low_h, att_low), (log_sums_h, log_sums),
            (qkv_raw_h, qkv_raw), (qkv_wh, qkv_w),
            (middle_h, middle), (d_middle_h, d_middle), (x_h, x_s),
        )
    ]
    turn_tables(angles, cos, sin)
    gain_g[...] = jnp.zeros_like(gain_g)
    d_keys[...] = jnp.zeros_like(d_keys)
    d_low[...] = jnp.zeros_like(d_low)
    d_values[...] = jnp.zeros_like(d_values)
    plane.middle(0)
    plane.middle(1)
    for k in range(2):
        ffn.cross(k)
    branch.forward(0)
    plane.combine(0)
    branch.forward(1)
    plane.middle(2)
    plane.combine(1)
    branch.end()
    for made in late:
        made.wait()

    root = 1.0 / math.sqrt(HEAD_DIM)
    seq = 4 * tokens

    def prepare(index):
        rows = pl.ds(pl.multiple_of(index * BLOCK, BLOCK), BLOCK)
        block = qkv_low[2, rows].astype(F32)
        low = low_half(block.shape)
        swapped = pltpu.roll(block, 64, 1)
        keys[rows] = jnp.where(low, block, swapped).astype(BF16)
        values[rows] = jnp.where(low, swapped, block).astype(BF16)
        for b in range(2):
            d_att[b, rows] = lax.dot_general(
                branch_all[index], out_w[b], NT, preferred_element_type=F32
            ).astype(BF16)

    row_loop(seq // BLOCK, prepare)
    for b in range(2):
        left = att_low[b].T
        for j in range(8):
            columns = slice(256 * j, 256 * (j + 1))
            right = branch_all[:, :, columns].reshape(seq, 256)
            out_g[b, :, columns] = jnp.dot(left, right, preferred_element_type=F32).astype(BF16)
    out_slot = links.slots(1)
    links.send(out_g.at[place.xo], out_x, out_slot, place.x_dev)
    plane.send_x(count - 1)
    links.settle(branch.sends)
    normed_load = links.local(normed_h, branch_all)
    plane.middle(3)

    def unturn(row, rows, grads, block):
        back = grads * cos[rows] + partner(grads * sin[rows])
        factor = lax.rsqrt(half_sums(block * block) * (1.0 / HEAD_DIM) + EPSILON)
        gain_term = jnp.sum(back * block * factor, axis=0, keepdims=True)
        scaled = back * head_gain[row : row + 1]
        inner = half_sums(scaled * block) * (1.0 / HEAD_DIM)
        return factor * scaled - block * (factor * factor * factor * inner), gain_term

    def heads(index):
        b, half = lax.div(index, 2), lax.rem(index, 2)
        for i in range(seq // SHORT):
            rows, span = pl.ds(i * SHORT, SHORT), (i + 1) * SHORT
            query = qkv_low[b, rows]
            lane = lax.broadcasted_iota(jnp.int32, query.shape, 1)
            side = lax.div(lane, 64) == half
            chosen = jnp.where(side, query, 0)
            d_chosen = jnp.where(side, d_att[b, rows], 0)
            logs = jnp.max(jnp.where(side, log_sums[b, rows], -1e30), axis=-1, keepdims=True)
            scores = attention_scores(chosen, keys[:span], key_bias[0:1], i * SHORT, span)
            probs = jnp.exp(scores - logs)
            d_probs = lax.dot_general(d_chosen, values[:span], NT, preferred_element_type=F32)
            delta = jnp.sum(probs * d_probs, axis=-1, keepdims=True)
            d_scores = (probs * (d_probs - delta)).astype(BF16)
            d_query = jnp.dot(d_scores, keys[:span], preferred_element_type=F32) * root
            d_keys[:span] += lax.dot_general(d_scores, chosen, TN, preferred_element_type=F32)
            d_values[:span] += lax.dot_general(
                probs.astype(BF16), d_chosen, TN, preferred_element_type=F32
            )
            d_low[b, rows] = jnp.where(side, d_query.astype(BF16), d_low[b, rows])

    def unturn_queries(index):
        rows = pl.ds(pl.multiple_of(index * BLOCK, BLOCK), BLOCK)
        for b in range(2):
            grads = d_low[b, rows].astype(F32)
            d_block, gain_term = unturn(0, rows, grads, qkv_raw[b, rows])
            d_low[b, rows] = d_block.astype(BF16)
            gain_g[0:1] += gain_term

    row_loop(2, heads)
    plane.combine(2)
    end(0)
    row_loop(2, heads, 2)
    plane.middle(4)
    plane.combine(3)
    end(1)
    row_loop(seq // BLOCK, unturn_queries)

    def finish(index):
        rows = pl.ds(pl.multiple_of(index * BLOCK, BLOCK), BLOCK)
        k_sum, v_sum = d_keys[rows], d_values[rows]
        low = low_half(k_sum.shape)
        k_sum = (k_sum + pltpu.roll(k_sum, 64, 1)) * root
        v_sum = v_sum + pltpu.roll(v_sum, 64, 1)
        grads = jnp.where(low, k_sum, v_sum).astype(BF16).astype(F32)
        d_block, gain_term = unturn(2, rows, grads, qkv_raw[2, rows])
        d_low[2, rows] = jnp.where(low, d_block, grads).astype(BF16)
        gain_g[1:2] += gain_term
        for j in range(4):
            columns = slice(512 * j, 512 * (j + 1))
            sums = jnp.zeros((BLOCK, 512), F32)
            for b in range(3):
                weight = qkv_w[columns, 128 * b : 128 * (b + 1)]
                sums += lax.dot_general(d_low[b, rows], weight, NT, preferred_element_type=F32)
            part[index, :, columns] = sums.astype(BF16)

    row_loop(seq // BLOCK, finish)

    dnorm = ReduceCtx(links, place, part, parts, None, from_core2, to_y2, from_y2)
    dnorm.begin()
    normed_load.wait()
    for b in range(3):
        left = d_low[b].T
        for f in range(8):
            right = branch_all[:, :, 256 * f : 256 * (f + 1)].reshape(seq, 256)
            qkv_g[f // 2, f % 2, 128 * b : 128 * (b + 1)] = jnp.dot(
                left, right, preferred_element_type=F32
            ).astype(BF16)
    qkv_step = qkv_x.shape[2]
    qkv_rows = [pl.ds(k * qkv_step, qkv_step) for k in range(qkv_x.shape[0])]
    qkv_chunks = [lambda x, rows=rows: qkv_g.at[:, x, rows] for rows in qkv_rows]
    qkv_plane = ReducePlane(links, place, qkv_chunks, qkv_x, qkv_z)
    qkv_outs = [SpreadCtx(links, place, qkv_all, [rows]) for rows in qkv_rows]
    for k in range(len(qkv_chunks)):
        qkv_plane.send_x(k)
    links.arrive(out_x, out_slot)
    root_slot, final_slot = links.slots(3), links.slots(1)
    holds = place.z == place.c
    out_mine = out_g.at[place.x]
    out_mine[...] = (out_mine[...].astype(F32) + out_x[...].astype(F32)).astype(BF16)
    rank = place.rank(place.z, place.c)
    to_root = links.copy(
        out_mine,
        out_z.at[lax.rem(rank, 3)],
        root_slot + lax.rem(rank, 3),
        (place.c * 2 + place.x, place.c),
    )

    @pl.when(jnp.logical_not(holds))
    def _():
        to_root.start()

    for k in range(2):
        dnorm.cross(k)
    plane.combine(4)
    end(2)
    outs[0].forward(0)
    outs[1].forward(0)
    end(3)
    for k, rows in enumerate(parts):
        value = middle[rows] + ffn.total(k)
        positions = lax.broadcasted_iota(jnp.int32, (value.shape[0], 1), 0)
        positions += tokens * place.c + k * value.shape[0]
        layer_out[rows] = jnp.where(positions < lengths[0], value, 0.0).astype(BF16)
    plane.middle(5)
    outs[2].forward(0)
    attn_gain = None
    for k, rows in enumerate(parts):
        grad, term = norm_back(dnorm.total(k), x_s[rows].astype(F32), gains[0:1])
        attn_gain = term if attn_gain is None else attn_gain + term
        input_grad[rows] = (d_middle[rows] + grad).astype(BF16)
    mine[...] = jnp.zeros_like(mine)
    for f in range(8):
        mine[f, 0:1] = attn_gain[:, 256 * f : 256 * (f + 1)]
        mine[f, 1:2] = ffn_gain[:, 256 * f : 256 * (f + 1)]
        mine[f, 2:3, 0:128] = gain_g[0:1]
        mine[f, 2:3, 128:256] = gain_g[1:2]
    plane_slot, ctx_slot = links.slots(8), links.slots(4)
    for f in fellows:
        links.send(mine.at[f], plane_stats.at[place.f], plane_slot + place.f, (f, place.c))
    plane_stats[place.f] = mine[place.f]

    end(4)
    outs[3].forward(0)
    for k in range(len(qkv_chunks)):
        qkv_plane.middle(k)
    plane.combine(5)
    end(5)
    for f in fellows:
        links.arrive(plane_stats.at[f], plane_slot + f)
    sums = plane_stats[0]
    for f in range(1, 8):
        sums += plane_stats[f]
    ctx_stats[place.c] = sums
    for device in (place.core_dev, place.y_dev, place.diag_dev):
        links.send(ctx_stats.at[place.c], ctx_stats.at[place.c], ctx_slot + place.c, device)

    final = [
        links.copy(out_all, out_all, final_slot, device)
        for device in (place.core_dev, place.y_dev)
    ]
    onward = links.copy(out_all, out_all, final_slot, place.core_dev)

    @pl.when(holds)
    def _():
        sums = out_mine[...].astype(F32)
        for other in range(3):
            links.arrive(out_z.at[other], root_slot + other)
            sums += out_z[other].astype(F32)
        out_all[...] = sums.astype(BF16)
        for made in final:
            made.start()

    for k in range(len(qkv_chunks)):
        total = qkv_plane.end(k)
        qkv_outs[k].begin(0, total)
        kept.append(links.local(total, qkv_all.at[place.c, qkv_rows[k]]))
    for k in range(4, count):
        outs[k].forward(0)
    relays = place.c_y == place.z

    @pl.when(jnp.logical_not(holds))
    def _():
        links.arrive(out_all, final_slot)

    @pl.when(relays)
    def _():
        onward.start()

    for c in (place.c_core, place.c_y, place.c_diag):
        links.arrive(ctx_stats.at[c], ctx_slot + c)
    stats[...] = ((ctx_stats[0] + ctx_stats[1]) + ctx_stats[2]) + ctx_stats[3]
    for out in qkv_outs:
        out.forward(0)
    for out in outs + qkv_outs:
        out.end()
    for made in kept:
        made.wait()
    links.finish()
    plane.finish()
    qkv_plane.finish()

    @pl.when(jnp.logical_not(holds))
    def _():
        to_root.wait_send()

    @pl.when(relays)
    def _():
        onward.wait_send()

    @pl.when(holds)
    def _():
        for made in final:
            made.wait_send()


def finish_kernel(
    gu_parts, dn_parts, out_s, qkv_parts, layer_s, input_s, stats,
    out, dn_out, out_out, qkv_out, layer_out, input_out, attn_out, ffn_out, pairs, sems,
):
    rows = gu_parts.shape[1]
    first = pl.multiple_of(pl.program_id(0) * rows, rows)
    sent = []
    for c in range(4):
        for f in range(8):
            b = 4 * f + c
            for side in range(2):
                column = 1024 * side + 128 * f
                block = gu_parts[c, :, column : column + 128]
                pairs[b, pl.ds(side, rows, stride=2), :] = block.astype(F32)
            made = pltpu.make_async_copy(
                pairs.at[b].reshape(rows, 2, 128),
                out.at[pl.ds(first, rows), :, pl.ds(128 * b, 128)],
                sems.at[b],
            )
            made.start()
            sent.append(made)
    dn_out[...] = dn_parts[...].astype(F32)
    out_out[...] = out_s[...].astype(F32)
    layer_out[...] = layer_s[...]
    input_out[...] = input_s[...]

    @pl.when(pl.program_id(0) == 0)
    def _():
        attn_out[...] = stats[0:1]
        ffn_out[...] = stats[1:2]
        for c in range(4):
            qkv_out[:, 256 * c : 256 * (c + 1)] = qkv_parts[c, 0:256].astype(F32).T
        for y in range(2):
            for j in range(2):
                from_row = 256 + 64 * j
                both = [qkv_parts[2 * y + core, from_row : from_row + 64] for core in range(2)]
                column = 1024 + 256 * j + 128 * y
                qkv_out[:, column : column + 128] = jnp.concatenate(both, axis=0).astype(F32).T

    for made in sent:
        made.wait()


def shaped(shape, kind=BF16):
    return jax.ShapeDtypeStruct(shape, kind)


def call(kernel, ins, outs, scratch=(), sems=None, number=None, flops=0):
    scratch = list(scratch)
    extra = {}
    if sems is not None:
        scratch += [pltpu.SemaphoreType.DMA((n,)) for n in sems]
        extra = dict(collective_id=number, has_side_effects=True)
    return pl.pallas_call(
        kernel,
        out_shape=tuple(shape for shape, _ in outs),
        in_specs=[spec for _, spec in ins],
        out_specs=tuple(spec for _, spec in outs),
        scratch_shapes=scratch,
        compiler_params=pltpu.CompilerParams(vmem_limit_bytes=VMEM_BYTES, **extra),
    )(*[array for array, _ in ins])


def split_heads(
    inputs,
    cotangent,
    lengths,
    qkv_weight,
    out_weight,
    gate_up,
    down_weight,
    attn_gain,
    ffn_gain,
    qk_gain,
):
    tokens, width = inputs.shape[1:]
    seq = tokens * 4
    source = inputs[0]
    rows, parts, units = gate_up.shape
    down_rows = down_weight.shape[0] // 4
    gain_s = jnp.concatenate(
        [attn_gain[None], ffn_gain[None], jnp.zeros((6, rows), BF16)], axis=0
    ).astype(F32)

    half_dim = HEAD_DIM // 2
    frequency = 10000.0 ** (-2.0 * np.arange(half_dim) / HEAD_DIM)
    turns = [np.arange(0, seq, 64)[:, None] * frequency, np.arange(64)[:, None] * frequency]
    signs = np.repeat([-1.0, 1.0, -1.0, 1.0], half_dim)
    angles = jnp.asarray(
        np.concatenate(
            [part for t in turns for part in (np.tile(np.cos(t), 4), np.tile(np.sin(t), 4) * signs)]
        ),
        F32,
    )
    table = pltpu.VMEM((seq, 128), F32)
    (
        qkv_w, out_w, gains, normed, qkv_raw, qkv_low, att_low, log_sums,
        gu_w, dn_w, dout_all, middle, mid_all, head_gain, key_bias,
    ) = call(
        forward_kernel,
        [(lengths, pl.BlockSpec(memory_space=pltpu.SMEM))]
        + [
            (a, HBM)
            for a in (qkv_weight, out_weight, gain_s, source, gate_up, down_weight, cotangent[0])
        ]
        + [(angles, VMEM), (qk_gain, VMEM)],
        [
            (shaped((8, rows, 384)), HBM),
            (shaped((2, out_weight.shape[0], width)), HBM),
            (shaped((8, width), F32), VMEM),
            (shaped((seq, width)), HBM),
            (shaped((3, seq, 128), F32), HBM),
            (shaped((3, seq, 128)), HBM),
            (shaped((2, seq, 128)), HBM),
            (shaped((2, seq, 128), F32), HBM),
            (shaped((8, rows, width)), HBM),
            (shaped((8, down_rows, width)), HBM),
            (shaped((4, tokens, width)), HBM),
            (shaped((tokens, width), F32), VMEM),
            (shaped((4, tokens, width)), HBM),
            (shaped((8, 128), F32), VMEM),
            (shaped((8, seq), F32), VMEM),
        ],
        [
            pltpu.VMEM((2, rows, 128), BF16),
            pltpu.VMEM((rows, 128), BF16),
            pltpu.VMEM((tokens, width), BF16),
            table,
            table,
            pltpu.VMEM((8, 8, rows), F32),
            pltpu.VMEM((8, rows, 384), BF16),
            pltpu.VMEM((2, out_weight.shape[0], width), BF16),
            pltpu.VMEM((4, tokens, width), BF16),
            pltpu.VMEM((seq, width), BF16),
            pltpu.VMEM((3, seq, 128), F32),
            pltpu.VMEM((3, seq, 128), BF16),
            pltpu.VMEM((2, seq, 128), BF16),
            pltpu.VMEM((2, seq, 128), F32),
            pltpu.VMEM((4, tokens, width), BF16),
            pltpu.VMEM((seq, 128), BF16),
            pltpu.VMEM((seq, 128), BF16),
            pltpu.VMEM((2, tokens, width), BF16),
            pltpu.VMEM((tokens, width), BF16),
            pltpu.VMEM((tokens, width), BF16),
            pltpu.VMEM((tokens, width), BF16),
            pltpu.VMEM((8, rows, 2, 128), BF16),
            pltpu.VMEM((2 * rows, 128), F32),
            pltpu.VMEM((rows, width), BF16),
        ],
        sems=(180, 170, 32),
        number=0,
    )
    qkv_w = qkv_w.reshape(width, 384)
    block = pltpu.VMEM((tokens, width), BF16)
    pair = pltpu.VMEM((2, tokens, width), BF16)
    whole = pltpu.VMEM((4, tokens, width), BF16)
    hidden_units = units // 4
    gu_g, dn_pair, ffn_part, d_middle, branch_s, ffn_gain_part = call(
        feed_kernel,
        [(a, HBM) for a in (gu_w, dn_w, dout_all, mid_all, middle)] + [(gains, VMEM)],
        [
            (shaped((4, 2, rows, width)), HBM),
            (shaped((4, down_rows, width)), HBM),
            (shaped((4, tokens, width)), HBM),
            (shaped((tokens, width), F32), HBM),
            (shaped((tokens, width)), HBM),
            (shaped((1, width), F32), VMEM),
        ],
        [
            pltpu.VMEM((8, rows, width), BF16),
            pltpu.VMEM((8, down_rows, width), BF16),
            whole,
            whole,
            pltpu.VMEM((seq, hidden_units), BF16),
            pltpu.VMEM((seq, parts * hidden_units), BF16),
            pltpu.VMEM((4, 2, down_rows, width), BF16),
            pltpu.VMEM((4, down_rows, width), BF16),
            pltpu.VMEM((2, rows, width), BF16),
            whole,
            pair,
            block,
            block,
            pltpu.VMEM((tokens, width), F32),
            pltpu.VMEM((tokens, width), F32),
            block,
        ],
        sems=(16, 16, 24),
        number=2,
    )
    step = 64
    count = (rows + down_rows) // step
    heads = pltpu.VMEM((seq, 128), BF16)
    gu_all, dn_all, layer_out, qkv_all, out_all, input_grad, stats = call(
        backward_kernel,
        [
            (gu_g, HBM),
            (dn_pair, HBM),
            (ffn_part, HBM),
            (middle, HBM),
            (d_middle, HBM),
            (branch_s, HBM),
            (source, HBM),
            (lengths, pl.BlockSpec(memory_space=pltpu.SMEM)),
            (gains, VMEM),
            (ffn_gain_part, VMEM),
            (angles, VMEM),
            (head_gain, VMEM),
            (key_bias, VMEM),
            (normed.reshape(4, tokens, width), HBM),
        ]
        + [(a, HBM) for a in (qkv_raw, qkv_low, att_low, log_sums, qkv_w, out_w)],
        [
            (shaped((4, rows, width)), HBM),
            (shaped((4, down_rows, width)), HBM),
            (shaped((tokens, width)), VMEM),
            (shaped((4, 384, rows)), HBM),
            (shaped((128, width)), VMEM),
            (shaped((tokens, width)), VMEM),
            (shaped((8, rows), F32), VMEM),
        ],
        [
            pltpu.VMEM((4, 4, step, width), BF16),
            pltpu.VMEM((rows // step, 4, step, width), BF16),
            pltpu.VMEM((count, 2, step, width), BF16),
            pltpu.VMEM((count, 2, step, width), BF16),
            block, pair, block, block, pair, block, block,
            pltpu.VMEM((tokens, width), F32),
            block,
            pltpu.VMEM((tokens, width), F32),
            pltpu.VMEM((4, tokens, width), BF16),
            pltpu.VMEM((4, tokens, width), BF16),
            table,
            table,
            pltpu.VMEM((3, seq, 128), F32),
            pltpu.VMEM((3, seq, 128), BF16),
            pltpu.VMEM((2, seq, 128), BF16),
            pltpu.VMEM((2, seq, 128), F32),
            pltpu.VMEM((width, 384), BF16),
            pltpu.VMEM((2, 128, width), BF16),
            heads,
            heads,
            pltpu.VMEM((2, seq, 128), BF16),
            pltpu.VMEM((3, seq, 128), BF16),
            table,
            table,
            pltpu.VMEM((8, 128), F32),
            pltpu.VMEM((4, 2, 384, rows), BF16),
            pltpu.VMEM((2, 4, 192, rows), BF16),
            pltpu.VMEM((2, 3, 192, rows), BF16),
            pltpu.VMEM((2, 128, width), BF16),
            pltpu.VMEM((128, width), BF16),
            pltpu.VMEM((3, 128, width), BF16),
            pltpu.VMEM((8, 8, rows), F32),
            pltpu.VMEM((8, 8, rows), F32),
            pltpu.VMEM((4, 8, rows), F32),
        ],
        sems=(120, 120, 50),
        number=1,
    )
    some = 64
    steps = rows // some
    few = down_rows // steps
    out_rows = out_weight.shape[0]
    block_of = lambda n: pl.BlockSpec((n, width), lambda i: (i, 0))
    fixed = lambda *shape: pl.BlockSpec(shape, lambda i: (0,) * len(shape))
    gate_up_grad, down_grad, out_grad, qkv_grad, layer_out, input_grad, attn_g, ffn_g = pl.pallas_call(
        finish_kernel,
        grid=(steps,),
        in_specs=[
            pl.BlockSpec((4, some, width), lambda i: (0, i, 0)),
            pl.BlockSpec((4, few, width), lambda i: (0, i, 0)),
            block_of(out_rows // steps),
            fixed(4, 384, rows),
            block_of(tokens // steps),
            block_of(tokens // steps),
            fixed(8, rows),
        ],
        out_specs=[
            HBM,
            pl.BlockSpec((4, few, width), lambda i: (0, i, 0)),
            block_of(out_rows // steps),
            fixed(rows, qkv_weight.shape[1]),
            block_of(tokens // steps),
            block_of(tokens // steps),
            fixed(1, rows),
            fixed(1, rows),
        ],
        out_shape=[
            shaped((rows, parts, units), F32),
            shaped((4, down_rows, width), F32),
            shaped((out_rows, width), F32),
            shaped((rows, qkv_weight.shape[1]), F32),
            shaped((tokens, width)),
            shaped((tokens, width)),
            shaped((1, rows), F32),
            shaped((1, rows), F32),
        ],
        scratch_shapes=[
            pltpu.VMEM((32, 2 * some, 128), F32),
            pltpu.SemaphoreType.DMA((32,)),
        ],
        compiler_params=pltpu.CompilerParams(vmem_limit_bytes=VMEM_BYTES),
    )(gu_all, dn_all, out_all, qkv_all, layer_out, input_grad, stats)
    return (
        layer_out[None],
        input_grad[None],
        qkv_grad,
        out_grad,
        gate_up_grad,
        down_grad.reshape(4 * down_rows, width),
        attn_g[0],
        ffn_g[0],
        jnp.stack([stats[2, :64] + stats[2, 64:128], stats[2, 128:192]]),
    )


def solution(mesh):
    sizes = (mesh.shape["fsdp"], mesh.shape["ctx"])
    return jax.shard_map(
        split_heads if sizes == (8, 4) else on_device,
        mesh=mesh,
        in_specs=(
            P("fsdp", "ctx", None),
            P("fsdp", "ctx", None),
            P("fsdp"),
            P("fsdp", None),
            P("fsdp", None),
            P("fsdp", None, None),
            P("fsdp", None),
            P("fsdp"),
            P("fsdp"),
            P(),
        ),
        out_specs=(
            P("fsdp", "ctx", None),
            P("fsdp", "ctx", None),
            P("fsdp", None),
            P("fsdp", None),
            P("fsdp", None, None),
            P("fsdp", None),
            P("fsdp"),
            P("fsdp"),
            P(),
        ),
        check_vma=False,
    )
```

```python
import functools
import math

import jax
import jax.numpy as jnp
import numpy as np
from jax import lax
from jax.experimental import pallas as pl
from jax.experimental.pallas import tpu as pltpu
from jax.sharding import PartitionSpec as P

HEADS = 16
KV_HEADS = 4
HEAD_DIM = 64


EPSILON = 1e-06


def root_norm(values, norm_gain):
    factor = lax.rsqrt(jnp.mean(values * values, axis=-1, keepdims=True) + EPSILON)
    return values * factor * norm_gain


def rotation_tables(positions):
    half_dim = HEAD_DIM // 2
    frequency = 10000.0 ** (-(2.0 * jnp.arange(half_dim, dtype=jnp.float32)) / HEAD_DIM)
    angles = positions.astype(jnp.float32)[:, None] * frequency[None, :]
    return (jnp.cos(angles), jnp.sin(angles))


def rotate(values, cos_table, sin_table):
    half_dim = values.shape[-1] // 2
    lower_half = values[..., :half_dim]
    upper_half = values[..., half_dim:]
    cos_part = cos_table[:, None, :]
    sin_part = sin_table[:, None, :]
    return jnp.concatenate(
        [
            lower_half * cos_part - upper_half * sin_part,
            upper_half * cos_part + lower_half * sin_part,
        ],
        axis=-1,
    )


def prepare_heads(qkv_out, head_gain, cos_table, sin_table):
    row_count = qkv_out.shape[0]
    query_cols = HEADS * HEAD_DIM
    key_cols = KV_HEADS * HEAD_DIM
    queries = qkv_out[:, :query_cols].reshape(row_count, HEADS, HEAD_DIM)
    key_part = qkv_out[:, query_cols : query_cols + key_cols].reshape(row_count, KV_HEADS, HEAD_DIM)
    value_part = qkv_out[:, query_cols + key_cols :]
    queries = rotate(root_norm(queries, head_gain[0]), cos_table, sin_table).reshape(
        row_count, query_cols
    )
    key_part = rotate(root_norm(key_part, head_gain[1]), cos_table, sin_table).reshape(
        row_count, key_cols
    )
    return (queries, key_part, value_part)


def activate(projected):
    gate_part = projected[:, 0]
    return gate_part * jax.nn.sigmoid(gate_part) * projected[:, 1]


def contract_rows(left, right):
    return lax.dot_general(
        left, right, (((0,), (0,)), ((), ())), preferred_element_type=jnp.float32
    )


def contract_cols(left, right):
    return lax.dot_general(
        left, right, (((1,), (1,)), ((), ())), preferred_element_type=jnp.float32
    )


def on_device(
    inputs,
    cotangent,
    lengths,
    qkv_weight,
    out_weight,
    gate_up,
    down_weight,
    attn_gain,
    ffn_gain,
    qk_gain,
):
    token_count = inputs.shape[1]
    group = HEADS // KV_HEADS
    key_cols = KV_HEADS * HEAD_DIM
    seq_len = token_count * lax.axis_size("ctx")
    positions = lax.axis_index("ctx") * token_count + jnp.arange(token_count, dtype=jnp.int32)
    length = lengths[0]
    row_keep = (positions < length).astype(jnp.float32)[:, None]
    inv_root = 1.0 / math.sqrt(HEAD_DIM)
    source = inputs[0].astype(jnp.float32)
    qkv_full, out_full, attn_full, ffn_full = (
        lax.all_gather(qkv_weight, "fsdp", axis=0, tiled=True),
        lax.all_gather(out_weight, "fsdp", axis=0, tiled=True),
        lax.all_gather(attn_gain, "fsdp", axis=0, tiled=True),
        lax.all_gather(ffn_gain, "fsdp", axis=0, tiled=True),
    )
    attn_norm = attn_full.astype(jnp.float32)
    ffn_norm = ffn_full.astype(jnp.float32)
    normed = root_norm(source, attn_norm).astype(jnp.bfloat16)
    qkv_out = jnp.dot(normed, qkv_full, preferred_element_type=jnp.float32)
    cos_table, sin_table = rotation_tables(positions)
    head_gain = qk_gain.astype(jnp.float32)

    def head_pieces(qkv_values, gain_values):
        return prepare_heads(qkv_values, gain_values, cos_table, sin_table)

    head_values, head_pull = jax.vjp(head_pieces, qkv_out, head_gain)
    queries, key_part, value_part = head_values
    query_low = queries.astype(jnp.bfloat16).reshape(token_count, KV_HEADS, group, HEAD_DIM)
    kv_local = jnp.concatenate([key_part, value_part], axis=1).astype(jnp.bfloat16)
    kv_whole = lax.all_gather(kv_local, "ctx", axis=0, tiled=True)
    block = 512
    block_total = seq_len // block
    kv_blocks = kv_whole.reshape(block_total, block, 2, KV_HEADS, HEAD_DIM)
    starts = jnp.arange(block_total, dtype=jnp.int32) * block

    def block_scores(key_block, block_start):
        scores = (
            jnp.einsum("bhgd,thd->hgbt", query_low, key_block, preferred_element_type=jnp.float32)
            * inv_root
        )
        key_pos = block_start + jnp.arange(key_block.shape[0], dtype=jnp.int32)
        visible = (key_pos[None, :] <= positions[:, None]) & (key_pos[None, :] < length)
        return (scores, visible)

    def max_step(state, item):
        running_max, running_sum = state
        kv_block, block_start = item
        scores, visible = block_scores(kv_block[:, 0], block_start)
        new_max = jnp.maximum(running_max, jnp.max(jnp.where(visible, scores, -1e30), axis=-1))
        expanded = jnp.where(visible, jnp.exp(scores - new_max[..., None]), 0.0)
        running_sum = running_sum * jnp.exp(running_max - new_max) + jnp.sum(expanded, axis=-1)
        return ((new_max, running_sum), None)

    stat_shape = (KV_HEADS, group, token_count)
    start_state = (jnp.full(stat_shape, -1e30, jnp.float32), jnp.zeros(stat_shape, jnp.float32))
    final_state, unused_out = lax.scan(max_step, start_state, (kv_blocks, starts))
    log_total = final_state[0] + jnp.log(final_state[1])

    def block_probs(kv_block, block_start):
        scores, visible = block_scores(kv_block[:, 0], block_start)
        return jnp.where(visible, jnp.exp(scores - log_total[..., None]), 0.0)

    def value_step(totals, item):
        kv_block, block_start = item
        probs_low = block_probs(kv_block, block_start).astype(jnp.bfloat16)
        return (
            totals
            + jnp.einsum(
                "hgbt,thd->bhgd", probs_low, kv_block[:, 1], preferred_element_type=jnp.float32
            ),
            None,
        )

    attended, unused_out = lax.scan(
        value_step,
        jnp.zeros((token_count, KV_HEADS, group, HEAD_DIM), jnp.float32),
        (kv_blocks, starts),
    )
    attended_low = attended.reshape(token_count, HEADS * HEAD_DIM).astype(jnp.bfloat16)
    middle = source + jnp.dot(attended_low, out_full, preferred_element_type=jnp.float32)
    normed_mid = root_norm(middle, ffn_norm).astype(jnp.bfloat16)
    columns = normed_mid
    projected = jnp.einsum(
        "td,dgf->tgf",
        columns,
        lax.all_gather(gate_up, "fsdp", axis=0, tiled=True),
        preferred_element_type=jnp.float32,
    )
    act_value, act_pull = jax.vjp(activate, projected)
    hidden = act_value.astype(jnp.bfloat16)
    columns = hidden
    ffn_out = jnp.dot(
        columns,
        lax.all_gather(down_weight, "fsdp", axis=0, tiled=True),
        preferred_element_type=jnp.float32,
    )
    layer_out = (row_keep * (middle + ffn_out)).astype(jnp.bfloat16)[None]
    d_out = row_keep * cotangent[0].astype(jnp.float32)
    d_out_low = d_out.astype(jnp.bfloat16)
    down_shard = lax.psum_scatter(
        contract_rows(hidden, d_out_low).astype(jnp.bfloat16),
        "fsdp",
        scatter_dimension=0,
        tiled=True,
    )
    d_hidden = contract_cols(d_out_low, lax.all_gather(down_weight, "fsdp", axis=0, tiled=True))
    d_proj_low = act_pull(d_hidden)[0].astype(jnp.bfloat16)
    columns = normed_mid
    gate_up_shard = lax.psum_scatter(
        jnp.einsum("td,tgf->dgf", columns, d_proj_low, preferred_element_type=jnp.float32).astype(
            jnp.bfloat16
        ),
        "fsdp",
        scatter_dimension=0,
        tiled=True,
    )
    d_normed_mid = jnp.einsum(
        "tgf,dgf->td",
        d_proj_low,
        lax.all_gather(gate_up, "fsdp", axis=0, tiled=True),
        preferred_element_type=jnp.float32,
    )
    mid_value, mid_pull = jax.vjp(root_norm, middle, ffn_norm)
    d_mid_norm, ffn_gain_part = mid_pull(d_normed_mid)
    d_middle = d_out + d_mid_norm
    d_branch = d_middle.astype(jnp.bfloat16)
    out_term = contract_rows(attended_low, d_branch)
    d_attended = (
        contract_cols(d_branch, out_full)
        .astype(jnp.bfloat16)
        .reshape(token_count, KV_HEADS, group, HEAD_DIM)
    )
    delta = jnp.transpose(jnp.sum(d_attended.astype(jnp.float32) * attended, axis=-1), (1, 2, 0))

    def block_grads(kv_block, block_start):
        probs = block_probs(kv_block, block_start)
        d_probs = jnp.einsum(
            "bhgd,thd->hgbt", d_attended, kv_block[:, 1], preferred_element_type=jnp.float32
        )
        d_scores = (probs * (d_probs - delta[..., None])).astype(jnp.bfloat16)
        return (probs.astype(jnp.bfloat16), d_scores)

    def query_step(totals, item):
        kv_block, block_start = item
        probs_low, d_scores = block_grads(kv_block, block_start)
        return (
            totals
            + jnp.einsum(
                "hgbt,thd->bhgd", d_scores, kv_block[:, 0], preferred_element_type=jnp.float32
            ),
            None,
        )

    d_query_sum, unused_out = lax.scan(
        query_step,
        jnp.zeros((token_count, KV_HEADS, group, HEAD_DIM), jnp.float32),
        (kv_blocks, starts),
    )
    d_query = (d_query_sum * inv_root).reshape(token_count, HEADS * HEAD_DIM).astype(jnp.bfloat16)
    sub_block = 512
    sub_total = token_count * lax.axis_size("ctx") // sub_block
    pieces = kv_whole.reshape(sub_total, sub_block, 2, KV_HEADS, HEAD_DIM)
    sub_starts = jnp.arange(sub_total, dtype=jnp.int32) * sub_block

    def key_grads(item):
        kv_block, block_start = item
        probs_low, d_scores = block_grads(kv_block, block_start)
        d_keys = (
            jnp.einsum("hgbt,bhgd->thd", d_scores, query_low, preferred_element_type=jnp.float32)
            * inv_root
        )
        d_values = jnp.einsum(
            "hgbt,bhgd->thd", probs_low, d_attended, preferred_element_type=jnp.float32
        )
        return jnp.concatenate(
            [d_keys.reshape(sub_block, key_cols), d_values.reshape(sub_block, key_cols)], axis=1
        )

    kv_grad = lax.psum_scatter(
        lax.map(key_grads, (pieces, sub_starts))
        .reshape(token_count * lax.axis_size("ctx"), 2 * key_cols)
        .astype(jnp.bfloat16),
        "ctx",
        scatter_dimension=0,
        tiled=True,
    ).astype(jnp.float32)
    d_key_low = kv_grad[:, :key_cols].astype(jnp.bfloat16).astype(jnp.float32)
    d_value_low = kv_grad[:, key_cols:].astype(jnp.bfloat16).astype(jnp.float32)
    d_qkv_out, qk_part = head_pull((d_query.astype(jnp.float32), d_key_low, d_value_low))
    d_qkv = d_qkv_out.astype(jnp.bfloat16)
    qkv_term = contract_rows(normed, d_qkv)
    d_normed = contract_cols(d_qkv, qkv_full)
    first_value, first_pull = jax.vjp(root_norm, source, attn_norm)
    d_source_norm, attn_gain_part = first_pull(d_normed)
    input_grad = (d_middle + d_source_norm).astype(jnp.bfloat16)[None]
    qkv_shard, out_shard, attn_shard, ffn_shard = (
        lax.psum_scatter(
            qkv_term.astype(jnp.bfloat16), "fsdp", scatter_dimension=0, tiled=True
        ).astype(jnp.float32),
        lax.psum_scatter(
            out_term.astype(jnp.bfloat16), "fsdp", scatter_dimension=0, tiled=True
        ).astype(jnp.float32),
        lax.psum_scatter(
            attn_gain_part.astype(jnp.bfloat16), "fsdp", scatter_dimension=0, tiled=True
        ).astype(jnp.float32),
        lax.psum_scatter(
            ffn_gain_part.astype(jnp.bfloat16), "fsdp", scatter_dimension=0, tiled=True
        ).astype(jnp.float32),
    )
    summed = (
        lax.psum(qkv_shard.astype(jnp.bfloat16), "ctx").astype(jnp.float32),
        lax.psum(out_shard.astype(jnp.bfloat16), "ctx").astype(jnp.float32),
        lax.psum(gate_up_shard, "ctx").astype(jnp.float32),
        lax.psum(down_shard, "ctx").astype(jnp.float32),
        lax.psum(attn_shard.astype(jnp.bfloat16), "ctx").astype(jnp.float32),
        lax.psum(ffn_shard.astype(jnp.bfloat16), "ctx").astype(jnp.float32),
    )
    qk_total = lax.psum(qk_part, ("fsdp", "ctx"))
    return (
        layer_out,
        input_grad,
        summed[0],
        summed[1],
        summed[2],
        summed[3],
        summed[4],
        summed[5],
        qk_total,
    )


MESH = pl.DeviceIdType.MESH
F32 = jnp.float32
BF16 = jnp.bfloat16
VMEM_BYTES = 60 << 20
HBM = pl.BlockSpec(memory_space=pl.ANY)
VMEM = pl.BlockSpec(memory_space=pltpu.VMEM)


class Place:
    def __init__(self):
        self.f = lax.axis_index("fsdp")
        self.c = lax.axis_index("ctx")
        self.z, self.x = lax.div(self.f, 2), lax.rem(self.f, 2)
        self.y, self.core = lax.div(self.c, 2), lax.rem(self.c, 2)
        self.xo, self.yo, self.co = 1 - self.x, 1 - self.y, 1 - self.core
        upper = lax.div(self.z, 2)
        self.others = (self.z + 1 - 2 * lax.rem(self.z, 2), 2 - upper, 3 - 3 * upper)
        self.inner = lax.rem(self.z, 2) + upper == 1
        self.far = 2 - 2 * upper
        self.x_dev = (self.z * 2 + self.xo, self.c)
        self.c_core = self.y * 2 + self.co
        self.c_y = self.yo * 2 + self.core
        self.c_diag = self.yo * 2 + self.co
        self.core_dev = (self.f, self.c_core)
        self.y_dev = (self.f, self.c_y)
        self.diag_dev = (self.f, self.c_diag)

    def rank(self, source, target):
        return jnp.where(source > target, source - 1, source)

    def z_dev(self, z):
        return (z * 2 + self.x, self.c)

    def meet(self, partners):
        barrier = pltpu.get_barrier_semaphore()
        for partner in partners:
            pl.semaphore_signal(barrier, inc=1, device_id=partner, device_id_type=MESH)
        pl.semaphore_wait(barrier, len(partners))

    def neighbours(self):
        return [self.z_dev(o) for o in self.others] + [self.x_dev, self.core_dev, self.y_dev]


class Links:
    def __init__(self, place, send_sems, recv_sems, local_sems):
        self.place = place
        self.send_sems, self.recv_sems, self.local_sems = send_sems, recv_sems, local_sems
        self.sends = self.recvs = self.locals = 0
        self.open = []

    def slots(self, count):
        first = self.recvs
        self.recvs += count
        return first

    def copy(self, src, dst, slot, device):
        made = pltpu.make_async_remote_copy(
            src_ref=src,
            dst_ref=dst,
            send_sem=self.send_sems.at[self.sends],
            recv_sem=self.recv_sems.at[slot],
            device_id=device,
            device_id_type=MESH,
        )
        self.sends += 1
        return made

    def send(self, src, dst, slot, device):
        made = self.copy(src, dst, slot, device)
        made.start()
        self.open.append(made)
        return made

    def settle(self, sends):
        for made in sends:
            made.wait_send()
            self.open = [one for one in self.open if one is not made]

    def arrive(self, ref, slot):
        pltpu.make_async_remote_copy(
            src_ref=ref,
            dst_ref=ref,
            send_sem=self.send_sems.at[0],
            recv_sem=self.recv_sems.at[slot],
            device_id=self.place.x_dev,
            device_id_type=MESH,
        ).wait_recv()

    def local(self, src, dst):
        made = pltpu.make_async_copy(src, dst, self.local_sems.at[self.locals])
        self.locals += 1
        made.start()
        return made

    def finish(self):
        for made in self.open:
            made.wait_send()
        self.open = []


class SpreadPlane:
    def __init__(self, links, place, chunks):
        self.links, self.place, self.chunks = links, place, chunks
        self.z_slot, self.x_slot = links.slots(4 * len(chunks)), links.slots(4 * len(chunks))

    def begin_z(self):
        place = self.place
        for k, (src, dst) in enumerate(self.chunks):
            slot = self.z_slot + 4 * k + place.z
            for other in place.others:
                self.links.send(src, dst(place.f), slot, place.z_dev(other))

    def begin_x(self, k):
        src, dst = self.chunks[k]
        slot = self.x_slot + 4 * k + self.place.z
        self.links.send(src, dst(self.place.f), slot, self.place.x_dev)

    def forward(self, k):
        place, dst = self.place, self.chunks[k][1]
        for other in place.others:
            block = dst(other * 2 + place.x)
            self.links.arrive(block, self.z_slot + 4 * k + other)
            self.links.send(block, block, self.x_slot + 4 * k + other, place.x_dev)

    def end(self):
        for k in range(len(self.chunks)):
            for z in range(4):
                block = self.chunks[k][1](z * 2 + self.place.xo)
                self.links.arrive(block, self.x_slot + 4 * k + z)


class SpreadTree(SpreadPlane):
    def __init__(self, links, place, chunks, crossed):
        super().__init__(links, place, chunks)
        self.plain = len(chunks) - crossed
        self.passed = []

    def begin_z(self, ahead=4):
        place = self.place
        self.near = {}
        for k, (src, dst) in enumerate(self.chunks):
            slot = self.z_slot + 4 * k + place.z
            near = self.links.copy(src, dst(place.f), slot, place.z_dev(place.others[0]))
            self.links.open.append(near)
            if k < ahead:
                near.start()
            else:
                pl.when(jnp.logical_not(place.inner))(near.start)
                self.near[k - ahead] = near
            self.links.send(src, dst(place.f), slot, place.z_dev(place.others[1]))

    def cross_z(self, k):
        place = self.place
        block = self.chunks[k][1](place.z * 2 + place.xo)
        slot = self.x_slot + 4 * k + place.z
        self.links.arrive(block, slot)
        for other in place.others[:2]:
            self.links.send(block, block, slot, place.z_dev(other))

    def blocks(self, k, other):
        place, dst = self.place, self.chunks[k][1]
        found = [(dst(other * 2 + place.x), self.z_slot + 4 * k + other)]
        if k >= self.plain:
            found.append((dst(other * 2 + place.xo), self.x_slot + 4 * k + other))
        return found

    def onward(self, k):
        place = self.place
        blocks = [pair for other in place.others[1:] for pair in self.blocks(k, other)]
        made = [
            self.links.copy(block, block, slot, place.z_dev(place.others[0]))
            for block, slot in blocks
        ]
        self.passed += made

        @pl.when(place.inner)
        def _():
            for (block, slot), one in zip(blocks, made):
                self.links.arrive(block, slot)
                one.start()
            if k in self.near:
                self.near[k].start()

    def forward(self, k):
        place = self.place
        near, *far = [self.blocks(k, other) for other in place.others]
        far = far[0] + far[1]
        for pair in near:
            self.links.arrive(*pair)
        if k < self.plain:
            slot = self.x_slot + 4 * k + place.others[0]
            self.links.send(near[0][0], near[0][0], slot, place.x_dev)

        @pl.when(jnp.logical_not(place.inner))
        def _():
            for pair in far:
                self.links.arrive(*pair)

        if k < self.plain:
            for other, (block, _) in zip(place.others[1:], far):
                self.links.send(block, block, self.x_slot + 4 * k + other, place.x_dev)

    def end(self):
        for k in range(self.plain):
            for z in range(4):
                block = self.chunks[k][1](z * 2 + self.place.xo)
                self.links.arrive(block, self.x_slot + 4 * k + z)

    def finish(self):
        @pl.when(self.place.inner)
        def _():
            for made in self.passed:
                made.wait_send()


class ReducePlane:
    def __init__(self, links, place, chunks, from_x, from_z, own=None):
        self.links, self.place, self.chunks = links, place, chunks
        self.from_x, self.from_z, self.own = from_x, from_z, own
        self.summed = 0
        self.x_slot, self.z_slot = links.slots(len(chunks)), links.slots(3 * len(chunks))
        self.loads, self.z_sends = {}, {}

    def send_x(self, k):
        place = self.place
        from_x = self.from_x.at[k - self.summed]
        self.links.send(self.chunks[k](place.xo), from_x, self.x_slot + k, place.x_dev)

    def load(self, k):
        slots = self.own.shape[0]
        for made in self.z_sends.pop(k - slots, []):
            made.wait_send()
        self.loads[k] = self.links.local(self.chunks[k](self.place.x), self.own.at[k % slots])

    def mine(self, k):
        if self.own is None:
            return self.chunks[k](self.place.x)
        return self.own.at[k % self.own.shape[0]]

    def middle(self, k):
        place = self.place
        self.links.arrive(self.from_x.at[k], self.x_slot + k)
        if k in self.loads:
            self.loads[k].wait()
        mine = self.mine(k)
        self.z_sends[k] = []
        for other in place.others:
            mine[other] = (mine[other].astype(F32) + self.from_x[k, other].astype(F32)).astype(BF16)
            rank = place.rank(place.z, other)
            made = self.links.copy(
                mine.at[other],
                self.from_z.at[k, rank],
                self.z_slot + 3 * k + rank,
                place.z_dev(other),
            )
            made.start()
            self.z_sends[k].append(made)

    def end(self, k):
        place = self.place
        mine = self.mine(k)
        sums = mine[place.z].astype(F32) + self.from_x[k, place.z].astype(F32)
        for rank in range(3):
            self.links.arrive(self.from_z.at[k, rank], self.z_slot + 3 * k + rank)
            sums += self.from_z[k, rank].astype(F32)
        total = self.from_x.at[k, place.z]
        total[...] = sums.astype(BF16)
        return total

    def finish(self):
        for sends in self.z_sends.values():
            for made in sends:
                made.wait_send()


class ReduceTree(ReducePlane):
    def __init__(self, links, place, chunks, from_x, from_z, via, own, summed):
        super().__init__(links, place, chunks, from_x, from_z, own)
        self.summed = summed
        self.via, self.via_slot = via, links.slots(len(chunks))
        self.outer = jnp.logical_not(place.inner)

    def load(self, k):
        slots = self.own.shape[0]
        self.settle(self.z_sends.pop(k - slots, []))
        self.loads[k] = self.links.local(self.chunks[k](self.place.x), self.own.at[k % slots])

    def settle(self, sends):
        for made, when in sends:
            if when is None:
                made.wait_send()
            else:
                pl.when(when)(made.wait_send)

    def middle(self, k):
        place = self.place
        self.loads[k].wait()
        mine = self.mine(k)
        if k >= self.summed:
            from_x = self.from_x.at[k - self.summed]
            self.links.arrive(from_x, self.x_slot + k)
            for other in place.others:
                pair = mine[other].astype(F32) + from_x[other].astype(F32)
                mine[other] = pair.astype(BF16)
        near = place.others[0]
        device = place.z_dev(near)
        direct = self.links.copy(mine.at[near], self.from_z.at[k, 0], self.z_slot + 3 * k, device)
        direct.start()
        far = self.links.copy(
            mine.at[pl.ds(place.far, 2)], self.via.at[k], self.via_slot + k, device
        )
        pl.when(self.outer)(far.start)
        self.z_sends[k] = [(direct, None), (far, self.outer)]

    def combine(self, k):
        place = self.place
        mine = self.mine(k)

        sent = [
            self.links.copy(
                mine.at[place.far + j],
                self.from_z.at[k, 1],
                self.z_slot + 3 * k + 1,
                place.z_dev(place.far + j),
            )
            for j in range(2)
        ]

        @pl.when(place.inner)
        def _():
            self.links.arrive(self.via.at[k], self.via_slot + k)
            for j in range(2):
                here = mine[place.far + j].astype(F32) + self.via[k, j].astype(F32)
                mine[place.far + j] = here.astype(BF16)
                sent[j].start()

        self.z_sends[k] += [(made, place.inner) for made in sent]

    def end(self, k):
        place = self.place
        sums = self.mine(k)[place.z].astype(F32)
        if k >= self.summed:
            sums += self.from_x[k - self.summed, place.z].astype(F32)
        for side in range(2):
            self.links.arrive(self.from_z.at[k, side], self.z_slot + 3 * k + side)
            sums += self.from_z[k, side].astype(F32)
        total = self.from_z.at[k, 0]
        total[...] = sums.astype(BF16)
        return total

    def finish(self):
        for sends in self.z_sends.values():
            self.settle(sends)


class SpreadCtx:
    def __init__(self, links, place, out, parts):
        self.links, self.place, self.out, self.parts = links, place, out, parts
        self.slot = links.slots(3 * len(parts))
        self.sends = []

    def begin(self, k, src):
        place, rows = self.place, self.parts[k]
        out = self.out.at[place.c, rows]
        self.sends.append(self.links.send(src, out, self.slot + 3 * k + 1, place.y_dev))
        self.sends.append(self.links.send(src, out, self.slot + 3 * k, place.core_dev))

    def forward(self, k):
        place = self.place
        block = self.out.at[place.c_y, self.parts[k]]
        self.links.arrive(block, self.slot + 3 * k + 1)
        self.sends.append(self.links.send(block, block, self.slot + 3 * k + 2, place.core_dev))

    def end(self):
        place = self.place
        for k, rows in enumerate(self.parts):
            self.links.arrive(self.out.at[place.c_core, rows], self.slot + 3 * k)
            self.links.arrive(self.out.at[place.c_diag, rows], self.slot + 3 * k + 2)


class ReduceCtx:
    def __init__(self, links, place, part, parts, own, from_core, to_y, from_y):
        self.links, self.place, self.part = links, place, part
        self.parts = [rows if isinstance(rows, tuple) else (rows,) for rows in parts]
        self.own, self.from_core, self.to_y, self.from_y = own, from_core, to_y, from_y
        self.slot = links.slots(3 * len(parts))
        self.loads, self.sends = {}, []

    def begin(self, only=None):
        place = self.place
        for side, y in ((0, place.yo), (1, place.y)):
            for k, rows in enumerate(self.parts):
                if only not in (None, k):
                    continue
                self.links.send(
                    self.part.at[y * 2 + place.co, *rows],
                    self.from_core.at[side, *rows],
                    self.slot + 3 * k + side,
                    place.core_dev,
                )
                if self.own is not None and side == 0:
                    self.load(0, k)

    def load(self, side, k):
        rows = self.parts[k]
        y = self.place.y if side else self.place.yo
        self.loads[side, k] = self.links.local(
            self.part.at[y * 2 + self.place.core, *rows], self.own.at[rows]
        )

    def pair(self, side, k):
        rows = self.parts[k]
        self.links.arrive(self.from_core.at[side, *rows], self.slot + 3 * k + side)
        if self.own is None:
            y = self.place.y if side else self.place.yo
            own = self.part[y * 2 + self.place.core, *rows]
        else:
            self.loads[side, k].wait()
            own = self.own[rows]
        return own.astype(F32) + self.from_core[side, *rows].astype(F32)

    def cross(self, k):
        rows = self.parts[k]
        self.to_y[rows] = self.pair(0, k).astype(BF16)
        if self.own is not None:
            self.load(1, k)
        made = self.links.send(
            self.to_y.at[rows], self.from_y.at[rows], self.slot + 3 * k + 2, self.place.y_dev
        )
        self.sends.append(made)

    def total(self, k):
        rows = self.parts[k]
        sums = self.pair(1, k)
        self.links.arrive(self.from_y.at[rows], self.slot + 3 * k + 2)
        return sums + self.from_y[rows].astype(F32)


def halves(rows):
    return [pl.ds(0, rows // 2), pl.ds(rows // 2, rows // 2)]


def row_factor(values):
    return lax.rsqrt(jnp.mean(values * values, axis=-1, keepdims=True) + EPSILON)


def low_half(shape):
    return lax.rem(lax.broadcasted_iota(jnp.int32, shape, len(shape) - 1), 128) < 64


def partner(values):
    lane = lax.broadcasted_iota(jnp.int32, values.shape, len(values.shape) - 1)
    first = lax.rem(lane, 64) < 32
    return jnp.where(first, pltpu.roll(values, 96, 1), pltpu.roll(values, 32, 1))


def half_sums(values):
    low = low_half(values.shape)
    first = jnp.sum(jnp.where(low, values, 0.0), axis=-1, keepdims=True)
    second = jnp.sum(jnp.where(low, 0.0, values), axis=-1, keepdims=True)
    return jnp.where(low, first, second)


def row_loop(count, body, first=0):
    def step(index, carry):
        body(index)
        return carry

    lax.fori_loop(first, first + count, step, 0)


BLOCK = 256
SHORT = 128


def attention_scores(query, keys, key_bias, first, span):
    scores = lax.dot_general(
        query, keys, (((1,), (1,)), ((), ())), preferred_element_type=F32
    ) * (1.0 / math.sqrt(HEAD_DIM))
    rows = first + lax.broadcasted_iota(jnp.int32, scores.shape, 0)
    columns = lax.broadcasted_iota(jnp.int32, scores.shape, 1)
    return jnp.where(columns <= rows, scores, -1e30) + key_bias[:, :span]


def turn_tables(angles, cos, sin):
    for i in range(16):
        rows = slice(64 * i, 64 * (i + 1))
        cos_high, sin_high = angles[i : i + 1], angles[16 + i : 17 + i]
        cos_low, sin_low = angles[32:96], angles[96:160]
        cos[rows] = cos_high * cos_low - sin_high * sin_low
        sin[rows] = sin_high * cos_low + cos_high * sin_low


def forward_kernel(
    lengths, qkv_weight, out_s, gain_s, x_s, gate_up, down_weight, cotangent, angles, qk_gain,
    qkv_wh, out_wh, gains, normed_h, qkv_raw_h, qkv_low_h, att_low_h, log_sums_h,
    gu_w, dn_w, dout_all, middle, mid_all, head_gain, key_bias,
    kv_pairs, kv_s, dout_s, cos, sin, gain_blocks, qkv_w, out_w, x_all, normed, qkv_raw, qkv_low, att_low, log_sums,
    part, keys, values, from_core, to_y, from_y, mid_low, gu_pairs, gu_rows, gu_s, send_sems, recv_sems, local_sems,
):
    place = Place()
    links = Links(place, send_sems, recv_sems, local_sems)
    fellows = [lax.rem(place.f + d, 8) for d in range(1, 8)]
    place.meet([(f, place.c) for f in fellows] + [place.core_dev, place.y_dev])

    q_columns = pl.ds(pl.multiple_of(256 * place.c, 256), 256)
    for j in range(2):
        pair = pl.ds(pl.multiple_of(1024 + 256 * j + 128 * place.y, 128), 128)
        links.local(qkv_weight.at[:, pair], kv_pairs.at[j]).wait()
    cot_load = links.local(cotangent, dout_s)
    low = low_half(kv_pairs.shape[1:])
    first, second = [], []
    for j in range(2):
        value = kv_pairs[j].astype(F32)
        swapped = pltpu.roll(value, 64, 1)
        first.append(jnp.where(place.core == 0, value, swapped))
        second.append(jnp.where(place.core == 0, swapped, value))
    kv_s[...] = jnp.where(low, first[0], second[1]).astype(BF16)
    qkv_plane = SpreadPlane(
        links,
        place,
        [
            (qkv_weight.at[:, q_columns], lambda f: qkv_w.at[f, :, 0:256]),
            (kv_s, lambda f: qkv_w.at[f, :, 256:384]),
        ],
    )
    qkv_plane.begin_z()
    qkv_plane.begin_x(0)
    qkv_plane.begin_x(1)
    picks = []
    for f in range(8):
        start = pl.multiple_of(512 * f + 128 * place.c, 128)
        picks.append(links.local(gate_up.at[:, :, pl.ds(start, 128)], gu_pairs.at[f]))
    tokens = x_s.shape[0]
    parts = halves(tokens)
    x_spread = SpreadCtx(links, place, x_all, parts)
    for k, rows in enumerate(parts):
        x_spread.begin(k, x_s.at[rows])
    gain_slot = links.slots(8)
    for f in fellows:
        links.send(gain_s, gain_blocks.at[place.f], gain_slot + place.f, (f, place.c))
    kept = [
        links.local(qkv_weight.at[:, q_columns], qkv_w.at[place.f, :, 0:256]),
        links.local(kv_s, qkv_w.at[place.f, :, 256:384]),
        links.local(gain_s, gain_blocks.at[place.f]),
        links.local(x_s, x_all.at[place.c]),
    ]

    root_slot, side_slot = links.slots(1), links.slots(1)
    holds = place.z == place.c
    down = [
        links.copy(out_s, out_w.at[place.x], root_slot, place.z_dev(other))
        for other in place.others[:2]
    ]
    relay = links.copy(out_w.at[place.x], out_w.at[place.x], root_slot, place.z_dev(place.others[0]))
    across = lax.div(place.c, 2) != lax.div(place.z, 2)
    relays = jnp.logical_and(place.inner, across)
    sideways = links.copy(out_s, out_w.at[place.x], side_slot, place.x_dev)
    onward = links.copy(out_w.at[place.x], out_w.at[place.x], side_slot, place.x_dev)
    own = pltpu.make_async_copy(out_s, out_w.at[place.x], local_sems.at[links.locals])
    links.locals += 1

    @pl.when(holds)
    def _():
        for made in down:
            made.start()
        sideways.start()
        own.start()

    rows = gu_s.shape[0]
    for f in range(8):
        picks[f].wait()
        gu_rows[...] = gu_pairs.at[f].reshape(2 * rows, 128)[...].astype(F32)
        for side in range(2):
            first = 1024 * side + 128 * f
            picked = gu_rows[pl.ds(side, rows, stride=2), :]
            gu_s[:, first : first + 128] = picked.astype(BF16)
    step = 32
    chunks = []
    dn_s = down_weight.at[pl.ds(pl.multiple_of(128 * place.c, 128), dn_w.shape[1])]
    for src, dst in ((dn_s, dn_w), (gu_s, gu_w)):
        for first in range(0, src.shape[0], step):
            rows = pl.ds(first, step)
            chunks.append((src.at[rows], lambda f, dst=dst, rows=rows: dst.at[f, rows]))
    plane = SpreadTree(links, place, chunks, 2)
    plane.begin_z()
    cot_load.wait()
    length = lengths[0]
    positions = tokens * place.c + lax.broadcasted_iota(jnp.int32, (tokens, 1), 0)
    dout_s[...] = jnp.where(positions < length, dout_s[...].astype(F32), 0.0).astype(BF16)
    for k in range(plane.plain, len(chunks)):
        plane.begin_x(k)
    for k in range(3):
        plane.begin_x(k)
    qkv_plane.forward(0)
    qkv_plane.forward(1)
    for k in range(3, plane.plain):
        plane.begin_x(k)
    for k in range(plane.plain, len(chunks)):
        plane.cross_z(k)
    last = [
        links.local(gu_s, gu_w.at[place.f]),
        links.local(dn_s, dn_w.at[place.f]),
        links.local(dout_s, dout_all.at[place.c]),
    ]
    turn_tables(angles, cos, sin)
    columns = lax.broadcasted_iota(jnp.int32, key_bias.shape, 1)
    key_bias[...] = jnp.where(columns < length, 0.0, -1e30)
    ones = jnp.ones((1, HEAD_DIM), F32)
    q_gain, k_gain = qk_gain[0:1].astype(F32), qk_gain[1:2].astype(F32)
    head_gain[...] = jnp.zeros_like(head_gain)
    for b in range(2):
        head_gain[b : b + 1] = jnp.concatenate([q_gain, q_gain], axis=1)
    head_gain[2:3] = jnp.concatenate([k_gain, ones], axis=1)
    for f in fellows:
        links.arrive(gain_blocks.at[f], gain_slot + f)
    for made in kept:
        made.wait()
    gains[...] = jnp.zeros_like(gains)
    for f in range(8):
        gains[0:2, 256 * f : 256 * (f + 1)] = gain_blocks[f, 0:2]
    dout = SpreadCtx(links, place, dout_all, parts)
    for k, rows in enumerate(parts):
        x_spread.forward(k)
        dout.begin(k, dout_s.at[rows])
    x_spread.end()
    qkv_plane.end()

    def project(index):
        rows = pl.ds(pl.multiple_of(index * BLOCK, BLOCK), BLOCK)
        source = x_all[index].astype(F32)
        normed[rows] = (source * row_factor(source) * gains[0:1]).astype(BF16)
        weight = qkv_w[...].reshape(normed.shape[1], qkv_w.shape[2])
        raw = jnp.dot(normed[rows], weight, preferred_element_type=F32)
        for b in range(3):
            block = raw[:, 128 * b : 128 * (b + 1)]
            qkv_raw[b, rows] = block
            factor = lax.rsqrt(half_sums(block * block) * (1.0 / HEAD_DIM) + EPSILON)
            scaled = block * factor * head_gain[b : b + 1]
            turned = scaled * cos[rows] + partner(scaled) * sin[rows]
            if b == 2:
                turned = jnp.where(low_half(turned.shape), turned, block)
            qkv_low[b, rows] = turned.astype(BF16)
            if b == 2:
                low = low_half(turned.shape)
                swapped = pltpu.roll(turned, 64, 1)
                keys[rows] = jnp.where(low, turned, swapped).astype(BF16)
                values[rows] = jnp.where(low, swapped, turned).astype(BF16)

    seq = normed.shape[0]
    att_low[...] = jnp.zeros_like(att_low)
    log_sums[...] = jnp.zeros_like(log_sums)
    row_loop(seq // BLOCK, project)
    last += [
        links.local(normed, normed_h),
        links.local(qkv_raw, qkv_raw_h),
        links.local(qkv_low, qkv_low_h),
        links.local(qkv_w, qkv_wh),
    ]

    def heads(index):
        b, half = lax.div(index, 2), lax.rem(index, 2)
        for i in range(seq // BLOCK):
            rows, span = pl.ds(i * BLOCK, BLOCK), (i + 1) * BLOCK
            query = qkv_low[b, rows]
            side = lax.div(lax.broadcasted_iota(jnp.int32, query.shape, 1), 64) == half
            chosen = jnp.where(side, query, 0)
            scores = attention_scores(chosen, keys[:span], key_bias[0:1], i * BLOCK, span)
            top = jnp.max(scores, axis=-1, keepdims=True)
            expanded = jnp.exp(scores - top)
            sums = jnp.sum(expanded, axis=-1, keepdims=True)
            probs = (expanded * (1.0 / sums)).astype(BF16)
            out = jnp.dot(probs, values[:span], preferred_element_type=F32)
            att_low[b, rows] = jnp.where(side, out.astype(BF16), att_low[b, rows])
            log_sums[b, rows] = jnp.where(side, top + jnp.log(sums), log_sums[b, rows])

    @pl.when(relays)
    def _():
        links.arrive(out_w.at[place.x], root_slot)
        relay.start()
        onward.start()

    plane.onward(0)
    row_loop(2, heads)
    plane.onward(1)
    plane.onward(2)
    plane.forward(0)
    row_loop(2, heads, 2)
    plane.onward(3)
    for k in range(1, 3):
        plane.forward(k)

    @pl.when(jnp.logical_not(jnp.logical_or(holds, relays)))
    def _():
        links.arrive(out_w.at[place.x], root_slot)
        onward.start()

    @pl.when(holds)
    def _():
        own.wait()

    for k in range(len(parts)):
        dout.forward(k)
    links.arrive(out_w.at[place.xo], side_slot)

    def project_out(index):
        rows = pl.ds(pl.multiple_of(index * BLOCK, BLOCK), BLOCK)
        sums = jnp.dot(att_low[0, rows], out_w[0], preferred_element_type=F32)
        sums += jnp.dot(att_low[1, rows], out_w[1], preferred_element_type=F32)
        part[index] = sums.astype(BF16)

    row_loop(seq // BLOCK, project_out)
    reduce = ReduceCtx(links, place, part, parts, None, from_core, to_y, from_y)
    reduce.begin()
    last += [
        links.local(att_low, att_low_h),
        links.local(log_sums, log_sums_h),
        links.local(out_w, out_wh),
    ]
    plane.onward(4)
    for k in range(2):
        reduce.cross(k)
    plane.forward(3)
    plane.onward(5)
    plane.onward(6)
    plane.forward(4)
    plane.onward(7)
    plane.forward(5)
    plane.onward(8)
    plane.forward(6)
    mid = SpreadCtx(links, place, mid_all, parts)
    for k, rows in enumerate(parts):
        value = x_all[place.c, rows].astype(F32) + reduce.total(k)
        middle[rows] = value
        mid_low[rows] = (value * row_factor(value) * gains[1:2]).astype(BF16)
        mid.begin(k, mid_low.at[rows])
        last.append(links.local(mid_low.at[rows], mid_all.at[place.c, rows]))
    plane.onward(9)
    plane.forward(7)
    plane.forward(8)
    for k in range(2):
        mid.forward(k)
    plane.forward(9)
    for k in range(plane.plain, len(chunks)):
        plane.onward(k)
    for k in range(plane.plain, len(chunks)):
        plane.forward(k)
    plane.end()
    mid.end()
    dout.end()
    for made in last:
        made.wait()
    links.finish()
    plane.finish()

    @pl.when(holds)
    def _():
        for made in down:
            made.wait_send()
        sideways.wait_send()

    @pl.when(relays)
    def _():
        relay.wait_send()

    @pl.when(jnp.logical_not(holds))
    def _():
        onward.wait_send()


NT = (((1,), (1,)), ((), ()))
TN = (((0,), (0,)), ((), ()))


def norm_back(d_norm, value, gain):
    factor = row_factor(value)
    gain_sum = jnp.sum(d_norm * value * factor, axis=0, keepdims=True)
    scaled = d_norm * gain
    inner = jnp.mean(scaled * value, axis=-1, keepdims=True)
    return factor * scaled - value * (factor * factor * factor * inner), gain_sum


def feed_kernel(
    gu_h, dn_h, dout_h, mid_h, middle_h, gains,
    gu_g, dn_pair, ffn_h, d_middle_h, branch_s, ffn_gain,
    gu_w, dn_w, dout, mid, hidden, d_proj, dn_g, from_x, stage,
    part, from_core, to_y, from_y, middle, d_norm, branch, send_sems, recv_sems, local_sems,
):
    place = Place()
    links = Links(place, send_sems, recv_sems, local_sems)
    shards, rows, width = gu_w.shape
    units, seq = hidden.shape[1], hidden.shape[0]
    tokens = mid.shape[1]
    first = [links.local(mid_h, mid)]
    later, loads = [], []
    for n in range(units // 256):
        gate, up = pl.ds(256 * n, 256), pl.ds(units + 256 * n, 256)
        loads.append([
            links.local(gu_h.at[:, :, gate], gu_w.at[:, :, gate]),
            links.local(gu_h.at[:, :, up], gu_w.at[:, :, up]),
        ])
        if n == 0:
            first += [links.local(dout_h, dout), links.local(dn_h, dn_w)]
    later.append(links.local(middle_h, middle))
    place.meet([place.x_dev, place.core_dev, place.y_dev])
    for made in first:
        made.wait()

    x_slot = links.slots(4)
    for n in range(units // 256):
        for made in loads[n]:
            made.wait()
        gate_columns, up_columns = slice(256 * n, 256 * (n + 1)), slice(units + 256 * n, units + 256 * (n + 1))

        def activation(index, gate_columns=gate_columns, up_columns=up_columns, n=n):
            two = pl.ds(2 * index, 2)
            low = mid[two].reshape(2 * tokens, width)
            gate = jnp.dot(
                low, gu_w[:, :, gate_columns].reshape(width, 256), preferred_element_type=F32
            )
            up = jnp.dot(
                low, gu_w[:, :, up_columns].reshape(width, 256), preferred_element_type=F32
            )
            d_hidden = lax.dot_general(
                dout[two].reshape(2 * tokens, width), dn_w[2 * n : 2 * n + 2].reshape(256, width), NT,
                preferred_element_type=F32,
            )
            at = pl.ds(pl.multiple_of(index * 2 * tokens, 2 * tokens), 2 * tokens)
            sigmoid = 1.0 / (1.0 + jnp.exp(-gate))
            silu = gate * sigmoid
            hidden[at, gate_columns] = (silu * up).astype(BF16)
            d_gate = d_hidden * up * (sigmoid * (1.0 + gate * (1.0 - sigmoid)))
            d_proj[at, gate_columns] = d_gate.astype(BF16)
            d_proj[at, up_columns] = (d_hidden * silu).astype(BF16)

        row_loop(2, activation)
        left = hidden[:, gate_columns].T

        def down_grad(j, left=left, n=n):
            wide = pl.ds(pl.multiple_of(512 * j, 512), 512)
            right = dout[:, :, wide].reshape(seq, 512)
            grad = jnp.dot(left, right, preferred_element_type=F32).astype(BF16)
            dn_g[n, 0, :, wide] = grad[:128]
            dn_g[n, 1, :, wide] = grad[128:]

        row_loop(4, down_grad)
        links.send(dn_g.at[n, place.xo], from_x.at[n], x_slot + n, place.x_dev)

    def mid_grad(f):
        grad = lax.dot_general(d_proj[...], gu_w[f], NT, preferred_element_type=F32)
        columns = pl.ds(pl.multiple_of(rows * f, rows), rows)
        part[:, :, columns] = grad.astype(BF16).reshape(4, tokens, rows)

    parts = halves(tokens)
    sides = [(slice(None), side) for side in halves(width)]
    dmid = ReduceCtx(links, place, part, sides, None, from_core, to_y, from_y)
    quarter = shards // 4
    row_loop(2 * quarter, mid_grad)
    dmid.begin(0)
    row_loop(quarter, mid_grad, 2 * quarter)
    dmid.cross(0)
    row_loop(quarter, mid_grad, 3 * quarter)
    dmid.begin(1)

    def gate_up_grad(z):
        columns = pl.ds(pl.multiple_of(2 * rows * z, 2 * rows), 2 * rows)
        left = mid[:, :, columns].reshape(seq, 2 * rows).T
        for j in range(4):
            wide = slice(512 * j, 512 * (j + 1))
            grad = jnp.dot(left, d_proj[:, wide], preferred_element_type=F32)
            stage[:, :, wide] = grad.astype(BF16).reshape(2, rows, 512)
        made = pltpu.make_async_copy(stage, gu_g.at[z], local_sems.at[links.locals])
        made.start()
        made.wait()

    row_loop(1, gate_up_grad)
    dmid.cross(1)
    row_loop(3, gate_up_grad, 1)
    links.locals += 1

    def feed_out(index):
        at = pl.ds(pl.multiple_of(index * 2 * tokens, 2 * tokens), 2 * tokens)
        for j in range(4):
            wide = slice(512 * j, 512 * (j + 1))
            right = dn_w[:, :, wide].reshape(units, 512)
            sums = jnp.dot(hidden[at], right, preferred_element_type=F32)
            mid[pl.ds(2 * index, 2), :, wide] = sums.astype(BF16).reshape(2, tokens, 512)

    row_loop(2, feed_out)
    later.append(links.local(mid, ffn_h))
    later[0].wait()
    for k in range(2):
        d_norm[sides[k]] = dmid.total(k)
    gain_sum = None
    for k, at in enumerate(parts):
        grad, term = norm_back(d_norm[at], middle[at], gains[1:2])
        gain_sum = term if gain_sum is None else gain_sum + term
        middle[at] = grad + dout[place.c, at].astype(F32)
        branch[at] = middle[at].astype(BF16)
        later.append(links.local(middle.at[at], d_middle_h.at[at]))
        later.append(links.local(branch.at[at], branch_s.at[at]))
    ffn_gain[...] = gain_sum
    for n in range(4):
        links.arrive(from_x.at[n], x_slot + n)
        pair = dn_g[n, place.x].astype(F32) + from_x[n].astype(F32)
        from_x[n] = pair.astype(BF16)
        later.append(links.local(from_x.at[n], dn_pair.at[n]))
    for made in later[1:]:
        made.wait()
    links.finish()


def backward_kernel(
    gu_g, dn_pair, ffn_part, middle_h, d_middle_h, branch_s, x_h, lengths, gains, ffn_gain,
    angles, head_gain, key_bias,
    normed_h, qkv_raw_h, qkv_low_h, att_low_h, log_sums_h, qkv_wh, out_wh,
    gu_all, dn_all, layer_out, qkv_all, out_all, input_grad, stats,
    own, from_x, from_z, via,
    ctx_own, from_core1, to_y1, from_y1, from_core2, to_y2, from_y2,
    middle, x_s, d_middle, branch_all, part,
    cos, sin, qkv_raw, qkv_low, att_low, log_sums, qkv_w, out_w,
    keys, values, d_att, d_low, d_keys, d_values, gain_g,
    qkv_g, qkv_x, qkv_z, out_g, out_x, out_z,
    mine, plane_stats, ctx_stats, send_sems, recv_sems, local_sems,
):
    place = Place()
    links = Links(place, send_sems, recv_sems, local_sems)
    fellows = [lax.rem(place.f + d, 8) for d in range(1, 8)]
    place.meet(
        [(f, place.c) for f in fellows] + [place.core_dev, place.y_dev, place.diag_dev]
    )
    step = from_x.shape[2]
    chunks, where = [], []
    for first in range(0, dn_pair.shape[1], step):
        rows = pl.ds(first, step)
        chunks.append(lambda x, rows=rows: dn_pair.at[:, rows])
        where.append((dn_all, rows))
    summed = len(chunks)
    for first in range(0, gu_g.shape[2], step):
        rows = pl.ds(first, step)
        chunks.append(lambda x, rows=rows: gu_g.at[:, x, rows])
        where.append((gu_all, rows))
    count = len(chunks)
    plane = ReduceTree(links, place, chunks, from_x, from_z, via, own, summed)
    outs = [SpreadCtx(links, place, out, [rows]) for out, rows in where]
    kept = []

    def end(k):
        total = plane.end(k)
        if k + own.shape[0] < count:
            plane.load(k + own.shape[0])
        out, rows = where[k]
        outs[k].begin(0, total)
        kept.append(links.local(total, out.at[place.c, rows]))

    tokens, width = middle.shape
    parts = halves(tokens)
    branch = SpreadCtx(links, place, branch_all, parts)
    for k, rows in enumerate(parts):
        branch.begin(k, branch_s.at[rows])
    for k in range(summed, count - 1):
        plane.send_x(k)
    ffn = ReduceCtx(links, place, ffn_part, parts, ctx_own, from_core1, to_y1, from_y1)
    ffn.begin()
    for k in range(own.shape[0]):
        plane.load(k)
    late = [
        links.local(a, b)
        for a, b in (
            (branch_s, branch_all.at[place.c]),
            (out_wh, out_w), (qkv_low_h, qkv_low), (att_low_h, att_low), (log_sums_h, log_sums),
            (qkv_raw_h, qkv_raw), (qkv_wh, qkv_w),
            (middle_h, middle), (d_middle_h, d_middle), (x_h, x_s),
        )
    ]
    turn_tables(angles, cos, sin)
    gain_g[...] = jnp.zeros_like(gain_g)
    d_keys[...] = jnp.zeros_like(d_keys)
    d_low[...] = jnp.zeros_like(d_low)
    d_values[...] = jnp.zeros_like(d_values)
    plane.middle(0)
    plane.middle(1)
    for k in range(2):
        ffn.cross(k)
    branch.forward(0)
    plane.combine(0)
    branch.forward(1)
    plane.middle(2)
    plane.combine(1)
    branch.end()
    for made in late:
        made.wait()

    root = 1.0 / math.sqrt(HEAD_DIM)
    seq = 4 * tokens

    def prepare(index):
        rows = pl.ds(pl.multiple_of(index * BLOCK, BLOCK), BLOCK)
        block = qkv_low[2, rows].astype(F32)
        low = low_half(block.shape)
        swapped = pltpu.roll(block, 64, 1)
        keys[rows] = jnp.where(low, block, swapped).astype(BF16)
        values[rows] = jnp.where(low, swapped, block).astype(BF16)
        for b in range(2):
            d_att[b, rows] = lax.dot_general(
                branch_all[index], out_w[b], NT, preferred_element_type=F32
            ).astype(BF16)

    row_loop(seq // BLOCK, prepare)
    for b in range(2):
        left = att_low[b].T
        for j in range(8):
            columns = slice(256 * j, 256 * (j + 1))
            right = branch_all[:, :, columns].reshape(seq, 256)
            out_g[b, :, columns] = jnp.dot(left, right, preferred_element_type=F32).astype(BF16)
    out_slot = links.slots(1)
    links.send(out_g.at[place.xo], out_x, out_slot, place.x_dev)
    plane.send_x(count - 1)
    links.settle(branch.sends)
    normed_load = links.local(normed_h, branch_all)
    plane.middle(3)

    def unturn(row, rows, grads, block):
        back = grads * cos[rows] + partner(grads * sin[rows])
        factor = lax.rsqrt(half_sums(block * block) * (1.0 / HEAD_DIM) + EPSILON)
        gain_term = jnp.sum(back * block * factor, axis=0, keepdims=True)
        scaled = back * head_gain[row : row + 1]
        inner = half_sums(scaled * block) * (1.0 / HEAD_DIM)
        return factor * scaled - block * (factor * factor * factor * inner), gain_term

    def heads(index):
        b, half = lax.div(index, 2), lax.rem(index, 2)
        for i in range(seq // SHORT):
            rows, span = pl.ds(i * SHORT, SHORT), (i + 1) * SHORT
            query = qkv_low[b, rows]
            lane = lax.broadcasted_iota(jnp.int32, query.shape, 1)
            side = lax.div(lane, 64) == half
            chosen = jnp.where(side, query, 0)
            d_chosen = jnp.where(side, d_att[b, rows], 0)
            logs = jnp.max(jnp.where(side, log_sums[b, rows], -1e30), axis=-1, keepdims=True)
            scores = attention_scores(chosen, keys[:span], key_bias[0:1], i * SHORT, span)
            probs = jnp.exp(scores - logs)
            d_probs = lax.dot_general(d_chosen, values[:span], NT, preferred_element_type=F32)
            delta = jnp.sum(probs * d_probs, axis=-1, keepdims=True)
            d_scores = (probs * (d_probs - delta)).astype(BF16)
            d_query = jnp.dot(d_scores, keys[:span], preferred_element_type=F32) * root
            d_keys[:span] += lax.dot_general(d_scores, chosen, TN, preferred_element_type=F32)
            d_values[:span] += lax.dot_general(
                probs.astype(BF16), d_chosen, TN, preferred_element_type=F32
            )
            d_low[b, rows] = jnp.where(side, d_query.astype(BF16), d_low[b, rows])

    def unturn_queries(index):
        rows = pl.ds(pl.multiple_of(index * BLOCK, BLOCK), BLOCK)
        for b in range(2):
            grads = d_low[b, rows].astype(F32)
            d_block, gain_term = unturn(0, rows, grads, qkv_raw[b, rows])
            d_low[b, rows] = d_block.astype(BF16)
            gain_g[0:1] += gain_term

    row_loop(2, heads)
    plane.combine(2)
    end(0)
    row_loop(2, heads, 2)
    plane.middle(4)
    plane.combine(3)
    end(1)
    row_loop(seq // BLOCK, unturn_queries)

    def finish(index):
        rows = pl.ds(pl.multiple_of(index * BLOCK, BLOCK), BLOCK)
        k_sum, v_sum = d_keys[rows], d_values[rows]
        low = low_half(k_sum.shape)
        k_sum = (k_sum + pltpu.roll(k_sum, 64, 1)) * root
        v_sum = v_sum + pltpu.roll(v_sum, 64, 1)
        grads = jnp.where(low, k_sum, v_sum).astype(BF16).astype(F32)
        d_block, gain_term = unturn(2, rows, grads, qkv_raw[2, rows])
        d_low[2, rows] = jnp.where(low, d_block, grads).astype(BF16)
        gain_g[1:2] += gain_term
        for j in range(4):
            columns = slice(512 * j, 512 * (j + 1))
            sums = jnp.zeros((BLOCK, 512), F32)
            for b in range(3):
                weight = qkv_w[columns, 128 * b : 128 * (b + 1)]
                sums += lax.dot_general(d_low[b, rows], weight, NT, preferred_element_type=F32)
            part[index, :, columns] = sums.astype(BF16)

    row_loop(seq // BLOCK, finish)

    dnorm = ReduceCtx(links, place, part, parts, None, from_core2, to_y2, from_y2)
    dnorm.begin()
    normed_load.wait()
    for b in range(3):
        left = d_low[b].T
        for f in range(8):
            right = branch_all[:, :, 256 * f : 256 * (f + 1)].reshape(seq, 256)
            qkv_g[f // 2, f % 2, 128 * b : 128 * (b + 1)] = jnp.dot(
                left, right, preferred_element_type=F32
            ).astype(BF16)
    qkv_step = qkv_x.shape[2]
    qkv_rows = [pl.ds(k * qkv_step, qkv_step) for k in range(qkv_x.shape[0])]
    qkv_chunks = [lambda x, rows=rows: qkv_g.at[:, x, rows] for rows in qkv_rows]
    qkv_plane = ReducePlane(links, place, qkv_chunks, qkv_x, qkv_z)
    qkv_outs = [SpreadCtx(links, place, qkv_all, [rows]) for rows in qkv_rows]
    for k in range(len(qkv_chunks)):
        qkv_plane.send_x(k)
    links.arrive(out_x, out_slot)
    root_slot, final_slot = links.slots(3), links.slots(1)
    holds = place.z == place.c
    out_mine = out_g.at[place.x]
    out_mine[...] = (out_mine[...].astype(F32) + out_x[...].astype(F32)).astype(BF16)
    rank = place.rank(place.z, place.c)
    to_root = links.copy(
        out_mine,
        out_z.at[lax.rem(rank, 3)],
        root_slot + lax.rem(rank, 3),
        (place.c * 2 + place.x, place.c),
    )

    @pl.when(jnp.logical_not(holds))
    def _():
        to_root.start()

    for k in range(2):
        dnorm.cross(k)
    plane.combine(4)
    end(2)
    outs[0].forward(0)
    outs[1].forward(0)
    end(3)
    for k, rows in enumerate(parts):
        value = middle[rows] + ffn.total(k)
        positions = lax.broadcasted_iota(jnp.int32, (value.shape[0], 1), 0)
        positions += tokens * place.c + k * value.shape[0]
        layer_out[rows] = jnp.where(positions < lengths[0], value, 0.0).astype(BF16)
    plane.middle(5)
    outs[2].forward(0)
    attn_gain = None
    for k, rows in enumerate(parts):
        grad, term = norm_back(dnorm.total(k), x_s[rows].astype(F32), gains[0:1])
        attn_gain = term if attn_gain is None else attn_gain + term
        input_grad[rows] = (d_middle[rows] + grad).astype(BF16)
    mine[...] = jnp.zeros_like(mine)
    for f in range(8):
        mine[f, 0:1] = attn_gain[:, 256 * f : 256 * (f + 1)]
        mine[f, 1:2] = ffn_gain[:, 256 * f : 256 * (f + 1)]
        mine[f, 2:3, 0:128] = gain_g[0:1]
        mine[f, 2:3, 128:256] = gain_g[1:2]
    plane_slot, ctx_slot = links.slots(8), links.slots(4)
    for f in fellows:
        links.send(mine.at[f], plane_stats.at[place.f], plane_slot + place.f, (f, place.c))
    plane_stats[place.f] = mine[place.f]

    end(4)
    outs[3].forward(0)
    for k in range(len(qkv_chunks)):
        qkv_plane.middle(k)
    plane.combine(5)
    end(5)
    for f in fellows:
        links.arrive(plane_stats.at[f], plane_slot + f)
    sums = plane_stats[0]
    for f in range(1, 8):
        sums += plane_stats[f]
    ctx_stats[place.c] = sums
    for device in (place.core_dev, place.y_dev, place.diag_dev):
        links.send(ctx_stats.at[place.c], ctx_stats.at[place.c], ctx_slot + place.c, device)

    final = [
        links.copy(out_all, out_all, final_slot, device)
        for device in (place.core_dev, place.y_dev)
    ]
    onward = links.copy(out_all, out_all, final_slot, place.core_dev)

    @pl.when(holds)
    def _():
        sums = out_mine[...].astype(F32)
        for other in range(3):
            links.arrive(out_z.at[other], root_slot + other)
            sums += out_z[other].astype(F32)
        out_all[...] = sums.astype(BF16)
        for made in final:
            made.start()

    for k in range(len(qkv_chunks)):
        total = qkv_plane.end(k)
        qkv_outs[k].begin(0, total)
        kept.append(links.local(total, qkv_all.at[place.c, qkv_rows[k]]))
    for k in range(4, count):
        outs[k].forward(0)
    relays = place.c_y == place.z

    @pl.when(jnp.logical_not(holds))
    def _():
        links.arrive(out_all, final_slot)

    @pl.when(relays)
    def _():
        onward.start()

    for c in (place.c_core, place.c_y, place.c_diag):
        links.arrive(ctx_stats.at[c], ctx_slot + c)
    stats[...] = ((ctx_stats[0] + ctx_stats[1]) + ctx_stats[2]) + ctx_stats[3]
    for out in qkv_outs:
        out.forward(0)
    for out in outs + qkv_outs:
        out.end()
    for made in kept:
        made.wait()
    links.finish()
    plane.finish()
    qkv_plane.finish()

    @pl.when(jnp.logical_not(holds))
    def _():
        to_root.wait_send()

    @pl.when(relays)
    def _():
        onward.wait_send()

    @pl.when(holds)
    def _():
        for made in final:
            made.wait_send()


def finish_kernel(
    gu_parts, dn_parts, out_s, qkv_parts, layer_s, input_s, stats,
    out, dn_out, out_out, qkv_out, layer_out, input_out, attn_out, ffn_out, pairs, sems,
):
    rows = gu_parts.shape[1]
    first = pl.multiple_of(pl.program_id(0) * rows, rows)
    sent = []
    for c in range(4):
        for f in range(8):
            b = 4 * f + c
            for side in range(2):
                column = 1024 * side + 128 * f
                block = gu_parts[c, :, column : column + 128]
                pairs[b, pl.ds(side, rows, stride=2), :] = block.astype(F32)
            made = pltpu.make_async_copy(
                pairs.at[b].reshape(rows, 2, 128),
                out.at[pl.ds(first, rows), :, pl.ds(128 * b, 128)],
                sems.at[b],
            )
            made.start()
            sent.append(made)
    dn_out[...] = dn_parts[...].astype(F32)
    out_out[...] = out_s[...].astype(F32)
    layer_out[...] = layer_s[...]
    input_out[...] = input_s[...]

    @pl.when(pl.program_id(0) == 0)
    def _():
        attn_out[...] = stats[0:1]
        ffn_out[...] = stats[1:2]
        for c in range(4):
            qkv_out[:, 256 * c : 256 * (c + 1)] = qkv_parts[c, 0:256].astype(F32).T
        for y in range(2):
            for j in range(2):
                from_row = 256 + 64 * j
                both = [qkv_parts[2 * y + core, from_row : from_row + 64] for core in range(2)]
                column = 1024 + 256 * j + 128 * y
                qkv_out[:, column : column + 128] = jnp.concatenate(both, axis=0).astype(F32).T

    for made in sent:
        made.wait()


def shaped(shape, kind=BF16):
    return jax.ShapeDtypeStruct(shape, kind)


def call(kernel, ins, outs, scratch=(), sems=None, number=None, flops=0):
    scratch = list(scratch)
    extra = {}
    if sems is not None:
        scratch += [pltpu.SemaphoreType.DMA((n,)) for n in sems]
        extra = dict(collective_id=number, has_side_effects=True)
    return pl.pallas_call(
        kernel,
        out_shape=tuple(shape for shape, _ in outs),
        in_specs=[spec for _, spec in ins],
        out_specs=tuple(spec for _, spec in outs),
        scratch_shapes=scratch,
        compiler_params=pltpu.CompilerParams(vmem_limit_bytes=VMEM_BYTES, **extra),
    )(*[array for array, _ in ins])


def split_heads(
    inputs,
    cotangent,
    lengths,
    qkv_weight,
    out_weight,
    gate_up,
    down_weight,
    attn_gain,
    ffn_gain,
    qk_gain,
):
    tokens, width = inputs.shape[1:]
    seq = tokens * 4
    source = inputs[0]
    rows, parts, units = gate_up.shape
    down_rows = down_weight.shape[0] // 4
    gain_s = jnp.concatenate(
        [attn_gain[None], ffn_gain[None], jnp.zeros((6, rows), BF16)], axis=0
    ).astype(F32)

    half_dim = HEAD_DIM // 2
    frequency = 10000.0 ** (-2.0 * np.arange(half_dim) / HEAD_DIM)
    turns = [np.arange(0, seq, 64)[:, None] * frequency, np.arange(64)[:, None] * frequency]
    signs = np.repeat([-1.0, 1.0, -1.0, 1.0], half_dim)
    angles = jnp.asarray(
        np.concatenate(
            [part for t in turns for part in (np.tile(np.cos(t), 4), np.tile(np.sin(t), 4) * signs)]
        ),
        F32,
    )
    table = pltpu.VMEM((seq, 128), F32)
    (
        qkv_w, out_w, gains, normed, qkv_raw, qkv_low, att_low, log_sums,
        gu_w, dn_w, dout_all, middle, mid_all, head_gain, key_bias,
    ) = call(
        forward_kernel,
        [(lengths, pl.BlockSpec(memory_space=pltpu.SMEM))]
        + [
            (a, HBM)
            for a in (qkv_weight, out_weight, gain_s, source, gate_up, down_weight, cotangent[0])
        ]
        + [(angles, VMEM), (qk_gain, VMEM)],
        [
            (shaped((8, rows, 384)), HBM),
            (shaped((2, out_weight.shape[0], width)), HBM),
            (shaped((8, width), F32), VMEM),
            (shaped((seq, width)), HBM),
            (shaped((3, seq, 128), F32), HBM),
            (shaped((3, seq, 128)), HBM),
            (shaped((2, seq, 128)), HBM),
            (shaped((2, seq, 128), F32), HBM),
            (shaped((8, rows, width)), HBM),
            (shaped((8, down_rows, width)), HBM),
            (shaped((4, tokens, width)), HBM),
            (shaped((tokens, width), F32), VMEM),
            (shaped((4, tokens, width)), HBM),
            (shaped((8, 128), F32), VMEM),
            (shaped((8, seq), F32), VMEM),
        ],
        [
            pltpu.VMEM((2, rows, 128), BF16),
            pltpu.VMEM((rows, 128), BF16),
            pltpu.VMEM((tokens, width), BF16),
            table,
            table,
            pltpu.VMEM((8, 8, rows), F32),
            pltpu.VMEM((8, rows, 384), BF16),
            pltpu.VMEM((2, out_weight.shape[0], width), BF16),
            pltpu.VMEM((4, tokens, width), BF16),
            pltpu.VMEM((seq, width), BF16),
            pltpu.VMEM((3, seq, 128), F32),
            pltpu.VMEM((3, seq, 128), BF16),
            pltpu.VMEM((2, seq, 128), BF16),
            pltpu.VMEM((2, seq, 128), F32),
            pltpu.VMEM((4, tokens, width), BF16),
            pltpu.VMEM((seq, 128), BF16),
            pltpu.VMEM((seq, 128), BF16),
            pltpu.VMEM((2, tokens, width), BF16),
            pltpu.VMEM((tokens, width), BF16),
            pltpu.VMEM((tokens, width), BF16),
            pltpu.VMEM((tokens, width), BF16),
            pltpu.VMEM((8, rows, 2, 128), BF16),
            pltpu.VMEM((2 * rows, 128), F32),
            pltpu.VMEM((rows, width), BF16),
        ],
        sems=(180, 170, 32),
        number=0,
    )
    qkv_w = qkv_w.reshape(width, 384)
    block = pltpu.VMEM((tokens, width), BF16)
    pair = pltpu.VMEM((2, tokens, width), BF16)
    whole = pltpu.VMEM((4, tokens, width), BF16)
    hidden_units = units // 4
    gu_g, dn_pair, ffn_part, d_middle, branch_s, ffn_gain_part = call(
        feed_kernel,
        [(a, HBM) for a in (gu_w, dn_w, dout_all, mid_all, middle)] + [(gains, VMEM)],
        [
            (shaped((4, 2, rows, width)), HBM),
            (shaped((4, down_rows, width)), HBM),
            (shaped((4, tokens, width)), HBM),
            (shaped((tokens, width), F32), HBM),
            (shaped((tokens, width)), HBM),
            (shaped((1, width), F32), VMEM),
        ],
        [
            pltpu.VMEM((8, rows, width), BF16),
            pltpu.VMEM((8, down_rows, width), BF16),
            whole,
            whole,
            pltpu.VMEM((seq, hidden_units), BF16),
            pltpu.VMEM((seq, parts * hidden_units), BF16),
            pltpu.VMEM((4, 2, down_rows, width), BF16),
            pltpu.VMEM((4, down_rows, width), BF16),
            pltpu.VMEM((2, rows, width), BF16),
            whole,
            pair,
            block,
            block,
            pltpu.VMEM((tokens, width), F32),
            pltpu.VMEM((tokens, width), F32),
            block,
        ],
        sems=(16, 16, 24),
        number=2,
    )
    step = 64
    count = (rows + down_rows) // step
    heads = pltpu.VMEM((seq, 128), BF16)
    gu_all, dn_all, layer_out, qkv_all, out_all, input_grad, stats = call(
        backward_kernel,
        [
            (gu_g, HBM),
            (dn_pair, HBM),
            (ffn_part, HBM),
            (middle, HBM),
            (d_middle, HBM),
            (branch_s, HBM),
            (source, HBM),
            (lengths, pl.BlockSpec(memory_space=pltpu.SMEM)),
            (gains, VMEM),
            (ffn_gain_part, VMEM),
            (angles, VMEM),
            (head_gain, VMEM),
            (key_bias, VMEM),
            (normed.reshape(4, tokens, width), HBM),
        ]
        + [(a, HBM) for a in (qkv_raw, qkv_low, att_low, log_sums, qkv_w, out_w)],
        [
            (shaped((4, rows, width)), HBM),
            (shaped((4, down_rows, width)), HBM),
            (shaped((tokens, width)), VMEM),
            (shaped((4, 384, rows)), HBM),
            (shaped((128, width)), VMEM),
            (shaped((tokens, width)), VMEM),
            (shaped((8, rows), F32), VMEM),
        ],
        [
            pltpu.VMEM((4, 4, step, width), BF16),
            pltpu.VMEM((rows // step, 4, step, width), BF16),
            pltpu.VMEM((count, 2, step, width), BF16),
            pltpu.VMEM((count, 2, step, width), BF16),
            block, pair, block, block, pair, block, block,
            pltpu.VMEM((tokens, width), F32),
            block,
            pltpu.VMEM((tokens, width), F32),
            pltpu.VMEM((4, tokens, width), BF16),
            pltpu.VMEM((4, tokens, width), BF16),
            table,
            table,
            pltpu.VMEM((3, seq, 128), F32),
            pltpu.VMEM((3, seq, 128), BF16),
            pltpu.VMEM((2, seq, 128), BF16),
            pltpu.VMEM((2, seq, 128), F32),
            pltpu.VMEM((width, 384), BF16),
            pltpu.VMEM((2, 128, width), BF16),
            heads,
            heads,
            pltpu.VMEM((2, seq, 128), BF16),
            pltpu.VMEM((3, seq, 128), BF16),
            table,
            table,
            pltpu.VMEM((8, 128), F32),
            pltpu.VMEM((4, 2, 384, rows), BF16),
            pltpu.VMEM((2, 4, 192, rows), BF16),
            pltpu.VMEM((2, 3, 192, rows), BF16),
            pltpu.VMEM((2, 128, width), BF16),
            pltpu.VMEM((128, width), BF16),
            pltpu.VMEM((3, 128, width), BF16),
            pltpu.VMEM((8, 8, rows), F32),
            pltpu.VMEM((8, 8, rows), F32),
            pltpu.VMEM((4, 8, rows), F32),
        ],
        sems=(120, 120, 50),
        number=1,
    )
    some = 64
    steps = rows // some
    few = down_rows // steps
    out_rows = out_weight.shape[0]
    block_of = lambda n: pl.BlockSpec((n, width), lambda i: (i, 0))
    fixed = lambda *shape: pl.BlockSpec(shape, lambda i: (0,) * len(shape))
    gate_up_grad, down_grad, out_grad, qkv_grad, layer_out, input_grad, attn_g, ffn_g = pl.pallas_call(
        finish_kernel,
        grid=(steps,),
        in_specs=[
            pl.BlockSpec((4, some, width), lambda i: (0, i, 0)),
            pl.BlockSpec((4, few, width), lambda i: (0, i, 0)),
            block_of(out_rows // steps),
            fixed(4, 384, rows),
            block_of(tokens // steps),
            block_of(tokens // steps),
            fixed(8, rows),
        ],
        out_specs=[
            HBM,
            pl.BlockSpec((4, few, width), lambda i: (0, i, 0)),
            block_of(out_rows // steps),
            fixed(rows, qkv_weight.shape[1]),
            block_of(tokens // steps),
            block_of(tokens // steps),
            fixed(1, rows),
            fixed(1, rows),
        ],
        out_shape=[
            shaped((rows, parts, units), F32),
            shaped((4, down_rows, width), F32),
            shaped((out_rows, width), F32),
            shaped((rows, qkv_weight.shape[1]), F32),
            shaped((tokens, width)),
            shaped((tokens, width)),
            shaped((1, rows), F32),
            shaped((1, rows), F32),
        ],
        scratch_shapes=[
            pltpu.VMEM((32, 2 * some, 128), F32),
            pltpu.SemaphoreType.DMA((32,)),
        ],
        compiler_params=pltpu.CompilerParams(vmem_limit_bytes=VMEM_BYTES),
    )(gu_all, dn_all, out_all, qkv_all, layer_out, input_grad, stats)
    return (
        layer_out[None],
        input_grad[None],
        qkv_grad,
        out_grad,
        gate_up_grad,
        down_grad.reshape(4 * down_rows, width),
        attn_g[0],
        ffn_g[0],
        jnp.stack([stats[2, :64] + stats[2, 64:128], stats[2, 128:192]]),
    )


def solution(mesh):
    sizes = (mesh.shape["fsdp"], mesh.shape["ctx"])
    return jax.shard_map(
        split_heads if sizes == (8, 4) else on_device,
        mesh=mesh,
        in_specs=(
            P("fsdp", "ctx", None),
            P("fsdp", "ctx", None),
            P("fsdp"),
            P("fsdp", None),
            P("fsdp", None),
            P("fsdp", None, None),
            P("fsdp", None),
            P("fsdp"),
            P("fsdp"),
            P(),
        ),
        out_specs=(
            P("fsdp", "ctx", None),
            P("fsdp", "ctx", None),
            P("fsdp", None),
            P("fsdp", None),
            P("fsdp", None, None),
            P("fsdp", None),
            P("fsdp"),
            P("fsdp"),
            P(),
        ),
        check_vma=False,
    )
```

```python
import functools
import math

import jax
import jax.numpy as jnp
import numpy as np
from jax import lax
from jax.experimental import pallas as pl
from jax.experimental.pallas import tpu as pltpu
from jax.sharding import PartitionSpec as P

HEADS = 16
KV_HEADS = 4
HEAD_DIM = 64


EPSILON = 1e-06


def root_norm(values, norm_gain):
    factor = lax.rsqrt(jnp.mean(values * values, axis=-1, keepdims=True) + EPSILON)
    return values * factor * norm_gain


def rotation_tables(positions):
    half_dim = HEAD_DIM // 2
    frequency = 10000.0 ** (-(2.0 * jnp.arange(half_dim, dtype=jnp.float32)) / HEAD_DIM)
    angles = positions.astype(jnp.float32)[:, None] * frequency[None, :]
    return (jnp.cos(angles), jnp.sin(angles))


def rotate(values, cos_table, sin_table):
    half_dim = values.shape[-1] // 2
    lower_half = values[..., :half_dim]
    upper_half = values[..., half_dim:]
    cos_part = cos_table[:, None, :]
    sin_part = sin_table[:, None, :]
    return jnp.concatenate(
        [
            lower_half * cos_part - upper_half * sin_part,
            upper_half * cos_part + lower_half * sin_part,
        ],
        axis=-1,
    )


def prepare_heads(qkv_out, head_gain, cos_table, sin_table):
    row_count = qkv_out.shape[0]
    query_cols = HEADS * HEAD_DIM
    key_cols = KV_HEADS * HEAD_DIM
    queries = qkv_out[:, :query_cols].reshape(row_count, HEADS, HEAD_DIM)
    key_part = qkv_out[:, query_cols : query_cols + key_cols].reshape(row_count, KV_HEADS, HEAD_DIM)
    value_part = qkv_out[:, query_cols + key_cols :]
    queries = rotate(root_norm(queries, head_gain[0]), cos_table, sin_table).reshape(
        row_count, query_cols
    )
    key_part = rotate(root_norm(key_part, head_gain[1]), cos_table, sin_table).reshape(
        row_count, key_cols
    )
    return (queries, key_part, value_part)


def activate(projected):
    gate_part = projected[:, 0]
    return gate_part * jax.nn.sigmoid(gate_part) * projected[:, 1]


def contract_rows(left, right):
    return lax.dot_general(
        left, right, (((0,), (0,)), ((), ())), preferred_element_type=jnp.float32
    )


def contract_cols(left, right):
    return lax.dot_general(
        left, right, (((1,), (1,)), ((), ())), preferred_element_type=jnp.float32
    )


def on_device(
    inputs,
    cotangent,
    lengths,
    qkv_weight,
    out_weight,
    gate_up,
    down_weight,
    attn_gain,
    ffn_gain,
    qk_gain,
):
    token_count = inputs.shape[1]
    group = HEADS // KV_HEADS
    key_cols = KV_HEADS * HEAD_DIM
    seq_len = token_count * lax.axis_size("ctx")
    positions = lax.axis_index("ctx") * token_count + jnp.arange(token_count, dtype=jnp.int32)
    length = lengths[0]
    row_keep = (positions < length).astype(jnp.float32)[:, None]
    inv_root = 1.0 / math.sqrt(HEAD_DIM)
    source = inputs[0].astype(jnp.float32)
    qkv_full, out_full, attn_full, ffn_full = (
        lax.all_gather(qkv_weight, "fsdp", axis=0, tiled=True),
        lax.all_gather(out_weight, "fsdp", axis=0, tiled=True),
        lax.all_gather(attn_gain, "fsdp", axis=0, tiled=True),
        lax.all_gather(ffn_gain, "fsdp", axis=0, tiled=True),
    )
    attn_norm = attn_full.astype(jnp.float32)
    ffn_norm = ffn_full.astype(jnp.float32)
    normed = root_norm(source, attn_norm).astype(jnp.bfloat16)
    qkv_out = jnp.dot(normed, qkv_full, preferred_element_type=jnp.float32)
    cos_table, sin_table = rotation_tables(positions)
    head_gain = qk_gain.astype(jnp.float32)

    def head_pieces(qkv_values, gain_values):
        return prepare_heads(qkv_values, gain_values, cos_table, sin_table)

    head_values, head_pull = jax.vjp(head_pieces, qkv_out, head_gain)
    queries, key_part, value_part = head_values
    query_low = queries.astype(jnp.bfloat16).reshape(token_count, KV_HEADS, group, HEAD_DIM)
    kv_local = jnp.concatenate([key_part, value_part], axis=1).astype(jnp.bfloat16)
    kv_whole = lax.all_gather(kv_local, "ctx", axis=0, tiled=True)
    block = 512
    block_total = seq_len // block
    kv_blocks = kv_whole.reshape(block_total, block, 2, KV_HEADS, HEAD_DIM)
    starts = jnp.arange(block_total, dtype=jnp.int32) * block

    def block_scores(key_block, block_start):
        scores = (
            jnp.einsum("bhgd,thd->hgbt", query_low, key_block, preferred_element_type=jnp.float32)
            * inv_root
        )
        key_pos = block_start + jnp.arange(key_block.shape[0], dtype=jnp.int32)
        visible = (key_pos[None, :] <= positions[:, None]) & (key_pos[None, :] < length)
        return (scores, visible)

    def max_step(state, item):
        running_max, running_sum = state
        kv_block, block_start = item
        scores, visible = block_scores(kv_block[:, 0], block_start)
        new_max = jnp.maximum(running_max, jnp.max(jnp.where(visible, scores, -1e30), axis=-1))
        expanded = jnp.where(visible, jnp.exp(scores - new_max[..., None]), 0.0)
        running_sum = running_sum * jnp.exp(running_max - new_max) + jnp.sum(expanded, axis=-1)
        return ((new_max, running_sum), None)

    stat_shape = (KV_HEADS, group, token_count)
    start_state = (jnp.full(stat_shape, -1e30, jnp.float32), jnp.zeros(stat_shape, jnp.float32))
    final_state, unused_out = lax.scan(max_step, start_state, (kv_blocks, starts))
    log_total = final_state[0] + jnp.log(final_state[1])

    def block_probs(kv_block, block_start):
        scores, visible = block_scores(kv_block[:, 0], block_start)
        return jnp.where(visible, jnp.exp(scores - log_total[..., None]), 0.0)

    def value_step(totals, item):
        kv_block, block_start = item
        probs_low = block_probs(kv_block, block_start).astype(jnp.bfloat16)
        return (
            totals
            + jnp.einsum(
                "hgbt,thd->bhgd", probs_low, kv_block[:, 1], preferred_element_type=jnp.float32
            ),
            None,
        )

    attended, unused_out = lax.scan(
        value_step,
        jnp.zeros((token_count, KV_HEADS, group, HEAD_DIM), jnp.float32),
        (kv_blocks, starts),
    )
    attended_low = attended.reshape(token_count, HEADS * HEAD_DIM).astype(jnp.bfloat16)
    middle = source + jnp.dot(attended_low, out_full, preferred_element_type=jnp.float32)
    normed_mid = root_norm(middle, ffn_norm).astype(jnp.bfloat16)
    columns = normed_mid
    projected = jnp.einsum(
        "td,dgf->tgf",
        columns,
        lax.all_gather(gate_up, "fsdp", axis=0, tiled=True),
        preferred_element_type=jnp.float32,
    )
    act_value, act_pull = jax.vjp(activate, projected)
    hidden = act_value.astype(jnp.bfloat16)
    columns = hidden
    ffn_out = jnp.dot(
        columns,
        lax.all_gather(down_weight, "fsdp", axis=0, tiled=True),
        preferred_element_type=jnp.float32,
    )
    layer_out = (row_keep * (middle + ffn_out)).astype(jnp.bfloat16)[None]
    d_out = row_keep * cotangent[0].astype(jnp.float32)
    d_out_low = d_out.astype(jnp.bfloat16)
    down_shard = lax.psum_scatter(
        contract_rows(hidden, d_out_low).astype(jnp.bfloat16),
        "fsdp",
        scatter_dimension=0,
        tiled=True,
    )
    d_hidden = contract_cols(d_out_low, lax.all_gather(down_weight, "fsdp", axis=0, tiled=True))
    d_proj_low = act_pull(d_hidden)[0].astype(jnp.bfloat16)
    columns = normed_mid
    gate_up_shard = lax.psum_scatter(
        jnp.einsum("td,tgf->dgf", columns, d_proj_low, preferred_element_type=jnp.float32).astype(
            jnp.bfloat16
        ),
        "fsdp",
        scatter_dimension=0,
        tiled=True,
    )
    d_normed_mid = jnp.einsum(
        "tgf,dgf->td",
        d_proj_low,
        lax.all_gather(gate_up, "fsdp", axis=0, tiled=True),
        preferred_element_type=jnp.float32,
    )
    mid_value, mid_pull = jax.vjp(root_norm, middle, ffn_norm)
    d_mid_norm, ffn_gain_part = mid_pull(d_normed_mid)
    d_middle = d_out + d_mid_norm
    d_branch = d_middle.astype(jnp.bfloat16)
    out_term = contract_rows(attended_low, d_branch)
    d_attended = (
        contract_cols(d_branch, out_full)
        .astype(jnp.bfloat16)
        .reshape(token_count, KV_HEADS, group, HEAD_DIM)
    )
    delta = jnp.transpose(jnp.sum(d_attended.astype(jnp.float32) * attended, axis=-1), (1, 2, 0))

    def block_grads(kv_block, block_start):
        probs = block_probs(kv_block, block_start)
        d_probs = jnp.einsum(
            "bhgd,thd->hgbt", d_attended, kv_block[:, 1], preferred_element_type=jnp.float32
        )
        d_scores = (probs * (d_probs - delta[..., None])).astype(jnp.bfloat16)
        return (probs.astype(jnp.bfloat16), d_scores)

    def query_step(totals, item):
        kv_block, block_start = item
        probs_low, d_scores = block_grads(kv_block, block_start)
        return (
            totals
            + jnp.einsum(
                "hgbt,thd->bhgd", d_scores, kv_block[:, 0], preferred_element_type=jnp.float32
            ),
            None,
        )

    d_query_sum, unused_out = lax.scan(
        query_step,
        jnp.zeros((token_count, KV_HEADS, group, HEAD_DIM), jnp.float32),
        (kv_blocks, starts),
    )
    d_query = (d_query_sum * inv_root).reshape(token_count, HEADS * HEAD_DIM).astype(jnp.bfloat16)
    sub_block = 512
    sub_total = token_count * lax.axis_size("ctx") // sub_block
    pieces = kv_whole.reshape(sub_total, sub_block, 2, KV_HEADS, HEAD_DIM)
    sub_starts = jnp.arange(sub_total, dtype=jnp.int32) * sub_block

    def key_grads(item):
        kv_block, block_start = item
        probs_low, d_scores = block_grads(kv_block, block_start)
        d_keys = (
            jnp.einsum("hgbt,bhgd->thd", d_scores, query_low, preferred_element_type=jnp.float32)
            * inv_root
        )
        d_values = jnp.einsum(
            "hgbt,bhgd->thd", probs_low, d_attended, preferred_element_type=jnp.float32
        )
        return jnp.concatenate(
            [d_keys.reshape(sub_block, key_cols), d_values.reshape(sub_block, key_cols)], axis=1
        )

    kv_grad = lax.psum_scatter(
        lax.map(key_grads, (pieces, sub_starts))
        .reshape(token_count * lax.axis_size("ctx"), 2 * key_cols)
        .astype(jnp.bfloat16),
        "ctx",
        scatter_dimension=0,
        tiled=True,
    ).astype(jnp.float32)
    d_key_low = kv_grad[:, :key_cols].astype(jnp.bfloat16).astype(jnp.float32)
    d_value_low = kv_grad[:, key_cols:].astype(jnp.bfloat16).astype(jnp.float32)
    d_qkv_out, qk_part = head_pull((d_query.astype(jnp.float32), d_key_low, d_value_low))
    d_qkv = d_qkv_out.astype(jnp.bfloat16)
    qkv_term = contract_rows(normed, d_qkv)
    d_normed = contract_cols(d_qkv, qkv_full)
    first_value, first_pull = jax.vjp(root_norm, source, attn_norm)
    d_source_norm, attn_gain_part = first_pull(d_normed)
    input_grad = (d_middle + d_source_norm).astype(jnp.bfloat16)[None]
    qkv_shard, out_shard, attn_shard, ffn_shard = (
        lax.psum_scatter(
            qkv_term.astype(jnp.bfloat16), "fsdp", scatter_dimension=0, tiled=True
        ).astype(jnp.float32),
        lax.psum_scatter(
            out_term.astype(jnp.bfloat16), "fsdp", scatter_dimension=0, tiled=True
        ).astype(jnp.float32),
        lax.psum_scatter(
            attn_gain_part.astype(jnp.bfloat16), "fsdp", scatter_dimension=0, tiled=True
        ).astype(jnp.float32),
        lax.psum_scatter(
            ffn_gain_part.astype(jnp.bfloat16), "fsdp", scatter_dimension=0, tiled=True
        ).astype(jnp.float32),
    )
    summed = (
        lax.psum(qkv_shard.astype(jnp.bfloat16), "ctx").astype(jnp.float32),
        lax.psum(out_shard.astype(jnp.bfloat16), "ctx").astype(jnp.float32),
        lax.psum(gate_up_shard, "ctx").astype(jnp.float32),
        lax.psum(down_shard, "ctx").astype(jnp.float32),
        lax.psum(attn_shard.astype(jnp.bfloat16), "ctx").astype(jnp.float32),
        lax.psum(ffn_shard.astype(jnp.bfloat16), "ctx").astype(jnp.float32),
    )
    qk_total = lax.psum(qk_part, ("fsdp", "ctx"))
    return (
        layer_out,
        input_grad,
        summed[0],
        summed[1],
        summed[2],
        summed[3],
        summed[4],
        summed[5],
        qk_total,
    )


MESH = pl.DeviceIdType.MESH
F32 = jnp.float32
BF16 = jnp.bfloat16
VMEM_BYTES = 60 << 20
HBM = pl.BlockSpec(memory_space=pl.ANY)
VMEM = pl.BlockSpec(memory_space=pltpu.VMEM)


class Place:
    def __init__(self):
        self.f = lax.axis_index("fsdp")
        self.c = lax.axis_index("ctx")
        self.z, self.x = lax.div(self.f, 2), lax.rem(self.f, 2)
        self.y, self.core = lax.div(self.c, 2), lax.rem(self.c, 2)
        self.xo, self.yo, self.co = 1 - self.x, 1 - self.y, 1 - self.core
        upper = lax.div(self.z, 2)
        self.others = (self.z + 1 - 2 * lax.rem(self.z, 2), 2 - upper, 3 - 3 * upper)
        self.inner = lax.rem(self.z, 2) + upper == 1
        self.far = 2 - 2 * upper
        self.x_dev = (self.z * 2 + self.xo, self.c)
        self.c_core = self.y * 2 + self.co
        self.c_y = self.yo * 2 + self.core
        self.c_diag = self.yo * 2 + self.co
        self.core_dev = (self.f, self.c_core)
        self.y_dev = (self.f, self.c_y)
        self.diag_dev = (self.f, self.c_diag)

    def rank(self, source, target):
        return jnp.where(source > target, source - 1, source)

    def z_dev(self, z):
        return (z * 2 + self.x, self.c)

    def meet(self, partners):
        barrier = pltpu.get_barrier_semaphore()
        for partner in partners:
            pl.semaphore_signal(barrier, inc=1, device_id=partner, device_id_type=MESH)
        pl.semaphore_wait(barrier, len(partners))

    def neighbours(self):
        return [self.z_dev(o) for o in self.others] + [self.x_dev, self.core_dev, self.y_dev]


class Links:
    def __init__(self, place, send_sems, recv_sems, local_sems):
        self.place = place
        self.send_sems, self.recv_sems, self.local_sems = send_sems, recv_sems, local_sems
        self.sends = self.recvs = self.locals = 0
        self.open = []

    def slots(self, count):
        first = self.recvs
        self.recvs += count
        return first

    def copy(self, src, dst, slot, device):
        made = pltpu.make_async_remote_copy(
            src_ref=src,
            dst_ref=dst,
            send_sem=self.send_sems.at[self.sends],
            recv_sem=self.recv_sems.at[slot],
            device_id=device,
            device_id_type=MESH,
        )
        self.sends += 1
        return made

    def send(self, src, dst, slot, device):
        made = self.copy(src, dst, slot, device)
        made.start()
        self.open.append(made)
        return made

    def settle(self, sends):
        for made in sends:
            made.wait_send()
            self.open = [one for one in self.open if one is not made]

    def arrive(self, ref, slot):
        pltpu.make_async_remote_copy(
            src_ref=ref,
            dst_ref=ref,
            send_sem=self.send_sems.at[0],
            recv_sem=self.recv_sems.at[slot],
            device_id=self.place.x_dev,
            device_id_type=MESH,
        ).wait_recv()

    def local(self, src, dst):
        made = pltpu.make_async_copy(src, dst, self.local_sems.at[self.locals])
        self.locals += 1
        made.start()
        return made

    def finish(self):
        for made in self.open:
            made.wait_send()
        self.open = []


class SpreadPlane:
    def __init__(self, links, place, chunks):
        self.links, self.place, self.chunks = links, place, chunks
        self.z_slot, self.x_slot = links.slots(4 * len(chunks)), links.slots(4 * len(chunks))

    def begin_z(self):
        place = self.place
        for k, (src, dst) in enumerate(self.chunks):
            slot = self.z_slot + 4 * k + place.z
            for other in place.others:
                self.links.send(src, dst(place.f), slot, place.z_dev(other))

    def begin_x(self, k):
        src, dst = self.chunks[k]
        slot = self.x_slot + 4 * k + self.place.z
        self.links.send(src, dst(self.place.f), slot, self.place.x_dev)

    def forward(self, k):
        place, dst = self.place, self.chunks[k][1]
        for other in place.others:
            block = dst(other * 2 + place.x)
            self.links.arrive(block, self.z_slot + 4 * k + other)
            self.links.send(block, block, self.x_slot + 4 * k + other, place.x_dev)

    def end(self):
        for k in range(len(self.chunks)):
            for z in range(4):
                block = self.chunks[k][1](z * 2 + self.place.xo)
                self.links.arrive(block, self.x_slot + 4 * k + z)


class SpreadTree(SpreadPlane):
    def __init__(self, links, place, chunks, crossed):
        super().__init__(links, place, chunks)
        self.plain = len(chunks) - crossed
        self.passed = []

    def begin_z(self, ahead=4):
        place = self.place
        self.near = {}
        for k, (src, dst) in enumerate(self.chunks):
            slot = self.z_slot + 4 * k + place.z
            near = self.links.copy(src, dst(place.f), slot, place.z_dev(place.others[0]))
            self.links.open.append(near)
            if k < ahead:
                near.start()
            else:
                pl.when(jnp.logical_not(place.inner))(near.start)
                self.near[k - ahead] = near
            self.links.send(src, dst(place.f), slot, place.z_dev(place.others[1]))

    def cross_z(self, k):
        place = self.place
        block = self.chunks[k][1](place.z * 2 + place.xo)
        slot = self.x_slot + 4 * k + place.z
        self.links.arrive(block, slot)
        for other in place.others[:2]:
            self.links.send(block, block, slot, place.z_dev(other))

    def blocks(self, k, other):
        place, dst = self.place, self.chunks[k][1]
        found = [(dst(other * 2 + place.x), self.z_slot + 4 * k + other)]
        if k >= self.plain:
            found.append((dst(other * 2 + place.xo), self.x_slot + 4 * k + other))
        return found

    def onward(self, k):
        place = self.place
        blocks = [pair for other in place.others[1:] for pair in self.blocks(k, other)]
        made = [
            self.links.copy(block, block, slot, place.z_dev(place.others[0]))
            for block, slot in blocks
        ]
        self.passed += made

        @pl.when(place.inner)
        def _():
            for (block, slot), one in zip(blocks, made):
                self.links.arrive(block, slot)
                one.start()
            if k in self.near:
                self.near[k].start()

    def forward(self, k):
        place = self.place
        near, *far = [self.blocks(k, other) for other in place.others]
        far = far[0] + far[1]
        for pair in near:
            self.links.arrive(*pair)
        if k < self.plain:
            slot = self.x_slot + 4 * k + place.others[0]
            self.links.send(near[0][0], near[0][0], slot, place.x_dev)

        @pl.when(jnp.logical_not(place.inner))
        def _():
            for pair in far:
                self.links.arrive(*pair)

        if k < self.plain:
            for other, (block, _) in zip(place.others[1:], far):
                self.links.send(block, block, self.x_slot + 4 * k + other, place.x_dev)

    def end(self):
        for k in range(self.plain):
            for z in range(4):
                block = self.chunks[k][1](z * 2 + self.place.xo)
                self.links.arrive(block, self.x_slot + 4 * k + z)

    def finish(self):
        @pl.when(self.place.inner)
        def _():
            for made in self.passed:
                made.wait_send()


class ReducePlane:
    def __init__(self, links, place, chunks, from_x, from_z, own=None):
        self.links, self.place, self.chunks = links, place, chunks
        self.from_x, self.from_z, self.own = from_x, from_z, own
        self.summed = 0
        self.x_slot, self.z_slot = links.slots(len(chunks)), links.slots(3 * len(chunks))
        self.loads, self.z_sends = {}, {}

    def send_x(self, k):
        place = self.place
        from_x = self.from_x.at[k - self.summed]
        self.links.send(self.chunks[k](place.xo), from_x, self.x_slot + k, place.x_dev)

    def load(self, k):
        slots = self.own.shape[0]
        for made in self.z_sends.pop(k - slots, []):
            made.wait_send()
        self.loads[k] = self.links.local(self.chunks[k](self.place.x), self.own.at[k % slots])

    def mine(self, k):
        if self.own is None:
            return self.chunks[k](self.place.x)
        return self.own.at[k % self.own.shape[0]]

    def middle(self, k):
        place = self.place
        self.links.arrive(self.from_x.at[k], self.x_slot + k)
        if k in self.loads:
            self.loads[k].wait()
        mine = self.mine(k)
        self.z_sends[k] = []
        for other in place.others:
            mine[other] = (mine[other].astype(F32) + self.from_x[k, other].astype(F32)).astype(BF16)
            rank = place.rank(place.z, other)
            made = self.links.copy(
                mine.at[other],
                self.from_z.at[k, rank],
                self.z_slot + 3 * k + rank,
                place.z_dev(other),
            )
            made.start()
            self.z_sends[k].append(made)

    def end(self, k):
        place = self.place
        mine = self.mine(k)
        sums = mine[place.z].astype(F32) + self.from_x[k, place.z].astype(F32)
        for rank in range(3):
            self.links.arrive(self.from_z.at[k, rank], self.z_slot + 3 * k + rank)
            sums += self.from_z[k, rank].astype(F32)
        total = self.from_x.at[k, place.z]
        total[...] = sums.astype(BF16)
        return total

    def finish(self):
        for sends in self.z_sends.values():
            for made in sends:
                made.wait_send()


class ReduceTree(ReducePlane):
    def __init__(self, links, place, chunks, from_x, from_z, via, own, summed):
        super().__init__(links, place, chunks, from_x, from_z, own)
        self.summed = summed
        self.via, self.via_slot = via, links.slots(len(chunks))
        self.outer = jnp.logical_not(place.inner)

    def load(self, k):
        slots = self.own.shape[0]
        self.settle(self.z_sends.pop(k - slots, []))
        self.loads[k] = self.links.local(self.chunks[k](self.place.x), self.own.at[k % slots])

    def settle(self, sends):
        for made, when in sends:
            if when is None:
                made.wait_send()
            else:
                pl.when(when)(made.wait_send)

    def middle(self, k):
        place = self.place
        self.loads[k].wait()
        mine = self.mine(k)
        if k >= self.summed:
            from_x = self.from_x.at[k - self.summed]
            self.links.arrive(from_x, self.x_slot + k)
            for other in place.others:
                pair = mine[other].astype(F32) + from_x[other].astype(F32)
                mine[other] = pair.astype(BF16)
        near = place.others[0]
        device = place.z_dev(near)
        direct = self.links.copy(mine.at[near], self.from_z.at[k, 0], self.z_slot + 3 * k, device)
        direct.start()
        far = self.links.copy(
            mine.at[pl.ds(place.far, 2)], self.via.at[k], self.via_slot + k, device
        )
        pl.when(self.outer)(far.start)
        self.z_sends[k] = [(direct, None), (far, self.outer)]

    def combine(self, k):
        place = self.place
        mine = self.mine(k)

        sent = [
            self.links.copy(
                mine.at[place.far + j],
                self.from_z.at[k, 1],
                self.z_slot + 3 * k + 1,
                place.z_dev(place.far + j),
            )
            for j in range(2)
        ]

        @pl.when(place.inner)
        def _():
            self.links.arrive(self.via.at[k], self.via_slot + k)
            for j in range(2):
                here = mine[place.far + j].astype(F32) + self.via[k, j].astype(F32)
                mine[place.far + j] = here.astype(BF16)
                sent[j].start()

        self.z_sends[k] += [(made, place.inner) for made in sent]

    def end(self, k):
        place = self.place
        sums = self.mine(k)[place.z].astype(F32)
        if k >= self.summed:
            sums += self.from_x[k - self.summed, place.z].astype(F32)
        for side in range(2):
            self.links.arrive(self.from_z.at[k, side], self.z_slot + 3 * k + side)
            sums += self.from_z[k, side].astype(F32)
        total = self.from_z.at[k, 0]
        total[...] = sums.astype(BF16)
        return total

    def finish(self):
        for sends in self.z_sends.values():
            self.settle(sends)


class SpreadCtx:
    def __init__(self, links, place, out, parts):
        self.links, self.place, self.out, self.parts = links, place, out, parts
        self.slot = links.slots(3 * len(parts))
        self.sends = []

    def begin(self, k, src):
        place, rows = self.place, self.parts[k]
        out = self.out.at[place.c, rows]
        self.sends.append(self.links.send(src, out, self.slot + 3 * k + 1, place.y_dev))
        self.sends.append(self.links.send(src, out, self.slot + 3 * k, place.core_dev))

    def forward(self, k):
        place = self.place
        block = self.out.at[place.c_y, self.parts[k]]
        self.links.arrive(block, self.slot + 3 * k + 1)
        self.sends.append(self.links.send(block, block, self.slot + 3 * k + 2, place.core_dev))

    def end(self):
        place = self.place
        for k, rows in enumerate(self.parts):
            self.links.arrive(self.out.at[place.c_core, rows], self.slot + 3 * k)
            self.links.arrive(self.out.at[place.c_diag, rows], self.slot + 3 * k + 2)


class ReduceCtx:
    def __init__(self, links, place, part, parts, own, from_core, to_y, from_y):
        self.links, self.place, self.part = links, place, part
        self.parts = [rows if isinstance(rows, tuple) else (rows,) for rows in parts]
        self.own, self.from_core, self.to_y, self.from_y = own, from_core, to_y, from_y
        self.slot = links.slots(3 * len(parts))
        self.loads, self.sends = {}, []

    def begin(self, only=None):
        place = self.place
        for side, y in ((0, place.yo), (1, place.y)):
            for k, rows in enumerate(self.parts):
                if only not in (None, k):
                    continue
                self.links.send(
                    self.part.at[y * 2 + place.co, *rows],
                    self.from_core.at[side, *rows],
                    self.slot + 3 * k + side,
                    place.core_dev,
                )
                if self.own is not None and side == 0:
                    self.load(0, k)

    def load(self, side, k):
        rows = self.parts[k]
        y = self.place.y if side else self.place.yo
        self.loads[side, k] = self.links.local(
            self.part.at[y * 2 + self.place.core, *rows], self.own.at[rows]
        )

    def pair(self, side, k):
        rows = self.parts[k]
        self.links.arrive(self.from_core.at[side, *rows], self.slot + 3 * k + side)
        if self.own is None:
            y = self.place.y if side else self.place.yo
            own = self.part[y * 2 + self.place.core, *rows]
        else:
            self.loads[side, k].wait()
            own = self.own[rows]
        return own.astype(F32) + self.from_core[side, *rows].astype(F32)

    def cross(self, k):
        rows = self.parts[k]
        self.to_y[rows] = self.pair(0, k).astype(BF16)
        if self.own is not None:
            self.load(1, k)
        made = self.links.send(
            self.to_y.at[rows], self.from_y.at[rows], self.slot + 3 * k + 2, self.place.y_dev
        )
        self.sends.append(made)

    def total(self, k):
        rows = self.parts[k]
        sums = self.pair(1, k)
        self.links.arrive(self.from_y.at[rows], self.slot + 3 * k + 2)
        return sums + self.from_y[rows].astype(F32)


def halves(rows):
    return [pl.ds(0, rows // 2), pl.ds(rows // 2, rows // 2)]


def row_factor(values):
    return lax.rsqrt(jnp.mean(values * values, axis=-1, keepdims=True) + EPSILON)


def low_half(shape):
    return lax.rem(lax.broadcasted_iota(jnp.int32, shape, len(shape) - 1), 128) < 64


def partner(values):
    lane = lax.broadcasted_iota(jnp.int32, values.shape, len(values.shape) - 1)
    first = lax.rem(lane, 64) < 32
    return jnp.where(first, pltpu.roll(values, 96, 1), pltpu.roll(values, 32, 1))


def half_sums(values):
    low = low_half(values.shape)
    first = jnp.sum(jnp.where(low, values, 0.0), axis=-1, keepdims=True)
    second = jnp.sum(jnp.where(low, 0.0, values), axis=-1, keepdims=True)
    return jnp.where(low, first, second)


def row_loop(count, body, first=0):
    def step(index, carry):
        body(index)
        return carry

    lax.fori_loop(first, first + count, step, 0)


BLOCK = 256
SHORT = 128


def attention_scores(query, keys, key_bias, first, span):
    scores = lax.dot_general(
        query, keys, (((1,), (1,)), ((), ())), preferred_element_type=F32
    ) * (1.0 / math.sqrt(HEAD_DIM))
    rows = first + lax.broadcasted_iota(jnp.int32, scores.shape, 0)
    columns = lax.broadcasted_iota(jnp.int32, scores.shape, 1)
    return jnp.where(columns <= rows, scores, -1e30) + key_bias[:, :span]


def turn_tables(angles, cos, sin):
    for i in range(16):
        rows = slice(64 * i, 64 * (i + 1))
        cos_high, sin_high = angles[i : i + 1], angles[16 + i : 17 + i]
        cos_low, sin_low = angles[32:96], angles[96:160]
        cos[rows] = cos_high * cos_low - sin_high * sin_low
        sin[rows] = sin_high * cos_low + cos_high * sin_low


def forward_kernel(
    lengths, qkv_weight, out_s, gain_s, x_s, gate_up, down_weight, cotangent, angles, qk_gain,
    qkv_wh, out_wh, gains, normed_h, qkv_raw_h, qkv_low_h, att_low_h, log_sums_h,
    gu_w, dn_w, dout_all, middle, mid_all, head_gain, key_bias,
    kv_pairs, kv_s, dout_s, cos, sin, gain_blocks, qkv_w, out_w, x_all, normed, qkv_raw, qkv_low, att_low, log_sums,
    part, keys, values, from_core, to_y, from_y, mid_low, gu_pairs, gu_rows, gu_s, send_sems, recv_sems, local_sems,
):
    place = Place()
    links = Links(place, send_sems, recv_sems, local_sems)
    fellows = [lax.rem(place.f + d, 8) for d in range(1, 8)]
    place.meet([(f, place.c) for f in fellows] + [place.core_dev, place.y_dev])

    q_columns = pl.ds(pl.multiple_of(256 * place.c, 256), 256)
    for j in range(2):
        pair = pl.ds(pl.multiple_of(1024 + 256 * j + 128 * place.y, 128), 128)
        links.local(qkv_weight.at[:, pair], kv_pairs.at[j]).wait()
    cot_load = links.local(cotangent, dout_s)
    low = low_half(kv_pairs.shape[1:])
    first, second = [], []
    for j in range(2):
        value = kv_pairs[j].astype(F32)
        swapped = pltpu.roll(value, 64, 1)
        first.append(jnp.where(place.core == 0, value, swapped))
        second.append(jnp.where(place.core == 0, swapped, value))
    kv_s[...] = jnp.where(low, first[0], second[1]).astype(BF16)
    qkv_plane = SpreadPlane(
        links,
        place,
        [
            (qkv_weight.at[:, q_columns], lambda f: qkv_w.at[f, :, 0:256]),
            (kv_s, lambda f: qkv_w.at[f, :, 256:384]),
        ],
    )
    qkv_plane.begin_z()
    qkv_plane.begin_x(0)
    qkv_plane.begin_x(1)
    picks = []
    for f in range(8):
        start = pl.multiple_of(512 * f + 128 * place.c, 128)
        picks.append(links.local(gate_up.at[:, :, pl.ds(start, 128)], gu_pairs.at[f]))
    tokens = x_s.shape[0]
    parts = halves(tokens)
    x_spread = SpreadCtx(links, place, x_all, parts)
    for k, rows in enumerate(parts):
        x_spread.begin(k, x_s.at[rows])
    gain_slot = links.slots(8)
    for f in fellows:
        links.send(gain_s, gain_blocks.at[place.f], gain_slot + place.f, (f, place.c))
    kept = [
        links.local(qkv_weight.at[:, q_columns], qkv_w.at[place.f, :, 0:256]),
        links.local(kv_s, qkv_w.at[place.f, :, 256:384]),
        links.local(gain_s, gain_blocks.at[place.f]),
        links.local(x_s, x_all.at[place.c]),
    ]

    root_slot, side_slot = links.slots(1), links.slots(1)
    holds = place.z == place.c
    down = [
        links.copy(out_s, out_w.at[place.x], root_slot, place.z_dev(other))
        for other in place.others[:2]
    ]
    relay = links.copy(out_w.at[place.x], out_w.at[place.x], root_slot, place.z_dev(place.others[0]))
    across = lax.div(place.c, 2) != lax.div(place.z, 2)
    relays = jnp.logical_and(place.inner, across)
    sideways = links.copy(out_s, out_w.at[place.x], side_slot, place.x_dev)
    onward = links.copy(out_w.at[place.x], out_w.at[place.x], side_slot, place.x_dev)
    own = pltpu.make_async_copy(out_s, out_w.at[place.x], local_sems.at[links.locals])
    links.locals += 1

    @pl.when(holds)
    def _():
        for made in down:
            made.start()
        sideways.start()
        own.start()

    rows = gu_s.shape[0]
    for f in range(8):
        picks[f].wait()
        gu_rows[...] = gu_pairs.at[f].reshape(2 * rows, 128)[...].astype(F32)
        for side in range(2):
            first = 1024 * side + 128 * f
            picked = gu_rows[pl.ds(side, rows, stride=2), :]
            gu_s[:, first : first + 128] = picked.astype(BF16)
    step = 32
    chunks = []
    dn_s = down_weight.at[pl.ds(pl.multiple_of(128 * place.c, 128), dn_w.shape[1])]
    for src, dst in ((dn_s, dn_w), (gu_s, gu_w)):
        for first in range(0, src.shape[0], step):
            rows = pl.ds(first, step)
            chunks.append((src.at[rows], lambda f, dst=dst, rows=rows: dst.at[f, rows]))
    plane = SpreadTree(links, place, chunks, 2)
    plane.begin_z()
    cot_load.wait()
    length = lengths[0]
    positions = tokens * place.c + lax.broadcasted_iota(jnp.int32, (tokens, 1), 0)
    dout_s[...] = jnp.where(positions < length, dout_s[...].astype(F32), 0.0).astype(BF16)
    for k in range(plane.plain, len(chunks)):
        plane.begin_x(k)
    for k in range(3):
        plane.begin_x(k)
    qkv_plane.forward(0)
    qkv_plane.forward(1)
    for k in range(3, plane.plain):
        plane.begin_x(k)
    for k in range(plane.plain, len(chunks)):
        plane.cross_z(k)
    last = [
        links.local(gu_s, gu_w.at[place.f]),
        links.local(dn_s, dn_w.at[place.f]),
        links.local(dout_s, dout_all.at[place.c]),
    ]
    turn_tables(angles, cos, sin)
    columns = lax.broadcasted_iota(jnp.int32, key_bias.shape, 1)
    key_bias[...] = jnp.where(columns < length, 0.0, -1e30)
    ones = jnp.ones((1, HEAD_DIM), F32)
    q_gain, k_gain = qk_gain[0:1].astype(F32), qk_gain[1:2].astype(F32)
    head_gain[...] = jnp.zeros_like(head_gain)
    for b in range(2):
        head_gain[b : b + 1] = jnp.concatenate([q_gain, q_gain], axis=1)
    head_gain[2:3] = jnp.concatenate([k_gain, ones], axis=1)
    for f in fellows:
        links.arrive(gain_blocks.at[f], gain_slot + f)
    for made in kept:
        made.wait()
    gains[...] = jnp.zeros_like(gains)
    for f in range(8):
        gains[0:2, 256 * f : 256 * (f + 1)] = gain_blocks[f, 0:2]
    dout = SpreadCtx(links, place, dout_all, parts)
    for k, rows in enumerate(parts):
        x_spread.forward(k)
        dout.begin(k, dout_s.at[rows])
    x_spread.end()
    qkv_plane.end()

    def project(index):
        rows = pl.ds(pl.multiple_of(index * BLOCK, BLOCK), BLOCK)
        source = x_all[index].astype(F32)
        normed[rows] = (source * row_factor(source) * gains[0:1]).astype(BF16)
        weight = qkv_w[...].reshape(normed.shape[1], qkv_w.shape[2])
        raw = jnp.dot(normed[rows], weight, preferred_element_type=F32)
        for b in range(3):
            block = raw[:, 128 * b : 128 * (b + 1)]
            qkv_raw[b, rows] = block
            factor = lax.rsqrt(half_sums(block * block) * (1.0 / HEAD_DIM) + EPSILON)
            scaled = block * factor * head_gain[b : b + 1]
            turned = scaled * cos[rows] + partner(scaled) * sin[rows]
            if b == 2:
                turned = jnp.where(low_half(turned.shape), turned, block)
            qkv_low[b, rows] = turned.astype(BF16)
            if b == 2:
                low = low_half(turned.shape)
                swapped = pltpu.roll(turned, 64, 1)
                keys[rows] = jnp.where(low, turned, swapped).astype(BF16)
                values[rows] = jnp.where(low, swapped, turned).astype(BF16)

    seq = normed.shape[0]
    att_low[...] = jnp.zeros_like(att_low)
    log_sums[...] = jnp.zeros_like(log_sums)
    row_loop(seq // BLOCK, project)
    last += [
        links.local(normed, normed_h),
        links.local(qkv_raw, qkv_raw_h),
        links.local(qkv_low, qkv_low_h),
        links.local(qkv_w, qkv_wh),
    ]

    def heads(index):
        b, half = lax.div(index, 2), lax.rem(index, 2)
        for i in range(seq // BLOCK):
            rows, span = pl.ds(i * BLOCK, BLOCK), (i + 1) * BLOCK
            query = qkv_low[b, rows]
            side = lax.div(lax.broadcasted_iota(jnp.int32, query.shape, 1), 64) == half
            chosen = jnp.where(side, query, 0)
            scores = attention_scores(chosen, keys[:span], key_bias[0:1], i * BLOCK, span)
            top = jnp.max(scores, axis=-1, keepdims=True)
            expanded = jnp.exp(scores - top)
            sums = jnp.sum(expanded, axis=-1, keepdims=True)
            probs = (expanded * (1.0 / sums)).astype(BF16)
            out = jnp.dot(probs, values[:span], preferred_element_type=F32)
            att_low[b, rows] = jnp.where(side, out.astype(BF16), att_low[b, rows])
            log_sums[b, rows] = jnp.where(side, top + jnp.log(sums), log_sums[b, rows])

    @pl.when(relays)
    def _():
        links.arrive(out_w.at[place.x], root_slot)
        relay.start()
        onward.start()

    plane.onward(0)
    row_loop(2, heads)
    plane.onward(1)
    plane.onward(2)
    plane.forward(0)
    row_loop(2, heads, 2)
    plane.onward(3)
    for k in range(1, 3):
        plane.forward(k)

    @pl.when(jnp.logical_not(jnp.logical_or(holds, relays)))
    def _():
        links.arrive(out_w.at[place.x], root_slot)
        onward.start()

    @pl.when(holds)
    def _():
        own.wait()

    for k in range(len(parts)):
        dout.forward(k)
    links.arrive(out_w.at[place.xo], side_slot)

    def project_out(index):
        rows = pl.ds(pl.multiple_of(index * BLOCK, BLOCK), BLOCK)
        sums = jnp.dot(att_low[0, rows], out_w[0], preferred_element_type=F32)
        sums += jnp.dot(att_low[1, rows], out_w[1], preferred_element_type=F32)
        part[index] = sums.astype(BF16)

    row_loop(seq // BLOCK, project_out)
    reduce = ReduceCtx(links, place, part, parts, None, from_core, to_y, from_y)
    reduce.begin()
    last += [
        links.local(att_low, att_low_h),
        links.local(log_sums, log_sums_h),
        links.local(out_w, out_wh),
    ]
    plane.onward(4)
    for k in range(2):
        reduce.cross(k)
    plane.forward(3)
    plane.onward(5)
    plane.onward(6)
    plane.forward(4)
    plane.onward(7)
    plane.forward(5)
    plane.onward(8)
    plane.forward(6)
    mid = SpreadCtx(links, place, mid_all, parts)
    for k, rows in enumerate(parts):
        value = x_all[place.c, rows].astype(F32) + reduce.total(k)
        middle[rows] = value
        mid_low[rows] = (value * row_factor(value) * gains[1:2]).astype(BF16)
        mid.begin(k, mid_low.at[rows])
        last.append(links.local(mid_low.at[rows], mid_all.at[place.c, rows]))
    plane.onward(9)
    plane.forward(7)
    plane.forward(8)
    for k in range(2):
        mid.forward(k)
    plane.forward(9)
    for k in range(plane.plain, len(chunks)):
        plane.onward(k)
    for k in range(plane.plain, len(chunks)):
        plane.forward(k)
    plane.end()
    mid.end()
    dout.end()
    for made in last:
        made.wait()
    links.finish()
    plane.finish()

    @pl.when(holds)
    def _():
        for made in down:
            made.wait_send()
        sideways.wait_send()

    @pl.when(relays)
    def _():
        relay.wait_send()

    @pl.when(jnp.logical_not(holds))
    def _():
        onward.wait_send()


NT = (((1,), (1,)), ((), ()))
TN = (((0,), (0,)), ((), ()))


def norm_back(d_norm, value, gain):
    factor = row_factor(value)
    gain_sum = jnp.sum(d_norm * value * factor, axis=0, keepdims=True)
    scaled = d_norm * gain
    inner = jnp.mean(scaled * value, axis=-1, keepdims=True)
    return factor * scaled - value * (factor * factor * factor * inner), gain_sum


def feed_kernel(
    gu_h, dn_h, dout_h, mid_h, middle_h, gains,
    gu_g, dn_pair, ffn_h, d_middle_h, branch_s, ffn_gain,
    gu_w, dn_w, dout, mid, hidden, d_proj, dn_g, from_x, stage,
    part, from_core, to_y, from_y, middle, d_norm, branch, send_sems, recv_sems, local_sems,
):
    place = Place()
    links = Links(place, send_sems, recv_sems, local_sems)
    shards, rows, width = gu_w.shape
    units, seq = hidden.shape[1], hidden.shape[0]
    tokens = mid.shape[1]
    first = [links.local(mid_h, mid)]
    later, loads = [], []
    for n in range(units // 256):
        gate, up = pl.ds(256 * n, 256), pl.ds(units + 256 * n, 256)
        loads.append([
            links.local(gu_h.at[:, :, gate], gu_w.at[:, :, gate]),
            links.local(gu_h.at[:, :, up], gu_w.at[:, :, up]),
        ])
        if n == 0:
            first += [links.local(dout_h, dout), links.local(dn_h, dn_w)]
    later.append(links.local(middle_h, middle))
    place.meet([place.x_dev, place.core_dev, place.y_dev])
    for made in first:
        made.wait()

    x_slot = links.slots(4)
    for n in range(units // 256):
        for made in loads[n]:
            made.wait()
        gate_columns, up_columns = slice(256 * n, 256 * (n + 1)), slice(units + 256 * n, units + 256 * (n + 1))

        def activation(index, gate_columns=gate_columns, up_columns=up_columns, n=n):
            two = pl.ds(2 * index, 2)
            low = mid[two].reshape(2 * tokens, width)
            gate = jnp.dot(
                low, gu_w[:, :, gate_columns].reshape(width, 256), preferred_element_type=F32
            )
            up = jnp.dot(
                low, gu_w[:, :, up_columns].reshape(width, 256), preferred_element_type=F32
            )
            d_hidden = lax.dot_general(
                dout[two].reshape(2 * tokens, width), dn_w[2 * n : 2 * n + 2].reshape(256, width), NT,
                preferred_element_type=F32,
            )
            at = pl.ds(pl.multiple_of(index * 2 * tokens, 2 * tokens), 2 * tokens)
            sigmoid = 1.0 / (1.0 + jnp.exp(-gate))
            silu = gate * sigmoid
            hidden[at, gate_columns] = (silu * up).astype(BF16)
            d_gate = d_hidden * up * (sigmoid * (1.0 + gate * (1.0 - sigmoid)))
            d_proj[at, gate_columns] = d_gate.astype(BF16)
            d_proj[at, up_columns] = (d_hidden * silu).astype(BF16)

        row_loop(2, activation)
        left = hidden[:, gate_columns].T

        def down_grad(j, left=left, n=n):
            wide = pl.ds(pl.multiple_of(512 * j, 512), 512)
            right = dout[:, :, wide].reshape(seq, 512)
            grad = jnp.dot(left, right, preferred_element_type=F32).astype(BF16)
            dn_g[n, 0, :, wide] = grad[:128]
            dn_g[n, 1, :, wide] = grad[128:]

        row_loop(4, down_grad)
        links.send(dn_g.at[n, place.xo], from_x.at[n], x_slot + n, place.x_dev)

    def mid_grad(f):
        grad = lax.dot_general(d_proj[...], gu_w[f], NT, preferred_element_type=F32)
        columns = pl.ds(pl.multiple_of(rows * f, rows), rows)
        part[:, :, columns] = grad.astype(BF16).reshape(4, tokens, rows)

    parts = halves(tokens)
    sides = [(slice(None), side) for side in halves(width)]
    dmid = ReduceCtx(links, place, part, sides, None, from_core, to_y, from_y)
    quarter = shards // 4
    row_loop(2 * quarter, mid_grad)
    dmid.begin(0)
    row_loop(quarter, mid_grad, 2 * quarter)
    dmid.cross(0)
    row_loop(quarter, mid_grad, 3 * quarter)
    dmid.begin(1)

    def gate_up_grad(z):
        columns = pl.ds(pl.multiple_of(2 * rows * z, 2 * rows), 2 * rows)
        left = mid[:, :, columns].reshape(seq, 2 * rows).T
        for j in range(4):
            wide = slice(512 * j, 512 * (j + 1))
            grad = jnp.dot(left, d_proj[:, wide], preferred_element_type=F32)
            stage[:, :, wide] = grad.astype(BF16).reshape(2, rows, 512)
        made = pltpu.make_async_copy(stage, gu_g.at[z], local_sems.at[links.locals])
        made.start()
        made.wait()

    row_loop(1, gate_up_grad)
    dmid.cross(1)
    row_loop(3, gate_up_grad, 1)
    links.locals += 1

    def feed_out(index):
        at = pl.ds(pl.multiple_of(index * 2 * tokens, 2 * tokens), 2 * tokens)
        for j in range(4):
            wide = slice(512 * j, 512 * (j + 1))
            right = dn_w[:, :, wide].reshape(units, 512)
            sums = jnp.dot(hidden[at], right, preferred_element_type=F32)
            mid[pl.ds(2 * index, 2), :, wide] = sums.astype(BF16).reshape(2, tokens, 512)

    row_loop(2, feed_out)
    later.append(links.local(mid, ffn_h))
    later[0].wait()
    for k in range(2):
        d_norm[sides[k]] = dmid.total(k)
    gain_sum = None
    for k, at in enumerate(parts):
        grad, term = norm_back(d_norm[at], middle[at], gains[1:2])
        gain_sum = term if gain_sum is None else gain_sum + term
        middle[at] = grad + dout[place.c, at].astype(F32)
        branch[at] = middle[at].astype(BF16)
        later.append(links.local(middle.at[at], d_middle_h.at[at]))
        later.append(links.local(branch.at[at], branch_s.at[at]))
    ffn_gain[...] = gain_sum
    for n in range(4):
        links.arrive(from_x.at[n], x_slot + n)
        pair = dn_g[n, place.x].astype(F32) + from_x[n].astype(F32)
        from_x[n] = pair.astype(BF16)
        later.append(links.local(from_x.at[n], dn_pair.at[n]))
    for made in later[1:]:
        made.wait()
    links.finish()


def backward_kernel(
    gu_g, dn_pair, ffn_part, middle_h, d_middle_h, branch_s, x_h, lengths, gains, ffn_gain,
    angles, head_gain, key_bias,
    normed_h, qkv_raw_h, qkv_low_h, att_low_h, log_sums_h, qkv_wh, out_wh,
    gu_all, dn_all, layer_out, qkv_all, out_all, input_grad, stats,
    own, from_x, from_z, via,
    ctx_own, from_core1, to_y1, from_y1, from_core2, to_y2, from_y2,
    middle, x_s, d_middle, branch_all, part,
    cos, sin, qkv_raw, qkv_low, att_low, log_sums, qkv_w, out_w,
    keys, values, d_att, d_low, d_keys, d_values, gain_g,
    qkv_g, qkv_x, qkv_z, out_g, out_x, out_z,
    mine, plane_stats, ctx_stats, send_sems, recv_sems, local_sems,
):
    place = Place()
    links = Links(place, send_sems, recv_sems, local_sems)
    fellows = [lax.rem(place.f + d, 8) for d in range(1, 8)]
    place.meet(
        [(f, place.c) for f in fellows] + [place.core_dev, place.y_dev, place.diag_dev]
    )
    step = from_x.shape[2]
    chunks, where = [], []
    for first in range(0, dn_pair.shape[1], step):
        rows = pl.ds(first, step)
        chunks.append(lambda x, rows=rows: dn_pair.at[:, rows])
        where.append((dn_all, rows))
    summed = len(chunks)
    for first in range(0, gu_g.shape[2], step):
        rows = pl.ds(first, step)
        chunks.append(lambda x, rows=rows: gu_g.at[:, x, rows])
        where.append((gu_all, rows))
    count = len(chunks)
    plane = ReduceTree(links, place, chunks, from_x, from_z, via, own, summed)
    outs = [SpreadCtx(links, place, out, [rows]) for out, rows in where]
    kept = []

    def end(k):
        total = plane.end(k)
        if k + own.shape[0] < count:
            plane.load(k + own.shape[0])
        out, rows = where[k]
        outs[k].begin(0, total)
        kept.append(links.local(total, out.at[place.c, rows]))

    tokens, width = middle.shape
    parts = halves(tokens)
    branch = SpreadCtx(links, place, branch_all, parts)
    for k, rows in enumerate(parts):
        branch.begin(k, branch_s.at[rows])
    for k in range(summed, count - 2):
        plane.send_x(k)
    ffn = ReduceCtx(links, place, ffn_part, parts, ctx_own, from_core1, to_y1, from_y1)
    ffn.begin()
    for k in range(own.shape[0]):
        plane.load(k)
    late = [
        links.local(a, b)
        for a, b in (
            (branch_s, branch_all.at[place.c]),
            (out_wh, out_w), (qkv_low_h, qkv_low), (att_low_h, att_low), (log_sums_h, log_sums),
            (qkv_raw_h, qkv_raw), (qkv_wh, qkv_w),
            (middle_h, middle), (d_middle_h, d_middle), (x_h, x_s),
        )
    ]
    turn_tables(angles, cos, sin)
    gain_g[...] = jnp.zeros_like(gain_g)
    d_keys[...] = jnp.zeros_like(d_keys)
    d_low[...] = jnp.zeros_like(d_low)
    d_values[...] = jnp.zeros_like(d_values)
    for k in (0, 1):
        plane.middle(k)
    for k in (2, 3):
        plane.middle(k)
    for k in range(2):
        ffn.cross(k)
    branch.forward(0)
    for k in (0, 1):
        plane.combine(k)
    branch.forward(1)
    for k in (4, 5):
        plane.middle(k)
    for k in (2, 3):
        plane.combine(k)
    branch.end()
    for made in late:
        made.wait()

    root = 1.0 / math.sqrt(HEAD_DIM)
    seq = 4 * tokens

    def prepare(index):
        rows = pl.ds(pl.multiple_of(index * BLOCK, BLOCK), BLOCK)
        block = qkv_low[2, rows].astype(F32)
        low = low_half(block.shape)
        swapped = pltpu.roll(block, 64, 1)
        keys[rows] = jnp.where(low, block, swapped).astype(BF16)
        values[rows] = jnp.where(low, swapped, block).astype(BF16)
        for b in range(2):
            d_att[b, rows] = lax.dot_general(
                branch_all[index], out_w[b], NT, preferred_element_type=F32
            ).astype(BF16)

    row_loop(seq // BLOCK, prepare)
    for b in range(2):
        left = att_low[b].T
        for j in range(8):
            columns = slice(256 * j, 256 * (j + 1))
            right = branch_all[:, :, columns].reshape(seq, 256)
            out_g[b, :, columns] = jnp.dot(left, right, preferred_element_type=F32).astype(BF16)
    out_slot = links.slots(1)
    links.send(out_g.at[place.xo], out_x, out_slot, place.x_dev)
    for k in range(count - 2, count):
        plane.send_x(k)
    links.settle(branch.sends)
    normed_load = links.local(normed_h, branch_all)
    for k in (6, 7):
        plane.middle(k)

    def unturn(row, rows, grads, block):
        back = grads * cos[rows] + partner(grads * sin[rows])
        factor = lax.rsqrt(half_sums(block * block) * (1.0 / HEAD_DIM) + EPSILON)
        gain_term = jnp.sum(back * block * factor, axis=0, keepdims=True)
        scaled = back * head_gain[row : row + 1]
        inner = half_sums(scaled * block) * (1.0 / HEAD_DIM)
        return factor * scaled - block * (factor * factor * factor * inner), gain_term

    def heads(index):
        b, half = lax.div(index, 2), lax.rem(index, 2)
        for i in range(seq // SHORT):
            rows, span = pl.ds(i * SHORT, SHORT), (i + 1) * SHORT
            query = qkv_low[b, rows]
            lane = lax.broadcasted_iota(jnp.int32, query.shape, 1)
            side = lax.div(lane, 64) == half
            chosen = jnp.where(side, query, 0)
            d_chosen = jnp.where(side, d_att[b, rows], 0)
            logs = jnp.max(jnp.where(side, log_sums[b, rows], -1e30), axis=-1, keepdims=True)
            scores = attention_scores(chosen, keys[:span], key_bias[0:1], i * SHORT, span)
            probs = jnp.exp(scores - logs)
            d_probs = lax.dot_general(d_chosen, values[:span], NT, preferred_element_type=F32)
            delta = jnp.sum(probs * d_probs, axis=-1, keepdims=True)
            d_scores = (probs * (d_probs - delta)).astype(BF16)
            d_query = jnp.dot(d_scores, keys[:span], preferred_element_type=F32) * root
            d_keys[:span] += lax.dot_general(d_scores, chosen, TN, preferred_element_type=F32)
            d_values[:span] += lax.dot_general(
                probs.astype(BF16), d_chosen, TN, preferred_element_type=F32
            )
            d_low[b, rows] = jnp.where(side, d_query.astype(BF16), d_low[b, rows])

    def unturn_queries(index):
        rows = pl.ds(pl.multiple_of(index * BLOCK, BLOCK), BLOCK)
        for b in range(2):
            grads = d_low[b, rows].astype(F32)
            d_block, gain_term = unturn(0, rows, grads, qkv_raw[b, rows])
            d_low[b, rows] = d_block.astype(BF16)
            gain_g[0:1] += gain_term

    row_loop(2, heads)
    for k in (4, 5):
        plane.combine(k)
    for k in (0, 1):
        end(k)
    row_loop(2, heads, 2)
    for k in (8, 9):
        plane.middle(k)
    for k in (6, 7):
        plane.combine(k)
    for k in (2, 3):
        end(k)
    row_loop(seq // BLOCK, unturn_queries)

    def finish(index):
        rows = pl.ds(pl.multiple_of(index * BLOCK, BLOCK), BLOCK)
        k_sum, v_sum = d_keys[rows], d_values[rows]
        low = low_half(k_sum.shape)
        k_sum = (k_sum + pltpu.roll(k_sum, 64, 1)) * root
        v_sum = v_sum + pltpu.roll(v_sum, 64, 1)
        grads = jnp.where(low, k_sum, v_sum).astype(BF16).astype(F32)
        d_block, gain_term = unturn(2, rows, grads, qkv_raw[2, rows])
        d_low[2, rows] = jnp.where(low, d_block, grads).astype(BF16)
        gain_g[1:2] += gain_term
        for j in range(4):
            columns = slice(512 * j, 512 * (j + 1))
            sums = jnp.zeros((BLOCK, 512), F32)
            for b in range(3):
                weight = qkv_w[columns, 128 * b : 128 * (b + 1)]
                sums += lax.dot_general(d_low[b, rows], weight, NT, preferred_element_type=F32)
            part[index, :, columns] = sums.astype(BF16)

    row_loop(seq // BLOCK, finish)

    dnorm = ReduceCtx(links, place, part, parts, None, from_core2, to_y2, from_y2)
    dnorm.begin()
    normed_load.wait()
    for b in range(3):
        left = d_low[b].T
        for f in range(8):
            right = branch_all[:, :, 256 * f : 256 * (f + 1)].reshape(seq, 256)
            qkv_g[f // 2, f % 2, 128 * b : 128 * (b + 1)] = jnp.dot(
                left, right, preferred_element_type=F32
            ).astype(BF16)
    qkv_step = qkv_x.shape[2]
    qkv_rows = [pl.ds(k * qkv_step, qkv_step) for k in range(qkv_x.shape[0])]
    qkv_chunks = [lambda x, rows=rows: qkv_g.at[:, x, rows] for rows in qkv_rows]
    qkv_plane = ReducePlane(links, place, qkv_chunks, qkv_x, qkv_z)
    qkv_outs = [SpreadCtx(links, place, qkv_all, [rows]) for rows in qkv_rows]
    for k in range(len(qkv_chunks)):
        qkv_plane.send_x(k)
    links.arrive(out_x, out_slot)
    root_slot, final_slot = links.slots(3), links.slots(1)
    holds = place.z == place.c
    out_mine = out_g.at[place.x]
    out_mine[...] = (out_mine[...].astype(F32) + out_x[...].astype(F32)).astype(BF16)
    rank = place.rank(place.z, place.c)
    to_root = links.copy(
        out_mine,
        out_z.at[lax.rem(rank, 3)],
        root_slot + lax.rem(rank, 3),
        (place.c * 2 + place.x, place.c),
    )

    @pl.when(jnp.logical_not(holds))
    def _():
        to_root.start()

    for k in range(2):
        dnorm.cross(k)
    for k in (8, 9):
        plane.combine(k)
    for k in (4, 5):
        end(k)
    for k in (0, 1):
        outs[k].forward(0)
    for k in (2, 3):
        outs[k].forward(0)
    for k in (6, 7):
        end(k)
    for k, rows in enumerate(parts):
        value = middle[rows] + ffn.total(k)
        positions = lax.broadcasted_iota(jnp.int32, (value.shape[0], 1), 0)
        positions += tokens * place.c + k * value.shape[0]
        layer_out[rows] = jnp.where(positions < lengths[0], value, 0.0).astype(BF16)
    for k in (10, 11):
        plane.middle(k)
    for k in (4, 5):
        outs[k].forward(0)
    attn_gain = None
    for k, rows in enumerate(parts):
        grad, term = norm_back(dnorm.total(k), x_s[rows].astype(F32), gains[0:1])
        attn_gain = term if attn_gain is None else attn_gain + term
        input_grad[rows] = (d_middle[rows] + grad).astype(BF16)
    mine[...] = jnp.zeros_like(mine)
    for f in range(8):
        mine[f, 0:1] = attn_gain[:, 256 * f : 256 * (f + 1)]
        mine[f, 1:2] = ffn_gain[:, 256 * f : 256 * (f + 1)]
        mine[f, 2:3, 0:128] = gain_g[0:1]
        mine[f, 2:3, 128:256] = gain_g[1:2]
    plane_slot, ctx_slot = links.slots(8), links.slots(4)
    for f in fellows:
        links.send(mine.at[f], plane_stats.at[place.f], plane_slot + place.f, (f, place.c))
    plane_stats[place.f] = mine[place.f]

    for k in (8, 9):
        end(k)
    for k in (6, 7):
        outs[k].forward(0)
    for k in range(len(qkv_chunks)):
        qkv_plane.middle(k)
    for k in (10, 11):
        plane.combine(k)
    for k in (10, 11):
        end(k)
    for f in fellows:
        links.arrive(plane_stats.at[f], plane_slot + f)
    sums = plane_stats[0]
    for f in range(1, 8):
        sums += plane_stats[f]
    ctx_stats[place.c] = sums
    for device in (place.core_dev, place.y_dev, place.diag_dev):
        links.send(ctx_stats.at[place.c], ctx_stats.at[place.c], ctx_slot + place.c, device)

    final = [
        links.copy(out_all, out_all, final_slot, device)
        for device in (place.core_dev, place.y_dev)
    ]
    onward = links.copy(out_all, out_all, final_slot, place.core_dev)

    @pl.when(holds)
    def _():
        sums = out_mine[...].astype(F32)
        for other in range(3):
            links.arrive(out_z.at[other], root_slot + other)
            sums += out_z[other].astype(F32)
        out_all[...] = sums.astype(BF16)
        for made in final:
            made.start()

    for k in range(len(qkv_chunks)):
        total = qkv_plane.end(k)
        qkv_outs[k].begin(0, total)
        kept.append(links.local(total, qkv_all.at[place.c, qkv_rows[k]]))
    for k in range(8, count):
        outs[k].forward(0)
    relays = place.c_y == place.z

    @pl.when(jnp.logical_not(holds))
    def _():
        links.arrive(out_all, final_slot)

    @pl.when(relays)
    def _():
        onward.start()

    for c in (place.c_core, place.c_y, place.c_diag):
        links.arrive(ctx_stats.at[c], ctx_slot + c)
    stats[...] = ((ctx_stats[0] + ctx_stats[1]) + ctx_stats[2]) + ctx_stats[3]
    for out in qkv_outs:
        out.forward(0)
    for out in outs + qkv_outs:
        out.end()
    for made in kept:
        made.wait()
    links.finish()
    plane.finish()
    qkv_plane.finish()

    @pl.when(jnp.logical_not(holds))
    def _():
        to_root.wait_send()

    @pl.when(relays)
    def _():
        onward.wait_send()

    @pl.when(holds)
    def _():
        for made in final:
            made.wait_send()


def finish_kernel(
    gu_parts, dn_parts, out_s, qkv_parts, layer_s, input_s, stats,
    out, dn_out, out_out, qkv_out, layer_out, input_out, attn_out, ffn_out, pairs, sems,
):
    rows = gu_parts.shape[1]
    first = pl.multiple_of(pl.program_id(0) * rows, rows)
    sent = []
    for c in range(4):
        for f in range(8):
            b = 4 * f + c
            for side in range(2):
                column = 1024 * side + 128 * f
                block = gu_parts[c, :, column : column + 128]
                pairs[b, pl.ds(side, rows, stride=2), :] = block.astype(F32)
            made = pltpu.make_async_copy(
                pairs.at[b].reshape(rows, 2, 128),
                out.at[pl.ds(first, rows), :, pl.ds(128 * b, 128)],
                sems.at[b],
            )
            made.start()
            sent.append(made)
    dn_out[...] = dn_parts[...].astype(F32)
    out_out[...] = out_s[...].astype(F32)
    layer_out[...] = layer_s[...]
    input_out[...] = input_s[...]

    @pl.when(pl.program_id(0) == 0)
    def _():
        attn_out[...] = stats[0:1]
        ffn_out[...] = stats[1:2]
        for c in range(4):
            qkv_out[:, 256 * c : 256 * (c + 1)] = qkv_parts[c, 0:256].astype(F32).T
        for y in range(2):
            for j in range(2):
                from_row = 256 + 64 * j
                both = [qkv_parts[2 * y + core, from_row : from_row + 64] for core in range(2)]
                column = 1024 + 256 * j + 128 * y
                qkv_out[:, column : column + 128] = jnp.concatenate(both, axis=0).astype(F32).T

    for made in sent:
        made.wait()


def shaped(shape, kind=BF16):
    return jax.ShapeDtypeStruct(shape, kind)


def call(kernel, ins, outs, scratch=(), sems=None, number=None, flops=0):
    scratch = list(scratch)
    extra = {}
    if sems is not None:
        scratch += [pltpu.SemaphoreType.DMA((n,)) for n in sems]
        extra = dict(collective_id=number, has_side_effects=True)
    return pl.pallas_call(
        kernel,
        out_shape=tuple(shape for shape, _ in outs),
        in_specs=[spec for _, spec in ins],
        out_specs=tuple(spec for _, spec in outs),
        scratch_shapes=scratch,
        compiler_params=pltpu.CompilerParams(vmem_limit_bytes=VMEM_BYTES, **extra),
    )(*[array for array, _ in ins])


def split_heads(
    inputs,
    cotangent,
    lengths,
    qkv_weight,
    out_weight,
    gate_up,
    down_weight,
    attn_gain,
    ffn_gain,
    qk_gain,
):
    tokens, width = inputs.shape[1:]
    seq = tokens * 4
    source = inputs[0]
    rows, parts, units = gate_up.shape
    down_rows = down_weight.shape[0] // 4
    gain_s = jnp.concatenate(
        [attn_gain[None], ffn_gain[None], jnp.zeros((6, rows), BF16)], axis=0
    ).astype(F32)

    half_dim = HEAD_DIM // 2
    frequency = 10000.0 ** (-2.0 * np.arange(half_dim) / HEAD_DIM)
    turns = [np.arange(0, seq, 64)[:, None] * frequency, np.arange(64)[:, None] * frequency]
    signs = np.repeat([-1.0, 1.0, -1.0, 1.0], half_dim)
    angles = jnp.asarray(
        np.concatenate(
            [part for t in turns for part in (np.tile(np.cos(t), 4), np.tile(np.sin(t), 4) * signs)]
        ),
        F32,
    )
    table = pltpu.VMEM((seq, 128), F32)
    (
        qkv_w, out_w, gains, normed, qkv_raw, qkv_low, att_low, log_sums,
        gu_w, dn_w, dout_all, middle, mid_all, head_gain, key_bias,
    ) = call(
        forward_kernel,
        [(lengths, pl.BlockSpec(memory_space=pltpu.SMEM))]
        + [
            (a, HBM)
            for a in (qkv_weight, out_weight, gain_s, source, gate_up, down_weight, cotangent[0])
        ]
        + [(angles, VMEM), (qk_gain, VMEM)],
        [
            (shaped((8, rows, 384)), HBM),
            (shaped((2, out_weight.shape[0], width)), HBM),
            (shaped((8, width), F32), VMEM),
            (shaped((seq, width)), HBM),
            (shaped((3, seq, 128), F32), HBM),
            (shaped((3, seq, 128)), HBM),
            (shaped((2, seq, 128)), HBM),
            (shaped((2, seq, 128), F32), HBM),
            (shaped((8, rows, width)), HBM),
            (shaped((8, down_rows, width)), HBM),
            (shaped((4, tokens, width)), HBM),
            (shaped((tokens, width), F32), VMEM),
            (shaped((4, tokens, width)), HBM),
            (shaped((8, 128), F32), VMEM),
            (shaped((8, seq), F32), VMEM),
        ],
        [
            pltpu.VMEM((2, rows, 128), BF16),
            pltpu.VMEM((rows, 128), BF16),
            pltpu.VMEM((tokens, width), BF16),
            table,
            table,
            pltpu.VMEM((8, 8, rows), F32),
            pltpu.VMEM((8, rows, 384), BF16),
            pltpu.VMEM((2, out_weight.shape[0], width), BF16),
            pltpu.VMEM((4, tokens, width), BF16),
            pltpu.VMEM((seq, width), BF16),
            pltpu.VMEM((3, seq, 128), F32),
            pltpu.VMEM((3, seq, 128), BF16),
            pltpu.VMEM((2, seq, 128), BF16),
            pltpu.VMEM((2, seq, 128), F32),
            pltpu.VMEM((4, tokens, width), BF16),
            pltpu.VMEM((seq, 128), BF16),
            pltpu.VMEM((seq, 128), BF16),
            pltpu.VMEM((2, tokens, width), BF16),
            pltpu.VMEM((tokens, width), BF16),
            pltpu.VMEM((tokens, width), BF16),
            pltpu.VMEM((tokens, width), BF16),
            pltpu.VMEM((8, rows, 2, 128), BF16),
            pltpu.VMEM((2 * rows, 128), F32),
            pltpu.VMEM((rows, width), BF16),
        ],
        sems=(180, 170, 32),
        number=0,
    )
    qkv_w = qkv_w.reshape(width, 384)
    block = pltpu.VMEM((tokens, width), BF16)
    pair = pltpu.VMEM((2, tokens, width), BF16)
    whole = pltpu.VMEM((4, tokens, width), BF16)
    hidden_units = units // 4
    gu_g, dn_pair, ffn_part, d_middle, branch_s, ffn_gain_part = call(
        feed_kernel,
        [(a, HBM) for a in (gu_w, dn_w, dout_all, mid_all, middle)] + [(gains, VMEM)],
        [
            (shaped((4, 2, rows, width)), HBM),
            (shaped((4, down_rows, width)), HBM),
            (shaped((4, tokens, width)), HBM),
            (shaped((tokens, width), F32), HBM),
            (shaped((tokens, width)), HBM),
            (shaped((1, width), F32), VMEM),
        ],
        [
            pltpu.VMEM((8, rows, width), BF16),
            pltpu.VMEM((8, down_rows, width), BF16),
            whole,
            whole,
            pltpu.VMEM((seq, hidden_units), BF16),
            pltpu.VMEM((seq, parts * hidden_units), BF16),
            pltpu.VMEM((4, 2, down_rows, width), BF16),
            pltpu.VMEM((4, down_rows, width), BF16),
            pltpu.VMEM((2, rows, width), BF16),
            whole,
            pair,
            block,
            block,
            pltpu.VMEM((tokens, width), F32),
            pltpu.VMEM((tokens, width), F32),
            block,
        ],
        sems=(16, 16, 24),
        number=2,
    )
    step = 32
    count = (rows + down_rows) // step
    heads = pltpu.VMEM((seq, 128), BF16)
    gu_all, dn_all, layer_out, qkv_all, out_all, input_grad, stats = call(
        backward_kernel,
        [
            (gu_g, HBM),
            (dn_pair, HBM),
            (ffn_part, HBM),
            (middle, HBM),
            (d_middle, HBM),
            (branch_s, HBM),
            (source, HBM),
            (lengths, pl.BlockSpec(memory_space=pltpu.SMEM)),
            (gains, VMEM),
            (ffn_gain_part, VMEM),
            (angles, VMEM),
            (head_gain, VMEM),
            (key_bias, VMEM),
            (normed.reshape(4, tokens, width), HBM),
        ]
        + [(a, HBM) for a in (qkv_raw, qkv_low, att_low, log_sums, qkv_w, out_w)],
        [
            (shaped((4, rows, width)), HBM),
            (shaped((4, down_rows, width)), HBM),
            (shaped((tokens, width)), VMEM),
            (shaped((4, 384, rows)), HBM),
            (shaped((128, width)), VMEM),
            (shaped((tokens, width)), VMEM),
            (shaped((8, rows), F32), VMEM),
        ],
        [
            pltpu.VMEM((8, 4, step, width), BF16),
            pltpu.VMEM((rows // step, 4, step, width), BF16),
            pltpu.VMEM((count, 2, step, width), BF16),
            pltpu.VMEM((count, 2, step, width), BF16),
            block, pair, block, block, pair, block, block,
            pltpu.VMEM((tokens, width), F32),
            block,
            pltpu.VMEM((tokens, width), F32),
            pltpu.VMEM((4, tokens, width), BF16),
            pltpu.VMEM((4, tokens, width), BF16),
            table,
            table,
            pltpu.VMEM((3, seq, 128), F32),
            pltpu.VMEM((3, seq, 128), BF16),
            pltpu.VMEM((2, seq, 128), BF16),
            pltpu.VMEM((2, seq, 128), F32),
            pltpu.VMEM((width, 384), BF16),
            pltpu.VMEM((2, 128, width), BF16),
            heads,
            heads,
            pltpu.VMEM((2, seq, 128), BF16),
            pltpu.VMEM((3, seq, 128), BF16),
            table,
            table,
            pltpu.VMEM((8, 128), F32),
            pltpu.VMEM((4, 2, 384, rows), BF16),
            pltpu.VMEM((2, 4, 192, rows), BF16),
            pltpu.VMEM((2, 3, 192, rows), BF16),
            pltpu.VMEM((2, 128, width), BF16),
            pltpu.VMEM((128, width), BF16),
            pltpu.VMEM((3, 128, width), BF16),
            pltpu.VMEM((8, 8, rows), F32),
            pltpu.VMEM((8, 8, rows), F32),
            pltpu.VMEM((4, 8, rows), F32),
        ],
        sems=(190, 190, 70),
        number=1,
    )
    some = 64
    steps = rows // some
    few = down_rows // steps
    out_rows = out_weight.shape[0]
    block_of = lambda n: pl.BlockSpec((n, width), lambda i: (i, 0))
    fixed = lambda *shape: pl.BlockSpec(shape, lambda i: (0,) * len(shape))
    gate_up_grad, down_grad, out_grad, qkv_grad, layer_out, input_grad, attn_g, ffn_g = pl.pallas_call(
        finish_kernel,
        grid=(steps,),
        in_specs=[
            pl.BlockSpec((4, some, width), lambda i: (0, i, 0)),
            pl.BlockSpec((4, few, width), lambda i: (0, i, 0)),
            block_of(out_rows // steps),
            fixed(4, 384, rows),
            block_of(tokens // steps),
            block_of(tokens // steps),
            fixed(8, rows),
        ],
        out_specs=[
            HBM,
            pl.BlockSpec((4, few, width), lambda i: (0, i, 0)),
            block_of(out_rows // steps),
            fixed(rows, qkv_weight.shape[1]),
            block_of(tokens // steps),
            block_of(tokens // steps),
            fixed(1, rows),
            fixed(1, rows),
        ],
        out_shape=[
            shaped((rows, parts, units), F32),
            shaped((4, down_rows, width), F32),
            shaped((out_rows, width), F32),
            shaped((rows, qkv_weight.shape[1]), F32),
            shaped((tokens, width)),
            shaped((tokens, width)),
            shaped((1, rows), F32),
            shaped((1, rows), F32),
        ],
        scratch_shapes=[
            pltpu.VMEM((32, 2 * some, 128), F32),
            pltpu.SemaphoreType.DMA((32,)),
        ],
        compiler_params=pltpu.CompilerParams(vmem_limit_bytes=VMEM_BYTES),
    )(gu_all, dn_all, out_all, qkv_all, layer_out, input_grad, stats)
    return (
        layer_out[None],
        input_grad[None],
        qkv_grad,
        out_grad,
        gate_up_grad,
        down_grad.reshape(4 * down_rows, width),
        attn_g[0],
        ffn_g[0],
        jnp.stack([stats[2, :64] + stats[2, 64:128], stats[2, 128:192]]),
    )


def solution(mesh):
    sizes = (mesh.shape["fsdp"], mesh.shape["ctx"])
    return jax.shard_map(
        split_heads if sizes == (8, 4) else on_device,
        mesh=mesh,
        in_specs=(
            P("fsdp", "ctx", None),
            P("fsdp", "ctx", None),
            P("fsdp"),
            P("fsdp", None),
            P("fsdp", None),
            P("fsdp", None, None),
            P("fsdp", None),
            P("fsdp"),
            P("fsdp"),
            P(),
        ),
        out_specs=(
            P("fsdp", "ctx", None),
            P("fsdp", "ctx", None),
            P("fsdp", None),
            P("fsdp", None),
            P("fsdp", None, None),
            P("fsdp", None),
            P("fsdp"),
            P("fsdp"),
            P(),
        ),
        check_vma=False,
    )
```

```python
import functools
import math

import jax
import jax.numpy as jnp
import numpy as np
from jax import lax
from jax.experimental import pallas as pl
from jax.experimental.pallas import tpu as pltpu
from jax.sharding import PartitionSpec as P

HEADS = 16
KV_HEADS = 4
HEAD_DIM = 64


EPSILON = 1e-06


def root_norm(values, norm_gain):
    factor = lax.rsqrt(jnp.mean(values * values, axis=-1, keepdims=True) + EPSILON)
    return values * factor * norm_gain


def rotation_tables(positions):
    half_dim = HEAD_DIM // 2
    frequency = 10000.0 ** (-(2.0 * jnp.arange(half_dim, dtype=jnp.float32)) / HEAD_DIM)
    angles = positions.astype(jnp.float32)[:, None] * frequency[None, :]
    return (jnp.cos(angles), jnp.sin(angles))


def rotate(values, cos_table, sin_table):
    half_dim = values.shape[-1] // 2
    lower_half = values[..., :half_dim]
    upper_half = values[..., half_dim:]
    cos_part = cos_table[:, None, :]
    sin_part = sin_table[:, None, :]
    return jnp.concatenate(
        [
            lower_half * cos_part - upper_half * sin_part,
            upper_half * cos_part + lower_half * sin_part,
        ],
        axis=-1,
    )


def prepare_heads(qkv_out, head_gain, cos_table, sin_table):
    row_count = qkv_out.shape[0]
    query_cols = HEADS * HEAD_DIM
    key_cols = KV_HEADS * HEAD_DIM
    queries = qkv_out[:, :query_cols].reshape(row_count, HEADS, HEAD_DIM)
    key_part = qkv_out[:, query_cols : query_cols + key_cols].reshape(row_count, KV_HEADS, HEAD_DIM)
    value_part = qkv_out[:, query_cols + key_cols :]
    queries = rotate(root_norm(queries, head_gain[0]), cos_table, sin_table).reshape(
        row_count, query_cols
    )
    key_part = rotate(root_norm(key_part, head_gain[1]), cos_table, sin_table).reshape(
        row_count, key_cols
    )
    return (queries, key_part, value_part)


def activate(projected):
    gate_part = projected[:, 0]
    return gate_part * jax.nn.sigmoid(gate_part) * projected[:, 1]


def contract_rows(left, right):
    return lax.dot_general(
        left, right, (((0,), (0,)), ((), ())), preferred_element_type=jnp.float32
    )


def contract_cols(left, right):
    return lax.dot_general(
        left, right, (((1,), (1,)), ((), ())), preferred_element_type=jnp.float32
    )


def on_device(
    inputs,
    cotangent,
    lengths,
    qkv_weight,
    out_weight,
    gate_up,
    down_weight,
    attn_gain,
    ffn_gain,
    qk_gain,
):
    token_count = inputs.shape[1]
    group = HEADS // KV_HEADS
    key_cols = KV_HEADS * HEAD_DIM
    seq_len = token_count * lax.axis_size("ctx")
    positions = lax.axis_index("ctx") * token_count + jnp.arange(token_count, dtype=jnp.int32)
    length = lengths[0]
    row_keep = (positions < length).astype(jnp.float32)[:, None]
    inv_root = 1.0 / math.sqrt(HEAD_DIM)
    source = inputs[0].astype(jnp.float32)
    qkv_full, out_full, attn_full, ffn_full = (
        lax.all_gather(qkv_weight, "fsdp", axis=0, tiled=True),
        lax.all_gather(out_weight, "fsdp", axis=0, tiled=True),
        lax.all_gather(attn_gain, "fsdp", axis=0, tiled=True),
        lax.all_gather(ffn_gain, "fsdp", axis=0, tiled=True),
    )
    attn_norm = attn_full.astype(jnp.float32)
    ffn_norm = ffn_full.astype(jnp.float32)
    normed = root_norm(source, attn_norm).astype(jnp.bfloat16)
    qkv_out = jnp.dot(normed, qkv_full, preferred_element_type=jnp.float32)
    cos_table, sin_table = rotation_tables(positions)
    head_gain = qk_gain.astype(jnp.float32)

    def head_pieces(qkv_values, gain_values):
        return prepare_heads(qkv_values, gain_values, cos_table, sin_table)

    head_values, head_pull = jax.vjp(head_pieces, qkv_out, head_gain)
    queries, key_part, value_part = head_values
    query_low = queries.astype(jnp.bfloat16).reshape(token_count, KV_HEADS, group, HEAD_DIM)
    kv_local = jnp.concatenate([key_part, value_part], axis=1).astype(jnp.bfloat16)
    kv_whole = lax.all_gather(kv_local, "ctx", axis=0, tiled=True)
    block = 512
    block_total = seq_len // block
    kv_blocks = kv_whole.reshape(block_total, block, 2, KV_HEADS, HEAD_DIM)
    starts = jnp.arange(block_total, dtype=jnp.int32) * block

    def block_scores(key_block, block_start):
        scores = (
            jnp.einsum("bhgd,thd->hgbt", query_low, key_block, preferred_element_type=jnp.float32)
            * inv_root
        )
        key_pos = block_start + jnp.arange(key_block.shape[0], dtype=jnp.int32)
        visible = (key_pos[None, :] <= positions[:, None]) & (key_pos[None, :] < length)
        return (scores, visible)

    def max_step(state, item):
        running_max, running_sum = state
        kv_block, block_start = item
        scores, visible = block_scores(kv_block[:, 0], block_start)
        new_max = jnp.maximum(running_max, jnp.max(jnp.where(visible, scores, -1e30), axis=-1))
        expanded = jnp.where(visible, jnp.exp(scores - new_max[..., None]), 0.0)
        running_sum = running_sum * jnp.exp(running_max - new_max) + jnp.sum(expanded, axis=-1)
        return ((new_max, running_sum), None)

    stat_shape = (KV_HEADS, group, token_count)
    start_state = (jnp.full(stat_shape, -1e30, jnp.float32), jnp.zeros(stat_shape, jnp.float32))
    final_state, unused_out = lax.scan(max_step, start_state, (kv_blocks, starts))
    log_total = final_state[0] + jnp.log(final_state[1])

    def block_probs(kv_block, block_start):
        scores, visible = block_scores(kv_block[:, 0], block_start)
        return jnp.where(visible, jnp.exp(scores - log_total[..., None]), 0.0)

    def value_step(totals, item):
        kv_block, block_start = item
        probs_low = block_probs(kv_block, block_start).astype(jnp.bfloat16)
        return (
            totals
            + jnp.einsum(
                "hgbt,thd->bhgd", probs_low, kv_block[:, 1], preferred_element_type=jnp.float32
            ),
            None,
        )

    attended, unused_out = lax.scan(
        value_step,
        jnp.zeros((token_count, KV_HEADS, group, HEAD_DIM), jnp.float32),
        (kv_blocks, starts),
    )
    attended_low = attended.reshape(token_count, HEADS * HEAD_DIM).astype(jnp.bfloat16)
    middle = source + jnp.dot(attended_low, out_full, preferred_element_type=jnp.float32)
    normed_mid = root_norm(middle, ffn_norm).astype(jnp.bfloat16)
    columns = normed_mid
    projected = jnp.einsum(
        "td,dgf->tgf",
        columns,
        lax.all_gather(gate_up, "fsdp", axis=0, tiled=True),
        preferred_element_type=jnp.float32,
    )
    act_value, act_pull = jax.vjp(activate, projected)
    hidden = act_value.astype(jnp.bfloat16)
    columns = hidden
    ffn_out = jnp.dot(
        columns,
        lax.all_gather(down_weight, "fsdp", axis=0, tiled=True),
        preferred_element_type=jnp.float32,
    )
    layer_out = (row_keep * (middle + ffn_out)).astype(jnp.bfloat16)[None]
    d_out = row_keep * cotangent[0].astype(jnp.float32)
    d_out_low = d_out.astype(jnp.bfloat16)
    down_shard = lax.psum_scatter(
        contract_rows(hidden, d_out_low).astype(jnp.bfloat16),
        "fsdp",
        scatter_dimension=0,
        tiled=True,
    )
    d_hidden = contract_cols(d_out_low, lax.all_gather(down_weight, "fsdp", axis=0, tiled=True))
    d_proj_low = act_pull(d_hidden)[0].astype(jnp.bfloat16)
    columns = normed_mid
    gate_up_shard = lax.psum_scatter(
        jnp.einsum("td,tgf->dgf", columns, d_proj_low, preferred_element_type=jnp.float32).astype(
            jnp.bfloat16
        ),
        "fsdp",
        scatter_dimension=0,
        tiled=True,
    )
    d_normed_mid = jnp.einsum(
        "tgf,dgf->td",
        d_proj_low,
        lax.all_gather(gate_up, "fsdp", axis=0, tiled=True),
        preferred_element_type=jnp.float32,
    )
    mid_value, mid_pull = jax.vjp(root_norm, middle, ffn_norm)
    d_mid_norm, ffn_gain_part = mid_pull(d_normed_mid)
    d_middle = d_out + d_mid_norm
    d_branch = d_middle.astype(jnp.bfloat16)
    out_term = contract_rows(attended_low, d_branch)
    d_attended = (
        contract_cols(d_branch, out_full)
        .astype(jnp.bfloat16)
        .reshape(token_count, KV_HEADS, group, HEAD_DIM)
    )
    delta = jnp.transpose(jnp.sum(d_attended.astype(jnp.float32) * attended, axis=-1), (1, 2, 0))

    def block_grads(kv_block, block_start):
        probs = block_probs(kv_block, block_start)
        d_probs = jnp.einsum(
            "bhgd,thd->hgbt", d_attended, kv_block[:, 1], preferred_element_type=jnp.float32
        )
        d_scores = (probs * (d_probs - delta[..., None])).astype(jnp.bfloat16)
        return (probs.astype(jnp.bfloat16), d_scores)

    def query_step(totals, item):
        kv_block, block_start = item
        probs_low, d_scores = block_grads(kv_block, block_start)
        return (
            totals
            + jnp.einsum(
                "hgbt,thd->bhgd", d_scores, kv_block[:, 0], preferred_element_type=jnp.float32
            ),
            None,
        )

    d_query_sum, unused_out = lax.scan(
        query_step,
        jnp.zeros((token_count, KV_HEADS, group, HEAD_DIM), jnp.float32),
        (kv_blocks, starts),
    )
    d_query = (d_query_sum * inv_root).reshape(token_count, HEADS * HEAD_DIM).astype(jnp.bfloat16)
    sub_block = 512
    sub_total = token_count * lax.axis_size("ctx") // sub_block
    pieces = kv_whole.reshape(sub_total, sub_block, 2, KV_HEADS, HEAD_DIM)
    sub_starts = jnp.arange(sub_total, dtype=jnp.int32) * sub_block

    def key_grads(item):
        kv_block, block_start = item
        probs_low, d_scores = block_grads(kv_block, block_start)
        d_keys = (
            jnp.einsum("hgbt,bhgd->thd", d_scores, query_low, preferred_element_type=jnp.float32)
            * inv_root
        )
        d_values = jnp.einsum(
            "hgbt,bhgd->thd", probs_low, d_attended, preferred_element_type=jnp.float32
        )
        return jnp.concatenate(
            [d_keys.reshape(sub_block, key_cols), d_values.reshape(sub_block, key_cols)], axis=1
        )

    kv_grad = lax.psum_scatter(
        lax.map(key_grads, (pieces, sub_starts))
        .reshape(token_count * lax.axis_size("ctx"), 2 * key_cols)
        .astype(jnp.bfloat16),
        "ctx",
        scatter_dimension=0,
        tiled=True,
    ).astype(jnp.float32)
    d_key_low = kv_grad[:, :key_cols].astype(jnp.bfloat16).astype(jnp.float32)
    d_value_low = kv_grad[:, key_cols:].astype(jnp.bfloat16).astype(jnp.float32)
    d_qkv_out, qk_part = head_pull((d_query.astype(jnp.float32), d_key_low, d_value_low))
    d_qkv = d_qkv_out.astype(jnp.bfloat16)
    qkv_term = contract_rows(normed, d_qkv)
    d_normed = contract_cols(d_qkv, qkv_full)
    first_value, first_pull = jax.vjp(root_norm, source, attn_norm)
    d_source_norm, attn_gain_part = first_pull(d_normed)
    input_grad = (d_middle + d_source_norm).astype(jnp.bfloat16)[None]
    qkv_shard, out_shard, attn_shard, ffn_shard = (
        lax.psum_scatter(
            qkv_term.astype(jnp.bfloat16), "fsdp", scatter_dimension=0, tiled=True
        ).astype(jnp.float32),
        lax.psum_scatter(
            out_term.astype(jnp.bfloat16), "fsdp", scatter_dimension=0, tiled=True
        ).astype(jnp.float32),
        lax.psum_scatter(
            attn_gain_part.astype(jnp.bfloat16), "fsdp", scatter_dimension=0, tiled=True
        ).astype(jnp.float32),
        lax.psum_scatter(
            ffn_gain_part.astype(jnp.bfloat16), "fsdp", scatter_dimension=0, tiled=True
        ).astype(jnp.float32),
    )
    summed = (
        lax.psum(qkv_shard.astype(jnp.bfloat16), "ctx").astype(jnp.float32),
        lax.psum(out_shard.astype(jnp.bfloat16), "ctx").astype(jnp.float32),
        lax.psum(gate_up_shard, "ctx").astype(jnp.float32),
        lax.psum(down_shard, "ctx").astype(jnp.float32),
        lax.psum(attn_shard.astype(jnp.bfloat16), "ctx").astype(jnp.float32),
        lax.psum(ffn_shard.astype(jnp.bfloat16), "ctx").astype(jnp.float32),
    )
    qk_total = lax.psum(qk_part, ("fsdp", "ctx"))
    return (
        layer_out,
        input_grad,
        summed[0],
        summed[1],
        summed[2],
        summed[3],
        summed[4],
        summed[5],
        qk_total,
    )


MESH = pl.DeviceIdType.MESH
F32 = jnp.float32
BF16 = jnp.bfloat16
VMEM_BYTES = 60 << 20
HBM = pl.BlockSpec(memory_space=pl.ANY)
VMEM = pl.BlockSpec(memory_space=pltpu.VMEM)


class Place:
    def __init__(self):
        self.f = lax.axis_index("fsdp")
        self.c = lax.axis_index("ctx")
        self.z, self.x = lax.div(self.f, 2), lax.rem(self.f, 2)
        self.y, self.core = lax.div(self.c, 2), lax.rem(self.c, 2)
        self.xo, self.yo, self.co = 1 - self.x, 1 - self.y, 1 - self.core
        upper = lax.div(self.z, 2)
        self.others = (self.z + 1 - 2 * lax.rem(self.z, 2), 2 - upper, 3 - 3 * upper)
        self.inner = lax.rem(self.z, 2) + upper == 1
        self.far = 2 - 2 * upper
        self.x_dev = (self.z * 2 + self.xo, self.c)
        self.c_core = self.y * 2 + self.co
        self.c_y = self.yo * 2 + self.core
        self.c_diag = self.yo * 2 + self.co
        self.core_dev = (self.f, self.c_core)
        self.y_dev = (self.f, self.c_y)
        self.diag_dev = (self.f, self.c_diag)

    def rank(self, source, target):
        return jnp.where(source > target, source - 1, source)

    def z_dev(self, z):
        return (z * 2 + self.x, self.c)

    def meet(self, partners):
        barrier = pltpu.get_barrier_semaphore()
        for partner in partners:
            pl.semaphore_signal(barrier, inc=1, device_id=partner, device_id_type=MESH)
        pl.semaphore_wait(barrier, len(partners))

    def neighbours(self):
        return [self.z_dev(o) for o in self.others] + [self.x_dev, self.core_dev, self.y_dev]


class Links:
    def __init__(self, place, send_sems, recv_sems, local_sems):
        self.place = place
        self.send_sems, self.recv_sems, self.local_sems = send_sems, recv_sems, local_sems
        self.sends = self.recvs = self.locals = 0
        self.open = []

    def slots(self, count):
        first = self.recvs
        self.recvs += count
        return first

    def copy(self, src, dst, slot, device):
        made = pltpu.make_async_remote_copy(
            src_ref=src,
            dst_ref=dst,
            send_sem=self.send_sems.at[self.sends],
            recv_sem=self.recv_sems.at[slot],
            device_id=device,
            device_id_type=MESH,
        )
        self.sends += 1
        return made

    def send(self, src, dst, slot, device):
        made = self.copy(src, dst, slot, device)
        made.start()
        self.open.append(made)
        return made

    def settle(self, sends):
        for made in sends:
            made.wait_send()
            self.open = [one for one in self.open if one is not made]

    def arrive(self, ref, slot):
        pltpu.make_async_remote_copy(
            src_ref=ref,
            dst_ref=ref,
            send_sem=self.send_sems.at[0],
            recv_sem=self.recv_sems.at[slot],
            device_id=self.place.x_dev,
            device_id_type=MESH,
        ).wait_recv()

    def local(self, src, dst):
        made = pltpu.make_async_copy(src, dst, self.local_sems.at[self.locals])
        self.locals += 1
        made.start()
        return made

    def finish(self):
        for made in self.open:
            made.wait_send()
        self.open = []


class SpreadPlane:
    def __init__(self, links, place, chunks):
        self.links, self.place, self.chunks = links, place, chunks
        self.z_slot, self.x_slot = links.slots(4 * len(chunks)), links.slots(4 * len(chunks))

    def begin_z(self):
        place = self.place
        for k, (src, dst) in enumerate(self.chunks):
            slot = self.z_slot + 4 * k + place.z
            for other in place.others:
                self.links.send(src, dst(place.f), slot, place.z_dev(other))

    def begin_x(self, k):
        src, dst = self.chunks[k]
        slot = self.x_slot + 4 * k + self.place.z
        self.links.send(src, dst(self.place.f), slot, self.place.x_dev)

    def forward(self, k):
        place, dst = self.place, self.chunks[k][1]
        for other in place.others:
            block = dst(other * 2 + place.x)
            self.links.arrive(block, self.z_slot + 4 * k + other)
            self.links.send(block, block, self.x_slot + 4 * k + other, place.x_dev)

    def end(self):
        for k in range(len(self.chunks)):
            for z in range(4):
                block = self.chunks[k][1](z * 2 + self.place.xo)
                self.links.arrive(block, self.x_slot + 4 * k + z)


class SpreadTree(SpreadPlane):
    def __init__(self, links, place, chunks, crossed):
        super().__init__(links, place, chunks)
        self.plain = len(chunks) - crossed
        self.passed = []

    def begin_z(self, ahead=4):
        place = self.place
        self.near = {}
        for k, (src, dst) in enumerate(self.chunks):
            slot = self.z_slot + 4 * k + place.z
            near = self.links.copy(src, dst(place.f), slot, place.z_dev(place.others[0]))
            self.links.open.append(near)
            if k < ahead:
                near.start()
            else:
                pl.when(jnp.logical_not(place.inner))(near.start)
                self.near[k - ahead] = near
            self.links.send(src, dst(place.f), slot, place.z_dev(place.others[1]))

    def cross_z(self, k):
        place = self.place
        block = self.chunks[k][1](place.z * 2 + place.xo)
        slot = self.x_slot + 4 * k + place.z
        self.links.arrive(block, slot)
        for other in place.others[:2]:
            self.links.send(block, block, slot, place.z_dev(other))

    def blocks(self, k, other):
        place, dst = self.place, self.chunks[k][1]
        found = [(dst(other * 2 + place.x), self.z_slot + 4 * k + other)]
        if k >= self.plain:
            found.append((dst(other * 2 + place.xo), self.x_slot + 4 * k + other))
        return found

    def onward(self, k):
        place = self.place
        blocks = [pair for other in place.others[1:] for pair in self.blocks(k, other)]
        made = [
            self.links.copy(block, block, slot, place.z_dev(place.others[0]))
            for block, slot in blocks
        ]
        self.passed += made

        @pl.when(place.inner)
        def _():
            for (block, slot), one in zip(blocks, made):
                self.links.arrive(block, slot)
                one.start()
            if k in self.near:
                self.near[k].start()

    def forward(self, k):
        place = self.place
        near, *far = [self.blocks(k, other) for other in place.others]
        far = far[0] + far[1]
        for pair in near:
            self.links.arrive(*pair)
        if k < self.plain:
            slot = self.x_slot + 4 * k + place.others[0]
            self.links.send(near[0][0], near[0][0], slot, place.x_dev)

        @pl.when(jnp.logical_not(place.inner))
        def _():
            for pair in far:
                self.links.arrive(*pair)

        if k < self.plain:
            for other, (block, _) in zip(place.others[1:], far):
                self.links.send(block, block, self.x_slot + 4 * k + other, place.x_dev)

    def end(self):
        for k in range(self.plain):
            for z in range(4):
                block = self.chunks[k][1](z * 2 + self.place.xo)
                self.links.arrive(block, self.x_slot + 4 * k + z)

    def finish(self):
        @pl.when(self.place.inner)
        def _():
            for made in self.passed:
                made.wait_send()


class ReducePlane:
    def __init__(self, links, place, chunks, from_x, from_z, own=None):
        self.links, self.place, self.chunks = links, place, chunks
        self.from_x, self.from_z, self.own = from_x, from_z, own
        self.summed = 0
        self.x_slot, self.z_slot = links.slots(len(chunks)), links.slots(3 * len(chunks))
        self.loads, self.z_sends = {}, {}

    def send_x(self, k):
        place = self.place
        from_x = self.from_x.at[k - self.summed]
        self.links.send(self.chunks[k](place.xo), from_x, self.x_slot + k, place.x_dev)

    def load(self, k):
        slots = self.own.shape[0]
        for made in self.z_sends.pop(k - slots, []):
            made.wait_send()
        self.loads[k] = self.links.local(self.chunks[k](self.place.x), self.own.at[k % slots])

    def mine(self, k):
        if self.own is None:
            return self.chunks[k](self.place.x)
        return self.own.at[k % self.own.shape[0]]

    def middle(self, k):
        place = self.place
        self.links.arrive(self.from_x.at[k], self.x_slot + k)
        if k in self.loads:
            self.loads[k].wait()
        mine = self.mine(k)
        self.z_sends[k] = []
        for other in place.others:
            mine[other] = (mine[other].astype(F32) + self.from_x[k, other].astype(F32)).astype(BF16)
            rank = place.rank(place.z, other)
            made = self.links.copy(
                mine.at[other],
                self.from_z.at[k, rank],
                self.z_slot + 3 * k + rank,
                place.z_dev(other),
            )
            made.start()
            self.z_sends[k].append(made)

    def end(self, k):
        place = self.place
        mine = self.mine(k)
        sums = mine[place.z].astype(F32) + self.from_x[k, place.z].astype(F32)
        for rank in range(3):
            self.links.arrive(self.from_z.at[k, rank], self.z_slot + 3 * k + rank)
            sums += self.from_z[k, rank].astype(F32)
        total = self.from_x.at[k, place.z]
        total[...] = sums.astype(BF16)
        return total

    def finish(self):
        for sends in self.z_sends.values():
            for made in sends:
                made.wait_send()


class ReduceTree(ReducePlane):
    def __init__(self, links, place, chunks, from_x, from_z, via, own, summed):
        super().__init__(links, place, chunks, from_x, from_z, own)
        self.summed = summed
        self.via, self.via_slot = via, links.slots(len(chunks))
        self.outer = jnp.logical_not(place.inner)

    def load(self, k):
        slots = self.own.shape[0]
        self.settle(self.z_sends.pop(k - slots, []))
        self.loads[k] = self.links.local(self.chunks[k](self.place.x), self.own.at[k % slots])

    def settle(self, sends):
        for made, when in sends:
            if when is None:
                made.wait_send()
            else:
                pl.when(when)(made.wait_send)

    def middle(self, k):
        place = self.place
        self.loads[k].wait()
        mine = self.mine(k)
        if k >= self.summed:
            from_x = self.from_x.at[k - self.summed]
            self.links.arrive(from_x, self.x_slot + k)
            for other in place.others:
                pair = mine[other].astype(F32) + from_x[other].astype(F32)
                mine[other] = pair.astype(BF16)
        near = place.others[0]
        device = place.z_dev(near)
        direct = self.links.copy(mine.at[near], self.from_z.at[k, 0], self.z_slot + 3 * k, device)
        direct.start()
        far = self.links.copy(
            mine.at[pl.ds(place.far, 2)], self.via.at[k], self.via_slot + k, device
        )
        pl.when(self.outer)(far.start)
        self.z_sends[k] = [(direct, None), (far, self.outer)]

    def combine(self, k):
        place = self.place
        mine = self.mine(k)

        sent = [
            self.links.copy(
                mine.at[place.far + j],
                self.from_z.at[k, 1],
                self.z_slot + 3 * k + 1,
                place.z_dev(place.far + j),
            )
            for j in range(2)
        ]

        @pl.when(place.inner)
        def _():
            self.links.arrive(self.via.at[k], self.via_slot + k)
            for j in range(2):
                here = mine[place.far + j].astype(F32) + self.via[k, j].astype(F32)
                mine[place.far + j] = here.astype(BF16)
                sent[j].start()

        self.z_sends[k] += [(made, place.inner) for made in sent]

    def end(self, k):
        place = self.place
        sums = self.mine(k)[place.z].astype(F32)
        if k >= self.summed:
            sums += self.from_x[k - self.summed, place.z].astype(F32)
        for side in range(2):
            self.links.arrive(self.from_z.at[k, side], self.z_slot + 3 * k + side)
            sums += self.from_z[k, side].astype(F32)
        total = self.from_z.at[k, 0]
        total[...] = sums.astype(BF16)
        return total

    def finish(self):
        for sends in self.z_sends.values():
            self.settle(sends)


class SpreadCtx:
    def __init__(self, links, place, out, parts):
        self.links, self.place, self.out, self.parts = links, place, out, parts
        self.slot = links.slots(3 * len(parts))
        self.sends = []

    def begin(self, k, src):
        place, rows = self.place, self.parts[k]
        out = self.out.at[place.c, rows]
        self.sends.append(self.links.send(src, out, self.slot + 3 * k + 1, place.y_dev))
        self.sends.append(self.links.send(src, out, self.slot + 3 * k, place.core_dev))

    def forward(self, k):
        place = self.place
        block = self.out.at[place.c_y, self.parts[k]]
        self.links.arrive(block, self.slot + 3 * k + 1)
        self.sends.append(self.links.send(block, block, self.slot + 3 * k + 2, place.core_dev))

    def end(self):
        place = self.place
        for k, rows in enumerate(self.parts):
            self.links.arrive(self.out.at[place.c_core, rows], self.slot + 3 * k)
            self.links.arrive(self.out.at[place.c_diag, rows], self.slot + 3 * k + 2)


class ReduceCtx:
    def __init__(self, links, place, part, parts, own, from_core, to_y, from_y):
        self.links, self.place, self.part = links, place, part
        self.parts = [rows if isinstance(rows, tuple) else (rows,) for rows in parts]
        self.own, self.from_core, self.to_y, self.from_y = own, from_core, to_y, from_y
        self.slot = links.slots(3 * len(parts))
        self.loads, self.sends = {}, []

    def begin(self, only=None):
        place = self.place
        for side, y in ((0, place.yo), (1, place.y)):
            for k, rows in enumerate(self.parts):
                if only not in (None, k):
                    continue
                self.links.send(
                    self.part.at[y * 2 + place.co, *rows],
                    self.from_core.at[side, *rows],
                    self.slot + 3 * k + side,
                    place.core_dev,
                )
                if self.own is not None and side == 0:
                    self.load(0, k)

    def load(self, side, k):
        rows = self.parts[k]
        y = self.place.y if side else self.place.yo
        self.loads[side, k] = self.links.local(
            self.part.at[y * 2 + self.place.core, *rows], self.own.at[rows]
        )

    def pair(self, side, k):
        rows = self.parts[k]
        self.links.arrive(self.from_core.at[side, *rows], self.slot + 3 * k + side)
        if self.own is None:
            y = self.place.y if side else self.place.yo
            own = self.part[y * 2 + self.place.core, *rows]
        else:
            self.loads[side, k].wait()
            own = self.own[rows]
        return own.astype(F32) + self.from_core[side, *rows].astype(F32)

    def cross(self, k):
        rows = self.parts[k]
        self.to_y[rows] = self.pair(0, k).astype(BF16)
        if self.own is not None:
            self.load(1, k)
        made = self.links.send(
            self.to_y.at[rows], self.from_y.at[rows], self.slot + 3 * k + 2, self.place.y_dev
        )
        self.sends.append(made)

    def total(self, k):
        rows = self.parts[k]
        sums = self.pair(1, k)
        self.links.arrive(self.from_y.at[rows], self.slot + 3 * k + 2)
        return sums + self.from_y[rows].astype(F32)


def halves(rows):
    return [pl.ds(0, rows // 2), pl.ds(rows // 2, rows // 2)]


def row_factor(values):
    return lax.rsqrt(jnp.mean(values * values, axis=-1, keepdims=True) + EPSILON)


def low_half(shape):
    return lax.rem(lax.broadcasted_iota(jnp.int32, shape, len(shape) - 1), 128) < 64


def partner(values):
    lane = lax.broadcasted_iota(jnp.int32, values.shape, len(values.shape) - 1)
    first = lax.rem(lane, 64) < 32
    return jnp.where(first, pltpu.roll(values, 96, 1), pltpu.roll(values, 32, 1))


def half_sums(values):
    low = low_half(values.shape)
    first = jnp.sum(jnp.where(low, values, 0.0), axis=-1, keepdims=True)
    second = jnp.sum(jnp.where(low, 0.0, values), axis=-1, keepdims=True)
    return jnp.where(low, first, second)


def row_loop(count, body, first=0):
    def step(index, carry):
        body(index)
        return carry

    lax.fori_loop(first, first + count, step, 0)


BLOCK = 256
SHORT = 128


def attention_scores(query, keys, key_bias, first, span):
    scores = lax.dot_general(
        query, keys, (((1,), (1,)), ((), ())), preferred_element_type=F32
    ) * (1.0 / math.sqrt(HEAD_DIM))
    rows = first + lax.broadcasted_iota(jnp.int32, scores.shape, 0)
    columns = lax.broadcasted_iota(jnp.int32, scores.shape, 1)
    return jnp.where(columns <= rows, scores, -1e30) + key_bias[:, :span]


def turn_tables(angles, cos, sin):
    for i in range(16):
        rows = slice(64 * i, 64 * (i + 1))
        cos_high, sin_high = angles[i : i + 1], angles[16 + i : 17 + i]
        cos_low, sin_low = angles[32:96], angles[96:160]
        cos[rows] = cos_high * cos_low - sin_high * sin_low
        sin[rows] = sin_high * cos_low + cos_high * sin_low


def forward_kernel(
    lengths, qkv_weight, out_s, gain_s, x_s, gate_up, down_weight, cotangent, angles, qk_gain,
    qkv_wh, out_wh, gains, normed_h, qkv_raw_h, qkv_low_h, att_low_h, log_sums_h,
    gu_w, dn_w, dout_all, middle, mid_all, head_gain, key_bias,
    kv_pairs, kv_s, dout_s, cos, sin, gain_blocks, qkv_w, out_w, x_all, normed, qkv_raw, qkv_low, att_low, log_sums,
    part, keys, values, from_core, to_y, from_y, mid_low, gu_pairs, gu_rows, gu_s, send_sems, recv_sems, local_sems,
):
    place = Place()
    links = Links(place, send_sems, recv_sems, local_sems)
    fellows = [lax.rem(place.f + d, 8) for d in range(1, 8)]
    place.meet([(f, place.c) for f in fellows] + [place.core_dev, place.y_dev])

    q_columns = pl.ds(pl.multiple_of(256 * place.c, 256), 256)
    for j in range(2):
        pair = pl.ds(pl.multiple_of(1024 + 256 * j + 128 * place.y, 128), 128)
        links.local(qkv_weight.at[:, pair], kv_pairs.at[j]).wait()
    cot_load = links.local(cotangent, dout_s)
    low = low_half(kv_pairs.shape[1:])
    first, second = [], []
    for j in range(2):
        value = kv_pairs[j].astype(F32)
        swapped = pltpu.roll(value, 64, 1)
        first.append(jnp.where(place.core == 0, value, swapped))
        second.append(jnp.where(place.core == 0, swapped, value))
    kv_s[...] = jnp.where(low, first[0], second[1]).astype(BF16)
    qkv_plane = SpreadPlane(
        links,
        place,
        [
            (qkv_weight.at[:, q_columns], lambda f: qkv_w.at[f, :, 0:256]),
            (kv_s, lambda f: qkv_w.at[f, :, 256:384]),
        ],
    )
    qkv_plane.begin_z()
    qkv_plane.begin_x(0)
    qkv_plane.begin_x(1)
    picks = []
    for f in range(8):
        start = pl.multiple_of(512 * f + 128 * place.c, 128)
        picks.append(links.local(gate_up.at[:, :, pl.ds(start, 128)], gu_pairs.at[f]))
    tokens = x_s.shape[0]
    parts = halves(tokens)
    x_spread = SpreadCtx(links, place, x_all, parts)
    for k, rows in enumerate(parts):
        x_spread.begin(k, x_s.at[rows])
    gain_slot = links.slots(8)
    for f in fellows:
        links.send(gain_s, gain_blocks.at[place.f], gain_slot + place.f, (f, place.c))
    kept = [
        links.local(qkv_weight.at[:, q_columns], qkv_w.at[place.f, :, 0:256]),
        links.local(kv_s, qkv_w.at[place.f, :, 256:384]),
        links.local(gain_s, gain_blocks.at[place.f]),
        links.local(x_s, x_all.at[place.c]),
    ]

    root_slot, side_slot = links.slots(1), links.slots(1)
    holds = place.z == place.c
    down = [
        links.copy(out_s, out_w.at[place.x], root_slot, place.z_dev(other))
        for other in place.others[:2]
    ]
    relay = links.copy(out_w.at[place.x], out_w.at[place.x], root_slot, place.z_dev(place.others[0]))
    across = lax.div(place.c, 2) != lax.div(place.z, 2)
    relays = jnp.logical_and(place.inner, across)
    sideways = links.copy(out_s, out_w.at[place.x], side_slot, place.x_dev)
    onward = links.copy(out_w.at[place.x], out_w.at[place.x], side_slot, place.x_dev)
    own = pltpu.make_async_copy(out_s, out_w.at[place.x], local_sems.at[links.locals])
    links.locals += 1

    @pl.when(holds)
    def _():
        for made in down:
            made.start()
        sideways.start()
        own.start()

    rows = gu_s.shape[0]
    for f in range(8):
        picks[f].wait()
        gu_rows[...] = gu_pairs.at[f].reshape(2 * rows, 128)[...].astype(F32)
        for side in range(2):
            first = 1024 * side + 128 * f
            picked = gu_rows[pl.ds(side, rows, stride=2), :]
            gu_s[:, first : first + 128] = picked.astype(BF16)
    step = 32
    chunks = []
    dn_s = down_weight.at[pl.ds(pl.multiple_of(128 * place.c, 128), dn_w.shape[1])]
    for src, dst in ((dn_s, dn_w), (gu_s, gu_w)):
        for first in range(0, src.shape[0], step):
            rows = pl.ds(first, step)
            chunks.append((src.at[rows], lambda f, dst=dst, rows=rows: dst.at[f, rows]))
    plane = SpreadTree(links, place, chunks, 2)
    plane.begin_z()
    cot_load.wait()
    length = lengths[0]
    positions = tokens * place.c + lax.broadcasted_iota(jnp.int32, (tokens, 1), 0)
    dout_s[...] = jnp.where(positions < length, dout_s[...].astype(F32), 0.0).astype(BF16)
    for k in range(plane.plain, len(chunks)):
        plane.begin_x(k)
    for k in range(3):
        plane.begin_x(k)
    qkv_plane.forward(0)
    qkv_plane.forward(1)
    for k in range(3, plane.plain):
        plane.begin_x(k)
    for k in range(plane.plain, len(chunks)):
        plane.cross_z(k)
    last = [
        links.local(gu_s, gu_w.at[place.f]),
        links.local(dn_s, dn_w.at[place.f]),
        links.local(dout_s, dout_all.at[place.c]),
    ]
    turn_tables(angles, cos, sin)
    columns = lax.broadcasted_iota(jnp.int32, key_bias.shape, 1)
    key_bias[...] = jnp.where(columns < length, 0.0, -1e30)
    ones = jnp.ones((1, HEAD_DIM), F32)
    q_gain, k_gain = qk_gain[0:1].astype(F32), qk_gain[1:2].astype(F32)
    head_gain[...] = jnp.zeros_like(head_gain)
    for b in range(2):
        head_gain[b : b + 1] = jnp.concatenate([q_gain, q_gain], axis=1)
    head_gain[2:3] = jnp.concatenate([k_gain, ones], axis=1)
    for f in fellows:
        links.arrive(gain_blocks.at[f], gain_slot + f)
    for made in kept:
        made.wait()
    gains[...] = jnp.zeros_like(gains)
    for f in range(8):
        gains[0:2, 256 * f : 256 * (f + 1)] = gain_blocks[f, 0:2]
    dout = SpreadCtx(links, place, dout_all, parts)
    for k, rows in enumerate(parts):
        x_spread.forward(k)
        dout.begin(k, dout_s.at[rows])
    x_spread.end()
    qkv_plane.end()

    def project(index):
        rows = pl.ds(pl.multiple_of(index * BLOCK, BLOCK), BLOCK)
        source = x_all[index].astype(F32)
        normed[rows] = (source * row_factor(source) * gains[0:1]).astype(BF16)
        weight = qkv_w[...].reshape(normed.shape[1], qkv_w.shape[2])
        raw = jnp.dot(normed[rows], weight, preferred_element_type=F32)
        for b in range(3):
            block = raw[:, 128 * b : 128 * (b + 1)]
            qkv_raw[b, rows] = block
            factor = lax.rsqrt(half_sums(block * block) * (1.0 / HEAD_DIM) + EPSILON)
            scaled = block * factor * head_gain[b : b + 1]
            turned = scaled * cos[rows] + partner(scaled) * sin[rows]
            if b == 2:
                turned = jnp.where(low_half(turned.shape), turned, block)
            qkv_low[b, rows] = turned.astype(BF16)
            if b == 2:
                low = low_half(turned.shape)
                swapped = pltpu.roll(turned, 64, 1)
                keys[rows] = jnp.where(low, turned, swapped).astype(BF16)
                values[rows] = jnp.where(low, swapped, turned).astype(BF16)

    seq = normed.shape[0]
    att_low[...] = jnp.zeros_like(att_low)
    log_sums[...] = jnp.zeros_like(log_sums)
    row_loop(seq // BLOCK, project)
    last += [
        links.local(normed, normed_h),
        links.local(qkv_raw, qkv_raw_h),
        links.local(qkv_low, qkv_low_h),
        links.local(qkv_w, qkv_wh),
    ]

    def heads(index):
        b, half = lax.div(index, 2), lax.rem(index, 2)
        for i in range(seq // BLOCK):
            rows, span = pl.ds(i * BLOCK, BLOCK), (i + 1) * BLOCK
            query = qkv_low[b, rows]
            side = lax.div(lax.broadcasted_iota(jnp.int32, query.shape, 1), 64) == half
            chosen = jnp.where(side, query, 0)
            scores = attention_scores(chosen, keys[:span], key_bias[0:1], i * BLOCK, span)
            top = jnp.max(scores, axis=-1, keepdims=True)
            expanded = jnp.exp(scores - top)
            sums = jnp.sum(expanded, axis=-1, keepdims=True)
            probs = (expanded * (1.0 / sums)).astype(BF16)
            out = jnp.dot(probs, values[:span], preferred_element_type=F32)
            att_low[b, rows] = jnp.where(side, out.astype(BF16), att_low[b, rows])
            log_sums[b, rows] = jnp.where(side, top + jnp.log(sums), log_sums[b, rows])

    @pl.when(relays)
    def _():
        links.arrive(out_w.at[place.x], root_slot)
        relay.start()
        onward.start()

    plane.onward(0)
    row_loop(2, heads)
    plane.onward(1)
    plane.onward(2)
    plane.forward(0)
    row_loop(2, heads, 2)
    plane.onward(3)
    for k in range(1, 3):
        plane.forward(k)

    @pl.when(jnp.logical_not(jnp.logical_or(holds, relays)))
    def _():
        links.arrive(out_w.at[place.x], root_slot)
        onward.start()

    @pl.when(holds)
    def _():
        own.wait()

    for k in range(len(parts)):
        dout.forward(k)
    links.arrive(out_w.at[place.xo], side_slot)

    def project_out(index):
        rows = pl.ds(pl.multiple_of(index * BLOCK, BLOCK), BLOCK)
        sums = jnp.dot(att_low[0, rows], out_w[0], preferred_element_type=F32)
        sums += jnp.dot(att_low[1, rows], out_w[1], preferred_element_type=F32)
        part[index] = sums.astype(BF16)

    row_loop(seq // BLOCK, project_out)
    reduce = ReduceCtx(links, place, part, parts, None, from_core, to_y, from_y)
    reduce.begin()
    last += [
        links.local(att_low, att_low_h),
        links.local(log_sums, log_sums_h),
        links.local(out_w, out_wh),
    ]
    plane.onward(4)
    for k in range(2):
        reduce.cross(k)
    plane.forward(3)
    plane.onward(5)
    plane.onward(6)
    plane.forward(4)
    plane.onward(7)
    plane.forward(5)
    plane.onward(8)
    plane.forward(6)
    mid = SpreadCtx(links, place, mid_all, parts)
    for k, rows in enumerate(parts):
        value = x_all[place.c, rows].astype(F32) + reduce.total(k)
        middle[rows] = value
        mid_low[rows] = (value * row_factor(value) * gains[1:2]).astype(BF16)
        mid.begin(k, mid_low.at[rows])
        last.append(links.local(mid_low.at[rows], mid_all.at[place.c, rows]))
    plane.onward(9)
    plane.forward(7)
    plane.forward(8)
    for k in range(2):
        mid.forward(k)
    plane.forward(9)
    for k in range(plane.plain, len(chunks)):
        plane.onward(k)
    for k in range(plane.plain, len(chunks)):
        plane.forward(k)
    plane.end()
    mid.end()
    dout.end()
    for made in last:
        made.wait()
    links.finish()
    plane.finish()

    @pl.when(holds)
    def _():
        for made in down:
            made.wait_send()
        sideways.wait_send()

    @pl.when(relays)
    def _():
        relay.wait_send()

    @pl.when(jnp.logical_not(holds))
    def _():
        onward.wait_send()


NT = (((1,), (1,)), ((), ()))
TN = (((0,), (0,)), ((), ()))


def norm_back(d_norm, value, gain):
    factor = row_factor(value)
    gain_sum = jnp.sum(d_norm * value * factor, axis=0, keepdims=True)
    scaled = d_norm * gain
    inner = jnp.mean(scaled * value, axis=-1, keepdims=True)
    return factor * scaled - value * (factor * factor * factor * inner), gain_sum


def feed_kernel(
    gu_h, dn_h, dout_h, mid_h, middle_h, gains,
    gu_g, dn_pair, ffn_h, d_middle_h, branch_s, ffn_gain,
    gu_w, dn_w, dout, mid, hidden, d_proj, dn_g, from_x, stage,
    part, from_core, to_y, from_y, middle, d_norm, branch, send_sems, recv_sems, local_sems,
):
    place = Place()
    links = Links(place, send_sems, recv_sems, local_sems)
    shards, rows, width = gu_w.shape
    units, seq = hidden.shape[1], hidden.shape[0]
    tokens = mid.shape[1]
    first = [links.local(mid_h, mid)]
    later, loads = [], []
    for n in range(units // 256):
        gate, up = pl.ds(256 * n, 256), pl.ds(units + 256 * n, 256)
        loads.append([
            links.local(gu_h.at[:, :, gate], gu_w.at[:, :, gate]),
            links.local(gu_h.at[:, :, up], gu_w.at[:, :, up]),
        ])
        if n == 0:
            first += [links.local(dout_h, dout), links.local(dn_h, dn_w)]
    later.append(links.local(middle_h, middle))
    place.meet([place.x_dev, place.core_dev, place.y_dev])
    for made in first:
        made.wait()

    x_slot = links.slots(4)
    for n in range(units // 256):
        for made in loads[n]:
            made.wait()
        gate_columns, up_columns = slice(256 * n, 256 * (n + 1)), slice(units + 256 * n, units + 256 * (n + 1))

        def activation(index, gate_columns=gate_columns, up_columns=up_columns, n=n):
            two = pl.ds(2 * index, 2)
            low = mid[two].reshape(2 * tokens, width)
            gate = jnp.dot(
                low, gu_w[:, :, gate_columns].reshape(width, 256), preferred_element_type=F32
            )
            up = jnp.dot(
                low, gu_w[:, :, up_columns].reshape(width, 256), preferred_element_type=F32
            )
            d_hidden = lax.dot_general(
                dout[two].reshape(2 * tokens, width), dn_w[2 * n : 2 * n + 2].reshape(256, width), NT,
                preferred_element_type=F32,
            )
            at = pl.ds(pl.multiple_of(index * 2 * tokens, 2 * tokens), 2 * tokens)
            sigmoid = 1.0 / (1.0 + jnp.exp(-gate))
            silu = gate * sigmoid
            hidden[at, gate_columns] = (silu * up).astype(BF16)
            d_gate = d_hidden * up * (sigmoid * (1.0 + gate * (1.0 - sigmoid)))
            d_proj[at, gate_columns] = d_gate.astype(BF16)
            d_proj[at, up_columns] = (d_hidden * silu).astype(BF16)

        row_loop(2, activation)
        left = hidden[:, gate_columns].T

        def down_grad(j, left=left, n=n):
            wide = pl.ds(pl.multiple_of(512 * j, 512), 512)
            right = dout[:, :, wide].reshape(seq, 512)
            grad = jnp.dot(left, right, preferred_element_type=F32).astype(BF16)
            dn_g[n, 0, :, wide] = grad[:128]
            dn_g[n, 1, :, wide] = grad[128:]

        row_loop(4, down_grad)
        links.send(dn_g.at[n, place.xo], from_x.at[n], x_slot + n, place.x_dev)

    def mid_grad(f):
        grad = lax.dot_general(d_proj[...], gu_w[f], NT, preferred_element_type=F32)
        columns = pl.ds(pl.multiple_of(rows * f, rows), rows)
        part[:, :, columns] = grad.astype(BF16).reshape(4, tokens, rows)

    parts = halves(tokens)
    sides = [(slice(None), side) for side in halves(width)]
    dmid = ReduceCtx(links, place, part, sides, None, from_core, to_y, from_y)
    quarter = shards // 4
    row_loop(2 * quarter, mid_grad)
    dmid.begin(0)
    row_loop(quarter, mid_grad, 2 * quarter)
    dmid.cross(0)
    row_loop(quarter, mid_grad, 3 * quarter)
    dmid.begin(1)

    def gate_up_grad(z):
        columns = pl.ds(pl.multiple_of(2 * rows * z, 2 * rows), 2 * rows)
        left = mid[:, :, columns].reshape(seq, 2 * rows).T
        for j in range(4):
            wide = slice(512 * j, 512 * (j + 1))
            grad = jnp.dot(left, d_proj[:, wide], preferred_element_type=F32)
            stage[:, :, wide] = grad.astype(BF16).reshape(2, rows, 512)
        made = pltpu.make_async_copy(stage, gu_g.at[z], local_sems.at[links.locals])
        made.start()
        made.wait()

    row_loop(1, gate_up_grad)
    dmid.cross(1)
    row_loop(3, gate_up_grad, 1)
    links.locals += 1

    def feed_out(index):
        at = pl.ds(pl.multiple_of(index * 2 * tokens, 2 * tokens), 2 * tokens)
        for j in range(4):
            wide = slice(512 * j, 512 * (j + 1))
            right = dn_w[:, :, wide].reshape(units, 512)
            sums = jnp.dot(hidden[at], right, preferred_element_type=F32)
            mid[pl.ds(2 * index, 2), :, wide] = sums.astype(BF16).reshape(2, tokens, 512)

    row_loop(2, feed_out)
    later.append(links.local(mid, ffn_h))
    later[0].wait()
    for k in range(2):
        d_norm[sides[k]] = dmid.total(k)
    gain_sum = None
    for k, at in enumerate(parts):
        grad, term = norm_back(d_norm[at], middle[at], gains[1:2])
        gain_sum = term if gain_sum is None else gain_sum + term
        middle[at] = grad + dout[place.c, at].astype(F32)
        branch[at] = middle[at].astype(BF16)
        later.append(links.local(middle.at[at], d_middle_h.at[at]))
        later.append(links.local(branch.at[at], branch_s.at[at]))
    ffn_gain[...] = gain_sum
    for n in range(4):
        links.arrive(from_x.at[n], x_slot + n)
        pair = dn_g[n, place.x].astype(F32) + from_x[n].astype(F32)
        from_x[n] = pair.astype(BF16)
        later.append(links.local(from_x.at[n], dn_pair.at[n]))
    for made in later[1:]:
        made.wait()
    links.finish()


def backward_kernel(
    gu_g, dn_pair, ffn_part, middle_h, d_middle_h, branch_s, x_h, lengths, gains, ffn_gain,
    angles, head_gain, key_bias,
    normed_h, qkv_raw_h, qkv_low_h, att_low_h, log_sums_h, qkv_wh, out_wh,
    gu_all, dn_all, layer_out, qkv_all, out_all, input_grad, stats,
    own, from_x, from_z, via,
    ctx_own, from_core1, to_y1, from_y1, from_core2, to_y2, from_y2,
    middle, x_s, d_middle, branch_all, part,
    cos, sin, qkv_raw, qkv_low, att_low, log_sums, qkv_w, out_w,
    keys, values, d_att, d_low, d_keys, d_values, gain_g,
    qkv_g, qkv_x, qkv_z, out_g, out_x, out_z,
    mine, plane_stats, ctx_stats, send_sems, recv_sems, local_sems,
):
    place = Place()
    links = Links(place, send_sems, recv_sems, local_sems)
    fellows = [lax.rem(place.f + d, 8) for d in range(1, 8)]
    place.meet(
        [(f, place.c) for f in fellows] + [place.core_dev, place.y_dev, place.diag_dev]
    )
    step = from_x.shape[2]
    chunks, where = [], []
    for first in range(0, dn_pair.shape[1], step):
        rows = pl.ds(first, step)
        chunks.append(lambda x, rows=rows: dn_pair.at[:, rows])
        where.append((dn_all, rows))
    summed = len(chunks)
    for first in range(0, gu_g.shape[2], step):
        rows = pl.ds(first, step)
        chunks.append(lambda x, rows=rows: gu_g.at[:, x, rows])
        where.append((gu_all, rows))
    count = len(chunks)
    plane = ReduceTree(links, place, chunks, from_x, from_z, via, own, summed)
    outs = [SpreadCtx(links, place, out, [rows]) for out, rows in where]
    kept = []

    def end(k):
        total = plane.end(k)
        if k + own.shape[0] < count:
            plane.load(k + own.shape[0])
        out, rows = where[k]
        outs[k].begin(0, total)
        kept.append(links.local(total, out.at[place.c, rows]))

    tokens, width = middle.shape
    parts = halves(tokens)
    branch = SpreadCtx(links, place, branch_all, parts)
    for k, rows in enumerate(parts):
        branch.begin(k, branch_s.at[rows])
    for k in range(summed, count - 2):
        plane.send_x(k)
    ffn = ReduceCtx(links, place, ffn_part, parts, ctx_own, from_core1, to_y1, from_y1)
    ffn.begin()
    for k in range(own.shape[0]):
        plane.load(k)
    late = [
        links.local(a, b)
        for a, b in (
            (branch_s, branch_all.at[place.c]),
            (out_wh, out_w), (qkv_low_h, qkv_low), (att_low_h, att_low), (log_sums_h, log_sums),
            (qkv_raw_h, qkv_raw), (qkv_wh, qkv_w),
            (middle_h, middle), (d_middle_h, d_middle), (x_h, x_s),
        )
    ]
    turn_tables(angles, cos, sin)
    gain_g[...] = jnp.zeros_like(gain_g)
    d_keys[...] = jnp.zeros_like(d_keys)
    d_low[...] = jnp.zeros_like(d_low)
    d_values[...] = jnp.zeros_like(d_values)
    for k in (0, 1):
        plane.middle(k)
    for k in (2, 3):
        plane.middle(k)
    for k in range(2):
        ffn.cross(k)
    branch.forward(0)
    for k in (0, 1):
        plane.combine(k)
    branch.forward(1)
    for k in (4, 5):
        plane.middle(k)
    for k in (2, 3):
        plane.combine(k)
    branch.end()
    for made in late:
        made.wait()

    root = 1.0 / math.sqrt(HEAD_DIM)
    seq = 4 * tokens

    def prepare(index):
        rows = pl.ds(pl.multiple_of(index * BLOCK, BLOCK), BLOCK)
        block = qkv_low[2, rows].astype(F32)
        low = low_half(block.shape)
        swapped = pltpu.roll(block, 64, 1)
        keys[rows] = jnp.where(low, block, swapped).astype(BF16)
        values[rows] = jnp.where(low, swapped, block).astype(BF16)
        for b in range(2):
            d_att[b, rows] = lax.dot_general(
                branch_all[index], out_w[b], NT, preferred_element_type=F32
            ).astype(BF16)

    row_loop(seq // BLOCK, prepare)
    for b in range(2):
        left = att_low[b].T
        for j in range(8):
            columns = slice(256 * j, 256 * (j + 1))
            right = branch_all[:, :, columns].reshape(seq, 256)
            out_g[b, :, columns] = jnp.dot(left, right, preferred_element_type=F32).astype(BF16)
    out_slot = links.slots(1)
    links.send(out_g.at[place.xo], out_x, out_slot, place.x_dev)
    for k in range(count - 2, count):
        plane.send_x(k)
    links.settle(branch.sends)
    normed_load = links.local(normed_h, branch_all)
    for k in (6, 7):
        plane.middle(k)

    def unturn(row, rows, grads, block):
        back = grads * cos[rows] + partner(grads * sin[rows])
        factor = lax.rsqrt(half_sums(block * block) * (1.0 / HEAD_DIM) + EPSILON)
        gain_term = jnp.sum(back * block * factor, axis=0, keepdims=True)
        scaled = back * head_gain[row : row + 1]
        inner = half_sums(scaled * block) * (1.0 / HEAD_DIM)
        return factor * scaled - block * (factor * factor * factor * inner), gain_term

    def heads(index):
        b, half = lax.div(index, 2), lax.rem(index, 2)
        for i in range(seq // SHORT):
            rows, span = pl.ds(i * SHORT, SHORT), (i + 1) * SHORT
            query = qkv_low[b, rows]
            lane = lax.broadcasted_iota(jnp.int32, query.shape, 1)
            side = lax.div(lane, 64) == half
            chosen = jnp.where(side, query, 0)
            d_chosen = jnp.where(side, d_att[b, rows], 0)
            logs = jnp.max(jnp.where(side, log_sums[b, rows], -1e30), axis=-1, keepdims=True)
            scores = attention_scores(chosen, keys[:span], key_bias[0:1], i * SHORT, span)
            probs = jnp.exp(scores - logs)
            d_probs = lax.dot_general(d_chosen, values[:span], NT, preferred_element_type=F32)
            delta = jnp.sum(probs * d_probs, axis=-1, keepdims=True)
            d_scores = (probs * (d_probs - delta)).astype(BF16)
            d_query = jnp.dot(d_scores, keys[:span], preferred_element_type=F32) * root
            d_keys[:span] += lax.dot_general(d_scores, chosen, TN, preferred_element_type=F32)
            d_values[:span] += lax.dot_general(
                probs.astype(BF16), d_chosen, TN, preferred_element_type=F32
            )
            d_low[b, rows] = jnp.where(side, d_query.astype(BF16), d_low[b, rows])

    def unturn_queries(index):
        rows = pl.ds(pl.multiple_of(index * BLOCK, BLOCK), BLOCK)
        for b in range(2):
            grads = d_low[b, rows].astype(F32)
            d_block, gain_term = unturn(0, rows, grads, qkv_raw[b, rows])
            d_low[b, rows] = d_block.astype(BF16)
            gain_g[0:1] += gain_term

    row_loop(2, heads)
    for k in (4, 5):
        plane.combine(k)
    for k in (0, 1):
        end(k)
    row_loop(2, heads, 2)
    for k in (8, 9):
        plane.middle(k)
    for k in (6, 7):
        plane.combine(k)
    for k in (2, 3):
        end(k)
    row_loop(seq // BLOCK, unturn_queries)

    def finish(index):
        rows = pl.ds(pl.multiple_of(index * BLOCK, BLOCK), BLOCK)
        k_sum, v_sum = d_keys[rows], d_values[rows]
        low = low_half(k_sum.shape)
        k_sum = (k_sum + pltpu.roll(k_sum, 64, 1)) * root
        v_sum = v_sum + pltpu.roll(v_sum, 64, 1)
        grads = jnp.where(low, k_sum, v_sum).astype(BF16).astype(F32)
        d_block, gain_term = unturn(2, rows, grads, qkv_raw[2, rows])
        d_low[2, rows] = jnp.where(low, d_block, grads).astype(BF16)
        gain_g[1:2] += gain_term
        for j in range(4):
            columns = slice(512 * j, 512 * (j + 1))
            sums = jnp.zeros((BLOCK, 512), F32)
            for b in range(3):
                weight = qkv_w[columns, 128 * b : 128 * (b + 1)]
                sums += lax.dot_general(d_low[b, rows], weight, NT, preferred_element_type=F32)
            part[index, :, columns] = sums.astype(BF16)

    row_loop(seq // BLOCK, finish)

    dnorm = ReduceCtx(links, place, part, parts, None, from_core2, to_y2, from_y2)
    dnorm.begin()
    normed_load.wait()
    for b in range(3):
        left = d_low[b].T
        for f in range(8):
            right = branch_all[:, :, 256 * f : 256 * (f + 1)].reshape(seq, 256)
            qkv_g[f // 2, f % 2, 128 * b : 128 * (b + 1)] = jnp.dot(
                left, right, preferred_element_type=F32
            ).astype(BF16)
    qkv_step = qkv_x.shape[2]
    qkv_rows = [pl.ds(k * qkv_step, qkv_step) for k in range(qkv_x.shape[0])]
    qkv_chunks = [lambda x, rows=rows: qkv_g.at[:, x, rows] for rows in qkv_rows]
    qkv_plane = ReducePlane(links, place, qkv_chunks, qkv_x, qkv_z)
    qkv_outs = [SpreadCtx(links, place, qkv_all, [rows]) for rows in qkv_rows]
    for k in range(len(qkv_chunks)):
        qkv_plane.send_x(k)
    links.arrive(out_x, out_slot)
    root_slot, final_slot = links.slots(3), links.slots(1)
    holds = place.z == place.c
    out_mine = out_g.at[place.x]
    out_mine[...] = (out_mine[...].astype(F32) + out_x[...].astype(F32)).astype(BF16)
    rank = place.rank(place.z, place.c)
    to_root = links.copy(
        out_mine,
        out_z.at[lax.rem(rank, 3)],
        root_slot + lax.rem(rank, 3),
        (place.c * 2 + place.x, place.c),
    )

    @pl.when(jnp.logical_not(holds))
    def _():
        to_root.start()

    for k in range(2):
        dnorm.cross(k)
    for k in (8, 9):
        plane.combine(k)
    for k in (4, 5):
        end(k)
    for k in (0, 1):
        outs[k].forward(0)
    for k in (2, 3):
        outs[k].forward(0)
    for k in (6, 7):
        end(k)
    for k, rows in enumerate(parts):
        value = middle[rows] + ffn.total(k)
        positions = lax.broadcasted_iota(jnp.int32, (value.shape[0], 1), 0)
        positions += tokens * place.c + k * value.shape[0]
        layer_out[rows] = jnp.where(positions < lengths[0], value, 0.0).astype(BF16)
    for k in (10, 11):
        plane.middle(k)
    for k in (4, 5):
        outs[k].forward(0)
    attn_gain = None
    for k, rows in enumerate(parts):
        grad, term = norm_back(dnorm.total(k), x_s[rows].astype(F32), gains[0:1])
        attn_gain = term if attn_gain is None else attn_gain + term
        input_grad[rows] = (d_middle[rows] + grad).astype(BF16)
    mine[...] = jnp.zeros_like(mine)
    for f in range(8):
        mine[f, 0:1] = attn_gain[:, 256 * f : 256 * (f + 1)]
        mine[f, 1:2] = ffn_gain[:, 256 * f : 256 * (f + 1)]
        mine[f, 2:3, 0:128] = gain_g[0:1]
        mine[f, 2:3, 128:256] = gain_g[1:2]
    plane_slot, ctx_slot = links.slots(8), links.slots(4)
    for f in fellows:
        links.send(mine.at[f], plane_stats.at[place.f], plane_slot + place.f, (f, place.c))
    plane_stats[place.f] = mine[place.f]

    qkv_plane.middle(0)
    for k in (10, 11):
        plane.combine(k)
    qkv_plane.middle(1)
    for k in (8, 9):
        end(k)
    for k in (6, 7):
        outs[k].forward(0)
    for k in (10, 11):
        end(k)
    for f in fellows:
        links.arrive(plane_stats.at[f], plane_slot + f)
    sums = plane_stats[0]
    for f in range(1, 8):
        sums += plane_stats[f]
    ctx_stats[place.c] = sums
    for device in (place.core_dev, place.y_dev, place.diag_dev):
        links.send(ctx_stats.at[place.c], ctx_stats.at[place.c], ctx_slot + place.c, device)

    final = [
        links.copy(out_all, out_all, final_slot, device)
        for device in (place.core_dev, place.y_dev)
    ]
    onward = links.copy(out_all, out_all, final_slot, place.core_dev)

    @pl.when(holds)
    def _():
        sums = out_mine[...].astype(F32)
        for other in range(3):
            links.arrive(out_z.at[other], root_slot + other)
            sums += out_z[other].astype(F32)
        out_all[...] = sums.astype(BF16)
        for made in final:
            made.start()

    for k in range(len(qkv_chunks)):
        total = qkv_plane.end(k)
        qkv_outs[k].begin(0, total)
        kept.append(links.local(total, qkv_all.at[place.c, qkv_rows[k]]))
    for k in range(8, count):
        outs[k].forward(0)
    relays = place.c_y == place.z

    @pl.when(jnp.logical_not(holds))
    def _():
        links.arrive(out_all, final_slot)

    @pl.when(relays)
    def _():
        onward.start()

    for c in (place.c_core, place.c_y, place.c_diag):
        links.arrive(ctx_stats.at[c], ctx_slot + c)
    stats[...] = ((ctx_stats[0] + ctx_stats[1]) + ctx_stats[2]) + ctx_stats[3]
    for out in qkv_outs:
        out.forward(0)
    for out in outs + qkv_outs:
        out.end()
    for made in kept:
        made.wait()
    links.finish()
    plane.finish()
    qkv_plane.finish()

    @pl.when(jnp.logical_not(holds))
    def _():
        to_root.wait_send()

    @pl.when(relays)
    def _():
        onward.wait_send()

    @pl.when(holds)
    def _():
        for made in final:
            made.wait_send()


def finish_kernel(
    gu_parts, dn_parts, out_s, qkv_parts, layer_s, input_s, stats,
    out, dn_out, out_out, qkv_out, layer_out, input_out, attn_out, ffn_out, pairs, sems,
):
    rows = gu_parts.shape[1]
    first = pl.multiple_of(pl.program_id(0) * rows, rows)
    sent = []
    for c in range(4):
        for f in range(8):
            b = 4 * f + c
            for side in range(2):
                column = 1024 * side + 128 * f
                block = gu_parts[c, :, column : column + 128]
                pairs[b, pl.ds(side, rows, stride=2), :] = block.astype(F32)
            made = pltpu.make_async_copy(
                pairs.at[b].reshape(rows, 2, 128),
                out.at[pl.ds(first, rows), :, pl.ds(128 * b, 128)],
                sems.at[b],
            )
            made.start()
            sent.append(made)
    dn_out[...] = dn_parts[...].astype(F32)
    out_out[...] = out_s[...].astype(F32)
    layer_out[...] = layer_s[...]
    input_out[...] = input_s[...]

    @pl.when(pl.program_id(0) == 0)
    def _():
        attn_out[...] = stats[0:1]
        ffn_out[...] = stats[1:2]
        for c in range(4):
            qkv_out[:, 256 * c : 256 * (c + 1)] = qkv_parts[c, 0:256].astype(F32).T
        for y in range(2):
            for j in range(2):
                from_row = 256 + 64 * j
                both = [qkv_parts[2 * y + core, from_row : from_row + 64] for core in range(2)]
                column = 1024 + 256 * j + 128 * y
                qkv_out[:, column : column + 128] = jnp.concatenate(both, axis=0).astype(F32).T

    for made in sent:
        made.wait()


def shaped(shape, kind=BF16):
    return jax.ShapeDtypeStruct(shape, kind)


def call(kernel, ins, outs, scratch=(), sems=None, number=None, flops=0):
    scratch = list(scratch)
    extra = {}
    if sems is not None:
        scratch += [pltpu.SemaphoreType.DMA((n,)) for n in sems]
        extra = dict(collective_id=number, has_side_effects=True)
    return pl.pallas_call(
        kernel,
        out_shape=tuple(shape for shape, _ in outs),
        in_specs=[spec for _, spec in ins],
        out_specs=tuple(spec for _, spec in outs),
        scratch_shapes=scratch,
        compiler_params=pltpu.CompilerParams(vmem_limit_bytes=VMEM_BYTES, **extra),
    )(*[array for array, _ in ins])


def split_heads(
    inputs,
    cotangent,
    lengths,
    qkv_weight,
    out_weight,
    gate_up,
    down_weight,
    attn_gain,
    ffn_gain,
    qk_gain,
):
    tokens, width = inputs.shape[1:]
    seq = tokens * 4
    source = inputs[0]
    rows, parts, units = gate_up.shape
    down_rows = down_weight.shape[0] // 4
    gain_s = jnp.concatenate(
        [attn_gain[None], ffn_gain[None], jnp.zeros((6, rows), BF16)], axis=0
    ).astype(F32)

    half_dim = HEAD_DIM // 2
    frequency = 10000.0 ** (-2.0 * np.arange(half_dim) / HEAD_DIM)
    turns = [np.arange(0, seq, 64)[:, None] * frequency, np.arange(64)[:, None] * frequency]
    signs = np.repeat([-1.0, 1.0, -1.0, 1.0], half_dim)
    angles = jnp.asarray(
        np.concatenate(
            [part for t in turns for part in (np.tile(np.cos(t), 4), np.tile(np.sin(t), 4) * signs)]
        ),
        F32,
    )
    table = pltpu.VMEM((seq, 128), F32)
    (
        qkv_w, out_w, gains, normed, qkv_raw, qkv_low, att_low, log_sums,
        gu_w, dn_w, dout_all, middle, mid_all, head_gain, key_bias,
    ) = call(
        forward_kernel,
        [(lengths, pl.BlockSpec(memory_space=pltpu.SMEM))]
        + [
            (a, HBM)
            for a in (qkv_weight, out_weight, gain_s, source, gate_up, down_weight, cotangent[0])
        ]
        + [(angles, VMEM), (qk_gain, VMEM)],
        [
            (shaped((8, rows, 384)), HBM),
            (shaped((2, out_weight.shape[0], width)), HBM),
            (shaped((8, width), F32), VMEM),
            (shaped((seq, width)), HBM),
            (shaped((3, seq, 128), F32), HBM),
            (shaped((3, seq, 128)), HBM),
            (shaped((2, seq, 128)), HBM),
            (shaped((2, seq, 128), F32), HBM),
            (shaped((8, rows, width)), HBM),
            (shaped((8, down_rows, width)), HBM),
            (shaped((4, tokens, width)), HBM),
            (shaped((tokens, width), F32), VMEM),
            (shaped((4, tokens, width)), HBM),
            (shaped((8, 128), F32), VMEM),
            (shaped((8, seq), F32), VMEM),
        ],
        [
            pltpu.VMEM((2, rows, 128), BF16),
            pltpu.VMEM((rows, 128), BF16),
            pltpu.VMEM((tokens, width), BF16),
            table,
            table,
            pltpu.VMEM((8, 8, rows), F32),
            pltpu.VMEM((8, rows, 384), BF16),
            pltpu.VMEM((2, out_weight.shape[0], width), BF16),
            pltpu.VMEM((4, tokens, width), BF16),
            pltpu.VMEM((seq, width), BF16),
            pltpu.VMEM((3, seq, 128), F32),
            pltpu.VMEM((3, seq, 128), BF16),
            pltpu.VMEM((2, seq, 128), BF16),
            pltpu.VMEM((2, seq, 128), F32),
            pltpu.VMEM((4, tokens, width), BF16),
            pltpu.VMEM((seq, 128), BF16),
            pltpu.VMEM((seq, 128), BF16),
            pltpu.VMEM((2, tokens, width), BF16),
            pltpu.VMEM((tokens, width), BF16),
            pltpu.VMEM((tokens, width), BF16),
            pltpu.VMEM((tokens, width), BF16),
            pltpu.VMEM((8, rows, 2, 128), BF16),
            pltpu.VMEM((2 * rows, 128), F32),
            pltpu.VMEM((rows, width), BF16),
        ],
        sems=(180, 170, 32),
        number=0,
    )
    qkv_w = qkv_w.reshape(width, 384)
    block = pltpu.VMEM((tokens, width), BF16)
    pair = pltpu.VMEM((2, tokens, width), BF16)
    whole = pltpu.VMEM((4, tokens, width), BF16)
    hidden_units = units // 4
    gu_g, dn_pair, ffn_part, d_middle, branch_s, ffn_gain_part = call(
        feed_kernel,
        [(a, HBM) for a in (gu_w, dn_w, dout_all, mid_all, middle)] + [(gains, VMEM)],
        [
            (shaped((4, 2, rows, width)), HBM),
            (shaped((4, down_rows, width)), HBM),
            (shaped((4, tokens, width)), HBM),
            (shaped((tokens, width), F32), HBM),
            (shaped((tokens, width)), HBM),
            (shaped((1, width), F32), VMEM),
        ],
        [
            pltpu.VMEM((8, rows, width), BF16),
            pltpu.VMEM((8, down_rows, width), BF16),
            whole,
            whole,
            pltpu.VMEM((seq, hidden_units), BF16),
            pltpu.VMEM((seq, parts * hidden_units), BF16),
            pltpu.VMEM((4, 2, down_rows, width), BF16),
            pltpu.VMEM((4, down_rows, width), BF16),
            pltpu.VMEM((2, rows, width), BF16),
            whole,
            pair,
            block,
            block,
            pltpu.VMEM((tokens, width), F32),
            pltpu.VMEM((tokens, width), F32),
            block,
        ],
        sems=(16, 16, 24),
        number=2,
    )
    step = 32
    count = (rows + down_rows) // step
    heads = pltpu.VMEM((seq, 128), BF16)
    gu_all, dn_all, layer_out, qkv_all, out_all, input_grad, stats = call(
        backward_kernel,
        [
            (gu_g, HBM),
            (dn_pair, HBM),
            (ffn_part, HBM),
            (middle, HBM),
            (d_middle, HBM),
            (branch_s, HBM),
            (source, HBM),
            (lengths, pl.BlockSpec(memory_space=pltpu.SMEM)),
            (gains, VMEM),
            (ffn_gain_part, VMEM),
            (angles, VMEM),
            (head_gain, VMEM),
            (key_bias, VMEM),
            (normed.reshape(4, tokens, width), HBM),
        ]
        + [(a, HBM) for a in (qkv_raw, qkv_low, att_low, log_sums, qkv_w, out_w)],
        [
            (shaped((4, rows, width)), HBM),
            (shaped((4, down_rows, width)), HBM),
            (shaped((tokens, width)), VMEM),
            (shaped((4, 384, rows)), HBM),
            (shaped((128, width)), VMEM),
            (shaped((tokens, width)), VMEM),
            (shaped((8, rows), F32), VMEM),
        ],
        [
            pltpu.VMEM((8, 4, step, width), BF16),
            pltpu.VMEM((rows // step, 4, step, width), BF16),
            pltpu.VMEM((count, 2, step, width), BF16),
            pltpu.VMEM((count, 2, step, width), BF16),
            block, pair, block, block, pair, block, block,
            pltpu.VMEM((tokens, width), F32),
            block,
            pltpu.VMEM((tokens, width), F32),
            pltpu.VMEM((4, tokens, width), BF16),
            pltpu.VMEM((4, tokens, width), BF16),
            table,
            table,
            pltpu.VMEM((3, seq, 128), F32),
            pltpu.VMEM((3, seq, 128), BF16),
            pltpu.VMEM((2, seq, 128), BF16),
            pltpu.VMEM((2, seq, 128), F32),
            pltpu.VMEM((width, 384), BF16),
            pltpu.VMEM((2, 128, width), BF16),
            heads,
            heads,
            pltpu.VMEM((2, seq, 128), BF16),
            pltpu.VMEM((3, seq, 128), BF16),
            table,
            table,
            pltpu.VMEM((8, 128), F32),
            pltpu.VMEM((4, 2, 384, rows), BF16),
            pltpu.VMEM((2, 4, 192, rows), BF16),
            pltpu.VMEM((2, 3, 192, rows), BF16),
            pltpu.VMEM((2, 128, width), BF16),
            pltpu.VMEM((128, width), BF16),
            pltpu.VMEM((3, 128, width), BF16),
            pltpu.VMEM((8, 8, rows), F32),
            pltpu.VMEM((8, 8, rows), F32),
            pltpu.VMEM((4, 8, rows), F32),
        ],
        sems=(190, 190, 70),
        number=1,
    )
    some = 64
    steps = rows // some
    few = down_rows // steps
    out_rows = out_weight.shape[0]
    block_of = lambda n: pl.BlockSpec((n, width), lambda i: (i, 0))
    fixed = lambda *shape: pl.BlockSpec(shape, lambda i: (0,) * len(shape))
    gate_up_grad, down_grad, out_grad, qkv_grad, layer_out, input_grad, attn_g, ffn_g = pl.pallas_call(
        finish_kernel,
        grid=(steps,),
        in_specs=[
            pl.BlockSpec((4, some, width), lambda i: (0, i, 0)),
            pl.BlockSpec((4, few, width), lambda i: (0, i, 0)),
            block_of(out_rows // steps),
            fixed(4, 384, rows),
            block_of(tokens // steps),
            block_of(tokens // steps),
            fixed(8, rows),
        ],
        out_specs=[
            HBM,
            pl.BlockSpec((4, few, width), lambda i: (0, i, 0)),
            block_of(out_rows // steps),
            fixed(rows, qkv_weight.shape[1]),
            block_of(tokens // steps),
            block_of(tokens // steps),
            fixed(1, rows),
            fixed(1, rows),
        ],
        out_shape=[
            shaped((rows, parts, units), F32),
            shaped((4, down_rows, width), F32),
            shaped((out_rows, width), F32),
            shaped((rows, qkv_weight.shape[1]), F32),
            shaped((tokens, width)),
            shaped((tokens, width)),
            shaped((1, rows), F32),
            shaped((1, rows), F32),
        ],
        scratch_shapes=[
            pltpu.VMEM((32, 2 * some, 128), F32),
            pltpu.SemaphoreType.DMA((32,)),
        ],
        compiler_params=pltpu.CompilerParams(vmem_limit_bytes=VMEM_BYTES),
    )(gu_all, dn_all, out_all, qkv_all, layer_out, input_grad, stats)
    return (
        layer_out[None],
        input_grad[None],
        qkv_grad,
        out_grad,
        gate_up_grad,
        down_grad.reshape(4 * down_rows, width),
        attn_g[0],
        ffn_g[0],
        jnp.stack([stats[2, :64] + stats[2, 64:128], stats[2, 128:192]]),
    )


def solution(mesh):
    sizes = (mesh.shape["fsdp"], mesh.shape["ctx"])
    return jax.shard_map(
        split_heads if sizes == (8, 4) else on_device,
        mesh=mesh,
        in_specs=(
            P("fsdp", "ctx", None),
            P("fsdp", "ctx", None),
            P("fsdp"),
            P("fsdp", None),
            P("fsdp", None),
            P("fsdp", None, None),
            P("fsdp", None),
            P("fsdp"),
            P("fsdp"),
            P(),
        ),
        out_specs=(
            P("fsdp", "ctx", None),
            P("fsdp", "ctx", None),
            P("fsdp", None),
            P("fsdp", None),
            P("fsdp", None, None),
            P("fsdp", None),
            P("fsdp"),
            P("fsdp"),
            P(),
        ),
        check_vma=False,
    )
```
